32 devices in a mesh: seq: 2 (over x), fsdp: 2 (over y), ctx: 8 (over z, core).
Axes of the slice: x: 2, y: 2, z: 4, core: 2. Of those that a mesh axis runs over, the one named last changes fastest.
Arguments:
- tokens: bfloat16 [4, 1024, 960], P(('seq', 'fsdp'), 'ctx'), may hold values from -6 to 6
- cotangent: bfloat16 [4, 1024, 960], P(('seq', 'fsdp'), 'ctx'), may hold values from -6 to 6
- block_order: int32 [16], replicated, may hold values from 0 to 15, each once
- gain_attn: float32 [960], replicated, may hold values from 0.5 to 1.5
- gain_mlp: float32 [960], replicated, may hold values from 0.5 to 1.5
- w_query: bfloat16 [960, 960], P(('seq', 'fsdp'), 'ctx'), may hold values from -0.1875 to 0.1875
- w_key: bfloat16 [960, 320], P(('seq', 'fsdp'), 'ctx'), may hold values from -0.1875 to 0.1875
- w_value: bfloat16 [960, 320], P(('seq', 'fsdp'), 'ctx'), may hold values from -0.1875 to 0.1875
- w_out: bfloat16 [960, 960], P(('seq', 'fsdp'), 'ctx'), may hold values from -3 to 3
- w_gate: bfloat16 [960, 2560], P(('seq', 'fsdp'), 'ctx'), may hold values from -0.1875 to 0.1875
- w_up: bfloat16 [960, 2560], P(('seq', 'fsdp'), 'ctx'), may hold values from -0.1875 to 0.1875
- w_down: bfloat16 [2560, 960], P(('seq', 'fsdp'), 'ctx'), may hold values from -0.125 to 0.125
Outputs:
- output: bfloat16 [4, 1024, 960], P(('seq', 'fsdp'), 'ctx')
- input_grad: bfloat16 [4, 1024, 960], P(('seq', 'fsdp'), 'ctx')
- gain_attn_grad: float32 [960], replicated
- gain_mlp_grad: float32 [960], replicated
- query_grad: float32 [960, 960], P(('seq', 'fsdp'), 'ctx')
- key_grad: float32 [960, 320], P(('seq', 'fsdp'), 'ctx')
- value_grad: float32 [960, 320], P(('seq', 'fsdp'), 'ctx')
- out_grad: float32 [960, 960], P(('seq', 'fsdp'), 'ctx')
- gate_grad: float32 [960, 2560], P(('seq', 'fsdp'), 'ctx')
- up_grad: float32 [960, 2560], P(('seq', 'fsdp'), 'ctx')
- down_grad: float32 [2560, 960], P(('seq', 'fsdp'), 'ctx')
The draws below stay inside these ranges and needn't reach their ends.
Inputs may be any that keep to these rules, and one draw needn't show every extreme that they name: block_order names each block number of one sequence once.
All inputs are finite; a program needn't handle non-finite values.
Results may differ from the reference program's by a relative error of at most 0.023.
Values may be sent and summed in bfloat16 or wider, within the bound.
A program may use at most 128 MiB of HBM per device.

```python
import math
import jax
import jax.numpy as jnp
from jax import lax

D = 960
HEADS = 15
KV_HEADS = 5
HEAD_DIM = 64
FF = 2560
BLK = 64
BLOCKS = 16
SEQ_LEN = 1024
SEQS = 4


def block_scale(stream_key, extent, split, low, high):
    factor_of, own = 1.0, jax.random.fold_in(stream_key, 6)
    for axis_at, shards_of in split:
        draws = jnp.exp(jax.random.uniform(jax.random.fold_in(own, axis_at), (shards_of,), jnp.float32, low / len(split), high / len(split)))
        factor_of = factor_of * jnp.repeat(draws, extent[axis_at] // shards_of).reshape([-1 if axis == axis_at else 1 for axis in range(len(extent))])
    return factor_of


def noise(own_key, dims, deviation, reach, split=(), kind=jnp.bfloat16):
    array = deviation * jax.random.normal(own_key, dims, jnp.float32)
    if split:
        array = array * block_scale(own_key, dims, split, -0.22, 0.18)
    return jnp.clip(array, -reach, reach).astype(kind)


def setup_inputs(seed: int = 0) -> dict:
    splits = jax.random.split(jax.random.key(seed), 13)
    tokens = noise(splits[0], (SEQS, SEQ_LEN, D), 1.0, 6.0, ((0, 4), (1, 8)))
    cotangent = noise(splits[1], (SEQS, SEQ_LEN, D), 1.0, 6.0, ((0, 4), (1, 8)))
    block_order = jax.random.permutation(splits[2], BLOCKS).astype(jnp.int32)
    gain_attn = jnp.clip(1.0 + 0.1 * jax.random.normal(splits[3], (D,), jnp.float32), 0.5, 1.5)
    gain_mlp = jnp.clip(1.0 + 0.1 * jax.random.normal(splits[4], (D,), jnp.float32), 0.5, 1.5)
    w_query = noise(splits[5], (D, HEADS * HEAD_DIM), D ** -0.5, 0.1875, ((0, 4), (1, 8)))
    w_key = noise(splits[6], (D, KV_HEADS * HEAD_DIM), D ** -0.5, 0.1875, ((0, 4), (1, 8)))
    w_value = noise(splits[7], (D, KV_HEADS * HEAD_DIM), D ** -0.5, 0.1875, ((0, 4), (1, 8)))
    w_out = noise(splits[8], (HEADS * HEAD_DIM, D), 4 ** -0.5, 3.0, ((0, 4), (1, 8)))
    w_gate = noise(splits[9], (D, FF), D ** -0.5, 0.1875, ((0, 4), (1, 8)))
    w_up = noise(splits[10], (D, FF), D ** -0.5, 0.1875, ((0, 4), (1, 8)))
    w_down = noise(splits[11], (FF, D), FF ** -0.5, 0.125, ((0, 4), (1, 8)))
    return {"tokens": tokens, "cotangent": cotangent, "block_order": block_order, "gain_attn": gain_attn, "gain_mlp": gain_mlp, "w_query": w_query, "w_key": w_key, "w_value": w_value, "w_out": w_out, "w_gate": w_gate, "w_up": w_up, "w_down": w_down}


rope_base = 100000.0
norm_eps = 1e-05

def rope_tables(positions, half_dim):
    freq_index = jnp.arange(half_dim, dtype=jnp.float32)
    inverse = rope_base ** (-freq_index / half_dim)
    angles = positions.astype(jnp.float32)[:, None] * inverse[None, :]
    return (jnp.cos(angles), jnp.sin(angles))

def rotate(values, cosine, sine):
    half_dim = values.shape[-1] // 2
    first_half = values[..., :half_dim]
    second_half = values[..., half_dim:]
    cos_part = cosine[:, None, :]
    sin_part = sine[:, None, :]
    return jnp.concatenate([first_half * cos_part - second_half * sin_part, second_half * cos_part + first_half * sin_part], axis=-1)

def rotate_back(grads, cosine, sine):
    half_dim = grads.shape[-1] // 2
    first_half = grads[..., :half_dim]
    second_half = grads[..., half_dim:]
    cos_part = cosine[:, None, :]
    sin_part = sine[:, None, :]
    return jnp.concatenate([first_half * cos_part + second_half * sin_part, second_half * cos_part - first_half * sin_part], axis=-1)

def as_rounded(values):
    return lax.optimization_barrier(values.astype(jnp.bfloat16)).astype(jnp.float32)

def norm_forward(values, gain):
    inverse_rms = lax.rsqrt(lax.optimization_barrier(jnp.mean(values * values, axis=1, keepdims=True)) + norm_eps)
    scaled = values * inverse_rms
    return (inverse_rms, scaled, (scaled * gain).astype(jnp.bfloat16))

def norm_backward(grad_in, inverse_rms, scaled, gain):
    weighted = grad_in * gain
    back = inverse_rms * (weighted - scaled * lax.optimization_barrier(jnp.mean(weighted * scaled, axis=1, keepdims=True)))
    return (back, lax.optimization_barrier(jnp.sum(grad_in * scaled, axis=0)))

def attend(query_rot, key_rot, value_b, positions):
    seq_len = query_rot.shape[0]
    block_rows = min(512, seq_len)
    num_blocks = seq_len // block_rows
    group_size = HEADS // KV_HEADS
    scale = 1.0 / math.sqrt(HEAD_DIM)
    key_all = key_rot.astype(jnp.float32).reshape(seq_len, KV_HEADS, HEAD_DIM)
    value_all = value_b.astype(jnp.float32).reshape(seq_len, KV_HEADS, HEAD_DIM)

    def one_block(carry, inputs):
        query_block, pos_block = inputs
        query_group = query_block.astype(jnp.float32).reshape(block_rows, KV_HEADS, group_size, HEAD_DIM)
        scores = jnp.einsum('rgjd,kgd->gjrk', query_group, key_all) * scale
        causal_mask = positions[None, :] <= pos_block[:, None]
        exp_sum = lax.optimization_barrier(jnp.sum(jnp.where(causal_mask, jnp.exp(scores), 0.0), axis=-1))
        log_total = jnp.log(exp_sum)
        prob_bf = as_rounded(jnp.where(causal_mask, jnp.exp(scores - log_total[..., None]), 0.0))
        attn_out = jnp.einsum('gjrk,kgd->rgjd', prob_bf, value_all)
        return (carry, (log_total, attn_out.reshape(block_rows, HEADS * HEAD_DIM).astype(jnp.bfloat16)))
    unused, (log_total, attn_out) = lax.scan(one_block, jnp.zeros((), jnp.float32), (query_rot.reshape(num_blocks, block_rows, HEADS * HEAD_DIM), positions.reshape(num_blocks, block_rows)))
    return (log_total, attn_out.reshape(seq_len, HEADS * HEAD_DIM))

def attend_back(query_rot, key_rot, value_b, attn_out, grad_out, log_total, positions):
    seq_len = query_rot.shape[0]
    block_rows = min(512, seq_len)
    num_blocks = seq_len // block_rows
    group_size = HEADS // KV_HEADS
    scale = 1.0 / math.sqrt(HEAD_DIM)
    key_all = key_rot.astype(jnp.float32).reshape(seq_len, KV_HEADS, HEAD_DIM)
    value_all = value_b.astype(jnp.float32).reshape(seq_len, KV_HEADS, HEAD_DIM)

    def one_block(carry, inputs):
        key_grad, value_grad = carry
        query_block, out_block, grad_block, log_block, pos_block = inputs
        query_group = query_block.astype(jnp.float32).reshape(block_rows, KV_HEADS, group_size, HEAD_DIM)
        grad_group = grad_block.astype(jnp.float32).reshape(block_rows, KV_HEADS, group_size, HEAD_DIM)
        out_group = out_block.astype(jnp.float32).reshape(block_rows, KV_HEADS, group_size, HEAD_DIM)
        row_delta = jnp.transpose(lax.optimization_barrier(jnp.sum(grad_group * out_group, axis=-1)), (1, 2, 0))
        scores = jnp.einsum('rgjd,kgd->gjrk', query_group, key_all) * scale
        causal_mask = positions[None, :] <= pos_block[:, None]
        probs_full = jnp.where(causal_mask, jnp.exp(scores - log_block[..., None]), 0.0)
        prob_bf = as_rounded(probs_full)
        prod_grad = jnp.einsum('rgjd,kgd->gjrk', grad_group, value_all)
        score_grad = as_rounded(probs_full * (prod_grad - row_delta[..., None]) * scale)
        query_grad = jnp.einsum('gjrk,kgd->rgjd', score_grad, key_all)
        key_grad = key_grad + jnp.einsum('gjrk,rgjd->kgd', score_grad, query_group)
        value_grad = value_grad + jnp.einsum('gjrk,rgjd->kgd', prob_bf, grad_group)
        return ((key_grad, value_grad), query_grad.reshape(block_rows, HEADS, HEAD_DIM))
    start_grads = (jnp.zeros((seq_len, KV_HEADS, HEAD_DIM), jnp.float32), jnp.zeros((seq_len, KV_HEADS, HEAD_DIM), jnp.float32))
    shaped = (query_rot.reshape(num_blocks, block_rows, HEADS * HEAD_DIM), attn_out.reshape(num_blocks, block_rows, HEADS * HEAD_DIM), grad_out.reshape(num_blocks, block_rows, HEADS * HEAD_DIM), log_total, positions.reshape(num_blocks, block_rows))
    (key_grad, value_grad), query_grad = lax.scan(one_block, start_grads, shaped)
    return (query_grad.reshape(seq_len, HEADS, HEAD_DIM), key_grad, value_grad)

def reference(tokens, cotangent, block_order, gain_attn, gain_mlp, w_query, w_key, w_value, w_out, w_gate, w_up, w_down):
    slot_index = jnp.arange(SEQ_LEN, dtype=jnp.int32)
    positions = (block_order[slot_index // BLK] * BLK + slot_index % BLK).astype(jnp.int32)
    cosine, sine = rope_tables(positions, HEAD_DIM // 2)

    def one_sequence(carry, inputs):
        token_seq, cot_seq = inputs
        token_f32 = token_seq.astype(jnp.float32)
        rms_attn, unit_attn, normed_attn = norm_forward(token_f32, gain_attn)
        query_raw = jnp.dot(normed_attn, w_query, preferred_element_type=jnp.float32).reshape(SEQ_LEN, HEADS, HEAD_DIM)
        key_raw = jnp.dot(normed_attn, w_key, preferred_element_type=jnp.float32).reshape(SEQ_LEN, KV_HEADS, HEAD_DIM)
        value_raw = jnp.dot(normed_attn, w_value, preferred_element_type=jnp.float32)
        query_rot = rotate(query_raw, cosine, sine).reshape(SEQ_LEN, HEADS * HEAD_DIM).astype(jnp.bfloat16)
        key_rot = rotate(key_raw, cosine, sine).reshape(SEQ_LEN, KV_HEADS * HEAD_DIM).astype(jnp.bfloat16)
        value_b = value_raw.astype(jnp.bfloat16)
        log_total, attn_bf = attend(query_rot, key_rot, value_b, positions)
        middle = token_f32 + jnp.dot(attn_bf, w_out, preferred_element_type=jnp.float32)
        rms_mlp, unit_mlp, normed_mlp = norm_forward(middle, gain_mlp)
        gate_pre = jnp.dot(normed_mlp, w_gate, preferred_element_type=jnp.float32)
        up_pre = jnp.dot(normed_mlp, w_up, preferred_element_type=jnp.float32)
        sigmoid_gate = jax.nn.sigmoid(gate_pre)
        silu_gate = gate_pre * sigmoid_gate
        hidden = (silu_gate * up_pre).astype(jnp.bfloat16)
        result = (middle + jnp.dot(hidden, w_down, preferred_element_type=jnp.float32)).astype(jnp.bfloat16)
        hidden_grad = jnp.dot(cot_seq, w_down.T, preferred_element_type=jnp.float32)
        down_part = jnp.dot(hidden.T, cot_seq, preferred_element_type=jnp.float32)
        gate_back = (hidden_grad * up_pre * sigmoid_gate * (1.0 + gate_pre * (1.0 - sigmoid_gate))).astype(jnp.bfloat16)
        up_back = (hidden_grad * silu_gate).astype(jnp.bfloat16)
        normed_mlp_grad = jnp.dot(gate_back, w_gate.T, preferred_element_type=jnp.float32) + jnp.dot(up_back, w_up.T, preferred_element_type=jnp.float32)
        gate_part = jnp.dot(normed_mlp.T, gate_back, preferred_element_type=jnp.float32)
        up_part = jnp.dot(normed_mlp.T, up_back, preferred_element_type=jnp.float32)
        mlp_back, gain_mlp_part = norm_backward(normed_mlp_grad, rms_mlp, unit_mlp, gain_mlp)
        middle_grad = cot_seq.astype(jnp.float32) + mlp_back
        middle_grad_b = middle_grad.astype(jnp.bfloat16)
        out_part = jnp.dot(attn_bf.T, middle_grad_b, preferred_element_type=jnp.float32)
        attn_back = jnp.dot(middle_grad_b, w_out.T, preferred_element_type=jnp.float32).astype(jnp.bfloat16)
        query_rot_grad, key_rot_grad, value_b_grad = attend_back(query_rot, key_rot, value_b, attn_bf, attn_back, log_total, positions)
        query_back = rotate_back(query_rot_grad, cosine, sine).reshape(SEQ_LEN, HEADS * HEAD_DIM).astype(jnp.bfloat16)
        key_back = rotate_back(key_rot_grad, cosine, sine).reshape(SEQ_LEN, KV_HEADS * HEAD_DIM).astype(jnp.bfloat16)
        value_back = value_b_grad.reshape(SEQ_LEN, KV_HEADS * HEAD_DIM).astype(jnp.bfloat16)
        normed_attn_grad = jnp.dot(query_back, w_query.T, preferred_element_type=jnp.float32)
        normed_attn_grad = normed_attn_grad + jnp.dot(key_back, w_key.T, preferred_element_type=jnp.float32)
        normed_attn_grad = normed_attn_grad + jnp.dot(value_back, w_value.T, preferred_element_type=jnp.float32)
        query_part = jnp.dot(normed_attn.T, query_back, preferred_element_type=jnp.float32)
        key_part = jnp.dot(normed_attn.T, key_back, preferred_element_type=jnp.float32)
        value_part = jnp.dot(normed_attn.T, value_back, preferred_element_type=jnp.float32)
        attn_norm_back, gain_attn_part = norm_backward(normed_attn_grad, rms_attn, unit_attn, gain_attn)
        input_back = (middle_grad + attn_norm_back).astype(jnp.bfloat16)
        parts = (gain_attn_part, gain_mlp_part, query_part, key_part, value_part, out_part, gate_part, up_part, down_part)
        new_carry = jax.tree.map(lambda summed, added: summed + added, carry, parts)
        return (new_carry, (result, input_back))
    start = (jnp.zeros((D,), jnp.float32), jnp.zeros((D,), jnp.float32), jnp.zeros(w_query.shape, jnp.float32), jnp.zeros(w_key.shape, jnp.float32), jnp.zeros(w_value.shape, jnp.float32), jnp.zeros(w_out.shape, jnp.float32), jnp.zeros(w_gate.shape, jnp.float32), jnp.zeros(w_up.shape, jnp.float32), jnp.zeros(w_down.shape, jnp.float32))
    totals, (outputs, input_grads) = lax.scan(one_sequence, start, (tokens, cotangent))
    return (outputs, input_grads, totals[0], totals[1], totals[2], totals[3], totals[4], totals[5], totals[6], totals[7], totals[8])
```

```python
import functools
import math

import jax
import jax.numpy as jnp
from jax import lax
from jax.experimental import pallas as pl
from jax.experimental.pallas import tpu as pltpu
from jax.sharding import PartitionSpec as P

HEADS = 15
KV_HEADS = 5
HEAD_DIM = 64
GROUP = HEADS // KV_HEADS
HALF = HEAD_DIM // 2
MESH = pl.DeviceIdType.MESH
MASKED = -1e30

rope_base = 100000.0
norm_eps = 1e-05
bf16 = jnp.bfloat16
f32 = jnp.float32


def norm_forward(values, gain):
    inverse_rms = lax.rsqrt(jnp.mean(values * values, axis=1, keepdims=True) + norm_eps)
    scaled = values * inverse_rms
    return (inverse_rms, scaled, (scaled * gain).astype(bf16))


def norm_backward(grad_in, inverse_rms, scaled, gain):
    weighted = grad_in * gain
    back = inverse_rms * (weighted - scaled * jnp.mean(weighted * scaled, axis=1, keepdims=True))
    return (back, jnp.sum(grad_in * scaled, axis=0))


def dot_nn(left, right):
    return jnp.dot(left, right, preferred_element_type=f32)


def dot_nt(left, right):
    return lax.dot_general(left, right, (((1,), (1,)), ((), ())), preferred_element_type=f32)


def dot_tn(left, right):
    return lax.dot_general(left, right, (((0,), (0,)), ((), ())), preferred_element_type=f32)


def wrap(index, count):
    return lax.rem(index + count, count)


class Place:
    def __init__(self, sizes):
        self.rows_outer, self.rows_inner, self.ctx = sizes
        self.row_parts = self.rows_outer * self.rows_inner
        self.chips = self.ctx // 2
        self.seq, self.fsdp, self.c = (lax.axis_index(n) for n in ("seq", "fsdp", "ctx"))
        self.row = self.seq * self.rows_inner + self.fsdp
        self.chip = self.c // 2
        self.core = self.c % 2

    def sibling(self):
        return (self.seq, self.fsdp, self.chip * 2 + 1 - self.core)

    def along(self, step):
        return (self.seq, self.fsdp, wrap(self.chip + step, self.chips) * 2 + self.core)

    def any_ctx(self, step):
        return (self.seq, self.fsdp, wrap(self.c + step, self.ctx))

    def across(self, step):
        row = wrap(self.row + step, self.row_parts)
        return (row // self.rows_inner, row % self.rows_inner, self.c)

    def chip_at(self, step):
        return wrap(self.chip + step, self.chips)

    def row_at(self, step):
        return wrap(self.row + step, self.row_parts)

    def greet(self, ctx=False, line=False, sibling=False, rows=False):
        devices = []
        if ctx:
            devices += [self.any_ctx(t) for t in range(1, self.ctx)]
        if line:
            devices += [self.along(t) for t in range(1, self.chips)]
        if sibling:
            devices += [self.sibling()]
        if rows:
            devices += [self.across(t) for t in range(1, self.row_parts)]
        barrier = pltpu.get_barrier_semaphore()
        for device in devices:
            pl.semaphore_signal(barrier, inc=1, device_id=device, device_id_type=MESH)
        pl.semaphore_wait(barrier, len(devices))


def remote(src, dst, send, recv, device):
    return pltpu.make_async_remote_copy(
        src_ref=src, dst_ref=dst, send_sem=send, recv_sem=recv, device_id=device, device_id_type=MESH
    )


def dma(*shape):
    return pltpu.SemaphoreType.DMA(shape)


class FullGather:
    def __init__(self, place, ref, out, sems):
        self.p, self.ref, self.out = place, ref, out
        self.zs, self.zr, self.xs, self.xr, self.bs, self.br = sems

    @staticmethod
    def scratch(sizes):
        chips, rows = sizes[2] // 2, sizes[0] * sizes[1]
        return [dma(chips), dma(chips), dma(chips, rows), dma(chips, rows), dma(chips, rows), dma(chips, rows)]

    def slot(self, step, row_step, core):
        return self.out.at[self.p.chip_at(-step) * 2 + core, self.p.row_at(-row_step)]

    def send_line(self, step):
        return remote(
            self.ref, self.slot(0, 0, self.p.core), self.zs.at[step], self.zr.at[step], self.p.along(step)
        )

    def recv_line(self, step):
        mine = self.slot(step, 0, self.p.core)
        return remote(mine, mine, self.zs.at[step], self.zr.at[step], self.p.along(step))

    def send_row(self, step, k):
        src = self.ref if step == 0 else self.slot(step, 0, self.p.core)
        return remote(
            src, self.slot(step, 0, self.p.core), self.xs.at[step, k], self.xr.at[step, k], self.p.across(k)
        )

    def recv_row(self, step, k):
        mine = self.slot(step, k, self.p.core)
        return remote(mine, mine, self.xs.at[step, k], self.xr.at[step, k], self.p.across(k))

    def send_sibling(self, step, k):
        src = self.ref if (step == 0 and k == 0) else self.slot(step, k, self.p.core)
        return remote(
            src, self.slot(step, k, self.p.core), self.bs.at[step, k], self.br.at[step, k], self.p.sibling()
        )

    def recv_sibling(self, step, k):
        mine = self.slot(step, k, 1 - self.p.core)
        return remote(mine, mine, self.bs.at[step, k], self.br.at[step, k], self.p.sibling())

    def start(self):
        for step in range(1, self.p.chips):
            self.send_line(step).start()
        for k in range(1, self.p.row_parts):
            self.send_row(0, k).start()
        self.send_sibling(0, 0).start()
        self.out[self.p.c, self.p.row] = self.ref[...]

    def forward_line(self, step):
        self.recv_line(step).wait_recv()
        for k in range(1, self.p.row_parts):
            self.send_row(step, k).start()
        self.send_sibling(step, 0).start()

    def forward_row(self, step):
        for k in range(1, self.p.row_parts):
            self.recv_row(step, k).wait_recv()
            self.send_sibling(step, k).start()

    def arrive(self):
        for step in range(self.p.chips):
            for k in range(self.p.row_parts):
                self.recv_sibling(step, k).wait_recv()

    def finish(self):
        for step in range(1, self.p.chips):
            self.send_line(step).wait_send()
        for step in range(self.p.chips):
            for k in range(1, self.p.row_parts):
                self.send_row(step, k).wait_send()
            for k in range(self.p.row_parts):
                self.send_sibling(step, k).wait_send()


class LineGather:
    def __init__(self, place, ref, out, sems):
        self.p, self.ref, self.out = place, ref, out
        self.zs, self.zr, self.bs, self.br = sems

    @staticmethod
    def scratch(sizes):
        chips = sizes[2] // 2
        return [dma(chips), dma(chips), dma(chips), dma(chips)]

    def slot(self, step, core):
        return self.out.at[self.p.chip_at(-step) * 2 + core]

    def send_line(self, step):
        return remote(self.ref, self.slot(0, self.p.core), self.zs.at[step], self.zr.at[step], self.p.along(step))

    def recv_line(self, step):
        mine = self.slot(step, self.p.core)
        return remote(mine, mine, self.zs.at[step], self.zr.at[step], self.p.along(step))

    def send_sibling(self, step, first=False):
        src = self.ref if first else self.slot(step, self.p.core)
        return remote(src, self.slot(step, self.p.core), self.bs.at[step], self.br.at[step], self.p.sibling())

    def recv_sibling(self, step):
        mine = self.slot(step, 1 - self.p.core)
        return remote(mine, mine, self.bs.at[step], self.br.at[step], self.p.sibling())

    def start(self):
        for step in range(1, self.p.chips):
            self.send_line(step).start()
        self.send_sibling(0, True).start()
        self.out[self.p.c] = self.ref[...]

    def forward(self, step):
        self.recv_line(step).wait_recv()
        self.send_sibling(step).start()

    def arrive(self):
        for step in range(self.p.chips):
            self.recv_sibling(step).wait_recv()

    def finish(self):
        for step in range(1, self.p.chips):
            self.send_line(step).wait_send()
        for step in range(self.p.chips):
            self.send_sibling(step).wait_send()


class RowExchange:
    def __init__(self, place, src_of, dst_of, sems):
        self.p, self.src_of, self.dst_of = place, src_of, dst_of
        self.xs, self.xr = sems

    @staticmethod
    def scratch(sizes):
        rows = sizes[0] * sizes[1]
        return [dma(rows), dma(rows)]

    def send(self, k):
        return remote(self.src_of(k), self.dst_of(k, 0), self.xs.at[k], self.xr.at[k], self.p.across(k))

    def recv(self, k):
        mine = self.dst_of(k, k)
        return remote(mine, mine, self.xs.at[k], self.xr.at[k], self.p.across(k))

    def start(self):
        for k in range(1, self.p.row_parts):
            self.send(k).start()

    def arrive(self):
        for k in range(1, self.p.row_parts):
            self.recv(k).wait_recv()

    def finish(self):
        for k in range(1, self.p.row_parts):
            self.send(k).wait_send()


class CtxExchange:
    def __init__(self, place, src_of, dst_of, sems):
        self.p, self.src_of, self.dst_of = place, src_of, dst_of
        self.ss, self.sr = sems

    @staticmethod
    def scratch(sizes):
        return [dma(sizes[2]), dma(sizes[2])]

    def send(self, t):
        return remote(
            self.src_of(wrap(self.p.c + t, self.p.ctx)),
            self.dst_of(self.p.c),
            self.ss.at[t],
            self.sr.at[t],
            self.p.any_ctx(t),
        )

    def recv(self, t):
        mine = self.dst_of(wrap(self.p.c - t, self.p.ctx))
        return remote(mine, mine, self.ss.at[t], self.sr.at[t], self.p.any_ctx(t))

    def start(self):
        for t in range(1, self.p.ctx):
            self.send(t).start()

    def arrive(self):
        for t in range(1, self.p.ctx):
            self.recv(t).wait_recv()

    def finish(self):
        for t in range(1, self.p.ctx):
            self.send(t).wait_send()


def take(refs, count):
    return [next(refs) for _ in range(count)]


def rotate_rows(rows, cosine, sine):
    first, second = rows[:HALF], rows[HALF:]
    return jnp.concatenate([first * cosine - second * sine, second * cosine + first * sine], axis=0)


def rotate_rows_back(rows, cosine, sine):
    first, second = rows[:HALF], rows[HALF:]
    return jnp.concatenate([first * cosine + second * sine, second * cosine - first * sine], axis=0)


def group_rows(ref, g):
    return jnp.concatenate(
        [ref[pl.ds((g * GROUP + j) * HEAD_DIM, HEAD_DIM), :] for j in range(GROUP)], axis=1
    )


def first_kernel(sizes, *refs):
    refs = iter(refs)
    (x_ref, gain_ref, wqkv_ref, wo_ref, wm_ref, wd_ref, cot_ref, cos_ref, sin_ref, posk_ref, posq_ref) = take(refs, 11)
    (attn_ref, q_ref, kv_ref, lse_ref, wqkv_full, wo_full, wm_full, wd_full, cot_full, n1_ref) = take(refs, 10)
    (qkv_raw, kv_own, wd_rows, score_ref) = take(refs, 4)
    qkv_sems, wo_sems = take(refs, 6), take(refs, 6)
    kv_sems, cot_sems = take(refs, 4), take(refs, 4)
    wm_sems, wd_sems, a2a_sems = take(refs, 2), take(refs, 2), take(refs, 2)

    place = Place(sizes)
    ctx, chips, row_parts = place.ctx, place.chips, place.row_parts
    tokens, width = x_ref.shape
    q_cols = HEADS * HEAD_DIM // ctx
    kv_cols = KV_HEADS * HEAD_DIM // ctx
    q_width, kv_width = HEADS * HEAD_DIM, KV_HEADS * HEAD_DIM
    qkv_cols = q_cols + 2 * kv_cols
    ff_part = wd_full.shape[1]
    per_row = ctx // row_parts

    qkv = FullGather(place, wqkv_ref, wqkv_full, qkv_sems)
    out = FullGather(place, wo_ref, wo_full, wo_sems)
    kv = LineGather(place, kv_own, kv_ref, kv_sems)
    cot = LineGather(place, cot_ref, cot_full, cot_sems)
    mlp = RowExchange(place, lambda k: wm_ref, lambda k, back: wm_full.at[place.row_at(-back)], wm_sems)
    down = RowExchange(place, lambda k: wd_ref, lambda k, back: wd_rows.at[place.row_at(-back)], wd_sems)

    def down_slice(c):
        return wd_rows.at[c // per_row, pl.ds(pl.multiple_of((c % per_row) * ff_part, 16), ff_part), :]

    spread = CtxExchange(place, down_slice, lambda c: wd_full.at[c], a2a_sems)

    place.greet(ctx=True, rows=True)
    qkv.start()
    values = x_ref[...].astype(f32)
    n1_ref[...] = norm_forward(values, gain_ref[...])[2]
    for step in range(1, chips):
        qkv.forward_line(step)
    for step in range(chips):
        qkv.forward_row(step)
    qkv.arrive()

    normed = n1_ref[...]
    for c in range(ctx):
        part = dot_nn(normed, wqkv_full[c].reshape(width, qkv_cols)).T
        qkv_raw[pl.ds(c * q_cols, q_cols), :] = part[:q_cols]
        qkv_raw[pl.ds(q_width + c * kv_cols, kv_cols), :] = part[q_cols : q_cols + kv_cols]
        qkv_raw[pl.ds(q_width + kv_width + c * kv_cols, kv_cols), :] = part[q_cols + kv_cols :]
    cosine, sine = cos_ref[...], sin_ref[...]
    for g in range(KV_HEADS):
        key = rotate_rows(qkv_raw[pl.ds(q_width + g * HEAD_DIM, HEAD_DIM), :], cosine, sine)
        value = qkv_raw[pl.ds(q_width + kv_width + g * HEAD_DIM, HEAD_DIM), :]
        pair = jnp.concatenate([key, value], axis=0).T
        kv_own[:, pl.ds(g * 2 * HEAD_DIM, 2 * HEAD_DIM)] = pair.astype(bf16)
    kv.start()
    out.start()
    down.start()
    mlp.start()
    wm_full[place.row] = wm_ref[...]
    wd_rows[place.row] = wd_ref[...]
    for h in range(HEADS):
        q_ref[pl.ds(h * HEAD_DIM, HEAD_DIM), :] = rotate_rows(
            qkv_raw[pl.ds(h * HEAD_DIM, HEAD_DIM), :], cosine, sine
        ).astype(bf16)
    for step in range(1, chips):
        kv.forward(step)
    cot.start()
    kv.arrive()

    scale = 1.0 / math.sqrt(HEAD_DIM)
    query_pos = posq_ref[...]
    chunk = 2 * tokens
    wide = GROUP * tokens
    for g in range(KV_HEADS):
        lanes = pl.ds(g * 2 * HEAD_DIM, 2 * HEAD_DIM)
        query = group_rows(q_ref, g) * jnp.asarray(scale, bf16)
        query = jnp.concatenate([query, jnp.zeros_like(query)], axis=0)

        def score(i, total, lanes=lanes, query=query):
            keys = kv_ref[pl.ds(2 * i, 2), :, lanes].reshape(chunk, 2 * HEAD_DIM)
            rows = pl.ds(pl.multiple_of(i * chunk, chunk), chunk)
            scores = jnp.where(posk_ref[rows, :] <= query_pos, dot_nn(keys, query), MASKED)
            score_ref[rows, :] = scores
            return total + jnp.sum(jnp.exp(scores), axis=0, keepdims=True)

        log_total = jnp.log(lax.fori_loop(0, chips, score, jnp.zeros((1, wide), f32)))
        lse_ref[g] = log_total

        def gather_values(i, total, lanes=lanes, log_total=log_total):
            keys = kv_ref[pl.ds(2 * i, 2), :, lanes].reshape(chunk, 2 * HEAD_DIM)
            rows = pl.ds(pl.multiple_of(i * chunk, chunk), chunk)
            prob = jnp.exp(score_ref[rows, :] - log_total).astype(bf16)
            return total + dot_tn(keys, prob)

        total = lax.fori_loop(0, chips, gather_values, jnp.zeros((2 * HEAD_DIM, wide), f32))
        for j in range(GROUP):
            attn_ref[pl.ds((g * GROUP + j) * HEAD_DIM, HEAD_DIM), :] = total[
                HEAD_DIM:, j * tokens : (j + 1) * tokens
            ].astype(bf16)
        if g == 0:
            down.arrive()
            spread.start()
            wd_full[place.c] = down_slice(place.c)[...]
            for step in range(1, chips):
                out.forward_line(step)
        if g == 2:
            for step in range(1, chips):
                cot.forward(step)
        if g == 3:
            for step in range(chips):
                out.forward_row(step)
    mlp.arrive()
    out.arrive()
    cot.arrive()
    spread.arrive()
    for part in (qkv, kv, out, mlp, down, cot, spread):
        part.finish()


def mlp_kernel(sizes, *refs):
    refs = iter(refs)
    n_ref, cot_ref, wm_ref, wd_ref = take(refs, 4)
    ngrad_ref, osum_ref, dwm_ref, dwd_ref = take(refs, 4)
    n_all, gub_all, hid_all, part_ref, sib_ref, far_ref = take(refs, 6)
    n_sems = take(refs, 4)
    bs, br, zs, zr = take(refs, 4)

    place = Place(sizes)
    ctx, chips = place.ctx, place.chips
    tokens, width = n_ref.shape
    ff = wd_ref.shape[0]
    chunk = 2 * tokens
    gather = LineGather(place, n_ref, n_all, n_sems)

    place.greet(line=True, sibling=True)
    gather.start()

    def work(j):
        p = place.chip_at(-j)
        rows = pl.ds(pl.multiple_of(p * chunk, chunk), chunk)
        normed = n_all[pl.ds(2 * p, 2)].reshape(chunk, width)
        cot = cot_ref[pl.ds(2 * p, 2)].reshape(chunk, width)
        gate_up = dot_nn(normed, wm_ref[...])
        gate, up = gate_up[:, :ff], gate_up[:, ff:]
        sigmoid_gate = jax.nn.sigmoid(gate)
        silu_gate = gate * sigmoid_gate
        hidden = (silu_gate * up).astype(bf16)
        hidden_grad = dot_nt(cot, wd_ref[...])
        gate_back = hidden_grad * up * sigmoid_gate * (1.0 + gate * (1.0 - sigmoid_gate))
        up_back = hidden_grad * silu_gate
        both = jnp.concatenate([gate_back, up_back], axis=1).astype(bf16)
        gub_all[rows, :] = both
        hid_all[rows, :] = hidden
        part_ref[j, :, 0] = dot_nt(both, wm_ref[...]).astype(bf16).reshape(2, tokens, width)
        part_ref[j, :, 1] = dot_nn(hidden, wd_ref[...]).astype(bf16).reshape(2, tokens, width)
        to_sibling(j).start()

    def to_sibling(j):
        return remote(part_ref.at[j, 1 - place.core], sib_ref.at[j], bs.at[j], br.at[j], place.sibling())

    def to_owner(j):
        return remote(part_ref.at[j, place.core], far_ref.at[j], zs.at[j], zr.at[j], place.along(-j))

    def settle(j):
        to_sibling(j).wait_recv()
        both = part_ref[j, place.core].astype(f32) + sib_ref[j].astype(f32)
        part_ref[j, place.core] = both.astype(bf16)

    gather.recv_sibling(0).wait_recv()
    work(0)

    def turn(j, carry):
        gather.recv_line(j).wait_recv()
        gather.send_sibling(j).start()
        gather.recv_sibling(j).wait_recv()
        work(j)

        @pl.when(j >= 2)
        def _():
            settle(j - 1)
            to_owner(j - 1).start()

        return carry

    lax.fori_loop(1, chips, turn, 0)
    settle(chips - 1)
    to_owner(chips - 1).start()
    settle(0)
    seq = ctx * tokens
    dwm_ref[...] = dot_tn(n_all[...].reshape(seq, width), gub_all[...]).astype(bf16)
    dwd_ref[...] = dot_tn(hid_all[...], cot_ref[...].reshape(seq, width)).astype(bf16)

    own = part_ref[0, place.core].astype(f32)
    grad_sum, out_sum = own[0], own[1]
    for j in range(1, chips):
        to_owner(j).wait_recv()
        grad_sum = grad_sum + far_ref[j, 0].astype(f32)
        out_sum = out_sum + far_ref[j, 1].astype(f32)
    ngrad_ref[...] = grad_sum
    osum_ref[...] = out_sum
    gather.finish()
    for j in range(chips):
        to_sibling(j).wait_send()
        if j:
            to_owner(j).wait_send()


def back_kernel(sizes, *refs):
    refs = iter(refs)
    (q_ref, g_ref, attn_ref, kv_ref, lse_ref, cos_ref, sin_ref, posk_ref, posq_ref, dwm_ref, dwd_ref) = take(refs, 11)
    qback_ref, kvsum_ref, fin_mlp, fin_down = take(refs, 4)
    delta_ref, qz_ref, gz_ref, acc_ref, part_ref, sib_ref, far_ref = take(refs, 7)
    dwm_recv, down_rows, down_recv = take(refs, 3)
    bs, br, zs, zr = take(refs, 4)
    wm_sems, a2a_sems, wd_sems = take(refs, 2), take(refs, 2), take(refs, 2)

    place = Place(sizes)
    ctx, chips, row_parts = place.ctx, place.chips, place.row_parts
    tokens = q_ref.shape[1]
    chunk, wide = 2 * tokens, GROUP * tokens
    ff_part = dwd_ref.shape[1]
    per_row = ctx // row_parts
    scale = 1.0 / math.sqrt(HEAD_DIM)

    mlp = RowExchange(place, lambda k: dwm_ref.at[place.row_at(k)], lambda k, back: dwm_recv.at[k], wm_sems)

    def down_slot(c):
        return down_rows.at[c // per_row, pl.ds(pl.multiple_of((c % per_row) * ff_part, 16), ff_part), :]

    spread = CtxExchange(place, lambda c: dwd_ref.at[c], down_slot, a2a_sems)
    down = RowExchange(place, lambda k: down_rows.at[place.row_at(k)], lambda k, back: down_recv.at[k], wd_sems)

    place.greet(ctx=True, rows=True)
    mlp.start()
    spread.start()
    down_slot(place.c)[...] = dwd_ref[place.c]

    zeros = jnp.zeros((HEAD_DIM, wide), bf16)
    for g in range(KV_HEADS):
        query = group_rows(q_ref, g) * jnp.asarray(scale, bf16)
        grad = group_rows(g_ref, g)
        qz_ref[g] = jnp.concatenate([query, zeros], axis=0)
        gz_ref[g] = jnp.concatenate([zeros, grad], axis=0)
        delta_ref[g] = jnp.sum(grad.astype(f32) * group_rows(attn_ref, g).astype(f32), axis=0, keepdims=True)
        acc_ref[g] = jnp.zeros_like(acc_ref[g])
    query_pos = posq_ref[...]

    def to_sibling(j):
        return remote(part_ref.at[j, 1 - place.core], sib_ref.at[j], bs.at[j], br.at[j], place.sibling())

    def to_owner(j):
        return remote(part_ref.at[j, place.core], far_ref.at[j], zs.at[j], zr.at[j], place.along(j))

    def settle(j):
        to_sibling(j).wait_recv()
        both = part_ref[j, place.core].astype(f32) + sib_ref[j].astype(f32)
        part_ref[j, place.core] = both.astype(bf16)

    def work(j):
        p = place.chip_at(j)
        rows = pl.ds(pl.multiple_of(p * chunk, chunk), chunk)
        allowed = posk_ref[rows, :] <= query_pos
        for g in range(KV_HEADS):
            lanes = pl.ds(g * 2 * HEAD_DIM, 2 * HEAD_DIM)
            keys = kv_ref[pl.ds(2 * p, 2), :, lanes].reshape(chunk, 2 * HEAD_DIM)
            query, grad = qz_ref[g], gz_ref[g]
            scores = jnp.where(allowed, dot_nn(keys, query), MASKED)
            prob = jnp.exp(scores - lse_ref[g])
            score_grad = (prob * (dot_nn(keys, grad) - delta_ref[g])).astype(bf16)
            both = dot_nt(score_grad, query) + dot_nt(prob.astype(bf16), grad)
            part_ref[j, :, :, lanes] = both.astype(bf16).reshape(2, tokens, 2 * HEAD_DIM)
            acc_ref[g] += dot_tn(keys, score_grad)
        to_sibling(j).start()

    work(1)

    def turn(j, carry):
        work(j)
        settle(j - 1)
        to_owner(j - 1).start()
        return carry

    lax.fori_loop(2, chips, turn, 0)
    spread.arrive()
    down.start()
    work(0)
    settle(chips - 1)
    to_owner(chips - 1).start()
    cosine, sine = cos_ref[...], sin_ref[...]
    for h in range(HEADS):
        g, j = h // GROUP, h % GROUP
        head = acc_ref[g, pl.ds(0, HEAD_DIM), pl.ds(j * tokens, tokens)] * scale
        qback_ref[pl.ds(h * HEAD_DIM, HEAD_DIM), :] = rotate_rows_back(head, cosine, sine).astype(bf16)
    settle(0)
    mlp.arrive()
    total = dwm_ref[place.row].astype(f32)
    for k in range(1, row_parts):
        total = total + dwm_recv[k].astype(f32)
    fin_mlp[...] = total
    total = part_ref[0, place.core].astype(f32)
    for j in range(1, chips):
        to_owner(j).wait_recv()
        total = total + far_ref[j].astype(f32)
    kvsum_ref[...] = total
    down.arrive()
    total = down_rows[place.row].astype(f32)
    for k in range(1, row_parts):
        total = total + down_recv[k].astype(f32)
    fin_down[...] = total
    for part in (mlp, spread, down):
        part.finish()
    for j in range(chips):
        to_sibling(j).wait_send()
        if j:
            to_owner(j).wait_send()


def last_kernel(sizes, *refs):
    refs = iter(refs)
    part_ref, gain_ref = take(refs, 2)
    fin_ref, gain_out = take(refs, 2)
    sib_ref, row_ref, far_send, far_ref = take(refs, 4)
    gain_sib, gain_row, gain_far, gain_a, gain_b, gain_c = take(refs, 6)
    bs, br, xs, xr, zs, zr = take(refs, 6)
    gb, gx, gz = take(refs, 2), take(refs, 2), take(refs, 2)

    place = Place(sizes)
    chips, row_parts = place.chips, place.row_parts
    place.greet(line=True, sibling=True, rows=True)

    def to_sibling(j):
        return remote(
            part_ref.at[place.chip_at(j) * 2 + 1 - place.core], sib_ref.at[j], bs.at[j], br.at[j], place.sibling()
        )

    def to_row(j, k):
        return remote(
            sib_ref.at[j, place.row_at(k)], row_ref.at[j, k], xs.at[j, k], xr.at[j, k], place.across(k)
        )

    def to_owner(j):
        return remote(far_send.at[j], far_ref.at[j], zs.at[j], zr.at[j], place.along(j))

    order = list(range(1, chips)) + [0]
    for j in order:
        to_sibling(j).start()

    core, row, chip = place.core, place.row, place.chip
    gain_a[...] = gain_ref[...]
    gain_sib[core] = gain_a[...]

    def g_sib():
        return remote(gain_a, gain_sib.at[core], gb[0].at[0], gb[1].at[0], place.sibling())

    def g_row(k):
        return remote(gain_b, gain_row.at[row], gx[0].at[k], gx[1].at[k], place.across(k))

    def g_far(j):
        return remote(gain_c, gain_far.at[chip], gz[0].at[j], gz[1].at[j], place.along(j))

    g_sib().start()

    for j in order:
        to_sibling(j).wait_recv()
        both = part_ref[place.chip_at(j) * 2 + core].astype(f32) + sib_ref[j].astype(f32)
        sib_ref[j] = both.astype(bf16)
        for k in range(1, row_parts):
            to_row(j, k).start()
    remote(gain_a, gain_sib.at[1 - core], gb[0].at[0], gb[1].at[0], place.sibling()).wait_recv()
    gain_b[...] = gain_sib[0] + gain_sib[1]
    gain_row[row] = gain_b[...]
    for k in range(1, row_parts):
        g_row(k).start()

    own = None
    for j in order:
        total = sib_ref[j, row].astype(f32)
        for k in range(1, row_parts):
            to_row(j, k).wait_recv()
            total = total + row_ref[j, k].astype(f32)
        if j:
            far_send[j] = total.astype(bf16)
            to_owner(j).start()
        else:
            fin_ref[...] = total
    for k in range(1, row_parts):
        remote(gain_b, gain_row.at[place.row_at(-k)], gx[0].at[k], gx[1].at[k], place.across(k)).wait_recv()
    total = gain_row[0]
    for k in range(1, row_parts):
        total = total + gain_row[k]
    gain_c[...] = total
    gain_far[chip] = gain_c[...]
    for j in range(1, chips):
        g_far(j).start()
    total = fin_ref[...]
    for j in range(1, chips):
        to_owner(j).wait_recv()
        total = total + far_ref[j].astype(f32)
    fin_ref[...] = total
    for j in range(1, chips):
        remote(gain_c, gain_far.at[place.chip_at(-j)], gz[0].at[j], gz[1].at[j], place.along(j)).wait_recv()
    total = gain_far[0]
    for j in range(1, chips):
        total = total + gain_far[j]
    gain_out[...] = total

    g_sib().wait_send()
    for k in range(1, row_parts):
        g_row(k).wait_send()
    for j in range(1, chips):
        g_far(j).wait_send()
    for j in order:
        to_sibling(j).wait_send()
        for k in range(1, row_parts):
            to_row(j, k).wait_send()
        if j:
            to_owner(j).wait_send()


def call(kernel, sizes, inputs, outs, scratch, collective_id):
    vmem = pl.BlockSpec(memory_space=pltpu.VMEM)
    return pl.pallas_call(
        functools.partial(kernel, sizes),
        out_shape=[jax.ShapeDtypeStruct(shape, kind) for shape, kind in outs],
        in_specs=[vmem] * len(inputs),
        out_specs=[vmem] * len(outs),
        scratch_shapes=scratch,
        compiler_params=pltpu.CompilerParams(
            collective_id=collective_id, has_side_effects=True, vmem_limit_bytes=60 * 1024 * 1024
        ),
    )(*inputs)


def on_device(
    tokens,
    cotangent,
    block_order,
    gain_attn,
    gain_mlp,
    w_query,
    w_key,
    w_value,
    w_out,
    w_gate,
    w_up,
    w_down,
):
    sizes = tuple(lax.axis_size(n) for n in ("seq", "fsdp", "ctx"))
    rows, ctx = sizes[0] * sizes[1], sizes[2]
    chips = ctx // 2
    row_count, width = tokens.shape[1], tokens.shape[2]
    seq_len = row_count * ctx
    block_total = block_order.shape[0]
    block_len = seq_len // block_total
    kv_width = KV_HEADS * HEAD_DIM
    q_width = HEADS * HEAD_DIM
    q_cols, kv_cols, ff_cols = w_query.shape[1], w_key.shape[1], w_gate.shape[1]
    out_cols, down_cols, down_rows = w_out.shape[1], w_down.shape[1], w_down.shape[0]
    in_rows = w_query.shape[0]
    qkv_cols = q_cols + 2 * kv_cols
    wide = GROUP * row_count

    slot_index = jnp.arange(seq_len, dtype=jnp.int32)
    owner_hit = (slot_index // block_len)[:, None] == jnp.arange(block_total, dtype=jnp.int32)[None, :]
    all_pos = (
        jnp.sum(jnp.where(owner_hit, block_order[None, :], 0), axis=1) * block_len + slot_index % block_len
    )
    own_pos = lax.dynamic_slice_in_dim(all_pos, lax.axis_index("ctx") * row_count, row_count)
    inverse = rope_base ** (-jnp.arange(HALF, dtype=f32) / HALF)
    angles = inverse[:, None] * own_pos.astype(f32)[None, :]
    cosine, sine = jnp.cos(angles), jnp.sin(angles)
    pos_keys = all_pos[:, None]
    pos_query = jnp.tile(own_pos, GROUP)[None, :]

    x = tokens[0]
    cot_rows = cotangent[0]
    w_qkv = jnp.concatenate([w_query, w_key, w_value], axis=1)
    w_mlp = jnp.concatenate([w_gate, w_up], axis=1)

    attn_t, query_t, kv_all, lse, qkv_full, out_full, mlp_full, down_full, cot_all, normed_attn = call(
        first_kernel,
        sizes,
        (x, gain_attn[None], w_qkv, w_out, w_mlp, w_down, cot_rows, cosine, sine, pos_keys, pos_query),
        [
            ((q_width, row_count), bf16),
            ((q_width, row_count), bf16),
            ((ctx, row_count, 2 * kv_width), bf16),
            ((KV_HEADS, 1, wide), f32),
            ((ctx, rows, in_rows, qkv_cols), bf16),
            ((ctx, rows, in_rows, out_cols), bf16),
            ((rows, in_rows, 2 * ff_cols), bf16),
            ((ctx, ff_cols, down_cols), bf16),
            ((ctx, row_count, width), bf16),
            ((row_count, width), bf16),
        ],
        [
            pltpu.VMEM((q_width + 2 * kv_width, row_count), f32),
            pltpu.VMEM((row_count, 2 * kv_width), bf16),
            pltpu.VMEM((rows, down_rows, down_cols), bf16),
            pltpu.VMEM((seq_len, wide), f32),
        ]
        + FullGather.scratch(sizes)
        + FullGather.scratch(sizes)
        + LineGather.scratch(sizes)
        + LineGather.scratch(sizes)
        + RowExchange.scratch(sizes)
        + RowExchange.scratch(sizes)
        + CtxExchange.scratch(sizes),
        1,
    )

    token_f32 = x.astype(f32)
    rms_attn, unit_attn, _ = norm_forward(token_f32, gain_attn)
    out_cat = jnp.transpose(out_full.reshape(ctx, q_width, out_cols), (1, 0, 2)).reshape(q_width, width)
    middle = token_f32 + dot_tn(attn_t, out_cat)
    rms_mlp, unit_mlp, normed_mlp = norm_forward(middle, gain_mlp)
    w_mlp_cat = mlp_full.reshape(width, 2 * ff_cols)
    down_cat = jnp.transpose(down_full, (1, 0, 2)).reshape(ff_cols, width)

    pair = pltpu.VMEM((chips, 2, row_count, width), bf16)
    normed_mlp_grad, output_sum, d_mlp, d_down = call(
        mlp_kernel,
        sizes,
        (normed_mlp, cot_all, w_mlp_cat, down_cat),
        [
            ((row_count, width), f32),
            ((row_count, width), f32),
            ((width, 2 * ff_cols), bf16),
            ((ff_cols, width), bf16),
        ],
        [
            pltpu.VMEM((ctx, row_count, width), bf16),
            pltpu.VMEM((seq_len, 2 * ff_cols), bf16),
            pltpu.VMEM((seq_len, ff_cols), bf16),
            pltpu.VMEM((chips, 2, 2, row_count, width), bf16),
            pair,
            pair,
        ]
        + LineGather.scratch(sizes)
        + [dma(chips)] * 4,
        2,
    )
    result = (middle + output_sum).astype(bf16)

    mlp_back, gain_mlp_part = norm_backward(normed_mlp_grad, rms_mlp, unit_mlp, gain_mlp)
    middle_grad = cot_rows.astype(f32) + mlp_back
    middle_grad_b = middle_grad.astype(bf16)
    attn_back_t = dot_nt(out_cat, middle_grad_b).astype(bf16)
    d_down_pieces = jnp.transpose(d_down.reshape(ff_cols, ctx, down_cols), (1, 0, 2))

    query_back_t, kv_sum, fin_mlp, fin_down = call(
        back_kernel,
        sizes,
        (
            query_t,
            attn_back_t,
            attn_t,
            kv_all,
            lse,
            cosine,
            sine,
            pos_keys,
            pos_query,
            d_mlp.reshape(rows, in_rows, 2 * ff_cols),
            d_down_pieces,
        ),
        [
            ((q_width, row_count), bf16),
            ((row_count, 2 * kv_width), f32),
            ((in_rows, 2 * ff_cols), f32),
            ((down_rows, down_cols), f32),
        ],
        [
            pltpu.VMEM((KV_HEADS, 1, wide), f32),
            pltpu.VMEM((KV_HEADS, 2 * HEAD_DIM, wide), bf16),
            pltpu.VMEM((KV_HEADS, 2 * HEAD_DIM, wide), bf16),
            pltpu.VMEM((KV_HEADS, 2 * HEAD_DIM, wide), f32),
            pltpu.VMEM((chips, 2, row_count, 2 * kv_width), bf16),
            pltpu.VMEM((chips, row_count, 2 * kv_width), bf16),
            pltpu.VMEM((chips, row_count, 2 * kv_width), bf16),
            pltpu.VMEM((rows, in_rows, 2 * ff_cols), bf16),
            pltpu.VMEM((rows, down_rows, down_cols), bf16),
            pltpu.VMEM((rows, down_rows, down_cols), bf16),
        ]
        + [dma(chips)] * 4
        + RowExchange.scratch(sizes)
        + CtxExchange.scratch(sizes)
        + RowExchange.scratch(sizes),
        3,
    )

    kv_t = jnp.transpose(kv_sum).reshape(KV_HEADS, 2, 2, HALF, row_count)
    key_back_t = jnp.stack(
        [
            kv_t[:, 0, 0] * cosine + kv_t[:, 0, 1] * sine,
            kv_t[:, 0, 1] * cosine - kv_t[:, 0, 0] * sine,
        ],
        axis=1,
    ).astype(bf16)
    key_back_t = key_back_t.reshape(kv_width, row_count)
    value_back_t = kv_t[:, 1].astype(bf16).reshape(kv_width, row_count)
    qkv_back_t = jnp.concatenate(
        [
            query_back_t.reshape(ctx, q_cols, row_count),
            key_back_t.reshape(ctx, kv_cols, row_count),
            value_back_t.reshape(ctx, kv_cols, row_count),
        ],
        axis=1,
    )
    qkv_w = qkv_full.reshape(ctx, width, qkv_cols)
    normed_attn_grad = jnp.einsum("cft,cdf->td", qkv_back_t, qkv_w, preferred_element_type=f32)
    qkv_part = jnp.einsum("td,cft->cdf", normed_attn, qkv_back_t, preferred_element_type=f32)
    out_part = jnp.einsum(
        "dt,tcf->cdf",
        attn_t,
        middle_grad_b.reshape(row_count, ctx, out_cols),
        preferred_element_type=f32,
    )
    attn_part = jnp.concatenate([qkv_part.astype(bf16), out_part.astype(bf16)], axis=2)
    attn_norm_back, gain_attn_part = norm_backward(normed_attn_grad, rms_attn, unit_attn, gain_attn)
    input_back = (middle_grad + attn_norm_back).astype(bf16)

    attn_cols = qkv_cols + out_cols
    gains = pltpu.VMEM((2, width), f32)
    fin_attn, gain_sums = call(
        last_kernel,
        sizes,
        (attn_part.reshape(ctx, rows, in_rows, attn_cols), jnp.stack([gain_attn_part, gain_mlp_part])),
        [((in_rows, attn_cols), f32), ((2, width), f32)],
        [
            pltpu.VMEM((chips, rows, in_rows, attn_cols), bf16),
            pltpu.VMEM((chips, rows, in_rows, attn_cols), bf16),
            pltpu.VMEM((chips, in_rows, attn_cols), bf16),
            pltpu.VMEM((chips, in_rows, attn_cols), bf16),
            pltpu.VMEM((2, 2, width), f32),
            pltpu.VMEM((rows, 2, width), f32),
            pltpu.VMEM((chips, 2, width), f32),
            gains,
            gains,
            gains,
            dma(chips),
            dma(chips),
            dma(chips, rows),
            dma(chips, rows),
            dma(chips),
            dma(chips),
            dma(1),
            dma(1),
            dma(rows),
            dma(rows),
            dma(chips),
            dma(chips),
        ],
        4,
    )
    return (
        result.reshape(1, row_count, width),
        input_back.reshape(1, row_count, width),
        gain_sums[0],
        gain_sums[1],
        fin_attn[:, :q_cols],
        fin_attn[:, q_cols : q_cols + kv_cols],
        fin_attn[:, q_cols + kv_cols : qkv_cols],
        fin_attn[:, qkv_cols:attn_cols],
        fin_mlp[:, :ff_cols],
        fin_mlp[:, ff_cols:],
        fin_down,
    )


def solution(mesh):
    return jax.shard_map(
        on_device,
        mesh=mesh,
        in_specs=(
            P(("seq", "fsdp"), "ctx", None),
            P(("seq", "fsdp"), "ctx", None),
            P(),
            P(),
            P(),
            P(("seq", "fsdp"), "ctx"),
            P(("seq", "fsdp"), "ctx"),
            P(("seq", "fsdp"), "ctx"),
            P(("seq", "fsdp"), "ctx"),
            P(("seq", "fsdp"), "ctx"),
            P(("seq", "fsdp"), "ctx"),
            P(("seq", "fsdp"), "ctx"),
        ),
        out_specs=(
            P(("seq", "fsdp"), "ctx", None),
            P(("seq", "fsdp"), "ctx", None),
            P(),
            P(),
            P(("seq", "fsdp"), "ctx"),
            P(("seq", "fsdp"), "ctx"),
            P(("seq", "fsdp"), "ctx"),
            P(("seq", "fsdp"), "ctx"),
            P(("seq", "fsdp"), "ctx"),
            P(("seq", "fsdp"), "ctx"),
            P(("seq", "fsdp"), "ctx"),
        ),
        check_vma=False,
    )
```

```python
import functools
import math

import jax
import jax.numpy as jnp
from jax import lax
from jax.experimental import pallas as pl
from jax.experimental.pallas import tpu as pltpu
from jax.sharding import PartitionSpec as P

HEADS = 15
KV_HEADS = 5
HEAD_DIM = 64
GROUP = HEADS // KV_HEADS
HALF = HEAD_DIM // 2
MESH = pl.DeviceIdType.MESH
MASKED = -1e30

rope_base = 100000.0
norm_eps = 1e-05
bf16 = jnp.bfloat16
f32 = jnp.float32


def norm_forward(values, gain):
    inverse_rms = lax.rsqrt(jnp.mean(values * values, axis=1, keepdims=True) + norm_eps)
    scaled = values * inverse_rms
    return (inverse_rms, scaled, (scaled * gain).astype(bf16))


def norm_backward(grad_in, inverse_rms, scaled, gain):
    weighted = grad_in * gain
    back = inverse_rms * (weighted - scaled * jnp.mean(weighted * scaled, axis=1, keepdims=True))
    return (back, jnp.sum(grad_in * scaled, axis=0))


def dot_nn(left, right):
    return jnp.dot(left, right, preferred_element_type=f32)


def dot_nt(left, right):
    return lax.dot_general(left, right, (((1,), (1,)), ((), ())), preferred_element_type=f32)


def dot_tn(left, right):
    return lax.dot_general(left, right, (((0,), (0,)), ((), ())), preferred_element_type=f32)


def wrap(index, count):
    return lax.rem(index + count, count)


class Place:
    def __init__(self, sizes):
        self.rows_outer, self.rows_inner, self.ctx = sizes
        self.row_parts = self.rows_outer * self.rows_inner
        self.chips = self.ctx // 2
        self.seq, self.fsdp, self.c = (lax.axis_index(n) for n in ("seq", "fsdp", "ctx"))
        self.row = self.seq * self.rows_inner + self.fsdp
        self.chip = self.c // 2
        self.core = self.c % 2

    def sibling(self):
        return (self.seq, self.fsdp, self.chip * 2 + 1 - self.core)

    def along(self, step):
        return (self.seq, self.fsdp, wrap(self.chip + step, self.chips) * 2 + self.core)

    def any_ctx(self, step):
        return (self.seq, self.fsdp, wrap(self.c + step, self.ctx))

    def across(self, step):
        row = wrap(self.row + step, self.row_parts)
        return (row // self.rows_inner, row % self.rows_inner, self.c)

    def chip_at(self, step):
        return wrap(self.chip + step, self.chips)

    def row_at(self, step):
        return wrap(self.row + step, self.row_parts)

    def greet(self, ctx=False, line=False, sibling=False, rows=False):
        devices = []
        if ctx:
            devices += [self.any_ctx(t) for t in range(1, self.ctx)]
        if line:
            devices += [self.along(t) for t in range(1, self.chips)]
        if sibling:
            devices += [self.sibling()]
        if rows:
            devices += [self.across(t) for t in range(1, self.row_parts)]
        barrier = pltpu.get_barrier_semaphore()
        for device in devices:
            pl.semaphore_signal(barrier, inc=1, device_id=device, device_id_type=MESH)
        pl.semaphore_wait(barrier, len(devices))


def remote(src, dst, send, recv, device):
    return pltpu.make_async_remote_copy(
        src_ref=src, dst_ref=dst, send_sem=send, recv_sem=recv, device_id=device, device_id_type=MESH
    )


def dma(*shape):
    return pltpu.SemaphoreType.DMA(shape)


class LineGather:
    def __init__(self, place, ref, out, sems):
        self.p, self.ref, self.out = place, ref, out
        self.zs, self.zr, self.bs, self.br = sems

    @staticmethod
    def scratch(sizes):
        chips = sizes[2] // 2
        return [dma(2, chips), dma(2, chips), dma(2, chips), dma(2, chips)]

    def source(self, way, d):
        return self.p.chip - d if way == 0 else self.p.chip + d

    def has(self, way, d):
        return self.p.chip >= d if way == 0 else self.p.chip + d < self.p.chips

    def onward(self, way):
        return self.p.chip + 1 < self.p.chips if way == 0 else self.p.chip >= 1

    def slot(self, way, d, core):
        return self.out.at[self.source(way, d) * 2 + core]

    def hop(self, way, d, own=False):
        mine = self.slot(way, d, self.p.core)
        src = self.ref if own else mine
        return remote(src, mine, self.zs.at[way, d], self.zr.at[way, d], self.p.along(1 - 2 * way))

    def landed(self, way, d):
        mine = self.slot(way, d, self.p.core)
        return remote(mine, mine, self.zs.at[way, d - 1], self.zr.at[way, d - 1], self.p.along(1 - 2 * way))

    def to_sibling(self, way, d, own=False):
        mine = self.slot(way, d, self.p.core)
        src = self.ref if own else mine
        return remote(src, mine, self.bs.at[way, d], self.br.at[way, d], self.p.sibling())

    def from_sibling(self, way, d):
        mine = self.slot(way, d, 1 - self.p.core)
        return remote(mine, mine, self.bs.at[way, d], self.br.at[way, d], self.p.sibling())

    def start(self):
        for way in range(2):
            pl.when(self.onward(way))(lambda way=way: self.hop(way, 0, True).start())
        self.to_sibling(0, 0, True).start()
        self.out[self.p.c] = self.ref[...]

    def forward_way(self, way, d):
        self.landed(way, d).wait_recv()
        pl.when(self.onward(way))(lambda: self.hop(way, d).start())
        self.to_sibling(way, d).start()

    def forward(self, d):
        for way in range(2):
            pl.when(self.has(way, d))(lambda way=way: self.forward_way(way, d))

    def arrive(self):
        self.from_sibling(0, 0).wait_recv()
        for d in range(1, self.p.chips):
            for way in range(2):
                pl.when(self.has(way, d))(lambda way=way, d=d: self.from_sibling(way, d).wait_recv())

    def finish(self):
        self.to_sibling(0, 0, True).wait_send()
        for d in range(self.p.chips):
            for way in range(2):

                @pl.when(self.has(way, d))
                def _(way=way, d=d):
                    pl.when(self.onward(way))(lambda: self.hop(way, d, d == 0).wait_send())
                    if d:
                        self.to_sibling(way, d).wait_send()


class FullGather:
    def __init__(self, place, ref, out, sems):
        self.p, self.ref, self.out = place, ref, out
        self.zs, self.zr = sems[:2]
        self.row_sems = sems[2:8]
        self.bs, self.br = sems[8:10]
        rows = ref.shape[0]
        self.half = (rows // 2 + 15) // 16 * 16
        self.parts = (pl.ds(0, self.half), pl.ds(self.half, rows - self.half))
        self.tags = [(0, 0)] + [(way, d) for d in range(1, place.chips) for way in range(2)]

    @staticmethod
    def scratch(sizes):
        chips = sizes[2] // 2
        count, outer, inner = 2 * chips - 1, sizes[0], sizes[1]
        line = [dma(2, chips)] * 2
        direct = [dma(count, 2, max(outer, inner))] * 2
        bent = [dma(count, 2, outer, inner)] * 2
        spare = [dma(1)] * 2
        return line + direct + bent + spare + [dma(count, outer, inner)] * 2

    def source(self, way, d):
        return self.p.chip - d if way == 0 else self.p.chip + d

    def has(self, way, d):
        return self.p.chip >= d if way == 0 else self.p.chip + d < self.p.chips

    def onward(self, way):
        return self.p.chip + 1 < self.p.chips if way == 0 else self.p.chip >= 1

    def when_has(self, tag, action):
        if tag[1] == 0:
            action()
        else:
            pl.when(self.has(*tag))(action)

    def row(self, a, b):
        seq = wrap(self.p.seq - a, self.p.rows_outer)
        return seq * self.p.rows_inner + wrap(self.p.fsdp - b, self.p.rows_inner)

    def slot(self, tag, core, a=0, b=0):
        return self.out.at[self.source(*tag) * 2 + core, self.row(a, b)]

    def device(self, a, b):
        return (wrap(self.p.seq + a, self.p.rows_outer), wrap(self.p.fsdp + b, self.p.rows_inner), self.p.c)

    def hop(self, way, d):
        mine = self.slot((way, d), self.p.core)
        src = self.ref if d == 0 else mine
        return remote(src, mine, self.zs.at[way, d], self.zr.at[way, d], self.p.along(1 - 2 * way))

    def landed(self, way, d):
        mine = self.slot((way, d), self.p.core)
        return remote(mine, mine, self.zs.at[way, d - 1], self.zr.at[way, d - 1], self.p.along(1 - 2 * way))

    def direct(self, tag, a, b):
        q, axis = self.tags.index(tag), 0 if a else 1
        mine = self.slot(tag, self.p.core)
        src = self.ref if tag[1] == 0 else mine
        sems = [sem.at[q, axis, a + b] for sem in self.row_sems[:2]]
        return remote(src, mine, *sems, self.device(a, b))

    def direct_in(self, tag, a, b):
        q, axis = self.tags.index(tag), 0 if a else 1
        mine = self.slot(tag, self.p.core, a, b)
        sems = [sem.at[q, axis, a + b] for sem in self.row_sems[:2]]
        return remote(mine, mine, *sems, self.device(a, b))

    def bent(self, tag, part, a, b):
        q = self.tags.index(tag)
        mine = (self.slot(tag, self.p.core, a, 0) if part == 0 else self.slot(tag, self.p.core, 0, b)).at[self.parts[part]]
        sems = [sem.at[q, part, a, b] for sem in self.row_sems[2:4]]
        return remote(mine, mine, *sems, self.device(0, b) if part == 0 else self.device(a, 0))

    def bent_in(self, tag, part, a, b):
        q = self.tags.index(tag)
        mine = self.slot(tag, self.p.core, a, b).at[self.parts[part]]
        sems = [sem.at[q, part, a, b] for sem in self.row_sems[2:4]]
        return remote(mine, mine, *sems, self.device(0, b))

    def to_sibling(self, tag, a, b):
        q = self.tags.index(tag)
        mine = self.slot(tag, self.p.core, a, b)
        src = self.ref if (tag[1] == 0 and a == 0 and b == 0) else mine
        return remote(src, mine, self.bs.at[q, a, b], self.br.at[q, a, b], self.p.sibling())

    def from_sibling(self, tag, a, b):
        q = self.tags.index(tag)
        mine = self.slot(tag, 1 - self.p.core, a, b)
        return remote(mine, mine, self.bs.at[q, a, b], self.br.at[q, a, b], self.p.sibling())

    def steps(self):
        outer = [(a, 0) for a in range(1, self.p.rows_outer)]
        inner = [(0, b) for b in range(1, self.p.rows_inner)]
        diagonal = [(a, b) for a in range(1, self.p.rows_outer) for b in range(1, self.p.rows_inner)]
        return outer, inner, diagonal

    def send_rows(self, tag):
        outer, inner, _ = self.steps()
        for a, b in outer + inner:
            self.direct(tag, a, b).start()
        self.to_sibling(tag, 0, 0).start()

    def start(self):
        for way in range(2):
            pl.when(self.onward(way))(lambda way=way: self.hop(way, 0).start())
        self.send_rows((0, 0))
        self.out[self.p.c, self.p.row] = self.ref[...]

    def forward(self, d):
        for way in range(2):

            @pl.when(self.has(way, d))
            def _(way=way):
                self.landed(way, d).wait_recv()
                pl.when(self.onward(way))(lambda: self.hop(way, d).start())
                self.send_rows((way, d))

    def bend(self, d):
        outer, inner, _ = self.steps()
        for tag in [(0, 0)] if d == 0 else [(0, d), (1, d)]:

            def action(tag=tag):
                for a, b in outer:
                    self.direct_in(tag, a, b).wait_recv()
                    for _, other in inner:
                        self.bent(tag, 0, a, other).start()
                    self.to_sibling(tag, a, b).start()
                for a, b in inner:
                    self.direct_in(tag, a, b).wait_recv()
                    for other, _ in outer:
                        self.bent(tag, 1, other, b).start()
                    self.to_sibling(tag, a, b).start()

            self.when_has(tag, action)

    def settle(self, d):
        for tag in [(0, 0)] if d == 0 else [(0, d), (1, d)]:

            def action(tag=tag):
                for a, b in self.steps()[2]:
                    for part in range(2):
                        self.bent_in(tag, part, a, b).wait_recv()
                    self.to_sibling(tag, a, b).start()

            self.when_has(tag, action)

    def every(self):
        return [(a, b) for a in range(self.p.rows_outer) for b in range(self.p.rows_inner)]

    def arrive(self):
        for tag in self.tags:

            def action(tag=tag):
                for a, b in self.every():
                    self.from_sibling(tag, a, b).wait_recv()

            self.when_has(tag, action)

    def finish(self):
        outer, inner, diagonal = self.steps()
        for tag in self.tags:

            def action(tag=tag):
                for way in range(2) if tag[1] == 0 else (tag[0],):
                    pl.when(self.onward(way))(lambda way=way: self.hop(way, tag[1]).wait_send())
                for a, b in outer + inner:
                    self.direct(tag, a, b).wait_send()
                for a, b in diagonal:
                    for part in range(2):
                        self.bent(tag, part, a, b).wait_send()
                for a, b in self.every():
                    self.to_sibling(tag, a, b).wait_send()

            self.when_has(tag, action)


class RowExchange:
    def __init__(self, place, src_of, dst_of, sems):
        self.p, self.src_of, self.dst_of = place, src_of, dst_of
        self.xs, self.xr = sems

    @staticmethod
    def scratch(sizes):
        rows = sizes[0] * sizes[1]
        return [dma(rows), dma(rows)]

    def send(self, k):
        return remote(self.src_of(k), self.dst_of(k, 0), self.xs.at[k], self.xr.at[k], self.p.across(k))

    def recv(self, k):
        mine = self.dst_of(k, k)
        return remote(mine, mine, self.xs.at[k], self.xr.at[k], self.p.across(k))

    def start(self):
        for k in range(1, self.p.row_parts):
            self.send(k).start()

    def arrive(self):
        for k in range(1, self.p.row_parts):
            self.recv(k).wait_recv()

    def finish(self):
        for k in range(1, self.p.row_parts):
            self.send(k).wait_send()


class CtxExchange:
    def __init__(self, place, src_of, dst_of, sems):
        self.p, self.src_of, self.dst_of = place, src_of, dst_of
        self.ss, self.sr = sems

    @staticmethod
    def scratch(sizes):
        return [dma(sizes[2]), dma(sizes[2])]

    def send(self, t):
        return remote(
            self.src_of(wrap(self.p.c + t, self.p.ctx)),
            self.dst_of(self.p.c),
            self.ss.at[t],
            self.sr.at[t],
            self.p.any_ctx(t),
        )

    def recv(self, t):
        mine = self.dst_of(wrap(self.p.c - t, self.p.ctx))
        return remote(mine, mine, self.ss.at[t], self.sr.at[t], self.p.any_ctx(t))

    def start(self):
        for t in range(1, self.p.ctx):
            self.send(t).start()

    def arrive(self):
        for t in range(1, self.p.ctx):
            self.recv(t).wait_recv()

    def finish(self):
        for t in range(1, self.p.ctx):
            self.send(t).wait_send()


def take(refs, count):
    return [next(refs) for _ in range(count)]


def rotate_rows(rows, cosine, sine):
    first, second = rows[:HALF], rows[HALF:]
    return jnp.concatenate([first * cosine - second * sine, second * cosine + first * sine], axis=0)


def rotate_rows_back(rows, cosine, sine):
    first, second = rows[:HALF], rows[HALF:]
    return jnp.concatenate([first * cosine + second * sine, second * cosine - first * sine], axis=0)


def group_rows(ref, g):
    return jnp.concatenate(
        [ref[pl.ds((g * GROUP + j) * HEAD_DIM, HEAD_DIM), :] for j in range(GROUP)], axis=1
    )


def first_kernel(sizes, *refs):
    refs = iter(refs)
    (x_in, gain_ref, wq_in, wk_in, wv_in, wo_in, wg_in, wu_in, wd_in, cot_in) = take(refs, 10)
    (cos_ref, sin_ref, posk_ref, posq_ref) = take(refs, 4)
    (attn_ref, q_ref, kv_ref, lse_ref, wqkv_full, wo_full, wm_full, wd_full, cot_full, n1_ref) = take(refs, 10)
    (qkv_raw, kv_own, wd_rows, score_ref) = take(refs, 4)
    (x_ref, wq_ref, wk_ref, wv_ref, wo_ref, wg_ref, wu_ref, wd_ref, cot_ref, wqkv_ref, wm_ref, load_sems) = take(refs, 12)
    qkv_sems, wo_sems = take(refs, 10), take(refs, 10)
    kv_sems, cot_sems = take(refs, 4), take(refs, 4)
    wm_sems, wd_sems, a2a_sems = take(refs, 2), take(refs, 2), take(refs, 2)

    place = Place(sizes)
    ctx, chips, row_parts = place.ctx, place.chips, place.row_parts
    tokens, width = x_ref.shape
    q_cols = HEADS * HEAD_DIM // ctx
    kv_cols = KV_HEADS * HEAD_DIM // ctx
    q_width, kv_width = HEADS * HEAD_DIM, KV_HEADS * HEAD_DIM
    qkv_cols = q_cols + 2 * kv_cols
    ff_part = wd_full.shape[1]
    per_row = ctx // row_parts

    qkv = FullGather(place, wqkv_ref, wqkv_full, qkv_sems)
    out = FullGather(place, wo_ref, wo_full, wo_sems)
    kv = LineGather(place, kv_own, kv_ref, kv_sems)
    cot = LineGather(place, cot_ref, cot_full, cot_sems)
    mlp = RowExchange(place, lambda k: wm_ref, lambda k, back: wm_full.at[place.row_at(-back)], wm_sems)
    down = RowExchange(place, lambda k: wd_ref, lambda k, back: wd_rows.at[place.row_at(-back)], wd_sems)

    def down_slice(c):
        return wd_rows.at[c // per_row, pl.ds(pl.multiple_of((c % per_row) * ff_part, 16), ff_part), :]

    spread = CtxExchange(place, down_slice, lambda c: wd_full.at[c], a2a_sems)

    loads = [
        pltpu.make_async_copy(src, dst, load_sems.at[i])
        for i, (src, dst) in enumerate(
            [
                (wq_in, wq_ref),
                (wk_in, wk_ref),
                (wv_in, wv_ref),
                (x_in.at[0], x_ref),
                (cot_in.at[0], cot_ref),
                (wo_in, wo_ref),
                (wg_in, wg_ref),
                (wu_in, wu_ref),
                (wd_in, wd_ref),
            ]
        )
    ]
    for load in loads:
        load.start()
    for load in loads[:3]:
        load.wait()
    wqkv_ref[...] = jnp.concatenate([wq_ref[...], wk_ref[...], wv_ref[...]], axis=1)
    place.greet(ctx=True, rows=True)
    qkv.start()
    for load in loads[3:]:
        load.wait()
    values = x_ref[...].astype(f32)
    n1_ref[...] = norm_forward(values, gain_ref[...])[2]
    wm_ref[...] = jnp.concatenate([wg_ref[...], wu_ref[...]], axis=1)
    for step in range(1, chips):
        qkv.forward(step)
        if step == 1:
            qkv.bend(0)
        if step >= 2:
            qkv.bend(step - 1)
            qkv.settle(step - 2)
    cot.start()
    down.start()
    wd_rows[place.row] = wd_ref[...]
    qkv.bend(chips - 1)
    qkv.settle(chips - 2)
    qkv.settle(chips - 1)
    mlp.start()
    wm_full[place.row] = wm_ref[...]
    cot.forward(1)
    qkv.arrive()

    normed = n1_ref[...]
    for c in range(ctx):
        part = dot_nn(normed, wqkv_full[c].reshape(width, qkv_cols)).T
        qkv_raw[pl.ds(c * q_cols, q_cols), :] = part[:q_cols]
        qkv_raw[pl.ds(q_width + c * kv_cols, kv_cols), :] = part[q_cols : q_cols + kv_cols]
        qkv_raw[pl.ds(q_width + kv_width + c * kv_cols, kv_cols), :] = part[q_cols + kv_cols :]
    cosine, sine = cos_ref[...], sin_ref[...]
    for g in range(KV_HEADS):
        key = rotate_rows(qkv_raw[pl.ds(q_width + g * HEAD_DIM, HEAD_DIM), :], cosine, sine)
        value = qkv_raw[pl.ds(q_width + kv_width + g * HEAD_DIM, HEAD_DIM), :]
        pair = jnp.concatenate([key, value], axis=0).T
        kv_own[:, pl.ds(g * 2 * HEAD_DIM, 2 * HEAD_DIM)] = pair.astype(bf16)
    kv.start()
    out.start()
    for h in range(HEADS):
        q_ref[pl.ds(h * HEAD_DIM, HEAD_DIM), :] = rotate_rows(
            qkv_raw[pl.ds(h * HEAD_DIM, HEAD_DIM), :], cosine, sine
        ).astype(bf16)
    for step in range(1, chips):
        kv.forward(step)
        if step + 1 < chips:
            cot.forward(step + 1)
    kv.arrive()

    scale = 1.0 / math.sqrt(HEAD_DIM)
    query_pos = posq_ref[...]
    chunk = 2 * tokens
    wide = GROUP * tokens
    for g in range(KV_HEADS):
        lanes = pl.ds(g * 2 * HEAD_DIM, 2 * HEAD_DIM)
        query = group_rows(q_ref, g) * jnp.asarray(scale, bf16)
        query = jnp.concatenate([query, jnp.zeros_like(query)], axis=0)

        def score(i, total, lanes=lanes, query=query):
            keys = kv_ref[pl.ds(2 * i, 2), :, lanes].reshape(chunk, 2 * HEAD_DIM)
            rows = pl.ds(pl.multiple_of(i * chunk, chunk), chunk)
            scores = jnp.where(posk_ref[rows, :] <= query_pos, dot_nn(keys, query), MASKED)
            score_ref[rows, :] = scores
            return total + jnp.sum(jnp.exp(scores), axis=0, keepdims=True)

        log_total = jnp.log(lax.fori_loop(0, chips, score, jnp.zeros((1, wide), f32)))
        lse_ref[g] = log_total

        def gather_values(i, total, lanes=lanes, log_total=log_total):
            keys = kv_ref[pl.ds(2 * i, 2), :, lanes].reshape(chunk, 2 * HEAD_DIM)
            rows = pl.ds(pl.multiple_of(i * chunk, chunk), chunk)
            prob = jnp.exp(score_ref[rows, :] - log_total).astype(bf16)
            return total + dot_tn(keys, prob)

        total = lax.fori_loop(0, chips, gather_values, jnp.zeros((2 * HEAD_DIM, wide), f32))
        for j in range(GROUP):
            attn_ref[pl.ds((g * GROUP + j) * HEAD_DIM, HEAD_DIM), :] = total[
                HEAD_DIM:, j * tokens : (j + 1) * tokens
            ].astype(bf16)
        if g == 0:
            down.arrive()
            spread.start()
            wd_full[place.c] = down_slice(place.c)[...]
            out.bend(0)
            for step in range(1, chips):
                out.forward(step)
        if g == 2:
            for step in range(1, chips):
                out.bend(step)
            out.settle(0)
        if g == 3:
            for step in range(1, chips):
                out.settle(step)
    mlp.arrive()
    out.arrive()
    cot.arrive()
    spread.arrive()
    for part in (qkv, kv, out, mlp, down, cot, spread):
        part.finish()


def mlp_kernel(sizes, *refs):
    refs = iter(refs)
    n_ref, cot_ref, wm_ref, wd_ref = take(refs, 4)
    ngrad_ref, osum_ref, dwm_ref, dwd_ref = take(refs, 4)
    n_all, gub_all, hid_all, part_ref, sib_ref, far_ref = take(refs, 6)
    n_sems = take(refs, 4)
    bs, br, zs, zr = take(refs, 4)

    place = Place(sizes)
    ctx, chips = place.ctx, place.chips
    tokens, width = n_ref.shape
    ff = wd_ref.shape[0]
    chunk = 2 * tokens
    gather = LineGather(place, n_ref, n_all, n_sems)

    place.greet(line=True, sibling=True)
    gather.start()

    def work(p):
        rows = pl.ds(pl.multiple_of(p * chunk, chunk), chunk)
        normed = n_all[pl.ds(2 * p, 2)].reshape(chunk, width)
        cot = cot_ref[pl.ds(2 * p, 2)].reshape(chunk, width)
        gate_up = dot_nn(normed, wm_ref[...])
        gate, up = gate_up[:, :ff], gate_up[:, ff:]
        sigmoid_gate = jax.nn.sigmoid(gate)
        silu_gate = gate * sigmoid_gate
        hidden = (silu_gate * up).astype(bf16)
        hidden_grad = dot_nt(cot, wd_ref[...])
        gate_back = hidden_grad * up * sigmoid_gate * (1.0 + gate * (1.0 - sigmoid_gate))
        up_back = hidden_grad * silu_gate
        both = jnp.concatenate([gate_back, up_back], axis=1).astype(bf16)
        gub_all[rows, :] = both
        hid_all[rows, :] = hidden
        part_ref[p, :, 0] = dot_nt(both, wm_ref[...]).astype(bf16).reshape(2, tokens, width)
        part_ref[p, :, 1] = dot_nn(hidden, wd_ref[...]).astype(bf16).reshape(2, tokens, width)
        to_sibling(p).start()

    def to_sibling(p):
        return remote(part_ref.at[p, 1 - place.core], sib_ref.at[p], bs.at[p], br.at[p], place.sibling())

    def settle(p):
        to_sibling(p).wait_recv()
        both = part_ref[p, place.core].astype(f32) + sib_ref[p].astype(f32)
        part_ref[p, place.core] = both.astype(bf16)

    def target(way, d):
        return place.chip + d if way == 0 else place.chip - d

    def exists(way, d):
        return place.chip + d < chips if way == 0 else place.chip >= d

    def upstream(way):
        return place.chip >= 1 if way == 0 else place.chip + 1 < chips

    def landing(way, d):
        return target(way, d) if (way == 0 or d) else chips

    def onward(way, d, kind):
        p = target(way, d)
        slot = p if (way == 0 or d > 1) else chips
        return remote(
            part_ref.at[p, place.core, kind],
            far_ref.at[slot, kind],
            zs.at[way, d, kind],
            zr.at[way, d, kind],
            place.along(1 - 2 * way),
        )

    def inward(way, d, kind):
        mine = far_ref.at[landing(way, d), kind]
        return remote(mine, mine, zs.at[way, d + 1, kind], zr.at[way, d + 1, kind], place.along(1 - 2 * way))

    gather.from_sibling(0, 0).wait_recv()
    work(place.chip)
    for d in range(1, chips):
        gather.forward(d)
        for way in range(2):
            @pl.when(exists(way, d))
            def _(way=way, d=d):
                gather.from_sibling(1 - way, d).wait_recv()
                work(target(way, d))

        if d == 1:
            settle(place.chip)
        for way in range(2):

            @pl.when(exists(way, d))
            def _(way=way, d=d):
                settle(target(way, d))

                @pl.when(jnp.logical_not(upstream(way)))
                def _():
                    for kind in range(2):
                        onward(way, d, kind).start()

    seq = ctx * tokens
    dwm_ref[...] = dot_tn(n_all[...].reshape(seq, width), gub_all[...]).astype(bf16)
    for d in range(chips - 1, 0, -1):
        for way in range(2):

            @pl.when(jnp.logical_and(exists(way, d), upstream(way)))
            def _(way=way, d=d):
                p = target(way, d)
                for kind in range(2):
                    inward(way, d, kind).wait_recv()
                    both = part_ref[p, place.core, kind].astype(f32) + far_ref[p, kind].astype(f32)
                    part_ref[p, place.core, kind] = both.astype(bf16)
                    onward(way, d, kind).start()

    dwd_ref[...] = dot_tn(hid_all[...], cot_ref[...].reshape(seq, width)).astype(bf16)
    for kind, out_ref in enumerate((ngrad_ref, osum_ref)):
        out_ref[...] = part_ref[place.chip, place.core, kind].astype(f32)
        for way in range(2):

            @pl.when(upstream(way))
            def _(way=way, kind=kind, out_ref=out_ref):
                inward(way, 0, kind).wait_recv()
                out_ref[...] += far_ref[landing(way, 0), kind].astype(f32)

    gather.finish()
    for p in range(chips):
        to_sibling(p).wait_send()
    for d in range(1, chips):
        for way in range(2):

            @pl.when(exists(way, d))
            def _(way=way, d=d):
                for kind in range(2):
                    onward(way, d, kind).wait_send()


def back_kernel(sizes, *refs):
    refs = iter(refs)
    (q_ref, g_ref, attn_ref, kv_ref, lse_ref, cos_ref, sin_ref, posk_ref, posq_ref, dwm_ref, dwd_ref) = take(refs, 11)
    qback_ref, kvsum_ref, fin_mlp, fin_down = take(refs, 4)
    delta_ref, qz_ref, gz_ref, acc_ref, part_ref, sib_ref, far_ref = take(refs, 7)
    dwm_recv, down_rows, down_recv = take(refs, 3)
    bs, br, zs, zr = take(refs, 4)
    wm_sems, a2a_sems, wd_sems = take(refs, 2), take(refs, 2), take(refs, 2)

    place = Place(sizes)
    ctx, chips, row_parts = place.ctx, place.chips, place.row_parts
    tokens = q_ref.shape[1]
    chunk, wide = 2 * tokens, GROUP * tokens
    ff_part = dwd_ref.shape[1]
    per_row = ctx // row_parts
    scale = 1.0 / math.sqrt(HEAD_DIM)

    mlp = RowExchange(place, lambda k: dwm_ref.at[place.row_at(k)], lambda k, back: dwm_recv.at[k], wm_sems)

    def down_slot(c):
        return down_rows.at[c // per_row, pl.ds(pl.multiple_of((c % per_row) * ff_part, 16), ff_part), :]

    spread = CtxExchange(place, lambda c: dwd_ref.at[c], down_slot, a2a_sems)
    down = RowExchange(place, lambda k: down_rows.at[place.row_at(k)], lambda k, back: down_recv.at[k], wd_sems)

    place.greet(ctx=True, rows=True)
    mlp.start()
    spread.start()
    down_slot(place.c)[...] = dwd_ref[place.c]

    zeros = jnp.zeros((HEAD_DIM, wide), bf16)
    for g in range(KV_HEADS):
        query = group_rows(q_ref, g) * jnp.asarray(scale, bf16)
        grad = group_rows(g_ref, g)
        qz_ref[g] = jnp.concatenate([query, zeros], axis=0)
        gz_ref[g] = jnp.concatenate([zeros, grad], axis=0)
        delta_ref[g] = jnp.sum(grad.astype(f32) * group_rows(attn_ref, g).astype(f32), axis=0, keepdims=True)
        acc_ref[g] = jnp.zeros_like(acc_ref[g])
    query_pos = posq_ref[...]

    def to_sibling(j):
        return remote(part_ref.at[j, 1 - place.core], sib_ref.at[j], bs.at[j], br.at[j], place.sibling())

    def to_owner(j):
        return remote(part_ref.at[j, place.core], far_ref.at[j], zs.at[j], zr.at[j], place.along(j))

    def settle(j):
        to_sibling(j).wait_recv()
        both = part_ref[j, place.core].astype(f32) + sib_ref[j].astype(f32)
        part_ref[j, place.core] = both.astype(bf16)

    def work(j):
        p = place.chip_at(j)
        rows = pl.ds(pl.multiple_of(p * chunk, chunk), chunk)
        allowed = posk_ref[rows, :] <= query_pos
        for g in range(KV_HEADS):
            lanes = pl.ds(g * 2 * HEAD_DIM, 2 * HEAD_DIM)
            keys = kv_ref[pl.ds(2 * p, 2), :, lanes].reshape(chunk, 2 * HEAD_DIM)
            query, grad = qz_ref[g], gz_ref[g]
            scores = jnp.where(allowed, dot_nn(keys, query), MASKED)
            prob = jnp.exp(scores - lse_ref[g])
            score_grad = (prob * (dot_nn(keys, grad) - delta_ref[g])).astype(bf16)
            both = dot_nt(score_grad, query) + dot_nt(prob.astype(bf16), grad)
            part_ref[j, :, :, lanes] = both.astype(bf16).reshape(2, tokens, 2 * HEAD_DIM)
            acc_ref[g] += dot_tn(keys, score_grad)
        to_sibling(j).start()

    work(1)

    def turn(j, carry):
        work(j)
        settle(j - 1)
        to_owner(j - 1).start()
        return carry

    lax.fori_loop(2, chips, turn, 0)
    spread.arrive()
    down.start()
    work(0)
    settle(chips - 1)
    to_owner(chips - 1).start()
    cosine, sine = cos_ref[...], sin_ref[...]
    for h in range(HEADS):
        g, j = h // GROUP, h % GROUP
        head = acc_ref[g, pl.ds(0, HEAD_DIM), pl.ds(j * tokens, tokens)] * scale
        qback_ref[pl.ds(h * HEAD_DIM, HEAD_DIM), :] = rotate_rows_back(head, cosine, sine).astype(bf16)
    settle(0)
    mlp.arrive()
    total = dwm_ref[place.row].astype(f32)
    for k in range(1, row_parts):
        total = total + dwm_recv[k].astype(f32)
    fin_mlp[...] = total
    total = part_ref[0, place.core].astype(f32)
    for j in range(1, chips):
        to_owner(j).wait_recv()
        total = total + far_ref[j].astype(f32)
    kvsum_ref[...] = total
    down.arrive()
    total = down_rows[place.row].astype(f32)
    for k in range(1, row_parts):
        total = total + down_recv[k].astype(f32)
    fin_down[...] = total
    for part in (mlp, spread, down):
        part.finish()
    for j in range(chips):
        to_sibling(j).wait_send()
        if j:
            to_owner(j).wait_send()


def last_kernel(sizes, *refs):
    refs = iter(refs)
    part_ref, gain_ref = take(refs, 2)
    fin_ref, gain_out = take(refs, 2)
    sib_ref, row_ref, far_send, far_ref = take(refs, 4)
    gain_sib, gain_row, gain_far, gain_a, gain_b, gain_c = take(refs, 6)
    bs, br, xs, xr, zs, zr = take(refs, 6)
    gb, gx, gz = take(refs, 2), take(refs, 2), take(refs, 2)

    place = Place(sizes)
    chips, row_parts = place.chips, place.row_parts
    place.greet(line=True, sibling=True, rows=True)

    def to_sibling(j):
        return remote(
            part_ref.at[place.chip_at(j) * 2 + 1 - place.core], sib_ref.at[j], bs.at[j], br.at[j], place.sibling()
        )

    def to_row(j, k):
        return remote(
            sib_ref.at[j, place.row_at(k)], row_ref.at[j, k], xs.at[j, k], xr.at[j, k], place.across(k)
        )

    def to_owner(j):
        return remote(far_send.at[j], far_ref.at[j], zs.at[j], zr.at[j], place.along(j))

    order = list(range(1, chips)) + [0]
    for j in order:
        to_sibling(j).start()

    core, row, chip = place.core, place.row, place.chip
    gain_a[...] = gain_ref[...]
    gain_sib[core] = gain_a[...]

    def g_sib():
        return remote(gain_a, gain_sib.at[core], gb[0].at[0], gb[1].at[0], place.sibling())

    def g_row(k):
        return remote(gain_b, gain_row.at[row], gx[0].at[k], gx[1].at[k], place.across(k))

    def g_far(j):
        return remote(gain_c, gain_far.at[chip], gz[0].at[j], gz[1].at[j], place.along(j))

    g_sib().start()

    for j in order:
        to_sibling(j).wait_recv()
        both = part_ref[place.chip_at(j) * 2 + core].astype(f32) + sib_ref[j].astype(f32)
        sib_ref[j] = both.astype(bf16)
        for k in range(1, row_parts):
            to_row(j, k).start()
    remote(gain_a, gain_sib.at[1 - core], gb[0].at[0], gb[1].at[0], place.sibling()).wait_recv()
    gain_b[...] = gain_sib[0] + gain_sib[1]
    gain_row[row] = gain_b[...]
    for k in range(1, row_parts):
        g_row(k).start()

    own = None
    for j in order:
        total = sib_ref[j, row].astype(f32)
        for k in range(1, row_parts):
            to_row(j, k).wait_recv()
            total = total + row_ref[j, k].astype(f32)
        if j:
            far_send[j] = total.astype(bf16)
            to_owner(j).start()
        else:
            fin_ref[...] = total
    for k in range(1, row_parts):
        remote(gain_b, gain_row.at[place.row_at(-k)], gx[0].at[k], gx[1].at[k], place.across(k)).wait_recv()
    total = gain_row[0]
    for k in range(1, row_parts):
        total = total + gain_row[k]
    gain_c[...] = total
    gain_far[chip] = gain_c[...]
    for j in range(1, chips):
        g_far(j).start()
    total = fin_ref[...]
    for j in range(1, chips):
        to_owner(j).wait_recv()
        total = total + far_ref[j].astype(f32)
    fin_ref[...] = total
    for j in range(1, chips):
        remote(gain_c, gain_far.at[place.chip_at(-j)], gz[0].at[j], gz[1].at[j], place.along(j)).wait_recv()
    total = gain_far[0]
    for j in range(1, chips):
        total = total + gain_far[j]
    gain_out[...] = total

    g_sib().wait_send()
    for k in range(1, row_parts):
        g_row(k).wait_send()
    for j in range(1, chips):
        g_far(j).wait_send()
    for j in order:
        to_sibling(j).wait_send()
        for k in range(1, row_parts):
            to_row(j, k).wait_send()
        if j:
            to_owner(j).wait_send()


def call(kernel, sizes, inputs, outs, scratch, collective_id, raw=()):
    vmem = pl.BlockSpec(memory_space=pltpu.VMEM)
    anywhere = pl.BlockSpec(memory_space=pl.ANY)
    return pl.pallas_call(
        functools.partial(kernel, sizes),
        out_shape=[jax.ShapeDtypeStruct(shape, kind) for shape, kind in outs],
        in_specs=[anywhere if i in raw else vmem for i in range(len(inputs))],
        out_specs=[vmem] * len(outs),
        scratch_shapes=scratch,
        compiler_params=pltpu.CompilerParams(
            collective_id=collective_id, has_side_effects=True, vmem_limit_bytes=60 * 1024 * 1024
        ),
    )(*inputs)


def on_device(
    tokens,
    cotangent,
    block_order,
    gain_attn,
    gain_mlp,
    w_query,
    w_key,
    w_value,
    w_out,
    w_gate,
    w_up,
    w_down,
):
    sizes = tuple(lax.axis_size(n) for n in ("seq", "fsdp", "ctx"))
    rows, ctx = sizes[0] * sizes[1], sizes[2]
    chips = ctx // 2
    row_count, width = tokens.shape[1], tokens.shape[2]
    seq_len = row_count * ctx
    block_total = block_order.shape[0]
    block_len = seq_len // block_total
    kv_width = KV_HEADS * HEAD_DIM
    q_width = HEADS * HEAD_DIM
    q_cols, kv_cols, ff_cols = w_query.shape[1], w_key.shape[1], w_gate.shape[1]
    out_cols, down_cols, down_rows = w_out.shape[1], w_down.shape[1], w_down.shape[0]
    in_rows = w_query.shape[0]
    qkv_cols = q_cols + 2 * kv_cols
    wide = GROUP * row_count

    slot_index = jnp.arange(seq_len, dtype=jnp.int32)
    owner_hit = (slot_index // block_len)[:, None] == jnp.arange(block_total, dtype=jnp.int32)[None, :]
    all_pos = (
        jnp.sum(jnp.where(owner_hit, block_order[None, :], 0), axis=1) * block_len + slot_index % block_len
    )
    own_pos = lax.dynamic_slice_in_dim(all_pos, lax.axis_index("ctx") * row_count, row_count)
    inverse = rope_base ** (-jnp.arange(HALF, dtype=f32) / HALF)
    angles = inverse[:, None] * own_pos.astype(f32)[None, :]
    cosine, sine = jnp.cos(angles), jnp.sin(angles)
    pos_keys = all_pos[:, None]
    pos_query = jnp.tile(own_pos, GROUP)[None, :]

    x = tokens[0]
    cot_rows = cotangent[0]

    attn_t, query_t, kv_all, lse, qkv_full, out_full, mlp_full, down_full, cot_all, normed_attn = call(
        first_kernel,
        sizes,
        (
            tokens,
            gain_attn[None],
            w_query,
            w_key,
            w_value,
            w_out,
            w_gate,
            w_up,
            w_down,
            cotangent,
            cosine,
            sine,
            pos_keys,
            pos_query,
        ),
        [
            ((q_width, row_count), bf16),
            ((q_width, row_count), bf16),
            ((ctx, row_count, 2 * kv_width), bf16),
            ((KV_HEADS, 1, wide), f32),
            ((ctx, rows, in_rows, qkv_cols), bf16),
            ((ctx, rows, in_rows, out_cols), bf16),
            ((rows, in_rows, 2 * ff_cols), bf16),
            ((ctx, ff_cols, down_cols), bf16),
            ((ctx, row_count, width), bf16),
            ((row_count, width), bf16),
        ],
        [
            pltpu.VMEM((q_width + 2 * kv_width, row_count), f32),
            pltpu.VMEM((row_count, 2 * kv_width), bf16),
            pltpu.VMEM((rows, down_rows, down_cols), bf16),
            pltpu.VMEM((seq_len, wide), f32),
            pltpu.VMEM((row_count, width), bf16),
        ]
        + [pltpu.VMEM(w.shape, bf16) for w in (w_query, w_key, w_value, w_out, w_gate, w_up, w_down)]
        + [
            pltpu.VMEM((row_count, width), bf16),
            pltpu.VMEM((in_rows, qkv_cols), bf16),
            pltpu.VMEM((in_rows, 2 * ff_cols), bf16),
            dma(9),
        ]
        + FullGather.scratch(sizes)
        + FullGather.scratch(sizes)
        + LineGather.scratch(sizes)
        + LineGather.scratch(sizes)
        + RowExchange.scratch(sizes)
        + RowExchange.scratch(sizes)
        + CtxExchange.scratch(sizes),
        1,
        raw=(0, 2, 3, 4, 5, 6, 7, 8, 9),
    )

    token_f32 = x.astype(f32)
    rms_attn, unit_attn, _ = norm_forward(token_f32, gain_attn)
    out_cat = jnp.transpose(out_full.reshape(ctx, q_width, out_cols), (1, 0, 2)).reshape(q_width, width)
    middle = token_f32 + dot_tn(attn_t, out_cat)
    rms_mlp, unit_mlp, normed_mlp = norm_forward(middle, gain_mlp)
    w_mlp_cat = mlp_full.reshape(width, 2 * ff_cols)
    down_cat = jnp.transpose(down_full, (1, 0, 2)).reshape(ff_cols, width)

    normed_mlp_grad, output_sum, d_mlp, d_down = call(
        mlp_kernel,
        sizes,
        (normed_mlp, cot_all, w_mlp_cat, down_cat),
        [
            ((row_count, width), f32),
            ((row_count, width), f32),
            ((width, 2 * ff_cols), bf16),
            ((ff_cols, width), bf16),
        ],
        [
            pltpu.VMEM((ctx, row_count, width), bf16),
            pltpu.VMEM((seq_len, 2 * ff_cols), bf16),
            pltpu.VMEM((seq_len, ff_cols), bf16),
            pltpu.VMEM((chips, 2, 2, row_count, width), bf16),
            pltpu.VMEM((chips, 2, row_count, width), bf16),
            pltpu.VMEM((chips + 1, 2, row_count, width), bf16),
        ]
        + LineGather.scratch(sizes)
        + [dma(chips)] * 2
        + [dma(2, chips, 2)] * 2,
        2,
    )
    result = (middle + output_sum).astype(bf16)

    mlp_back, gain_mlp_part = norm_backward(normed_mlp_grad, rms_mlp, unit_mlp, gain_mlp)
    middle_grad = cot_rows.astype(f32) + mlp_back
    middle_grad_b = middle_grad.astype(bf16)
    attn_back_t = dot_nt(out_cat, middle_grad_b).astype(bf16)
    d_down_pieces = jnp.transpose(d_down.reshape(ff_cols, ctx, down_cols), (1, 0, 2))

    query_back_t, kv_sum, fin_mlp, fin_down = call(
        back_kernel,
        sizes,
        (
            query_t,
            attn_back_t,
            attn_t,
            kv_all,
            lse,
            cosine,
            sine,
            pos_keys,
            pos_query,
            d_mlp.reshape(rows, in_rows, 2 * ff_cols),
            d_down_pieces,
        ),
        [
            ((q_width, row_count), bf16),
            ((row_count, 2 * kv_width), f32),
            ((in_rows, 2 * ff_cols), f32),
            ((down_rows, down_cols), f32),
        ],
        [
            pltpu.VMEM((KV_HEADS, 1, wide), f32),
            pltpu.VMEM((KV_HEADS, 2 * HEAD_DIM, wide), bf16),
            pltpu.VMEM((KV_HEADS, 2 * HEAD_DIM, wide), bf16),
            pltpu.VMEM((KV_HEADS, 2 * HEAD_DIM, wide), f32),
            pltpu.VMEM((chips, 2, row_count, 2 * kv_width), bf16),
            pltpu.VMEM((chips, row_count, 2 * kv_width), bf16),
            pltpu.VMEM((chips, row_count, 2 * kv_width), bf16),
            pltpu.VMEM((rows, in_rows, 2 * ff_cols), bf16),
            pltpu.VMEM((rows, down_rows, down_cols), bf16),
            pltpu.VMEM((rows, down_rows, down_cols), bf16),
        ]
        + [dma(chips)] * 4
        + RowExchange.scratch(sizes)
        + CtxExchange.scratch(sizes)
        + RowExchange.scratch(sizes),
        3,
    )

    kv_t = jnp.transpose(kv_sum).reshape(KV_HEADS, 2, 2, HALF, row_count)
    key_back_t = jnp.stack(
        [
            kv_t[:, 0, 0] * cosine + kv_t[:, 0, 1] * sine,
            kv_t[:, 0, 1] * cosine - kv_t[:, 0, 0] * sine,
        ],
        axis=1,
    ).astype(bf16)
    key_back_t = key_back_t.reshape(kv_width, row_count)
    value_back_t = kv_t[:, 1].astype(bf16).reshape(kv_width, row_count)
    qkv_back_t = jnp.concatenate(
        [
            query_back_t.reshape(ctx, q_cols, row_count),
            key_back_t.reshape(ctx, kv_cols, row_count),
            value_back_t.reshape(ctx, kv_cols, row_count),
        ],
        axis=1,
    )
    qkv_w = qkv_full.reshape(ctx, width, qkv_cols)
    normed_attn_grad = jnp.einsum("cft,cdf->td", qkv_back_t, qkv_w, preferred_element_type=f32)
    qkv_part = jnp.einsum("td,cft->cdf", normed_attn, qkv_back_t, preferred_element_type=f32)
    out_part = jnp.einsum(
        "dt,tcf->cdf",
        attn_t,
        middle_grad_b.reshape(row_count, ctx, out_cols),
        preferred_element_type=f32,
    )
    attn_part = jnp.concatenate([qkv_part.astype(bf16), out_part.astype(bf16)], axis=2)
    attn_norm_back, gain_attn_part = norm_backward(normed_attn_grad, rms_attn, unit_attn, gain_attn)
    input_back = (middle_grad + attn_norm_back).astype(bf16)

    attn_cols = qkv_cols + out_cols
    gains = pltpu.VMEM((2, width), f32)
    fin_attn, gain_sums = call(
        last_kernel,
        sizes,
        (attn_part.reshape(ctx, rows, in_rows, attn_cols), jnp.stack([gain_attn_part, gain_mlp_part])),
        [((in_rows, attn_cols), f32), ((2, width), f32)],
        [
            pltpu.VMEM((chips, rows, in_rows, attn_cols), bf16),
            pltpu.VMEM((chips, rows, in_rows, attn_cols), bf16),
            pltpu.VMEM((chips, in_rows, attn_cols), bf16),
            pltpu.VMEM((chips, in_rows, attn_cols), bf16),
            pltpu.VMEM((2, 2, width), f32),
            pltpu.VMEM((rows, 2, width), f32),
            pltpu.VMEM((chips, 2, width), f32),
            gains,
            gains,
            gains,
            dma(chips),
            dma(chips),
            dma(chips, rows),
            dma(chips, rows),
            dma(chips),
            dma(chips),
            dma(1),
            dma(1),
            dma(rows),
            dma(rows),
            dma(chips),
            dma(chips),
        ],
        4,
    )
    return (
        result.reshape(1, row_count, width),
        input_back.reshape(1, row_count, width),
        gain_sums[0],
        gain_sums[1],
        fin_attn[:, :q_cols],
        fin_attn[:, q_cols : q_cols + kv_cols],
        fin_attn[:, q_cols + kv_cols : qkv_cols],
        fin_attn[:, qkv_cols:attn_cols],
        fin_mlp[:, :ff_cols],
        fin_mlp[:, ff_cols:],
        fin_down,
    )


def solution(mesh):
    return jax.shard_map(
        on_device,
        mesh=mesh,
        in_specs=(
            P(("seq", "fsdp"), "ctx", None),
            P(("seq", "fsdp"), "ctx", None),
            P(),
            P(),
            P(),
            P(("seq", "fsdp"), "ctx"),
            P(("seq", "fsdp"), "ctx"),
            P(("seq", "fsdp"), "ctx"),
            P(("seq", "fsdp"), "ctx"),
            P(("seq", "fsdp"), "ctx"),
            P(("seq", "fsdp"), "ctx"),
            P(("seq", "fsdp"), "ctx"),
        ),
        out_specs=(
            P(("seq", "fsdp"), "ctx", None),
            P(("seq", "fsdp"), "ctx", None),
            P(),
            P(),
            P(("seq", "fsdp"), "ctx"),
            P(("seq", "fsdp"), "ctx"),
            P(("seq", "fsdp"), "ctx"),
            P(("seq", "fsdp"), "ctx"),
            P(("seq", "fsdp"), "ctx"),
            P(("seq", "fsdp"), "ctx"),
            P(("seq", "fsdp"), "ctx"),
        ),
        check_vma=False,
    )
```

```python
import functools
import math

import jax
import jax.numpy as jnp
from jax import lax
from jax.experimental import pallas as pl
from jax.experimental.pallas import tpu as pltpu
from jax.sharding import PartitionSpec as P

HEADS = 15
KV_HEADS = 5
HEAD_DIM = 64
GROUP = HEADS // KV_HEADS
HALF = HEAD_DIM // 2
MESH = pl.DeviceIdType.MESH
MASKED = -1e30

rope_base = 100000.0
norm_eps = 1e-05
bf16 = jnp.bfloat16
f32 = jnp.float32


def norm_forward(values, gain):
    inverse_rms = lax.rsqrt(jnp.mean(values * values, axis=1, keepdims=True) + norm_eps)
    scaled = values * inverse_rms
    return (inverse_rms, scaled, (scaled * gain).astype(bf16))


def norm_backward(grad_in, inverse_rms, scaled, gain):
    weighted = grad_in * gain
    back = inverse_rms * (weighted - scaled * jnp.mean(weighted * scaled, axis=1, keepdims=True))
    return (back, jnp.sum(grad_in * scaled, axis=0))


def dot_nn(left, right):
    return jnp.dot(left, right, preferred_element_type=f32)


def dot_nt(left, right):
    return lax.dot_general(left, right, (((1,), (1,)), ((), ())), preferred_element_type=f32)


def dot_tn(left, right):
    return lax.dot_general(left, right, (((0,), (0,)), ((), ())), preferred_element_type=f32)


def wrap(index, count):
    return lax.rem(index + count, count)


class Place:
    def __init__(self, sizes):
        self.rows_outer, self.rows_inner, self.ctx = sizes
        self.row_parts = self.rows_outer * self.rows_inner
        self.chips = self.ctx // 2
        self.seq, self.fsdp, self.c = (lax.axis_index(n) for n in ("seq", "fsdp", "ctx"))
        self.row = self.seq * self.rows_inner + self.fsdp
        self.chip = self.c // 2
        self.core = self.c % 2

    def sibling(self):
        return (self.seq, self.fsdp, self.chip * 2 + 1 - self.core)

    def along(self, step):
        return (self.seq, self.fsdp, wrap(self.chip + step, self.chips) * 2 + self.core)

    def any_ctx(self, step):
        return (self.seq, self.fsdp, wrap(self.c + step, self.ctx))

    def across(self, step):
        row = wrap(self.row + step, self.row_parts)
        return (row // self.rows_inner, row % self.rows_inner, self.c)

    def chip_at(self, step):
        return wrap(self.chip + step, self.chips)

    def row_at(self, step):
        return wrap(self.row + step, self.row_parts)

    def greet(self, ctx=False, line=False, sibling=False, rows=False):
        devices = []
        if ctx:
            devices += [self.any_ctx(t) for t in range(1, self.ctx)]
        if line:
            devices += [self.along(t) for t in range(1, self.chips)]
        if sibling:
            devices += [self.sibling()]
        if rows:
            devices += [self.across(t) for t in range(1, self.row_parts)]
        barrier = pltpu.get_barrier_semaphore()
        for device in devices:
            pl.semaphore_signal(barrier, inc=1, device_id=device, device_id_type=MESH)
        pl.semaphore_wait(barrier, len(devices))


def remote(src, dst, send, recv, device):
    return pltpu.make_async_remote_copy(
        src_ref=src, dst_ref=dst, send_sem=send, recv_sem=recv, device_id=device, device_id_type=MESH
    )


def dma(*shape):
    return pltpu.SemaphoreType.DMA(shape)


class LineGather:
    def __init__(self, place, ref, out, sems):
        self.p, self.ref, self.out = place, ref, out
        self.zs, self.zr, self.bs, self.br = sems

    @staticmethod
    def scratch(sizes):
        chips = sizes[2] // 2
        return [dma(2, chips), dma(2, chips), dma(2, chips), dma(2, chips)]

    def source(self, way, d):
        return self.p.chip - d if way == 0 else self.p.chip + d

    def has(self, way, d):
        return self.p.chip >= d if way == 0 else self.p.chip + d < self.p.chips

    def onward(self, way):
        return self.p.chip + 1 < self.p.chips if way == 0 else self.p.chip >= 1

    def slot(self, way, d, core):
        return self.out.at[self.source(way, d) * 2 + core]

    def hop(self, way, d, own=False):
        mine = self.slot(way, d, self.p.core)
        src = self.ref if own else mine
        return remote(src, mine, self.zs.at[way, d], self.zr.at[way, d], self.p.along(1 - 2 * way))

    def landed(self, way, d):
        mine = self.slot(way, d, self.p.core)
        return remote(mine, mine, self.zs.at[way, d - 1], self.zr.at[way, d - 1], self.p.along(1 - 2 * way))

    def to_sibling(self, way, d, own=False):
        mine = self.slot(way, d, self.p.core)
        src = self.ref if own else mine
        return remote(src, mine, self.bs.at[way, d], self.br.at[way, d], self.p.sibling())

    def from_sibling(self, way, d):
        mine = self.slot(way, d, 1 - self.p.core)
        return remote(mine, mine, self.bs.at[way, d], self.br.at[way, d], self.p.sibling())

    def start(self):
        for way in range(2):
            pl.when(self.onward(way))(lambda way=way: self.hop(way, 0, True).start())
        self.to_sibling(0, 0, True).start()
        self.out[self.p.c] = self.ref[...]

    def forward_way(self, way, d):
        self.landed(way, d).wait_recv()
        pl.when(self.onward(way))(lambda: self.hop(way, d).start())
        self.to_sibling(way, d).start()

    def forward(self, d):
        for way in range(2):
            pl.when(self.has(way, d))(lambda way=way: self.forward_way(way, d))

    def arrive(self):
        self.from_sibling(0, 0).wait_recv()
        for d in range(1, self.p.chips):
            for way in range(2):
                pl.when(self.has(way, d))(lambda way=way, d=d: self.from_sibling(way, d).wait_recv())

    def finish(self):
        self.to_sibling(0, 0, True).wait_send()
        for d in range(self.p.chips):
            for way in range(2):

                @pl.when(self.has(way, d))
                def _(way=way, d=d):
                    pl.when(self.onward(way))(lambda: self.hop(way, d, d == 0).wait_send())
                    if d:
                        self.to_sibling(way, d).wait_send()


class FullGather:
    def __init__(self, place, ref, out, sems):
        self.p, self.ref, self.out = place, ref, out
        self.zs, self.zr = sems[:2]
        self.row_sems = sems[2:8]
        self.bs, self.br = sems[8:10]
        rows = ref.shape[0]
        self.half = (rows // 2 + 15) // 16 * 16
        self.parts = (pl.ds(0, self.half), pl.ds(self.half, rows - self.half))
        self.tags = [(0, 0)] + [(way, d) for d in range(1, place.chips) for way in range(2)]

    @staticmethod
    def scratch(sizes):
        chips = sizes[2] // 2
        count, outer, inner = 2 * chips - 1, sizes[0], sizes[1]
        line = [dma(2, chips)] * 2
        direct = [dma(count, 2, max(outer, inner))] * 2
        bent = [dma(count, 2, outer, inner)] * 2
        spare = [dma(1)] * 2
        return line + direct + bent + spare + [dma(count, outer, inner)] * 2

    def source(self, way, d):
        return self.p.chip - d if way == 0 else self.p.chip + d

    def has(self, way, d):
        return self.p.chip >= d if way == 0 else self.p.chip + d < self.p.chips

    def onward(self, way):
        return self.p.chip + 1 < self.p.chips if way == 0 else self.p.chip >= 1

    def when_has(self, tag, action):
        if tag[1] == 0:
            action()
        else:
            pl.when(self.has(*tag))(action)

    def row(self, a, b):
        seq = wrap(self.p.seq - a, self.p.rows_outer)
        return seq * self.p.rows_inner + wrap(self.p.fsdp - b, self.p.rows_inner)

    def slot(self, tag, core, a=0, b=0):
        return self.out.at[self.source(*tag) * 2 + core, self.row(a, b)]

    def device(self, a, b):
        return (wrap(self.p.seq + a, self.p.rows_outer), wrap(self.p.fsdp + b, self.p.rows_inner), self.p.c)

    def hop(self, way, d):
        mine = self.slot((way, d), self.p.core)
        src = self.ref if d == 0 else mine
        return remote(src, mine, self.zs.at[way, d], self.zr.at[way, d], self.p.along(1 - 2 * way))

    def landed(self, way, d):
        mine = self.slot((way, d), self.p.core)
        return remote(mine, mine, self.zs.at[way, d - 1], self.zr.at[way, d - 1], self.p.along(1 - 2 * way))

    def direct(self, tag, a, b):
        q, axis = self.tags.index(tag), 0 if a else 1
        mine = self.slot(tag, self.p.core)
        src = self.ref if tag[1] == 0 else mine
        sems = [sem.at[q, axis, a + b] for sem in self.row_sems[:2]]
        return remote(src, mine, *sems, self.device(a, b))

    def direct_in(self, tag, a, b):
        q, axis = self.tags.index(tag), 0 if a else 1
        mine = self.slot(tag, self.p.core, a, b)
        sems = [sem.at[q, axis, a + b] for sem in self.row_sems[:2]]
        return remote(mine, mine, *sems, self.device(a, b))

    def bent(self, tag, part, a, b):
        q = self.tags.index(tag)
        mine = (self.slot(tag, self.p.core, a, 0) if part == 0 else self.slot(tag, self.p.core, 0, b)).at[self.parts[part]]
        sems = [sem.at[q, part, a, b] for sem in self.row_sems[2:4]]
        return remote(mine, mine, *sems, self.device(0, b) if part == 0 else self.device(a, 0))

    def bent_in(self, tag, part, a, b):
        q = self.tags.index(tag)
        mine = self.slot(tag, self.p.core, a, b).at[self.parts[part]]
        sems = [sem.at[q, part, a, b] for sem in self.row_sems[2:4]]
        return remote(mine, mine, *sems, self.device(0, b))

    def to_sibling(self, tag, a, b):
        q = self.tags.index(tag)
        mine = self.slot(tag, self.p.core, a, b)
        src = self.ref if (tag[1] == 0 and a == 0 and b == 0) else mine
        return remote(src, mine, self.bs.at[q, a, b], self.br.at[q, a, b], self.p.sibling())

    def from_sibling(self, tag, a, b):
        q = self.tags.index(tag)
        mine = self.slot(tag, 1 - self.p.core, a, b)
        return remote(mine, mine, self.bs.at[q, a, b], self.br.at[q, a, b], self.p.sibling())

    def steps(self):
        outer = [(a, 0) for a in range(1, self.p.rows_outer)]
        inner = [(0, b) for b in range(1, self.p.rows_inner)]
        diagonal = [(a, b) for a in range(1, self.p.rows_outer) for b in range(1, self.p.rows_inner)]
        return outer, inner, diagonal

    def send_rows(self, tag):
        outer, inner, _ = self.steps()
        for a, b in outer + inner:
            self.direct(tag, a, b).start()
        self.to_sibling(tag, 0, 0).start()

    def start(self):
        for way in range(2):
            pl.when(self.onward(way))(lambda way=way: self.hop(way, 0).start())
        self.send_rows((0, 0))
        self.out[self.p.c, self.p.row] = self.ref[...]

    def forward(self, d):
        for way in range(2):

            @pl.when(self.has(way, d))
            def _(way=way):
                self.landed(way, d).wait_recv()
                pl.when(self.onward(way))(lambda: self.hop(way, d).start())
                self.send_rows((way, d))

    def bend(self, d):
        outer, inner, _ = self.steps()
        for tag in [(0, 0)] if d == 0 else [(0, d), (1, d)]:

            def action(tag=tag):
                for a, b in outer:
                    self.direct_in(tag, a, b).wait_recv()
                    for _, other in inner:
                        self.bent(tag, 0, a, other).start()
                    self.to_sibling(tag, a, b).start()
                for a, b in inner:
                    self.direct_in(tag, a, b).wait_recv()
                    for other, _ in outer:
                        self.bent(tag, 1, other, b).start()
                    self.to_sibling(tag, a, b).start()

            self.when_has(tag, action)

    def settle(self, d):
        for tag in [(0, 0)] if d == 0 else [(0, d), (1, d)]:

            def action(tag=tag):
                for a, b in self.steps()[2]:
                    for part in range(2):
                        self.bent_in(tag, part, a, b).wait_recv()
                    self.to_sibling(tag, a, b).start()

            self.when_has(tag, action)

    def every(self):
        return [(a, b) for a in range(self.p.rows_outer) for b in range(self.p.rows_inner)]

    def arrive(self):
        for tag in self.tags:

            def action(tag=tag):
                for a, b in self.every():
                    self.from_sibling(tag, a, b).wait_recv()

            self.when_has(tag, action)

    def finish(self):
        outer, inner, diagonal = self.steps()
        for tag in self.tags:

            def action(tag=tag):
                for way in range(2) if tag[1] == 0 else (tag[0],):
                    pl.when(self.onward(way))(lambda way=way: self.hop(way, tag[1]).wait_send())
                for a, b in outer + inner:
                    self.direct(tag, a, b).wait_send()
                for a, b in diagonal:
                    for part in range(2):
                        self.bent(tag, part, a, b).wait_send()
                for a, b in self.every():
                    self.to_sibling(tag, a, b).wait_send()

            self.when_has(tag, action)


class RowExchange:
    def __init__(self, place, src_of, dst_of, sems):
        self.p, self.src_of, self.dst_of = place, src_of, dst_of
        self.xs, self.xr = sems

    @staticmethod
    def scratch(sizes):
        rows = sizes[0] * sizes[1]
        return [dma(rows), dma(rows)]

    def send(self, k):
        return remote(self.src_of(k), self.dst_of(k, 0), self.xs.at[k], self.xr.at[k], self.p.across(k))

    def recv(self, k):
        mine = self.dst_of(k, k)
        return remote(mine, mine, self.xs.at[k], self.xr.at[k], self.p.across(k))

    def start(self):
        for k in range(1, self.p.row_parts):
            self.send(k).start()

    def arrive(self):
        for k in range(1, self.p.row_parts):
            self.recv(k).wait_recv()

    def finish(self):
        for k in range(1, self.p.row_parts):
            self.send(k).wait_send()


class CtxExchange:
    def __init__(self, place, src_of, dst_of, sems):
        self.p, self.src_of, self.dst_of = place, src_of, dst_of
        self.ss, self.sr = sems

    @staticmethod
    def scratch(sizes):
        return [dma(sizes[2]), dma(sizes[2])]

    def send(self, t):
        return remote(
            self.src_of(wrap(self.p.c + t, self.p.ctx)),
            self.dst_of(self.p.c),
            self.ss.at[t],
            self.sr.at[t],
            self.p.any_ctx(t),
        )

    def recv(self, t):
        mine = self.dst_of(wrap(self.p.c - t, self.p.ctx))
        return remote(mine, mine, self.ss.at[t], self.sr.at[t], self.p.any_ctx(t))

    def start(self):
        for t in range(1, self.p.ctx):
            self.send(t).start()

    def arrive(self):
        for t in range(1, self.p.ctx):
            self.recv(t).wait_recv()

    def finish(self):
        for t in range(1, self.p.ctx):
            self.send(t).wait_send()


def take(refs, count):
    return [next(refs) for _ in range(count)]


def rotate_rows(rows, cosine, sine):
    first, second = rows[:HALF], rows[HALF:]
    return jnp.concatenate([first * cosine - second * sine, second * cosine + first * sine], axis=0)


def rotate_rows_back(rows, cosine, sine):
    first, second = rows[:HALF], rows[HALF:]
    return jnp.concatenate([first * cosine + second * sine, second * cosine - first * sine], axis=0)


def group_rows(ref, g):
    return jnp.concatenate(
        [ref[pl.ds((g * GROUP + j) * HEAD_DIM, HEAD_DIM), :] for j in range(GROUP)], axis=1
    )


def turn(values):
    return values.astype(f32).T.astype(values.dtype)


def norm_forward_turned(values, gain):
    inverse_rms = lax.rsqrt(jnp.mean(values * values, axis=0, keepdims=True) + norm_eps)
    return values * inverse_rms * gain


def first_kernel(sizes, *refs):
    refs = iter(refs)
    (x_in, gain_ref, gain2_ref, wq_in, wk_in, wv_in, wo_in, wg_in, wu_in, wd_in, cot_in) = take(refs, 11)
    (cos_ref, sin_ref, posk_ref, posq_ref) = take(refs, 4)
    (attn_ref, q_ref, kv_ref, lse_ref, wqkv_full, wo_full, wm_full, wd_turned, cot_full) = take(refs, 9)
    (n1_turned, mid_ref, n2_ref) = take(refs, 3)
    (qkv_raw, kv_own, wd_rows, score_ref, wd_full, mid_turned, wd_wide) = take(refs, 7)
    (x_turned, wq_ref, wk_turned, wv_turned, wo_ref, wg_turned, wu_turned, wd_in_ref, cot_turned) = take(refs, 9)
    (wqkv_ref, wm_ref, wd_ref, cot_ref, load_sems) = take(refs, 5)
    qkv_sems, wo_sems = take(refs, 10), take(refs, 10)
    kv_sems, cot_sems = take(refs, 4), take(refs, 4)
    wm_sems, wd_sems, a2a_sems = take(refs, 2), take(refs, 2), take(refs, 2)

    place = Place(sizes)
    ctx, chips, row_parts = place.ctx, place.chips, place.row_parts
    width, tokens = x_turned.shape
    q_cols = HEADS * HEAD_DIM // ctx
    kv_cols = KV_HEADS * HEAD_DIM // ctx
    q_width, kv_width = HEADS * HEAD_DIM, KV_HEADS * HEAD_DIM
    qkv_cols = q_cols + 2 * kv_cols
    ff_part = wd_full.shape[1]
    per_row = ctx // row_parts

    qkv = FullGather(place, wqkv_ref, wqkv_full, qkv_sems)
    out = FullGather(place, wo_ref, wo_full, wo_sems)
    kv = LineGather(place, kv_own, kv_ref, kv_sems)
    cot = LineGather(place, cot_ref, cot_full, cot_sems)
    mlp = RowExchange(place, lambda k: wm_ref, lambda k, back: wm_full.at[place.row_at(-back)], wm_sems)
    down = RowExchange(place, lambda k: wd_ref, lambda k, back: wd_rows.at[place.row_at(-back)], wd_sems)

    def down_slice(c):
        return wd_rows.at[c // per_row, pl.ds(pl.multiple_of((c % per_row) * ff_part, 16), ff_part), :]

    spread = CtxExchange(place, down_slice, lambda c: wd_full.at[c], a2a_sems)

    loads = [
        pltpu.make_async_copy(src, dst, load_sems.at[i])
        for i, (src, dst) in enumerate(
            [
                (wq_in, wq_ref),
                (wk_in, wk_turned),
                (wv_in, wv_turned),
                (x_in, x_turned),
                (cot_in, cot_turned),
                (wo_in, wo_ref),
                (wg_in, wg_turned),
                (wu_in, wu_turned),
                (wd_in, wd_in_ref),
            ]
        )
    ]
    for load in loads:
        load.start()
    for load in loads[:3]:
        load.wait()
    wqkv_ref[...] = jnp.concatenate([wq_ref[...], turn(wk_turned[...]), turn(wv_turned[...])], axis=1)
    place.greet(ctx=True, rows=True)
    qkv.start()
    for load in loads[3:]:
        load.wait()
    normed32 = norm_forward_turned(x_turned[...].astype(f32), gain_ref[...])
    n1_turned[...] = normed32.astype(bf16)
    normed = normed32.T.astype(bf16)
    cot_ref[...] = turn(cot_turned[...])
    for step in range(1, chips):
        qkv.forward(step)
        if step == 1:
            qkv.bend(0)
    cot.start()
    wd_ref[...] = turn(wd_in_ref[...])
    down.start()
    wd_rows[place.row] = wd_ref[...]
    wm_ref[...] = jnp.concatenate([turn(wg_turned[...]), turn(wu_turned[...])], axis=1)
    for step in range(1, chips):
        qkv.bend(step)
        qkv.settle(step - 1)
        if step == chips // 2:
            cot.forward(1)
    mlp.start()
    wm_full[place.row] = wm_ref[...]
    qkv.settle(chips - 1)
    for step in range(2, chips):
        cot.forward(step)
    qkv.arrive()

    for c in range(ctx):
        part = dot_nn(normed, wqkv_full[c].reshape(width, qkv_cols)).T
        qkv_raw[pl.ds(c * q_cols, q_cols), :] = part[:q_cols]
        qkv_raw[pl.ds(q_width + c * kv_cols, kv_cols), :] = part[q_cols : q_cols + kv_cols]
        qkv_raw[pl.ds(q_width + kv_width + c * kv_cols, kv_cols), :] = part[q_cols + kv_cols :]
    cosine, sine = cos_ref[...], sin_ref[...]
    for g in range(KV_HEADS):
        key = rotate_rows(qkv_raw[pl.ds(q_width + g * HEAD_DIM, HEAD_DIM), :], cosine, sine)
        value = qkv_raw[pl.ds(q_width + kv_width + g * HEAD_DIM, HEAD_DIM), :]
        pair = jnp.concatenate([key, value], axis=0).T
        kv_own[:, pl.ds(g * 2 * HEAD_DIM, 2 * HEAD_DIM)] = pair.astype(bf16)
    kv.start()
    out.start()
    for h in range(HEADS):
        q_ref[pl.ds(h * HEAD_DIM, HEAD_DIM), :] = rotate_rows(
            qkv_raw[pl.ds(h * HEAD_DIM, HEAD_DIM), :], cosine, sine
        ).astype(bf16)
    for step in range(1, chips):
        kv.forward(step)
    kv.arrive()

    scale = 1.0 / math.sqrt(HEAD_DIM)
    query_pos = posq_ref[...]
    chunk = 2 * tokens
    wide = GROUP * tokens
    for g in range(KV_HEADS):
        lanes = pl.ds(g * 2 * HEAD_DIM, 2 * HEAD_DIM)
        query = group_rows(q_ref, g) * jnp.asarray(scale, bf16)
        query = jnp.concatenate([query, jnp.zeros_like(query)], axis=0)

        def score(i, total, lanes=lanes, query=query):
            keys = kv_ref[pl.ds(2 * i, 2), :, lanes].reshape(chunk, 2 * HEAD_DIM)
            rows = pl.ds(pl.multiple_of(i * chunk, chunk), chunk)
            scores = jnp.where(posk_ref[rows, :] <= query_pos, dot_nn(keys, query), MASKED)
            score_ref[rows, :] = scores
            return total + jnp.sum(jnp.exp(scores), axis=0, keepdims=True)

        log_total = jnp.log(lax.fori_loop(0, chips, score, jnp.zeros((1, wide), f32)))
        lse_ref[g] = log_total

        def gather_values(i, total, lanes=lanes, log_total=log_total):
            keys = kv_ref[pl.ds(2 * i, 2), :, lanes].reshape(chunk, 2 * HEAD_DIM)
            rows = pl.ds(pl.multiple_of(i * chunk, chunk), chunk)
            prob = jnp.exp(score_ref[rows, :] - log_total).astype(bf16)
            return total + dot_tn(keys, prob)

        total = lax.fori_loop(0, chips, gather_values, jnp.zeros((2 * HEAD_DIM, wide), f32))
        for j in range(GROUP):
            attn_ref[pl.ds((g * GROUP + j) * HEAD_DIM, HEAD_DIM), :] = total[
                HEAD_DIM:, j * tokens : (j + 1) * tokens
            ].astype(bf16)
        if g == 0:
            down.arrive()
            spread.start()
            wd_full[place.c] = down_slice(place.c)[...]
            out.bend(0)
            for step in range(1, chips):
                out.forward(step)
        if g == 2:
            for step in range(1, chips):
                out.bend(step)
            out.settle(0)
        if g == 3:
            for step in range(1, chips):
                out.settle(step)
    out.arrive()
    out_cols = wo_ref.shape[1]
    attn = attn_ref[...]
    for c in range(ctx):
        rows = pl.ds(c * out_cols, out_cols)
        mid_turned[rows, :] = dot_tn(wo_full[c].reshape(q_width, out_cols), attn)
    middle = (x_turned[...].astype(f32) + mid_turned[...]).T
    mid_ref[...] = middle
    n2_ref[...] = norm_forward(middle, gain2_ref[...])[2]
    cot.arrive()
    mlp.arrive()
    spread.arrive()
    down_cols = wd_ref.shape[1]
    for c in range(ctx):
        wd_wide[pl.ds(c * down_cols, down_cols), :] = wd_full[c].astype(f32).T
    wd_turned[...] = wd_wide[...].astype(bf16)
    for part in (qkv, kv, out, mlp, down, cot, spread):
        part.finish()


def mlp_kernel(sizes, *refs):
    refs = iter(refs)
    n_ref, cot_ref, wm_ref, wd_ref = take(refs, 4)
    ngrad_ref, osum_ref, dwm_ref, dwd_ref = take(refs, 4)
    n_all, gub_all, hid_all, part_ref, sib_ref, far_ref, wide_ref = take(refs, 7)
    n_sems = take(refs, 4)
    bs, br, zs, zr = take(refs, 4)

    place = Place(sizes)
    ctx, chips = place.ctx, place.chips
    tokens, width = n_ref.shape
    ff = wd_ref.shape[1]
    chunk = 2 * tokens
    gather = LineGather(place, n_ref, n_all, n_sems)

    place.greet(line=True, sibling=True)
    gather.start()

    def work(p):
        rows = pl.ds(pl.multiple_of(p * chunk, chunk), chunk)
        normed = n_all[pl.ds(2 * p, 2)].reshape(chunk, width)
        cot = cot_ref[pl.ds(2 * p, 2)].reshape(chunk, width)
        gate_up = dot_nn(normed, wm_ref[...])
        gate, up = gate_up[:, :ff], gate_up[:, ff:]
        sigmoid_gate = jax.nn.sigmoid(gate)
        silu_gate = gate * sigmoid_gate
        hidden = (silu_gate * up).astype(bf16)
        hidden_grad = dot_nn(cot, wd_ref[...])
        gate_back = hidden_grad * up * sigmoid_gate * (1.0 + gate * (1.0 - sigmoid_gate))
        up_back = hidden_grad * silu_gate
        both = jnp.concatenate([gate_back, up_back], axis=1).astype(bf16)
        gub_all[rows, :] = both
        hid_all[rows, :] = hidden
        part_ref[p, :, 0] = dot_nt(both, wm_ref[...]).astype(bf16).reshape(2, tokens, width)
        part_ref[p, :, 1] = dot_nt(hidden, wd_ref[...]).astype(bf16).reshape(2, tokens, width)
        to_sibling(p).start()

    def to_sibling(p):
        return remote(part_ref.at[p, 1 - place.core], sib_ref.at[p], bs.at[p], br.at[p], place.sibling())

    def settle(p):
        to_sibling(p).wait_recv()
        both = part_ref[p, place.core].astype(f32) + sib_ref[p].astype(f32)
        part_ref[p, place.core] = both.astype(bf16)

    def target(way, d):
        return place.chip + d if way == 0 else place.chip - d

    def exists(way, d):
        return place.chip + d < chips if way == 0 else place.chip >= d

    def upstream(way):
        return place.chip >= 1 if way == 0 else place.chip + 1 < chips

    def landing(way, d):
        return target(way, d) if (way == 0 or d) else chips

    def onward(way, d, kind):
        p = target(way, d)
        slot = p if (way == 0 or d > 1) else chips
        return remote(
            part_ref.at[p, place.core, kind],
            far_ref.at[slot, kind],
            zs.at[way, d, kind],
            zr.at[way, d, kind],
            place.along(1 - 2 * way),
        )

    def inward(way, d, kind):
        mine = far_ref.at[landing(way, d), kind]
        return remote(mine, mine, zs.at[way, d + 1, kind], zr.at[way, d + 1, kind], place.along(1 - 2 * way))

    gather.from_sibling(0, 0).wait_recv()
    work(place.chip)
    for d in range(1, chips):
        gather.forward(d)
        for way in range(2):
            @pl.when(exists(way, d))
            def _(way=way, d=d):
                gather.from_sibling(1 - way, d).wait_recv()
                work(target(way, d))

        if d == 1:
            settle(place.chip)
        for way in range(2):

            @pl.when(exists(way, d))
            def _(way=way, d=d):
                settle(target(way, d))

                @pl.when(jnp.logical_not(upstream(way)))
                def _():
                    for kind in range(2):
                        onward(way, d, kind).start()

    seq = ctx * tokens
    dwm_ref[...] = dot_tn(n_all[...].reshape(seq, width), gub_all[...]).astype(bf16).reshape(dwm_ref.shape)
    for d in range(chips - 1, 0, -1):
        for way in range(2):

            @pl.when(jnp.logical_and(exists(way, d), upstream(way)))
            def _(way=way, d=d):
                p = target(way, d)
                for kind in range(2):
                    inward(way, d, kind).wait_recv()
                    both = part_ref[p, place.core, kind].astype(f32) + far_ref[p, kind].astype(f32)
                    part_ref[p, place.core, kind] = both.astype(bf16)
                    onward(way, d, kind).start()

    down_cols = dwd_ref.shape[2]
    wide_ref[...] = dot_tn(cot_ref[...].reshape(seq, width), hid_all[...])
    for c in range(ctx):
        dwd_ref[c] = wide_ref[pl.ds(c * down_cols, down_cols), :].T.astype(bf16)
    for kind, out_ref in enumerate((ngrad_ref, osum_ref)):
        out_ref[...] = part_ref[place.chip, place.core, kind].astype(f32)
        for way in range(2):

            @pl.when(upstream(way))
            def _(way=way, kind=kind, out_ref=out_ref):
                inward(way, 0, kind).wait_recv()
                out_ref[...] += far_ref[landing(way, 0), kind].astype(f32)

    gather.finish()
    for p in range(chips):
        to_sibling(p).wait_send()
    for d in range(1, chips):
        for way in range(2):

            @pl.when(exists(way, d))
            def _(way=way, d=d):
                for kind in range(2):
                    onward(way, d, kind).wait_send()


def back_kernel(sizes, *refs):
    refs = iter(refs)
    (q_ref, g_ref, attn_ref, kv_ref, lse_ref, cos_ref, sin_ref, posk_ref, posq_ref, dwm_ref, dwd_ref) = take(refs, 11)
    qback_ref, kvsum_ref, fin_mlp, fin_down = take(refs, 4)
    delta_ref, qz_ref, gz_ref, acc_ref, part_ref, sib_ref, far_ref = take(refs, 7)
    dwm_recv, down_rows, down_recv = take(refs, 3)
    bs, br, zs, zr = take(refs, 4)
    wm_sems, a2a_sems, wd_sems = take(refs, 2), take(refs, 2), take(refs, 2)

    place = Place(sizes)
    ctx, chips, row_parts = place.ctx, place.chips, place.row_parts
    tokens = q_ref.shape[1]
    chunk, wide = 2 * tokens, GROUP * tokens
    ff_part = dwd_ref.shape[1]
    per_row = ctx // row_parts
    scale = 1.0 / math.sqrt(HEAD_DIM)

    mlp = RowExchange(place, lambda k: dwm_ref.at[place.row_at(k)], lambda k, back: dwm_recv.at[k], wm_sems)

    def down_slot(c):
        return down_rows.at[c // per_row, pl.ds(pl.multiple_of((c % per_row) * ff_part, 16), ff_part), :]

    spread = CtxExchange(place, lambda c: dwd_ref.at[c], down_slot, a2a_sems)
    down = RowExchange(place, lambda k: down_rows.at[place.row_at(k)], lambda k, back: down_recv.at[k], wd_sems)

    place.greet(ctx=True, rows=True)
    mlp.start()
    spread.start()
    down_slot(place.c)[...] = dwd_ref[place.c]

    zeros = jnp.zeros((HEAD_DIM, wide), bf16)
    for g in range(KV_HEADS):
        query = group_rows(q_ref, g) * jnp.asarray(scale, bf16)
        grad = group_rows(g_ref, g)
        qz_ref[g] = jnp.concatenate([query, zeros], axis=0)
        gz_ref[g] = jnp.concatenate([zeros, grad], axis=0)
        delta_ref[g] = jnp.sum(grad.astype(f32) * group_rows(attn_ref, g).astype(f32), axis=0, keepdims=True)
        acc_ref[g] = jnp.zeros_like(acc_ref[g])
    query_pos = posq_ref[...]

    def to_sibling(j):
        return remote(part_ref.at[j, 1 - place.core], sib_ref.at[j], bs.at[j], br.at[j], place.sibling())

    def to_owner(j):
        return remote(part_ref.at[j, place.core], far_ref.at[j], zs.at[j], zr.at[j], place.along(j))

    def settle(j):
        to_sibling(j).wait_recv()
        both = part_ref[j, place.core].astype(f32) + sib_ref[j].astype(f32)
        part_ref[j, place.core] = both.astype(bf16)

    def work(j):
        p = place.chip_at(j)
        rows = pl.ds(pl.multiple_of(p * chunk, chunk), chunk)
        allowed = posk_ref[rows, :] <= query_pos
        for g in range(KV_HEADS):
            lanes = pl.ds(g * 2 * HEAD_DIM, 2 * HEAD_DIM)
            keys = kv_ref[pl.ds(2 * p, 2), :, lanes].reshape(chunk, 2 * HEAD_DIM)
            query, grad = qz_ref[g], gz_ref[g]
            scores = jnp.where(allowed, dot_nn(keys, query), MASKED)
            prob = jnp.exp(scores - lse_ref[g])
            score_grad = (prob * (dot_nn(keys, grad) - delta_ref[g])).astype(bf16)
            both = dot_nt(score_grad, query) + dot_nt(prob.astype(bf16), grad)
            part_ref[j, :, :, lanes] = both.astype(bf16).reshape(2, tokens, 2 * HEAD_DIM)
            acc_ref[g] += dot_tn(keys, score_grad)
        to_sibling(j).start()

    work(1)

    def turn(j, carry):
        work(j)
        settle(j - 1)
        to_owner(j - 1).start()
        return carry

    lax.fori_loop(2, chips, turn, 0)
    spread.arrive()
    down.start()
    work(0)
    settle(chips - 1)
    to_owner(chips - 1).start()
    cosine, sine = cos_ref[...], sin_ref[...]
    for h in range(HEADS):
        g, j = h // GROUP, h % GROUP
        head = acc_ref[g, pl.ds(0, HEAD_DIM), pl.ds(j * tokens, tokens)] * scale
        qback_ref[pl.ds(h * HEAD_DIM, HEAD_DIM), :] = rotate_rows_back(head, cosine, sine).astype(bf16)
    settle(0)
    mlp.arrive()
    total = dwm_ref[place.row].astype(f32)
    for k in range(1, row_parts):
        total = total + dwm_recv[k].astype(f32)
    fin_mlp[...] = total
    total = part_ref[0, place.core].astype(f32)
    for j in range(1, chips):
        to_owner(j).wait_recv()
        total = total + far_ref[j].astype(f32)
    kvsum_ref[...] = total
    down.arrive()
    total = down_rows[place.row].astype(f32)
    for k in range(1, row_parts):
        total = total + down_recv[k].astype(f32)
    fin_down[...] = total
    for part in (mlp, spread, down):
        part.finish()
    for j in range(chips):
        to_sibling(j).wait_send()
        if j:
            to_owner(j).wait_send()


def last_kernel(sizes, *refs):
    refs = iter(refs)
    n1_ref, qkvb_ref, attn_ref, midb_ref, gain_ref = take(refs, 5)
    fin_ref, gain_out = take(refs, 2)
    part_ref, sib_ref, bent_ref, row_ref, far_send, far_ref = take(refs, 6)
    gain_sib, gain_row, gain_far, gain_a, gain_b, gain_c = take(refs, 6)
    bs, br, vs, vr, xs, xr, zs, zr = take(refs, 8)
    gb, gx, gz = take(refs, 2), take(refs, 2), take(refs, 2)

    place = Place(sizes)
    chips, row_parts, outer, inner = place.chips, place.row_parts, place.rows_outer, place.rows_inner
    core, row, chip = place.core, place.row, place.chip
    in_rows = fin_ref.shape[0]
    half = (in_rows // 2 + 15) // 16 * 16
    parts = (pl.ds(0, half), pl.ds(half, in_rows - half))
    sized = (pl.ds(0, half), pl.ds(0, in_rows - half))
    sides = [(a, 0) for a in range(1, outer)] + [(0, b) for b in range(1, inner)]
    diagonal = [(a, b) for a in range(1, outer) for b in range(1, inner)]
    place.greet(line=True, sibling=True, rows=True)

    def row_of(a, b):
        return wrap(place.seq + a, outer) * inner + wrap(place.fsdp + b, inner)

    def device(a, b):
        return (wrap(place.seq + a, outer), wrap(place.fsdp + b, inner), place.c)

    def to_sibling(j):
        return remote(
            part_ref.at[place.chip_at(j) * 2 + 1 - core], sib_ref.at[j], bs.at[j], br.at[j], place.sibling()
        )

    def bent(j, part, n):
        a, b = diagonal[n]
        return remote(
            sib_ref.at[j, row_of(a, b), parts[part]],
            bent_ref.at[j, part, n, sized[part]],
            vs.at[j, part, n],
            vr.at[j, part, n],
            device(0, b) if part == 0 else device(a, 0),
        )

    def direct(j, n):
        a, b = sides[n]
        return remote(sib_ref.at[j, row_of(a, b)], row_ref.at[j, n], xs.at[j, n], xr.at[j, n], device(a, b))

    def to_owner(j):
        return remote(far_send.at[j], far_ref.at[j], zs.at[j], zr.at[j], place.along(j))

    gain_a[...] = gain_ref[...]
    gain_sib[core] = gain_a[...]

    def g_sib():
        return remote(gain_a, gain_sib.at[core], gb[0].at[0], gb[1].at[0], place.sibling())

    def g_row(k):
        return remote(gain_b, gain_row.at[row], gx[0].at[k], gx[1].at[k], place.across(k))

    def g_far(j):
        return remote(gain_c, gain_far.at[chip], gz[0].at[j], gz[1].at[j], place.along(j))

    g_sib().start()

    def multiply(j):
        for k in range(2):
            c = place.chip_at(j) * 2 + k
            both = jnp.concatenate(
                [dot_nt(n1_ref[...], qkvb_ref[c]), dot_nt(attn_ref[...], midb_ref[c])], axis=1
            )
            part_ref[c] = both.astype(bf16).reshape(part_ref.shape[1:])
        to_sibling(j).start()

    def add_sibling(j):
        to_sibling(j).wait_recv()
        both = part_ref[place.chip_at(j) * 2 + core].astype(f32) + sib_ref[j].astype(f32)
        sib_ref[j] = both.astype(bf16)
        for n in range(len(diagonal)):
            for part in range(2):
                bent(j, part, n).start()

    def add_bent(j):
        for n, (a, b) in enumerate(diagonal):
            for part in range(2):
                bent(j, part, n).wait_recv()
                at = (j, row_of(a, 0) if part == 0 else row_of(0, b), parts[part])
                both = sib_ref[at].astype(f32) + bent_ref[j, part, n, sized[part]].astype(f32)
                sib_ref[at] = both.astype(bf16)
        for n in range(len(sides)):
            direct(j, n).start()

    def add_rows(j):
        total = sib_ref[j, row].astype(f32)
        for n in range(len(sides)):
            direct(j, n).wait_recv()
            total = total + row_ref[j, n].astype(f32)
        if j:
            far_send[j] = total.astype(bf16)
            to_owner(j).start()
        else:
            fin_ref[...] = total

    order = list(range(1, chips)) + [0]
    stages = (multiply, add_sibling, add_bent, add_rows)
    for t in range(chips + len(stages) - 1):
        for depth, stage in enumerate(stages):
            if 0 <= t - depth < chips:
                stage(order[t - depth])
        if t == 1:
            remote(gain_a, gain_sib.at[1 - core], gb[0].at[0], gb[1].at[0], place.sibling()).wait_recv()
            gain_b[...] = gain_sib[0] + gain_sib[1]
            gain_row[row] = gain_b[...]
            for k in range(1, row_parts):
                g_row(k).start()

    for k in range(1, row_parts):
        remote(gain_b, gain_row.at[place.row_at(-k)], gx[0].at[k], gx[1].at[k], place.across(k)).wait_recv()
    total = gain_row[0]
    for k in range(1, row_parts):
        total = total + gain_row[k]
    gain_c[...] = total
    gain_far[chip] = gain_c[...]
    for j in range(1, chips):
        g_far(j).start()
    total = fin_ref[...]
    for j in range(1, chips):
        to_owner(j).wait_recv()
        total = total + far_ref[j].astype(f32)
    fin_ref[...] = total
    for j in range(1, chips):
        remote(gain_c, gain_far.at[place.chip_at(-j)], gz[0].at[j], gz[1].at[j], place.along(j)).wait_recv()
    total = gain_far[0]
    for j in range(1, chips):
        total = total + gain_far[j]
    gain_out[...] = total

    g_sib().wait_send()
    for k in range(1, row_parts):
        g_row(k).wait_send()
    for j in range(1, chips):
        g_far(j).wait_send()
    for j in order:
        to_sibling(j).wait_send()
        for n in range(len(diagonal)):
            for part in range(2):
                bent(j, part, n).wait_send()
        for n in range(len(sides)):
            direct(j, n).wait_send()
        if j:
            to_owner(j).wait_send()


def call(kernel, sizes, inputs, outs, scratch, collective_id, raw=()):
    vmem = pl.BlockSpec(memory_space=pltpu.VMEM)
    anywhere = pl.BlockSpec(memory_space=pl.ANY)
    return pl.pallas_call(
        functools.partial(kernel, sizes),
        out_shape=[jax.ShapeDtypeStruct(shape, kind) for shape, kind in outs],
        in_specs=[anywhere if i in raw else vmem for i in range(len(inputs))],
        out_specs=[vmem] * len(outs),
        scratch_shapes=scratch,
        compiler_params=pltpu.CompilerParams(
            collective_id=collective_id, has_side_effects=True, vmem_limit_bytes=60 * 1024 * 1024
        ),
    )(*inputs)


def on_device(
    tokens,
    cotangent,
    block_order,
    gain_attn,
    gain_mlp,
    w_query,
    w_key,
    w_value,
    w_out,
    w_gate,
    w_up,
    w_down,
):
    sizes = tuple(lax.axis_size(n) for n in ("seq", "fsdp", "ctx"))
    rows, ctx = sizes[0] * sizes[1], sizes[2]
    chips = ctx // 2
    row_count, width = tokens.shape[1], tokens.shape[2]
    seq_len = row_count * ctx
    block_total = block_order.shape[0]
    block_len = seq_len // block_total
    kv_width = KV_HEADS * HEAD_DIM
    q_width = HEADS * HEAD_DIM
    q_cols, kv_cols, ff_cols = w_query.shape[1], w_key.shape[1], w_gate.shape[1]
    out_cols, down_cols, down_rows = w_out.shape[1], w_down.shape[1], w_down.shape[0]
    in_rows = w_query.shape[0]
    qkv_cols = q_cols + 2 * kv_cols
    wide = GROUP * row_count

    slot_index = jnp.arange(seq_len, dtype=jnp.int32)
    owner_hit = (slot_index // block_len)[:, None] == jnp.arange(block_total, dtype=jnp.int32)[None, :]
    all_pos = (
        jnp.sum(jnp.where(owner_hit, block_order[None, :], 0), axis=1) * block_len + slot_index % block_len
    )
    own_pos = lax.dynamic_slice_in_dim(all_pos, lax.axis_index("ctx") * row_count, row_count)
    inverse = rope_base ** (-jnp.arange(HALF, dtype=f32) / HALF)
    angles = inverse[:, None] * own_pos.astype(f32)[None, :]
    cosine, sine = jnp.cos(angles), jnp.sin(angles)
    pos_keys = all_pos[:, None]
    pos_query = jnp.tile(own_pos, GROUP)[None, :]

    x = tokens[0]
    cot_rows = cotangent[0]
    turned = [jnp.transpose(w) for w in (w_key, w_value, w_gate, w_up, w_down)]
    wk_t, wv_t, wg_t, wu_t, wd_t = turned

    (
        attn_t,
        query_t,
        kv_all,
        lse,
        qkv_full,
        out_full,
        mlp_full,
        down_t,
        cot_all,
        normed_attn_t,
        middle,
        normed_mlp,
    ) = call(
        first_kernel,
        sizes,
        (
            jnp.transpose(x),
            gain_attn[:, None],
            gain_mlp[None],
            w_query,
            wk_t,
            wv_t,
            w_out,
            wg_t,
            wu_t,
            wd_t,
            jnp.transpose(cot_rows),
            cosine,
            sine,
            pos_keys,
            pos_query,
        ),
        [
            ((q_width, row_count), bf16),
            ((q_width, row_count), bf16),
            ((ctx, row_count, 2 * kv_width), bf16),
            ((KV_HEADS, 1, wide), f32),
            ((ctx, rows, in_rows, qkv_cols), bf16),
            ((ctx, rows, in_rows, out_cols), bf16),
            ((rows, in_rows, 2 * ff_cols), bf16),
            ((width, ff_cols), bf16),
            ((ctx, row_count, width), bf16),
            ((width, row_count), bf16),
            ((row_count, width), f32),
            ((row_count, width), bf16),
        ],
        [
            pltpu.VMEM((q_width + 2 * kv_width, row_count), f32),
            pltpu.VMEM((row_count, 2 * kv_width), bf16),
            pltpu.VMEM((rows, down_rows, down_cols), bf16),
            pltpu.VMEM((seq_len, wide), f32),
            pltpu.VMEM((ctx, ff_cols, down_cols), bf16),
            pltpu.VMEM((width, row_count), f32),
            pltpu.VMEM((width, ff_cols), f32),
            pltpu.VMEM((width, row_count), bf16),
        ]
        + [pltpu.VMEM(w.shape, bf16) for w in (w_query, wk_t, wv_t, w_out, wg_t, wu_t, wd_t)]
        + [
            pltpu.VMEM((width, row_count), bf16),
            pltpu.VMEM((in_rows, qkv_cols), bf16),
            pltpu.VMEM((in_rows, 2 * ff_cols), bf16),
            pltpu.VMEM(w_down.shape, bf16),
            pltpu.VMEM((row_count, width), bf16),
            dma(9),
        ]
        + FullGather.scratch(sizes)
        + FullGather.scratch(sizes)
        + LineGather.scratch(sizes)
        + LineGather.scratch(sizes)
        + RowExchange.scratch(sizes)
        + RowExchange.scratch(sizes)
        + CtxExchange.scratch(sizes),
        1,
        raw=(0, 3, 4, 5, 6, 7, 8, 9, 10),
    )

    rms_attn, unit_attn, _ = norm_forward(x.astype(f32), gain_attn)
    rms_mlp, unit_mlp, _ = norm_forward(middle, gain_mlp)
    out_cat = jnp.transpose(out_full.reshape(ctx, q_width, out_cols), (1, 0, 2)).reshape(q_width, width)
    w_mlp_cat = mlp_full.reshape(width, 2 * ff_cols)

    normed_mlp_grad, output_sum, d_mlp, d_down = call(
        mlp_kernel,
        sizes,
        (normed_mlp, cot_all, w_mlp_cat, down_t),
        [
            ((row_count, width), f32),
            ((row_count, width), f32),
            ((rows, in_rows, 2 * ff_cols), bf16),
            ((ctx, ff_cols, down_cols), bf16),
        ],
        [
            pltpu.VMEM((ctx, row_count, width), bf16),
            pltpu.VMEM((seq_len, 2 * ff_cols), bf16),
            pltpu.VMEM((seq_len, ff_cols), bf16),
            pltpu.VMEM((chips, 2, 2, row_count, width), bf16),
            pltpu.VMEM((chips, 2, row_count, width), bf16),
            pltpu.VMEM((chips + 1, 2, row_count, width), bf16),
            pltpu.VMEM((width, ff_cols), f32),
        ]
        + LineGather.scratch(sizes)
        + [dma(chips)] * 2
        + [dma(2, chips, 2)] * 2,
        2,
    )
    result = (middle + output_sum).astype(bf16)

    mlp_back, gain_mlp_part = norm_backward(normed_mlp_grad, rms_mlp, unit_mlp, gain_mlp)
    middle_grad = cot_rows.astype(f32) + mlp_back
    middle_grad_b = middle_grad.astype(bf16)
    attn_back_t = dot_nt(out_cat, middle_grad_b).astype(bf16)

    query_back_t, kv_sum, fin_mlp, fin_down = call(
        back_kernel,
        sizes,
        (
            query_t,
            attn_back_t,
            attn_t,
            kv_all,
            lse,
            cosine,
            sine,
            pos_keys,
            pos_query,
            d_mlp,
            d_down,
        ),
        [
            ((q_width, row_count), bf16),
            ((row_count, 2 * kv_width), f32),
            ((in_rows, 2 * ff_cols), f32),
            ((down_rows, down_cols), f32),
        ],
        [
            pltpu.VMEM((KV_HEADS, 1, wide), f32),
            pltpu.VMEM((KV_HEADS, 2 * HEAD_DIM, wide), bf16),
            pltpu.VMEM((KV_HEADS, 2 * HEAD_DIM, wide), bf16),
            pltpu.VMEM((KV_HEADS, 2 * HEAD_DIM, wide), f32),
            pltpu.VMEM((chips, 2, row_count, 2 * kv_width), bf16),
            pltpu.VMEM((chips, row_count, 2 * kv_width), bf16),
            pltpu.VMEM((chips, row_count, 2 * kv_width), bf16),
            pltpu.VMEM((rows, in_rows, 2 * ff_cols), bf16),
            pltpu.VMEM((rows, down_rows, down_cols), bf16),
            pltpu.VMEM((rows, down_rows, down_cols), bf16),
        ]
        + [dma(chips)] * 4
        + RowExchange.scratch(sizes)
        + CtxExchange.scratch(sizes)
        + RowExchange.scratch(sizes),
        3,
    )

    kv_t = jnp.transpose(kv_sum).reshape(KV_HEADS, 2, 2, HALF, row_count)
    key_back_t = jnp.stack(
        [
            kv_t[:, 0, 0] * cosine + kv_t[:, 0, 1] * sine,
            kv_t[:, 0, 1] * cosine - kv_t[:, 0, 0] * sine,
        ],
        axis=1,
    ).astype(bf16)
    key_back_t = key_back_t.reshape(kv_width, row_count)
    value_back_t = kv_t[:, 1].astype(bf16).reshape(kv_width, row_count)
    qkv_back_t = jnp.concatenate(
        [
            query_back_t.reshape(ctx, q_cols, row_count),
            key_back_t.reshape(ctx, kv_cols, row_count),
            value_back_t.reshape(ctx, kv_cols, row_count),
        ],
        axis=1,
    )
    qkv_w = qkv_full.reshape(ctx, width, qkv_cols)
    normed_attn_grad = jnp.einsum("cft,cdf->td", qkv_back_t, qkv_w, preferred_element_type=f32)
    attn_norm_back, gain_attn_part = norm_backward(normed_attn_grad, rms_attn, unit_attn, gain_attn)
    input_back = (middle_grad + attn_norm_back).astype(bf16)

    attn_cols = qkv_cols + out_cols
    gains = pltpu.VMEM((2, width), f32)
    half = (in_rows // 2 + 15) // 16 * 16
    corners, sides = (sizes[0] - 1) * (sizes[1] - 1), sizes[0] + sizes[1] - 2
    fin_attn, gain_sums = call(
        last_kernel,
        sizes,
        (
            normed_attn_t,
            qkv_back_t,
            attn_t,
            jnp.transpose(middle_grad_b).reshape(ctx, out_cols, row_count),
            jnp.stack([gain_attn_part, gain_mlp_part]),
        ),
        [((in_rows, attn_cols), f32), ((2, width), f32)],
        [
            pltpu.VMEM((ctx, rows, in_rows, attn_cols), bf16),
            pltpu.VMEM((chips, rows, in_rows, attn_cols), bf16),
            pltpu.VMEM((chips, 2, corners, half, attn_cols), bf16),
            pltpu.VMEM((chips, sides, in_rows, attn_cols), bf16),
            pltpu.VMEM((chips, in_rows, attn_cols), bf16),
            pltpu.VMEM((chips, in_rows, attn_cols), bf16),
            pltpu.VMEM((2, 2, width), f32),
            pltpu.VMEM((rows, 2, width), f32),
            pltpu.VMEM((chips, 2, width), f32),
            gains,
            gains,
            gains,
            dma(chips),
            dma(chips),
            dma(chips, 2, corners),
            dma(chips, 2, corners),
            dma(chips, sides),
            dma(chips, sides),
            dma(chips),
            dma(chips),
            dma(1),
            dma(1),
            dma(rows),
            dma(rows),
            dma(chips),
            dma(chips),
        ],
        4,
    )
    return (
        result.reshape(1, row_count, width),
        input_back.reshape(1, row_count, width),
        gain_sums[0],
        gain_sums[1],
        fin_attn[:, :q_cols],
        fin_attn[:, q_cols : q_cols + kv_cols],
        fin_attn[:, q_cols + kv_cols : qkv_cols],
        fin_attn[:, qkv_cols:attn_cols],
        fin_mlp[:, :ff_cols],
        fin_mlp[:, ff_cols:],
        fin_down,
    )


def solution(mesh):
    return jax.shard_map(
        on_device,
        mesh=mesh,
        in_specs=(
            P(("seq", "fsdp"), "ctx", None),
            P(("seq", "fsdp"), "ctx", None),
            P(),
            P(),
            P(),
            P(("seq", "fsdp"), "ctx"),
            P(("seq", "fsdp"), "ctx"),
            P(("seq", "fsdp"), "ctx"),
            P(("seq", "fsdp"), "ctx"),
            P(("seq", "fsdp"), "ctx"),
            P(("seq", "fsdp"), "ctx"),
            P(("seq", "fsdp"), "ctx"),
        ),
        out_specs=(
            P(("seq", "fsdp"), "ctx", None),
            P(("seq", "fsdp"), "ctx", None),
            P(),
            P(),
            P(("seq", "fsdp"), "ctx"),
            P(("seq", "fsdp"), "ctx"),
            P(("seq", "fsdp"), "ctx"),
            P(("seq", "fsdp"), "ctx"),
            P(("seq", "fsdp"), "ctx"),
            P(("seq", "fsdp"), "ctx"),
            P(("seq", "fsdp"), "ctx"),
        ),
        check_vma=False,
    )
```

```python
import functools
import math

import jax
import jax.numpy as jnp
from jax import lax
from jax.experimental import pallas as pl
from jax.experimental.pallas import tpu as pltpu
from jax.sharding import PartitionSpec as P

HEADS = 15
KV_HEADS = 5
HEAD_DIM = 64
GROUP = HEADS // KV_HEADS
HALF = HEAD_DIM // 2
MESH = pl.DeviceIdType.MESH
MASKED = -1e30

rope_base = 100000.0
norm_eps = 1e-05
bf16 = jnp.bfloat16
f32 = jnp.float32


def norm_forward(values, gain):
    inverse_rms = lax.rsqrt(jnp.mean(values * values, axis=1, keepdims=True) + norm_eps)
    scaled = values * inverse_rms
    return (inverse_rms, scaled, (scaled * gain).astype(bf16))


def norm_backward(grad_in, inverse_rms, scaled, gain):
    weighted = grad_in * gain
    back = inverse_rms * (weighted - scaled * jnp.mean(weighted * scaled, axis=1, keepdims=True))
    return (back, jnp.sum(grad_in * scaled, axis=0))


def dot_nn(left, right):
    return jnp.dot(left, right, preferred_element_type=f32)


def dot_nt(left, right):
    return lax.dot_general(left, right, (((1,), (1,)), ((), ())), preferred_element_type=f32)


def dot_tn(left, right):
    return lax.dot_general(left, right, (((0,), (0,)), ((), ())), preferred_element_type=f32)


def wrap(index, count):
    return lax.rem(index + count, count)


class Place:
    def __init__(self, sizes):
        self.rows_outer, self.rows_inner, self.ctx = sizes
        self.row_parts = self.rows_outer * self.rows_inner
        self.chips = self.ctx // 2
        self.seq, self.fsdp, self.c = (lax.axis_index(n) for n in ("seq", "fsdp", "ctx"))
        self.row = self.seq * self.rows_inner + self.fsdp
        self.chip = self.c // 2
        self.core = self.c % 2

    def sibling(self):
        return (self.seq, self.fsdp, self.chip * 2 + 1 - self.core)

    def along(self, step):
        return (self.seq, self.fsdp, wrap(self.chip + step, self.chips) * 2 + self.core)

    def any_ctx(self, step):
        return (self.seq, self.fsdp, wrap(self.c + step, self.ctx))

    def across(self, step):
        row = wrap(self.row + step, self.row_parts)
        return (row // self.rows_inner, row % self.rows_inner, self.c)

    def chip_at(self, step):
        return wrap(self.chip + step, self.chips)

    def row_at(self, step):
        return wrap(self.row + step, self.row_parts)

    def greet(self, ctx=False, line=False, sibling=False, rows=False):
        devices = []
        if ctx:
            devices += [self.any_ctx(t) for t in range(1, self.ctx)]
        if line:
            devices += [self.along(t) for t in range(1, self.chips)]
        if sibling:
            devices += [self.sibling()]
        if rows:
            devices += [self.across(t) for t in range(1, self.row_parts)]
        barrier = pltpu.get_barrier_semaphore()
        for device in devices:
            pl.semaphore_signal(barrier, inc=1, device_id=device, device_id_type=MESH)
        pl.semaphore_wait(barrier, len(devices))


def remote(src, dst, send, recv, device):
    return pltpu.make_async_remote_copy(
        src_ref=src, dst_ref=dst, send_sem=send, recv_sem=recv, device_id=device, device_id_type=MESH
    )


def dma(*shape):
    return pltpu.SemaphoreType.DMA(shape)


class LineGather:
    def __init__(self, place, ref, out, sems):
        self.p, self.ref, self.out = place, ref, out
        self.zs, self.zr, self.bs, self.br = sems

    @staticmethod
    def scratch(sizes):
        chips = sizes[2] // 2
        return [dma(2, chips), dma(2, chips), dma(2, chips), dma(2, chips)]

    def source(self, way, d):
        return self.p.chip - d if way == 0 else self.p.chip + d

    def has(self, way, d):
        return self.p.chip >= d if way == 0 else self.p.chip + d < self.p.chips

    def onward(self, way):
        return self.p.chip + 1 < self.p.chips if way == 0 else self.p.chip >= 1

    def slot(self, way, d, core):
        return self.out.at[self.source(way, d) * 2 + core]

    def hop(self, way, d, own=False):
        mine = self.slot(way, d, self.p.core)
        src = self.ref if own else mine
        return remote(src, mine, self.zs.at[way, d], self.zr.at[way, d], self.p.along(1 - 2 * way))

    def landed(self, way, d):
        mine = self.slot(way, d, self.p.core)
        return remote(mine, mine, self.zs.at[way, d - 1], self.zr.at[way, d - 1], self.p.along(1 - 2 * way))

    def to_sibling(self, way, d, own=False):
        mine = self.slot(way, d, self.p.core)
        src = self.ref if own else mine
        return remote(src, mine, self.bs.at[way, d], self.br.at[way, d], self.p.sibling())

    def from_sibling(self, way, d):
        mine = self.slot(way, d, 1 - self.p.core)
        return remote(mine, mine, self.bs.at[way, d], self.br.at[way, d], self.p.sibling())

    def start(self):
        for way in range(2):
            pl.when(self.onward(way))(lambda way=way: self.hop(way, 0, True).start())
        self.to_sibling(0, 0, True).start()
        self.out[self.p.c] = self.ref[...]

    def forward_way(self, way, d):
        self.landed(way, d).wait_recv()
        pl.when(self.onward(way))(lambda: self.hop(way, d).start())
        self.to_sibling(way, d).start()

    def forward(self, d):
        for way in range(2):
            pl.when(self.has(way, d))(lambda way=way: self.forward_way(way, d))

    def arrive(self):
        self.from_sibling(0, 0).wait_recv()
        for d in range(1, self.p.chips):
            for way in range(2):
                pl.when(self.has(way, d))(lambda way=way, d=d: self.from_sibling(way, d).wait_recv())

    def finish(self):
        self.to_sibling(0, 0, True).wait_send()
        for d in range(self.p.chips):
            for way in range(2):

                @pl.when(self.has(way, d))
                def _(way=way, d=d):
                    pl.when(self.onward(way))(lambda: self.hop(way, d, d == 0).wait_send())
                    if d:
                        self.to_sibling(way, d).wait_send()


class FullGather:
    def __init__(self, place, ref, out, sems):
        self.p, self.ref, self.out = place, ref, out
        self.zs, self.zr = sems[:2]
        self.row_sems = sems[2:8]
        self.bs, self.br = sems[8:10]
        rows = ref.shape[0]
        self.half = (rows // 2 + 15) // 16 * 16
        self.parts = (pl.ds(0, self.half), pl.ds(self.half, rows - self.half))
        self.tags = [(0, 0)] + [(way, d) for d in range(1, place.chips) for way in range(2)]

    @staticmethod
    def scratch(sizes):
        chips = sizes[2] // 2
        count, outer, inner = 2 * chips - 1, sizes[0], sizes[1]
        line = [dma(2, chips)] * 2
        direct = [dma(count, 2, max(outer, inner))] * 2
        bent = [dma(count, 2, outer, inner)] * 2
        spare = [dma(1)] * 2
        return line + direct + bent + spare + [dma(count, outer, inner)] * 2

    def source(self, way, d):
        return self.p.chip - d if way == 0 else self.p.chip + d

    def has(self, way, d):
        return self.p.chip >= d if way == 0 else self.p.chip + d < self.p.chips

    def onward(self, way):
        return self.p.chip + 1 < self.p.chips if way == 0 else self.p.chip >= 1

    def when_has(self, tag, action):
        if tag[1] == 0:
            action()
        else:
            pl.when(self.has(*tag))(action)

    def row(self, a, b):
        seq = wrap(self.p.seq - a, self.p.rows_outer)
        return seq * self.p.rows_inner + wrap(self.p.fsdp - b, self.p.rows_inner)

    def slot(self, tag, core, a=0, b=0):
        return self.out.at[self.source(*tag) * 2 + core, self.row(a, b)]

    def device(self, a, b):
        return (wrap(self.p.seq + a, self.p.rows_outer), wrap(self.p.fsdp + b, self.p.rows_inner), self.p.c)

    def hop(self, way, d):
        mine = self.slot((way, d), self.p.core)
        src = self.ref if d == 0 else mine
        return remote(src, mine, self.zs.at[way, d], self.zr.at[way, d], self.p.along(1 - 2 * way))

    def landed(self, way, d):
        mine = self.slot((way, d), self.p.core)
        return remote(mine, mine, self.zs.at[way, d - 1], self.zr.at[way, d - 1], self.p.along(1 - 2 * way))

    def direct(self, tag, a, b):
        q, axis = self.tags.index(tag), 0 if a else 1
        mine = self.slot(tag, self.p.core)
        src = self.ref if tag[1] == 0 else mine
        sems = [sem.at[q, axis, a + b] for sem in self.row_sems[:2]]
        return remote(src, mine, *sems, self.device(a, b))

    def direct_in(self, tag, a, b):
        q, axis = self.tags.index(tag), 0 if a else 1
        mine = self.slot(tag, self.p.core, a, b)
        sems = [sem.at[q, axis, a + b] for sem in self.row_sems[:2]]
        return remote(mine, mine, *sems, self.device(a, b))

    def bent(self, tag, part, a, b):
        q = self.tags.index(tag)
        mine = (self.slot(tag, self.p.core, a, 0) if part == 0 else self.slot(tag, self.p.core, 0, b)).at[self.parts[part]]
        sems = [sem.at[q, part, a, b] for sem in self.row_sems[2:4]]
        return remote(mine, mine, *sems, self.device(0, b) if part == 0 else self.device(a, 0))

    def bent_in(self, tag, part, a, b):
        q = self.tags.index(tag)
        mine = self.slot(tag, self.p.core, a, b).at[self.parts[part]]
        sems = [sem.at[q, part, a, b] for sem in self.row_sems[2:4]]
        return remote(mine, mine, *sems, self.device(0, b))

    def to_sibling(self, tag, a, b):
        q = self.tags.index(tag)
        mine = self.slot(tag, self.p.core, a, b)
        src = self.ref if (tag[1] == 0 and a == 0 and b == 0) else mine
        return remote(src, mine, self.bs.at[q, a, b], self.br.at[q, a, b], self.p.sibling())

    def from_sibling(self, tag, a, b):
        q = self.tags.index(tag)
        mine = self.slot(tag, 1 - self.p.core, a, b)
        return remote(mine, mine, self.bs.at[q, a, b], self.br.at[q, a, b], self.p.sibling())

    def steps(self):
        outer = [(a, 0) for a in range(1, self.p.rows_outer)]
        inner = [(0, b) for b in range(1, self.p.rows_inner)]
        diagonal = [(a, b) for a in range(1, self.p.rows_outer) for b in range(1, self.p.rows_inner)]
        return outer, inner, diagonal

    def send_rows(self, tag):
        outer, inner, _ = self.steps()
        for a, b in outer + inner:
            self.direct(tag, a, b).start()
        self.to_sibling(tag, 0, 0).start()

    def start(self, rows=True):
        for way in range(2):
            pl.when(self.onward(way))(lambda way=way: self.hop(way, 0).start())
        if rows:
            self.send_rows((0, 0))
        self.out[self.p.c, self.p.row] = self.ref[...]

    def forward(self, d, rows=True):
        for way in range(2):

            @pl.when(self.has(way, d))
            def _(way=way):
                self.landed(way, d).wait_recv()
                pl.when(self.onward(way))(lambda: self.hop(way, d).start())
                if rows:
                    self.send_rows((way, d))

    def cross(self):
        for tag in self.tags:
            self.when_has(tag, lambda tag=tag: self.send_rows(tag))

    def bend(self, d):
        outer, inner, _ = self.steps()
        for tag in [(0, 0)] if d == 0 else [(0, d), (1, d)]:

            def action(tag=tag):
                for a, b in outer:
                    self.direct_in(tag, a, b).wait_recv()
                    for _, other in inner:
                        self.bent(tag, 0, a, other).start()
                    self.to_sibling(tag, a, b).start()
                for a, b in inner:
                    self.direct_in(tag, a, b).wait_recv()
                    for other, _ in outer:
                        self.bent(tag, 1, other, b).start()
                    self.to_sibling(tag, a, b).start()

            self.when_has(tag, action)

    def settle(self, d):
        for tag in [(0, 0)] if d == 0 else [(0, d), (1, d)]:

            def action(tag=tag):
                for a, b in self.steps()[2]:
                    for part in range(2):
                        self.bent_in(tag, part, a, b).wait_recv()
                    self.to_sibling(tag, a, b).start()

            self.when_has(tag, action)

    def every(self):
        return [(a, b) for a in range(self.p.rows_outer) for b in range(self.p.rows_inner)]

    def arrive(self):
        for tag in self.tags:

            def action(tag=tag):
                for a, b in self.every():
                    self.from_sibling(tag, a, b).wait_recv()

            self.when_has(tag, action)

    def finish(self):
        outer, inner, diagonal = self.steps()
        for tag in self.tags:

            def action(tag=tag):
                for way in range(2) if tag[1] == 0 else (tag[0],):
                    pl.when(self.onward(way))(lambda way=way: self.hop(way, tag[1]).wait_send())
                for a, b in outer + inner:
                    self.direct(tag, a, b).wait_send()
                for a, b in diagonal:
                    for part in range(2):
                        self.bent(tag, part, a, b).wait_send()
                for a, b in self.every():
                    self.to_sibling(tag, a, b).wait_send()

            self.when_has(tag, action)


class RowExchange:
    def __init__(self, place, src_of, dst_of, sems):
        self.p, self.src_of, self.dst_of = place, src_of, dst_of
        self.xs, self.xr = sems

    @staticmethod
    def scratch(sizes):
        rows = sizes[0] * sizes[1]
        return [dma(rows), dma(rows)]

    def send(self, k):
        return remote(self.src_of(k), self.dst_of(k, 0), self.xs.at[k], self.xr.at[k], self.p.across(k))

    def recv(self, k):
        mine = self.dst_of(k, k)
        return remote(mine, mine, self.xs.at[k], self.xr.at[k], self.p.across(k))

    def start(self):
        for k in range(1, self.p.row_parts):
            self.send(k).start()

    def arrive(self):
        for k in range(1, self.p.row_parts):
            self.recv(k).wait_recv()

    def finish(self):
        for k in range(1, self.p.row_parts):
            self.send(k).wait_send()


class CtxExchange:
    def __init__(self, place, src_of, dst_of, sems):
        self.p, self.src_of, self.dst_of = place, src_of, dst_of
        self.ss, self.sr = sems

    @staticmethod
    def scratch(sizes):
        return [dma(sizes[2]), dma(sizes[2])]

    def send(self, t):
        return remote(
            self.src_of(wrap(self.p.c + t, self.p.ctx)),
            self.dst_of(self.p.c),
            self.ss.at[t],
            self.sr.at[t],
            self.p.any_ctx(t),
        )

    def recv(self, t):
        mine = self.dst_of(wrap(self.p.c - t, self.p.ctx))
        return remote(mine, mine, self.ss.at[t], self.sr.at[t], self.p.any_ctx(t))

    def start(self):
        for t in range(1, self.p.ctx):
            self.send(t).start()

    def arrive(self):
        for t in range(1, self.p.ctx):
            self.recv(t).wait_recv()

    def finish(self):
        for t in range(1, self.p.ctx):
            self.send(t).wait_send()


def take(refs, count):
    return [next(refs) for _ in range(count)]


def rotate_rows(rows, cosine, sine):
    first, second = rows[:HALF], rows[HALF:]
    return jnp.concatenate([first * cosine - second * sine, second * cosine + first * sine], axis=0)


def rotate_rows_back(rows, cosine, sine):
    first, second = rows[:HALF], rows[HALF:]
    return jnp.concatenate([first * cosine + second * sine, second * cosine - first * sine], axis=0)


def group_rows(ref, g):
    return jnp.concatenate(
        [ref[pl.ds((g * GROUP + j) * HEAD_DIM, HEAD_DIM), :] for j in range(GROUP)], axis=1
    )


def turn(values):
    return values.astype(f32).T.astype(values.dtype)


def norm_forward_turned(values, gain):
    inverse_rms = lax.rsqrt(jnp.mean(values * values, axis=0, keepdims=True) + norm_eps)
    return values * inverse_rms * gain


def first_kernel(sizes, *refs):
    refs = iter(refs)
    (x_in, gain_ref, gain2_ref, wq_in, wk_in, wv_in, wo_in, wg_in, wu_in, wd_in, cot_in) = take(refs, 11)
    (cos_ref, sin_ref, posk_ref, posq_ref) = take(refs, 4)
    (attn_ref, q_ref, kv_ref, lse_ref, wqkv_full, wo_full, wm_full, wd_turned, cot_full) = take(refs, 9)
    (n1_turned, mid_ref, n2_ref) = take(refs, 3)
    (qkv_raw, kv_own, wd_rows, score_ref, wd_full, mid_turned, wd_wide) = take(refs, 7)
    (x_turned, wq_ref, wk_turned, wv_turned, wo_ref, wg_turned, wu_turned, wd_in_ref, cot_turned) = take(refs, 9)
    (wqkv_ref, wm_ref, wd_ref, cot_ref, load_sems) = take(refs, 5)
    qkv_sems, wo_sems = take(refs, 10), take(refs, 10)
    kv_sems, cot_sems = take(refs, 4), take(refs, 4)
    wm_sems, wd_sems, a2a_sems = take(refs, 2), take(refs, 2), take(refs, 2)

    place = Place(sizes)
    ctx, chips, row_parts = place.ctx, place.chips, place.row_parts
    width, tokens = x_turned.shape
    q_cols = HEADS * HEAD_DIM // ctx
    kv_cols = KV_HEADS * HEAD_DIM // ctx
    q_width, kv_width = HEADS * HEAD_DIM, KV_HEADS * HEAD_DIM
    qkv_cols = q_cols + 2 * kv_cols
    ff_part = wd_full.shape[1]
    per_row = ctx // row_parts

    qkv = FullGather(place, wqkv_ref, wqkv_full, qkv_sems)
    out = FullGather(place, wo_ref, wo_full, wo_sems)
    kv = LineGather(place, kv_own, kv_ref, kv_sems)
    cot = LineGather(place, cot_ref, cot_full, cot_sems)
    mlp = RowExchange(place, lambda k: wm_ref, lambda k, back: wm_full.at[place.row_at(-back)], wm_sems)
    down = RowExchange(place, lambda k: wd_ref, lambda k, back: wd_rows.at[place.row_at(-back)], wd_sems)

    def down_slice(c):
        return wd_rows.at[c // per_row, pl.ds(pl.multiple_of((c % per_row) * ff_part, 16), ff_part), :]

    spread = CtxExchange(place, down_slice, lambda c: wd_full.at[c], a2a_sems)

    loads = [
        pltpu.make_async_copy(src, dst, load_sems.at[i])
        for i, (src, dst) in enumerate(
            [
                (wq_in, wq_ref),
                (wk_in, wk_turned),
                (wv_in, wv_turned),
                (x_in, x_turned),
                (cot_in, cot_turned),
                (wo_in, wo_ref),
                (wg_in, wg_turned),
                (wu_in, wu_turned),
                (wd_in, wd_in_ref),
            ]
        )
    ]
    for load in loads:
        load.start()
    for load in loads[:3]:
        load.wait()
    wqkv_ref[...] = jnp.concatenate([wq_ref[...], turn(wk_turned[...]), turn(wv_turned[...])], axis=1)
    place.greet(ctx=True, rows=True)
    qkv.start()
    for load in loads[3:]:
        load.wait()
    out.start(rows=False)
    normed32 = norm_forward_turned(x_turned[...].astype(f32), gain_ref[...])
    n1_turned[...] = normed32.astype(bf16)
    normed = normed32.T.astype(bf16)
    cot_ref[...] = turn(cot_turned[...])
    for step in range(1, chips):
        qkv.forward(step)
        if step == 1:
            qkv.bend(0)
    for step in range(1, chips):
        out.forward(step, rows=False)
    cot.start()
    wd_ref[...] = turn(wd_in_ref[...])
    wd_rows[place.row] = wd_ref[...]
    wm_ref[...] = jnp.concatenate([turn(wg_turned[...]), turn(wu_turned[...])], axis=1)
    for step in range(1, chips):
        qkv.bend(step)
        qkv.settle(step - 1)
        if step == chips // 2:
            cot.forward(1)
    wm_full[place.row] = wm_ref[...]
    qkv.settle(chips - 1)
    down.start()
    for step in range(2, chips):
        cot.forward(step)
    qkv.arrive()

    for c in range(ctx):
        part = dot_nn(normed, wqkv_full[c].reshape(width, qkv_cols)).T
        qkv_raw[pl.ds(c * q_cols, q_cols), :] = part[:q_cols]
        qkv_raw[pl.ds(q_width + c * kv_cols, kv_cols), :] = part[q_cols : q_cols + kv_cols]
        qkv_raw[pl.ds(q_width + kv_width + c * kv_cols, kv_cols), :] = part[q_cols + kv_cols :]
    cosine, sine = cos_ref[...], sin_ref[...]
    for g in range(KV_HEADS):
        key = rotate_rows(qkv_raw[pl.ds(q_width + g * HEAD_DIM, HEAD_DIM), :], cosine, sine)
        value = qkv_raw[pl.ds(q_width + kv_width + g * HEAD_DIM, HEAD_DIM), :]
        pair = jnp.concatenate([key, value], axis=0).T
        kv_own[:, pl.ds(g * 2 * HEAD_DIM, 2 * HEAD_DIM)] = pair.astype(bf16)
    kv.start()
    out.cross()
    mlp.start()
    for h in range(HEADS):
        q_ref[pl.ds(h * HEAD_DIM, HEAD_DIM), :] = rotate_rows(
            qkv_raw[pl.ds(h * HEAD_DIM, HEAD_DIM), :], cosine, sine
        ).astype(bf16)
    for step in range(1, chips):
        kv.forward(step)
    down.arrive()
    spread.start()
    wd_full[place.c] = down_slice(place.c)[...]
    kv.arrive()

    scale = 1.0 / math.sqrt(HEAD_DIM)
    query_pos = posq_ref[...]
    chunk = 2 * tokens
    wide = GROUP * tokens
    for g in range(KV_HEADS):
        lanes = pl.ds(g * 2 * HEAD_DIM, 2 * HEAD_DIM)
        query = group_rows(q_ref, g) * jnp.asarray(scale, bf16)
        query = jnp.concatenate([query, jnp.zeros_like(query)], axis=0)

        def score(i, total, lanes=lanes, query=query):
            keys = kv_ref[pl.ds(2 * i, 2), :, lanes].reshape(chunk, 2 * HEAD_DIM)
            rows = pl.ds(pl.multiple_of(i * chunk, chunk), chunk)
            scores = jnp.where(posk_ref[rows, :] <= query_pos, dot_nn(keys, query), MASKED)
            score_ref[rows, :] = scores
            return total + jnp.sum(jnp.exp(scores), axis=0, keepdims=True)

        log_total = jnp.log(lax.fori_loop(0, chips, score, jnp.zeros((1, wide), f32)))
        lse_ref[g] = log_total

        def gather_values(i, total, lanes=lanes, log_total=log_total):
            keys = kv_ref[pl.ds(2 * i, 2), :, lanes].reshape(chunk, 2 * HEAD_DIM)
            rows = pl.ds(pl.multiple_of(i * chunk, chunk), chunk)
            prob = jnp.exp(score_ref[rows, :] - log_total).astype(bf16)
            return total + dot_tn(keys, prob)

        total = lax.fori_loop(0, chips, gather_values, jnp.zeros((2 * HEAD_DIM, wide), f32))
        for j in range(GROUP):
            attn_ref[pl.ds((g * GROUP + j) * HEAD_DIM, HEAD_DIM), :] = total[
                HEAD_DIM:, j * tokens : (j + 1) * tokens
            ].astype(bf16)
        if g == 1:
            for step in range(chips):
                out.bend(step)
        if g == 3:
            for step in range(chips):
                out.settle(step)
    out.arrive()
    out_cols = wo_ref.shape[1]
    attn = attn_ref[...]
    for c in range(ctx):
        rows = pl.ds(c * out_cols, out_cols)
        mid_turned[rows, :] = dot_tn(wo_full[c].reshape(q_width, out_cols), attn)
    middle = (x_turned[...].astype(f32) + mid_turned[...]).T
    mid_ref[...] = middle
    n2_ref[...] = norm_forward(middle, gain2_ref[...])[2]
    cot.arrive()
    mlp.arrive()
    spread.arrive()
    down_cols = wd_ref.shape[1]
    for c in range(ctx):
        wd_wide[pl.ds(c * down_cols, down_cols), :] = wd_full[c].astype(f32).T
    wd_turned[...] = wd_wide[...].astype(bf16)
    for part in (qkv, kv, out, mlp, down, cot, spread):
        part.finish()


def mlp_kernel(sizes, *refs):
    refs = iter(refs)
    n_ref, cot_ref, wm_ref, wd_ref = take(refs, 4)
    ngrad_ref, osums_ref, dwm_ref, dwd_ref = take(refs, 4)
    n_all, gub_all, hid_all, part_ref, sib_ref, far_ref, wide_ref = take(refs, 7)
    n_sems = take(refs, 4)
    bs, br, zs, zr = take(refs, 4)

    place = Place(sizes)
    ctx, chips = place.ctx, place.chips
    tokens, width = n_ref.shape
    ff = wd_ref.shape[1]
    chunk = 2 * tokens
    gather = LineGather(place, n_ref, n_all, n_sems)

    place.greet(line=True, sibling=True)
    gather.start()

    def work(p):
        rows = pl.ds(pl.multiple_of(p * chunk, chunk), chunk)
        normed = n_all[pl.ds(2 * p, 2)].reshape(chunk, width)
        cot = cot_ref[pl.ds(2 * p, 2)].reshape(chunk, width)
        gate_up = dot_nn(normed, wm_ref[...])
        gate, up = gate_up[:, :ff], gate_up[:, ff:]
        sigmoid_gate = jax.nn.sigmoid(gate)
        silu_gate = gate * sigmoid_gate
        hidden = (silu_gate * up).astype(bf16)
        hidden_grad = dot_nn(cot, wd_ref[...])
        gate_back = hidden_grad * up * sigmoid_gate * (1.0 + gate * (1.0 - sigmoid_gate))
        up_back = hidden_grad * silu_gate
        both = jnp.concatenate([gate_back, up_back], axis=1).astype(bf16)
        gub_all[rows, :] = both
        hid_all[rows, :] = hidden
        part_ref[p, :, 0] = dot_nt(both, wm_ref[...]).astype(bf16).reshape(2, tokens, width)
        part_ref[p, :, 1] = dot_nt(hidden, wd_ref[...]).astype(bf16).reshape(2, tokens, width)
        to_sibling(p).start()

    def to_sibling(p):
        return remote(part_ref.at[p, 1 - place.core], sib_ref.at[p], bs.at[p], br.at[p], place.sibling())

    def settle(p):
        to_sibling(p).wait_recv()
        both = (part_ref[p, place.core].astype(f32) + sib_ref[p].astype(f32)).astype(bf16)
        part_ref[p, place.core, 0] = both[0]
        osums_ref[p] = both[1]

    def target(way, d):
        return place.chip + d if way == 0 else place.chip - d

    def exists(way, d):
        return place.chip + d < chips if way == 0 else place.chip >= d

    def upstream(way):
        return place.chip >= 1 if way == 0 else place.chip + 1 < chips

    def landing(way, d):
        return target(way, d) if (way == 0 or d) else chips

    def onward(way, d):
        p = target(way, d)
        slot = p if (way == 0 or d > 1) else chips
        return remote(
            part_ref.at[p, place.core, 0],
            far_ref.at[slot],
            zs.at[way, d],
            zr.at[way, d],
            place.along(1 - 2 * way),
        )

    def inward(way, d):
        mine = far_ref.at[landing(way, d)]
        return remote(mine, mine, zs.at[way, d + 1], zr.at[way, d + 1], place.along(1 - 2 * way))

    gather.from_sibling(0, 0).wait_recv()
    work(place.chip)
    for d in range(1, chips):
        gather.forward(d)
        for way in range(2):
            @pl.when(exists(way, d))
            def _(way=way, d=d):
                gather.from_sibling(1 - way, d).wait_recv()
                work(target(way, d))

        if d == 1:
            settle(place.chip)
        for way in range(2):

            @pl.when(exists(way, d))
            def _(way=way, d=d):
                settle(target(way, d))

                @pl.when(jnp.logical_not(upstream(way)))
                def _():
                    onward(way, d).start()

    seq = ctx * tokens
    dwm_ref[...] = dot_tn(n_all[...].reshape(seq, width), gub_all[...]).astype(bf16).reshape(dwm_ref.shape)
    for d in range(chips - 1, 0, -1):
        for way in range(2):

            @pl.when(jnp.logical_and(exists(way, d), upstream(way)))
            def _(way=way, d=d):
                p = target(way, d)
                inward(way, d).wait_recv()
                both = part_ref[p, place.core, 0].astype(f32) + far_ref[p].astype(f32)
                part_ref[p, place.core, 0] = both.astype(bf16)
                onward(way, d).start()

    down_cols = dwd_ref.shape[2]
    wide_ref[...] = dot_tn(cot_ref[...].reshape(seq, width), hid_all[...])
    for c in range(ctx):
        dwd_ref[c] = wide_ref[pl.ds(c * down_cols, down_cols), :].T.astype(bf16)
    ngrad_ref[...] = part_ref[place.chip, place.core, 0].astype(f32)
    for way in range(2):

        @pl.when(upstream(way))
        def _(way=way):
            inward(way, 0).wait_recv()
            ngrad_ref[...] += far_ref[landing(way, 0)].astype(f32)

    gather.finish()
    for p in range(chips):
        to_sibling(p).wait_send()
    for d in range(1, chips):
        for way in range(2):

            @pl.when(exists(way, d))
            def _(way=way, d=d):
                onward(way, d).wait_send()


def back_kernel(sizes, *refs):
    refs = iter(refs)
    (q_ref, g_ref, attn_ref, kv_ref, lse_ref, cos_ref, sin_ref, posk_ref, posq_ref, dwm_ref, dwd_ref) = take(refs, 11)
    qback_ref, kvsum_ref, fin_mlp, fin_down = take(refs, 4)
    delta_ref, qz_ref, gz_ref, acc_ref, part_ref, sib_ref, far_ref = take(refs, 7)
    dwm_recv, down_rows, down_recv = take(refs, 3)
    bs, br, zs, zr = take(refs, 4)
    wm_sems, a2a_sems, wd_sems = take(refs, 2), take(refs, 2), take(refs, 2)

    place = Place(sizes)
    ctx, chips, row_parts = place.ctx, place.chips, place.row_parts
    tokens = q_ref.shape[1]
    chunk, wide = 2 * tokens, GROUP * tokens
    ff_part = dwd_ref.shape[1]
    per_row = ctx // row_parts
    scale = 1.0 / math.sqrt(HEAD_DIM)

    mlp = RowExchange(place, lambda k: dwm_ref.at[place.row_at(k)], lambda k, back: dwm_recv.at[k], wm_sems)

    def down_slot(c):
        return down_rows.at[c // per_row, pl.ds(pl.multiple_of((c % per_row) * ff_part, 16), ff_part), :]

    spread = CtxExchange(place, lambda c: dwd_ref.at[c], down_slot, a2a_sems)
    down = RowExchange(place, lambda k: down_rows.at[place.row_at(k)], lambda k, back: down_recv.at[k], wd_sems)

    place.greet(ctx=True, rows=True)
    mlp.start()
    spread.start()
    down_slot(place.c)[...] = dwd_ref[place.c]

    zeros = jnp.zeros((HEAD_DIM, wide), bf16)
    for g in range(KV_HEADS):
        query = group_rows(q_ref, g) * jnp.asarray(scale, bf16)
        grad = group_rows(g_ref, g)
        qz_ref[g] = jnp.concatenate([query, zeros], axis=0)
        gz_ref[g] = jnp.concatenate([zeros, grad], axis=0)
        delta_ref[g] = jnp.sum(grad.astype(f32) * group_rows(attn_ref, g).astype(f32), axis=0, keepdims=True)
        acc_ref[g] = jnp.zeros_like(acc_ref[g])
    query_pos = posq_ref[...]

    def to_sibling(j):
        return remote(part_ref.at[j, 1 - place.core], sib_ref.at[j], bs.at[j], br.at[j], place.sibling())

    def to_owner(j):
        return remote(part_ref.at[j, place.core], far_ref.at[j], zs.at[j], zr.at[j], place.along(j))

    def settle(j):
        to_sibling(j).wait_recv()
        both = part_ref[j, place.core].astype(f32) + sib_ref[j].astype(f32)
        part_ref[j, place.core] = both.astype(bf16)

    def work(j):
        p = place.chip_at(j)
        rows = pl.ds(pl.multiple_of(p * chunk, chunk), chunk)
        allowed = posk_ref[rows, :] <= query_pos
        for g in range(KV_HEADS):
            lanes = pl.ds(g * 2 * HEAD_DIM, 2 * HEAD_DIM)
            keys = kv_ref[pl.ds(2 * p, 2), :, lanes].reshape(chunk, 2 * HEAD_DIM)
            query, grad = qz_ref[g], gz_ref[g]
            scores = jnp.where(allowed, dot_nn(keys, query), MASKED)
            prob = jnp.exp(scores - lse_ref[g])
            score_grad = (prob * (dot_nn(keys, grad) - delta_ref[g])).astype(bf16)
            both = dot_nt(score_grad, query) + dot_nt(prob.astype(bf16), grad)
            part_ref[j, :, :, lanes] = both.astype(bf16).reshape(2, tokens, 2 * HEAD_DIM)
            acc_ref[g] += dot_tn(keys, score_grad)
        to_sibling(j).start()

    work(1)

    def turn(j, carry):
        work(j)
        settle(j - 1)
        to_owner(j - 1).start()
        return carry

    lax.fori_loop(2, chips, turn, 0)
    spread.arrive()
    down.start()
    work(0)
    settle(chips - 1)
    to_owner(chips - 1).start()
    cosine, sine = cos_ref[...], sin_ref[...]
    for h in range(HEADS):
        g, j = h // GROUP, h % GROUP
        head = acc_ref[g, pl.ds(0, HEAD_DIM), pl.ds(j * tokens, tokens)] * scale
        qback_ref[pl.ds(h * HEAD_DIM, HEAD_DIM), :] = rotate_rows_back(head, cosine, sine).astype(bf16)
    settle(0)
    mlp.arrive()
    total = dwm_ref[place.row].astype(f32)
    for k in range(1, row_parts):
        total = total + dwm_recv[k].astype(f32)
    fin_mlp[...] = total
    total = part_ref[0, place.core].astype(f32)
    for j in range(1, chips):
        to_owner(j).wait_recv()
        total = total + far_ref[j].astype(f32)
    kvsum_ref[...] = total
    down.arrive()
    total = down_rows[place.row].astype(f32)
    for k in range(1, row_parts):
        total = total + down_recv[k].astype(f32)
    fin_down[...] = total
    for part in (mlp, spread, down):
        part.finish()
    for j in range(chips):
        to_sibling(j).wait_send()
        if j:
            to_owner(j).wait_send()


def last_kernel(sizes, *refs):
    refs = iter(refs)
    n1_ref, qkvb_ref, attn_ref, midb_ref, gain_ref, osums_ref, mid_ref = take(refs, 7)
    fin_ref, gain_out, result_ref = take(refs, 3)
    part_ref, sib_ref, bent_ref, row_ref, far_send, far_ref = take(refs, 6)
    gain_sib, gain_row, gain_far, gain_a, gain_b, gain_c = take(refs, 6)
    bs, br, vs, vr, xs, xr, zs, zr = take(refs, 8)
    gb, gx, gz = take(refs, 2), take(refs, 2), take(refs, 2)
    osum_far, os, orr = take(refs, 3)

    place = Place(sizes)
    chips, row_parts, outer, inner = place.chips, place.row_parts, place.rows_outer, place.rows_inner
    core, row, chip = place.core, place.row, place.chip
    in_rows = fin_ref.shape[0]
    half = (in_rows // 2 + 15) // 16 * 16
    parts = (pl.ds(0, half), pl.ds(half, in_rows - half))
    sized = (pl.ds(0, half), pl.ds(0, in_rows - half))
    sides = [(a, 0) for a in range(1, outer)] + [(0, b) for b in range(1, inner)]
    diagonal = [(a, b) for a in range(1, outer) for b in range(1, inner)]
    place.greet(line=True, sibling=True, rows=True)

    def row_of(a, b):
        return wrap(place.seq + a, outer) * inner + wrap(place.fsdp + b, inner)

    def device(a, b):
        return (wrap(place.seq + a, outer), wrap(place.fsdp + b, inner), place.c)

    def to_sibling(j):
        return remote(
            part_ref.at[place.chip_at(j) * 2 + 1 - core], sib_ref.at[j], bs.at[j], br.at[j], place.sibling()
        )

    def bent(j, part, n):
        a, b = diagonal[n]
        return remote(
            sib_ref.at[j, row_of(a, b), parts[part]],
            bent_ref.at[j, part, n, sized[part]],
            vs.at[j, part, n],
            vr.at[j, part, n],
            device(0, b) if part == 0 else device(a, 0),
        )

    def direct(j, n):
        a, b = sides[n]
        return remote(sib_ref.at[j, row_of(a, b)], row_ref.at[j, n], xs.at[j, n], xr.at[j, n], device(a, b))

    def to_owner(j):
        return remote(far_send.at[j], far_ref.at[j], zs.at[j], zr.at[j], place.along(j))

    gain_a[...] = gain_ref[...]
    gain_sib[core] = gain_a[...]

    def g_sib():
        return remote(gain_a, gain_sib.at[core], gb[0].at[0], gb[1].at[0], place.sibling())

    def g_row(k):
        return remote(gain_b, gain_row.at[row], gx[0].at[k], gx[1].at[k], place.across(k))

    def g_far(j):
        return remote(gain_c, gain_far.at[chip], gz[0].at[j], gz[1].at[j], place.along(j))

    g_sib().start()

    def multiply(j):
        for k in range(2):
            c = place.chip_at(j) * 2 + k
            both = jnp.concatenate(
                [dot_nt(n1_ref[...], qkvb_ref[c]), dot_nt(attn_ref[...], midb_ref[c])], axis=1
            )
            part_ref[c] = both.astype(bf16).reshape(part_ref.shape[1:])
        to_sibling(j).start()

    def add_sibling(j):
        to_sibling(j).wait_recv()
        both = part_ref[place.chip_at(j) * 2 + core].astype(f32) + sib_ref[j].astype(f32)
        sib_ref[j] = both.astype(bf16)
        for n in range(len(diagonal)):
            for part in range(2):
                bent(j, part, n).start()

    def add_bent(j):
        for n, (a, b) in enumerate(diagonal):
            for part in range(2):
                bent(j, part, n).wait_recv()
                at = (j, row_of(a, 0) if part == 0 else row_of(0, b), parts[part])
                both = sib_ref[at].astype(f32) + bent_ref[j, part, n, sized[part]].astype(f32)
                sib_ref[at] = both.astype(bf16)
        for n in range(len(sides)):
            direct(j, n).start()

    def add_rows(j):
        total = sib_ref[j, row].astype(f32)
        for n in range(len(sides)):
            direct(j, n).wait_recv()
            total = total + row_ref[j, n].astype(f32)
        if j:
            far_send[j] = total.astype(bf16)
            to_owner(j).start()
        else:
            fin_ref[...] = total

    def output_to(j):
        return remote(osums_ref.at[place.chip_at(j)], osum_far.at[j], os.at[j], orr.at[j], place.along(j))

    for j in range(1, chips):
        output_to(j).start()
    order = list(range(1, chips)) + [0]
    stages = (multiply, add_sibling, add_bent, add_rows)
    for t in range(chips + len(stages) - 1):
        for depth, stage in enumerate(stages):
            if 0 <= t - depth < chips:
                stage(order[t - depth])
        if t == 1:
            remote(gain_a, gain_sib.at[1 - core], gb[0].at[0], gb[1].at[0], place.sibling()).wait_recv()
            gain_b[...] = gain_sib[0] + gain_sib[1]
            gain_row[row] = gain_b[...]
            for k in range(1, row_parts):
                g_row(k).start()

    for k in range(1, row_parts):
        remote(gain_b, gain_row.at[place.row_at(-k)], gx[0].at[k], gx[1].at[k], place.across(k)).wait_recv()
    total = gain_row[0]
    for k in range(1, row_parts):
        total = total + gain_row[k]
    gain_c[...] = total
    gain_far[chip] = gain_c[...]
    for j in range(1, chips):
        g_far(j).start()
    total = mid_ref[...] + osums_ref[chip].astype(f32)
    for j in range(1, chips):
        output_to(j).wait_recv()
        total = total + osum_far[j].astype(f32)
    result_ref[...] = total.T.astype(bf16)
    total = fin_ref[...]
    for j in range(1, chips):
        to_owner(j).wait_recv()
        total = total + far_ref[j].astype(f32)
    fin_ref[...] = total
    for j in range(1, chips):
        remote(gain_c, gain_far.at[place.chip_at(-j)], gz[0].at[j], gz[1].at[j], place.along(j)).wait_recv()
    total = gain_far[0]
    for j in range(1, chips):
        total = total + gain_far[j]
    gain_out[...] = total

    g_sib().wait_send()
    for k in range(1, row_parts):
        g_row(k).wait_send()
    for j in range(1, chips):
        g_far(j).wait_send()
    for j in order:
        to_sibling(j).wait_send()
        for n in range(len(diagonal)):
            for part in range(2):
                bent(j, part, n).wait_send()
        for n in range(len(sides)):
            direct(j, n).wait_send()
        if j:
            to_owner(j).wait_send()
            output_to(j).wait_send()


def call(kernel, sizes, inputs, outs, scratch, collective_id, raw=()):
    vmem = pl.BlockSpec(memory_space=pltpu.VMEM)
    anywhere = pl.BlockSpec(memory_space=pl.ANY)
    return pl.pallas_call(
        functools.partial(kernel, sizes),
        out_shape=[jax.ShapeDtypeStruct(shape, kind) for shape, kind in outs],
        in_specs=[anywhere if i in raw else vmem for i in range(len(inputs))],
        out_specs=[vmem] * len(outs),
        scratch_shapes=scratch,
        compiler_params=pltpu.CompilerParams(
            collective_id=collective_id, has_side_effects=True, vmem_limit_bytes=60 * 1024 * 1024
        ),
    )(*inputs)


def on_device(
    tokens,
    cotangent,
    block_order,
    gain_attn,
    gain_mlp,
    w_query,
    w_key,
    w_value,
    w_out,
    w_gate,
    w_up,
    w_down,
):
    sizes = tuple(lax.axis_size(n) for n in ("seq", "fsdp", "ctx"))
    rows, ctx = sizes[0] * sizes[1], sizes[2]
    chips = ctx // 2
    row_count, width = tokens.shape[1], tokens.shape[2]
    seq_len = row_count * ctx
    block_total = block_order.shape[0]
    block_len = seq_len // block_total
    kv_width = KV_HEADS * HEAD_DIM
    q_width = HEADS * HEAD_DIM
    q_cols, kv_cols, ff_cols = w_query.shape[1], w_key.shape[1], w_gate.shape[1]
    out_cols, down_cols, down_rows = w_out.shape[1], w_down.shape[1], w_down.shape[0]
    in_rows = w_query.shape[0]
    qkv_cols = q_cols + 2 * kv_cols
    wide = GROUP * row_count

    slot_index = jnp.arange(seq_len, dtype=jnp.int32)
    owner_hit = (slot_index // block_len)[:, None] == jnp.arange(block_total, dtype=jnp.int32)[None, :]
    all_pos = (
        jnp.sum(jnp.where(owner_hit, block_order[None, :], 0), axis=1) * block_len + slot_index % block_len
    )
    own_pos = lax.dynamic_slice_in_dim(all_pos, lax.axis_index("ctx") * row_count, row_count)
    inverse = rope_base ** (-jnp.arange(HALF, dtype=f32) / HALF)
    angles = inverse[:, None] * own_pos.astype(f32)[None, :]
    cosine, sine = jnp.cos(angles), jnp.sin(angles)
    pos_keys = all_pos[:, None]
    pos_query = jnp.tile(own_pos, GROUP)[None, :]

    x = tokens[0]
    cot_rows = cotangent[0]
    turned = [jnp.transpose(w) for w in (w_key, w_value, w_gate, w_up, w_down)]
    wk_t, wv_t, wg_t, wu_t, wd_t = turned

    (
        attn_t,
        query_t,
        kv_all,
        lse,
        qkv_full,
        out_full,
        mlp_full,
        down_t,
        cot_all,
        normed_attn_t,
        middle,
        normed_mlp,
    ) = call(
        first_kernel,
        sizes,
        (
            jnp.transpose(x),
            gain_attn[:, None],
            gain_mlp[None],
            w_query,
            wk_t,
            wv_t,
            w_out,
            wg_t,
            wu_t,
            wd_t,
            jnp.transpose(cot_rows),
            cosine,
            sine,
            pos_keys,
            pos_query,
        ),
        [
            ((q_width, row_count), bf16),
            ((q_width, row_count), bf16),
            ((ctx, row_count, 2 * kv_width), bf16),
            ((KV_HEADS, 1, wide), f32),
            ((ctx, rows, in_rows, qkv_cols), bf16),
            ((ctx, rows, in_rows, out_cols), bf16),
            ((rows, in_rows, 2 * ff_cols), bf16),
            ((width, ff_cols), bf16),
            ((ctx, row_count, width), bf16),
            ((width, row_count), bf16),
            ((row_count, width), f32),
            ((row_count, width), bf16),
        ],
        [
            pltpu.VMEM((q_width + 2 * kv_width, row_count), f32),
            pltpu.VMEM((row_count, 2 * kv_width), bf16),
            pltpu.VMEM((rows, down_rows, down_cols), bf16),
            pltpu.VMEM((seq_len, wide), f32),
            pltpu.VMEM((ctx, ff_cols, down_cols), bf16),
            pltpu.VMEM((width, row_count), f32),
            pltpu.VMEM((width, ff_cols), f32),
            pltpu.VMEM((width, row_count), bf16),
        ]
        + [pltpu.VMEM(w.shape, bf16) for w in (w_query, wk_t, wv_t, w_out, wg_t, wu_t, wd_t)]
        + [
            pltpu.VMEM((width, row_count), bf16),
            pltpu.VMEM((in_rows, qkv_cols), bf16),
            pltpu.VMEM((in_rows, 2 * ff_cols), bf16),
            pltpu.VMEM(w_down.shape, bf16),
            pltpu.VMEM((row_count, width), bf16),
            dma(9),
        ]
        + FullGather.scratch(sizes)
        + FullGather.scratch(sizes)
        + LineGather.scratch(sizes)
        + LineGather.scratch(sizes)
        + RowExchange.scratch(sizes)
        + RowExchange.scratch(sizes)
        + CtxExchange.scratch(sizes),
        1,
        raw=(0, 3, 4, 5, 6, 7, 8, 9, 10),
    )

    rms_attn, unit_attn, _ = norm_forward(x.astype(f32), gain_attn)
    rms_mlp, unit_mlp, _ = norm_forward(middle, gain_mlp)
    out_cat = jnp.transpose(out_full.reshape(ctx, q_width, out_cols), (1, 0, 2)).reshape(q_width, width)
    w_mlp_cat = mlp_full.reshape(width, 2 * ff_cols)

    normed_mlp_grad, output_sums, d_mlp, d_down = call(
        mlp_kernel,
        sizes,
        (normed_mlp, cot_all, w_mlp_cat, down_t),
        [
            ((row_count, width), f32),
            ((chips, row_count, width), bf16),
            ((rows, in_rows, 2 * ff_cols), bf16),
            ((ctx, ff_cols, down_cols), bf16),
        ],
        [
            pltpu.VMEM((ctx, row_count, width), bf16),
            pltpu.VMEM((seq_len, 2 * ff_cols), bf16),
            pltpu.VMEM((seq_len, ff_cols), bf16),
            pltpu.VMEM((chips, 2, 2, row_count, width), bf16),
            pltpu.VMEM((chips, 2, row_count, width), bf16),
            pltpu.VMEM((chips + 1, row_count, width), bf16),
            pltpu.VMEM((width, ff_cols), f32),
        ]
        + LineGather.scratch(sizes)
        + [dma(chips)] * 2
        + [dma(2, chips)] * 2,
        2,
    )
    mlp_back, gain_mlp_part = norm_backward(normed_mlp_grad, rms_mlp, unit_mlp, gain_mlp)
    middle_grad = cot_rows.astype(f32) + mlp_back
    middle_grad_b = middle_grad.astype(bf16)
    attn_back_t = dot_nt(out_cat, middle_grad_b).astype(bf16)

    query_back_t, kv_sum, fin_mlp, fin_down = call(
        back_kernel,
        sizes,
        (
            query_t,
            attn_back_t,
            attn_t,
            kv_all,
            lse,
            cosine,
            sine,
            pos_keys,
            pos_query,
            d_mlp,
            d_down,
        ),
        [
            ((q_width, row_count), bf16),
            ((row_count, 2 * kv_width), f32),
            ((in_rows, 2 * ff_cols), f32),
            ((down_rows, down_cols), f32),
        ],
        [
            pltpu.VMEM((KV_HEADS, 1, wide), f32),
            pltpu.VMEM((KV_HEADS, 2 * HEAD_DIM, wide), bf16),
            pltpu.VMEM((KV_HEADS, 2 * HEAD_DIM, wide), bf16),
            pltpu.VMEM((KV_HEADS, 2 * HEAD_DIM, wide), f32),
            pltpu.VMEM((chips, 2, row_count, 2 * kv_width), bf16),
            pltpu.VMEM((chips, row_count, 2 * kv_width), bf16),
            pltpu.VMEM((chips, row_count, 2 * kv_width), bf16),
            pltpu.VMEM((rows, in_rows, 2 * ff_cols), bf16),
            pltpu.VMEM((rows, down_rows, down_cols), bf16),
            pltpu.VMEM((rows, down_rows, down_cols), bf16),
        ]
        + [dma(chips)] * 4
        + RowExchange.scratch(sizes)
        + CtxExchange.scratch(sizes)
        + RowExchange.scratch(sizes),
        3,
    )

    kv_t = jnp.transpose(kv_sum).reshape(KV_HEADS, 2, 2, HALF, row_count)
    key_back_t = jnp.stack(
        [
            kv_t[:, 0, 0] * cosine + kv_t[:, 0, 1] * sine,
            kv_t[:, 0, 1] * cosine - kv_t[:, 0, 0] * sine,
        ],
        axis=1,
    ).astype(bf16)
    key_back_t = key_back_t.reshape(kv_width, row_count)
    value_back_t = kv_t[:, 1].astype(bf16).reshape(kv_width, row_count)
    qkv_back_t = jnp.concatenate(
        [
            query_back_t.reshape(ctx, q_cols, row_count),
            key_back_t.reshape(ctx, kv_cols, row_count),
            value_back_t.reshape(ctx, kv_cols, row_count),
        ],
        axis=1,
    )
    qkv_w = qkv_full.reshape(ctx, width, qkv_cols)
    normed_attn_grad = jnp.einsum("cft,cdf->td", qkv_back_t, qkv_w, preferred_element_type=f32)
    attn_norm_back, gain_attn_part = norm_backward(normed_attn_grad, rms_attn, unit_attn, gain_attn)
    input_back = (middle_grad + attn_norm_back).astype(bf16)

    attn_cols = qkv_cols + out_cols
    gains = pltpu.VMEM((2, width), f32)
    half = (in_rows // 2 + 15) // 16 * 16
    corners, sides = (sizes[0] - 1) * (sizes[1] - 1), sizes[0] + sizes[1] - 2
    fin_attn, gain_sums, result_t = call(
        last_kernel,
        sizes,
        (
            normed_attn_t,
            qkv_back_t,
            attn_t,
            jnp.transpose(middle_grad_b).reshape(ctx, out_cols, row_count),
            jnp.stack([gain_attn_part, gain_mlp_part]),
            output_sums,
            middle,
        ),
        [((in_rows, attn_cols), f32), ((2, width), f32), ((width, row_count), bf16)],
        [
            pltpu.VMEM((ctx, rows, in_rows, attn_cols), bf16),
            pltpu.VMEM((chips, rows, in_rows, attn_cols), bf16),
            pltpu.VMEM((chips, 2, corners, half, attn_cols), bf16),
            pltpu.VMEM((chips, sides, in_rows, attn_cols), bf16),
            pltpu.VMEM((chips, in_rows, attn_cols), bf16),
            pltpu.VMEM((chips, in_rows, attn_cols), bf16),
            pltpu.VMEM((2, 2, width), f32),
            pltpu.VMEM((rows, 2, width), f32),
            pltpu.VMEM((chips, 2, width), f32),
            gains,
            gains,
            gains,
            dma(chips),
            dma(chips),
            dma(chips, 2, corners),
            dma(chips, 2, corners),
            dma(chips, sides),
            dma(chips, sides),
            dma(chips),
            dma(chips),
            dma(1),
            dma(1),
            dma(rows),
            dma(rows),
            dma(chips),
            dma(chips),
            pltpu.VMEM((chips, row_count, width), bf16),
            dma(chips),
            dma(chips),
        ],
        4,
    )
    return (
        jnp.transpose(result_t).reshape(1, row_count, width),
        input_back.reshape(1, row_count, width),
        gain_sums[0],
        gain_sums[1],
        fin_attn[:, :q_cols],
        fin_attn[:, q_cols : q_cols + kv_cols],
        fin_attn[:, q_cols + kv_cols : qkv_cols],
        fin_attn[:, qkv_cols:attn_cols],
        fin_mlp[:, :ff_cols],
        fin_mlp[:, ff_cols:],
        fin_down,
    )


def solution(mesh):
    return jax.shard_map(
        on_device,
        mesh=mesh,
        in_specs=(
            P(("seq", "fsdp"), "ctx", None),
            P(("seq", "fsdp"), "ctx", None),
            P(),
            P(),
            P(),
            P(("seq", "fsdp"), "ctx"),
            P(("seq", "fsdp"), "ctx"),
            P(("seq", "fsdp"), "ctx"),
            P(("seq", "fsdp"), "ctx"),
            P(("seq", "fsdp"), "ctx"),
            P(("seq", "fsdp"), "ctx"),
            P(("seq", "fsdp"), "ctx"),
        ),
        out_specs=(
            P(("seq", "fsdp"), "ctx", None),
            P(("seq", "fsdp"), "ctx", None),
            P(),
            P(),
            P(("seq", "fsdp"), "ctx"),
            P(("seq", "fsdp"), "ctx"),
            P(("seq", "fsdp"), "ctx"),
            P(("seq", "fsdp"), "ctx"),
            P(("seq", "fsdp"), "ctx"),
            P(("seq", "fsdp"), "ctx"),
            P(("seq", "fsdp"), "ctx"),
        ),
        check_vma=False,
    )
```

```python
import functools
import math

import jax
import jax.numpy as jnp
from jax import lax
from jax.experimental import pallas as pl
from jax.experimental.pallas import tpu as pltpu
from jax.sharding import PartitionSpec as P

HEADS = 15
KV_HEADS = 5
HEAD_DIM = 64
GROUP = HEADS // KV_HEADS
HALF = HEAD_DIM // 2
MESH = pl.DeviceIdType.MESH
MASKED = -1e30

rope_base = 100000.0
norm_eps = 1e-05
bf16 = jnp.bfloat16
f32 = jnp.float32


def norm_forward(values, gain):
    inverse_rms = lax.rsqrt(jnp.mean(values * values, axis=1, keepdims=True) + norm_eps)
    scaled = values * inverse_rms
    return (inverse_rms, scaled, (scaled * gain).astype(bf16))


def norm_backward(grad_in, inverse_rms, scaled, gain):
    weighted = grad_in * gain
    back = inverse_rms * (weighted - scaled * jnp.mean(weighted * scaled, axis=1, keepdims=True))
    return (back, jnp.sum(grad_in * scaled, axis=0))


def dot_nn(left, right):
    return jnp.dot(left, right, preferred_element_type=f32)


def dot_nt(left, right):
    return lax.dot_general(left, right, (((1,), (1,)), ((), ())), preferred_element_type=f32)


def dot_tn(left, right):
    return lax.dot_general(left, right, (((0,), (0,)), ((), ())), preferred_element_type=f32)


def wrap(index, count):
    return lax.rem(index + count, count)


class Place:
    def __init__(self, sizes):
        self.rows_outer, self.rows_inner, self.ctx = sizes
        self.row_parts = self.rows_outer * self.rows_inner
        self.chips = self.ctx // 2
        self.seq, self.fsdp, self.c = (lax.axis_index(n) for n in ("seq", "fsdp", "ctx"))
        self.row = self.seq * self.rows_inner + self.fsdp
        self.chip = self.c // 2
        self.core = self.c % 2

    def sibling(self):
        return (self.seq, self.fsdp, self.chip * 2 + 1 - self.core)

    def along(self, step):
        return (self.seq, self.fsdp, wrap(self.chip + step, self.chips) * 2 + self.core)

    def any_ctx(self, step):
        return (self.seq, self.fsdp, wrap(self.c + step, self.ctx))

    def across(self, step):
        row = wrap(self.row + step, self.row_parts)
        return (row // self.rows_inner, row % self.rows_inner, self.c)

    def chip_at(self, step):
        return wrap(self.chip + step, self.chips)

    def row_at(self, step):
        return wrap(self.row + step, self.row_parts)

    def greet(self, ctx=False, line=False, sibling=False, rows=False):
        devices = []
        if ctx:
            devices += [self.any_ctx(t) for t in range(1, self.ctx)]
        if line:
            devices += [self.along(t) for t in range(1, self.chips)]
        if sibling:
            devices += [self.sibling()]
        if rows:
            devices += [self.across(t) for t in range(1, self.row_parts)]
        barrier = pltpu.get_barrier_semaphore()
        for device in devices:
            pl.semaphore_signal(barrier, inc=1, device_id=device, device_id_type=MESH)
        pl.semaphore_wait(barrier, len(devices))


def remote(src, dst, send, recv, device):
    return pltpu.make_async_remote_copy(
        src_ref=src, dst_ref=dst, send_sem=send, recv_sem=recv, device_id=device, device_id_type=MESH
    )


def dma(*shape):
    return pltpu.SemaphoreType.DMA(shape)


class LineGather:
    def __init__(self, place, ref, out, sems):
        self.p, self.ref, self.out = place, ref, out
        self.zs, self.zr, self.bs, self.br = sems

    @staticmethod
    def scratch(sizes):
        chips = sizes[2] // 2
        return [dma(2, chips), dma(2, chips), dma(2, chips), dma(2, chips)]

    def source(self, way, d):
        return self.p.chip - d if way == 0 else self.p.chip + d

    def has(self, way, d):
        return self.p.chip >= d if way == 0 else self.p.chip + d < self.p.chips

    def onward(self, way):
        return self.p.chip + 1 < self.p.chips if way == 0 else self.p.chip >= 1

    def slot(self, way, d, core):
        return self.out.at[self.source(way, d) * 2 + core]

    def hop(self, way, d, own=False):
        mine = self.slot(way, d, self.p.core)
        src = self.ref if own else mine
        return remote(src, mine, self.zs.at[way, d], self.zr.at[way, d], self.p.along(1 - 2 * way))

    def landed(self, way, d):
        mine = self.slot(way, d, self.p.core)
        return remote(mine, mine, self.zs.at[way, d - 1], self.zr.at[way, d - 1], self.p.along(1 - 2 * way))

    def to_sibling(self, way, d, own=False):
        mine = self.slot(way, d, self.p.core)
        src = self.ref if own else mine
        return remote(src, mine, self.bs.at[way, d], self.br.at[way, d], self.p.sibling())

    def from_sibling(self, way, d):
        mine = self.slot(way, d, 1 - self.p.core)
        return remote(mine, mine, self.bs.at[way, d], self.br.at[way, d], self.p.sibling())

    def start(self):
        for way in range(2):
            pl.when(self.onward(way))(lambda way=way: self.hop(way, 0, True).start())
        self.to_sibling(0, 0, True).start()
        self.out[self.p.c] = self.ref[...]

    def forward_way(self, way, d):
        self.landed(way, d).wait_recv()
        pl.when(self.onward(way))(lambda: self.hop(way, d).start())
        self.to_sibling(way, d).start()

    def forward(self, d):
        for way in range(2):
            pl.when(self.has(way, d))(lambda way=way: self.forward_way(way, d))

    def arrive(self):
        self.from_sibling(0, 0).wait_recv()
        for d in range(1, self.p.chips):
            for way in range(2):
                pl.when(self.has(way, d))(lambda way=way, d=d: self.from_sibling(way, d).wait_recv())

    def finish(self):
        self.to_sibling(0, 0, True).wait_send()
        for d in range(self.p.chips):
            for way in range(2):

                @pl.when(self.has(way, d))
                def _(way=way, d=d):
                    pl.when(self.onward(way))(lambda: self.hop(way, d, d == 0).wait_send())
                    if d:
                        self.to_sibling(way, d).wait_send()


class FullGather:
    def __init__(self, place, ref, out, sems):
        self.p, self.ref, self.out = place, ref, out
        self.zs, self.zr = sems[:2]
        self.row_sems = sems[2:8]
        self.bs, self.br = sems[8:10]
        rows = ref.shape[0]
        self.half = (rows // 2 + 15) // 16 * 16
        self.parts = (pl.ds(0, self.half), pl.ds(self.half, rows - self.half))
        self.tags = [(0, 0)] + [(way, d) for d in range(1, place.chips) for way in range(2)]

    @staticmethod
    def scratch(sizes):
        chips = sizes[2] // 2
        count, outer, inner = 2 * chips - 1, sizes[0], sizes[1]
        line = [dma(2, chips)] * 2
        direct = [dma(count, 2, max(outer, inner))] * 2
        bent = [dma(count, 2, outer, inner)] * 2
        spare = [dma(1)] * 2
        return line + direct + bent + spare + [dma(count, outer, inner)] * 2

    def source(self, way, d):
        return self.p.chip - d if way == 0 else self.p.chip + d

    def has(self, way, d):
        return self.p.chip >= d if way == 0 else self.p.chip + d < self.p.chips

    def onward(self, way):
        return self.p.chip + 1 < self.p.chips if way == 0 else self.p.chip >= 1

    def when_has(self, tag, action):
        if tag[1] == 0:
            action()
        else:
            pl.when(self.has(*tag))(action)

    def row(self, a, b):
        seq = wrap(self.p.seq - a, self.p.rows_outer)
        return seq * self.p.rows_inner + wrap(self.p.fsdp - b, self.p.rows_inner)

    def slot(self, tag, core, a=0, b=0):
        return self.out.at[self.source(*tag) * 2 + core, self.row(a, b)]

    def device(self, a, b):
        return (wrap(self.p.seq + a, self.p.rows_outer), wrap(self.p.fsdp + b, self.p.rows_inner), self.p.c)

    def hop(self, way, d):
        mine = self.slot((way, d), self.p.core)
        src = self.ref if d == 0 else mine
        return remote(src, mine, self.zs.at[way, d], self.zr.at[way, d], self.p.along(1 - 2 * way))

    def landed(self, way, d):
        mine = self.slot((way, d), self.p.core)
        return remote(mine, mine, self.zs.at[way, d - 1], self.zr.at[way, d - 1], self.p.along(1 - 2 * way))

    def direct(self, tag, a, b):
        q, axis = self.tags.index(tag), 0 if a else 1
        mine = self.slot(tag, self.p.core)
        src = self.ref if tag[1] == 0 else mine
        sems = [sem.at[q, axis, a + b] for sem in self.row_sems[:2]]
        return remote(src, mine, *sems, self.device(a, b))

    def direct_in(self, tag, a, b):
        q, axis = self.tags.index(tag), 0 if a else 1
        mine = self.slot(tag, self.p.core, a, b)
        sems = [sem.at[q, axis, a + b] for sem in self.row_sems[:2]]
        return remote(mine, mine, *sems, self.device(a, b))

    def bent(self, tag, part, a, b):
        q = self.tags.index(tag)
        mine = (self.slot(tag, self.p.core, a, 0) if part == 0 else self.slot(tag, self.p.core, 0, b)).at[self.parts[part]]
        sems = [sem.at[q, part, a, b] for sem in self.row_sems[2:4]]
        return remote(mine, mine, *sems, self.device(0, b) if part == 0 else self.device(a, 0))

    def bent_in(self, tag, part, a, b):
        q = self.tags.index(tag)
        mine = self.slot(tag, self.p.core, a, b).at[self.parts[part]]
        sems = [sem.at[q, part, a, b] for sem in self.row_sems[2:4]]
        return remote(mine, mine, *sems, self.device(0, b))

    def to_sibling(self, tag, a, b):
        q = self.tags.index(tag)
        mine = self.slot(tag, self.p.core, a, b)
        src = self.ref if (tag[1] == 0 and a == 0 and b == 0) else mine
        return remote(src, mine, self.bs.at[q, a, b], self.br.at[q, a, b], self.p.sibling())

    def from_sibling(self, tag, a, b):
        q = self.tags.index(tag)
        mine = self.slot(tag, 1 - self.p.core, a, b)
        return remote(mine, mine, self.bs.at[q, a, b], self.br.at[q, a, b], self.p.sibling())

    def steps(self):
        outer = [(a, 0) for a in range(1, self.p.rows_outer)]
        inner = [(0, b) for b in range(1, self.p.rows_inner)]
        diagonal = [(a, b) for a in range(1, self.p.rows_outer) for b in range(1, self.p.rows_inner)]
        return outer, inner, diagonal

    def send_rows(self, tag):
        outer, inner, _ = self.steps()
        for a, b in outer + inner:
            self.direct(tag, a, b).start()
        self.to_sibling(tag, 0, 0).start()

    def start(self, rows=True):
        for way in range(2):
            pl.when(self.onward(way))(lambda way=way: self.hop(way, 0).start())
        if rows:
            self.send_rows((0, 0))
        self.out[self.p.c, self.p.row] = self.ref[...]

    def forward(self, d, rows=True):
        for way in range(2):

            @pl.when(self.has(way, d))
            def _(way=way):
                self.landed(way, d).wait_recv()
                pl.when(self.onward(way))(lambda: self.hop(way, d).start())
                if rows:
                    self.send_rows((way, d))

    def cross(self):
        for tag in self.tags:
            self.when_has(tag, lambda tag=tag: self.send_rows(tag))

    def bend(self, d):
        outer, inner, _ = self.steps()
        for tag in [(0, 0)] if d == 0 else [(0, d), (1, d)]:

            def action(tag=tag):
                for a, b in outer:
                    self.direct_in(tag, a, b).wait_recv()
                    for _, other in inner:
                        self.bent(tag, 0, a, other).start()
                    self.to_sibling(tag, a, b).start()
                for a, b in inner:
                    self.direct_in(tag, a, b).wait_recv()
                    for other, _ in outer:
                        self.bent(tag, 1, other, b).start()
                    self.to_sibling(tag, a, b).start()

            self.when_has(tag, action)

    def settle(self, d):
        for tag in [(0, 0)] if d == 0 else [(0, d), (1, d)]:

            def action(tag=tag):
                for a, b in self.steps()[2]:
                    for part in range(2):
                        self.bent_in(tag, part, a, b).wait_recv()
                    self.to_sibling(tag, a, b).start()

            self.when_has(tag, action)

    def every(self):
        return [(a, b) for a in range(self.p.rows_outer) for b in range(self.p.rows_inner)]

    def arrive(self):
        for tag in self.tags:

            def action(tag=tag):
                for a, b in self.every():
                    self.from_sibling(tag, a, b).wait_recv()

            self.when_has(tag, action)

    def finish(self):
        outer, inner, diagonal = self.steps()
        for tag in self.tags:

            def action(tag=tag):
                for way in range(2) if tag[1] == 0 else (tag[0],):
                    pl.when(self.onward(way))(lambda way=way: self.hop(way, tag[1]).wait_send())
                for a, b in outer + inner:
                    self.direct(tag, a, b).wait_send()
                for a, b in diagonal:
                    for part in range(2):
                        self.bent(tag, part, a, b).wait_send()
                for a, b in self.every():
                    self.to_sibling(tag, a, b).wait_send()

            self.when_has(tag, action)


class RowExchange:
    def __init__(self, place, src_of, dst_of, sems):
        self.p, self.src_of, self.dst_of = place, src_of, dst_of
        self.xs, self.xr = sems

    @staticmethod
    def scratch(sizes):
        rows = sizes[0] * sizes[1]
        return [dma(rows), dma(rows)]

    def send(self, k):
        return remote(self.src_of(k), self.dst_of(k, 0), self.xs.at[k], self.xr.at[k], self.p.across(k))

    def recv(self, k):
        mine = self.dst_of(k, k)
        return remote(mine, mine, self.xs.at[k], self.xr.at[k], self.p.across(k))

    def start(self):
        for k in range(1, self.p.row_parts):
            self.send(k).start()

    def arrive(self):
        for k in range(1, self.p.row_parts):
            self.recv(k).wait_recv()

    def finish(self):
        for k in range(1, self.p.row_parts):
            self.send(k).wait_send()


class CtxExchange:
    def __init__(self, place, src_of, dst_of, sems):
        self.p, self.src_of, self.dst_of = place, src_of, dst_of
        self.ss, self.sr = sems

    @staticmethod
    def scratch(sizes):
        return [dma(sizes[2]), dma(sizes[2])]

    def send(self, t):
        return remote(
            self.src_of(wrap(self.p.c + t, self.p.ctx)),
            self.dst_of(self.p.c),
            self.ss.at[t],
            self.sr.at[t],
            self.p.any_ctx(t),
        )

    def recv(self, t):
        mine = self.dst_of(wrap(self.p.c - t, self.p.ctx))
        return remote(mine, mine, self.ss.at[t], self.sr.at[t], self.p.any_ctx(t))

    def start(self):
        for t in range(1, self.p.ctx):
            self.send(t).start()

    def arrive(self):
        for t in range(1, self.p.ctx):
            self.recv(t).wait_recv()

    def finish(self):
        for t in range(1, self.p.ctx):
            self.send(t).wait_send()


def take(refs, count):
    return [next(refs) for _ in range(count)]


def rotate_rows(rows, cosine, sine):
    first, second = rows[:HALF], rows[HALF:]
    return jnp.concatenate([first * cosine - second * sine, second * cosine + first * sine], axis=0)


def rotate_rows_back(rows, cosine, sine):
    first, second = rows[:HALF], rows[HALF:]
    return jnp.concatenate([first * cosine + second * sine, second * cosine - first * sine], axis=0)


def group_rows(ref, g):
    return jnp.concatenate(
        [ref[pl.ds((g * GROUP + j) * HEAD_DIM, HEAD_DIM), :] for j in range(GROUP)], axis=1
    )


def turn(values):
    return values.astype(f32).T.astype(values.dtype)


def first_kernel(sizes, *refs):
    refs = iter(refs)
    (x_in, gain_ref, gain2_ref, wq_in, wk_in, wv_in, wo_in, wg_in, wu_in, wd_in, cot_in) = take(refs, 11)
    (cos_ref, sin_ref, posk_ref, posq_ref) = take(refs, 4)
    (attn_ref, q_ref, kv_ref, lse_ref, wqkv_full, wo_full, wm_full, wd_turned, cot_full) = take(refs, 9)
    (n1_turned, mid_ref, n2_ref) = take(refs, 3)
    (qkv_raw, kv_own, wd_rows, score_ref, wd_full, mid_turned, wd_wide) = take(refs, 7)
    (x_turned, wq_ref, wk_turned, wv_turned, wo_ref, wg_turned, wu_turned, wd_in_ref, cot_turned) = take(refs, 9)
    (wqkv_ref, wm_ref, wd_ref, cot_ref, load_sems) = take(refs, 5)
    qkv_sems, wo_sems = take(refs, 10), take(refs, 10)
    kv_sems, cot_sems = take(refs, 4), take(refs, 4)
    wm_sems, wd_sems, a2a_sems = take(refs, 2), take(refs, 2), take(refs, 2)

    place = Place(sizes)
    ctx, chips, row_parts = place.ctx, place.chips, place.row_parts
    width, tokens = x_turned.shape
    q_cols = HEADS * HEAD_DIM // ctx
    kv_cols = KV_HEADS * HEAD_DIM // ctx
    q_width, kv_width = HEADS * HEAD_DIM, KV_HEADS * HEAD_DIM
    qkv_cols = q_cols + 2 * kv_cols
    ff_part = wd_full.shape[1]
    per_row = ctx // row_parts

    qkv = FullGather(place, wqkv_ref, wqkv_full, qkv_sems)
    out = FullGather(place, wo_ref, wo_full, wo_sems)
    kv = LineGather(place, kv_own, kv_ref, kv_sems)
    cot = LineGather(place, cot_ref, cot_full, cot_sems)
    mlp = RowExchange(place, lambda k: wm_ref, lambda k, back: wm_full.at[place.row_at(-back)], wm_sems)
    down = RowExchange(place, lambda k: wd_ref, lambda k, back: wd_rows.at[place.row_at(-back)], wd_sems)

    def down_slice(c):
        return wd_rows.at[c // per_row, pl.ds(pl.multiple_of((c % per_row) * ff_part, 16), ff_part), :]

    spread = CtxExchange(place, down_slice, lambda c: wd_full.at[c], a2a_sems)

    loads = [
        pltpu.make_async_copy(src, dst, load_sems.at[i])
        for i, (src, dst) in enumerate(
            [
                (wq_in, wq_ref),
                (wk_in, wk_turned),
                (wv_in, wv_turned),
                (x_in, x_turned),
                (cot_in, cot_turned),
                (wo_in, wo_ref),
                (wg_in, wg_turned),
                (wu_in, wu_turned),
                (wd_in, wd_in_ref),
            ]
        )
    ]
    for load in loads:
        load.start()
    for load in loads[:3]:
        load.wait()
    wqkv_ref[...] = jnp.concatenate([wq_ref[...], turn(wk_turned[...]), turn(wv_turned[...])], axis=1)
    place.greet(ctx=True, rows=True)
    qkv.start()
    for load in loads[3:]:
        load.wait()
    out.start(rows=False)
    normed = norm_forward(x_turned[...].astype(f32).T, gain_ref[...])[2]
    n1_turned[...] = turn(normed)
    cot_ref[...] = turn(cot_turned[...])
    for step in range(1, chips):
        qkv.forward(step)
        if step == 1:
            qkv.bend(0)
    for step in range(1, chips):
        out.forward(step, rows=False)
    cot.start()
    wd_ref[...] = turn(wd_in_ref[...])
    wd_rows[place.row] = wd_ref[...]
    wm_ref[...] = jnp.concatenate([turn(wg_turned[...]), turn(wu_turned[...])], axis=1)
    for step in range(1, chips):
        qkv.bend(step)
        qkv.settle(step - 1)
        if step == chips // 2:
            cot.forward(1)
    wm_full[place.row] = wm_ref[...]
    qkv.settle(chips - 1)
    down.start()
    for step in range(2, chips):
        cot.forward(step)
    qkv.arrive()

    for c in range(ctx):
        part = dot_nn(normed, wqkv_full[c].reshape(width, qkv_cols)).T
        qkv_raw[pl.ds(c * q_cols, q_cols), :] = part[:q_cols]
        qkv_raw[pl.ds(q_width + c * kv_cols, kv_cols), :] = part[q_cols : q_cols + kv_cols]
        qkv_raw[pl.ds(q_width + kv_width + c * kv_cols, kv_cols), :] = part[q_cols + kv_cols :]
    cosine, sine = cos_ref[...], sin_ref[...]
    for g in range(KV_HEADS):
        key = rotate_rows(qkv_raw[pl.ds(q_width + g * HEAD_DIM, HEAD_DIM), :], cosine, sine)
        value = qkv_raw[pl.ds(q_width + kv_width + g * HEAD_DIM, HEAD_DIM), :]
        pair = jnp.concatenate([key, value], axis=0).T
        kv_own[:, pl.ds(g * 2 * HEAD_DIM, 2 * HEAD_DIM)] = pair.astype(bf16)
    kv.start()
    out.cross()
    mlp.start()
    for h in range(HEADS):
        q_ref[pl.ds(h * HEAD_DIM, HEAD_DIM), :] = rotate_rows(
            qkv_raw[pl.ds(h * HEAD_DIM, HEAD_DIM), :], cosine, sine
        ).astype(bf16)
    for step in range(1, chips):
        kv.forward(step)
    down.arrive()
    spread.start()
    wd_full[place.c] = down_slice(place.c)[...]
    kv.arrive()

    scale = 1.0 / math.sqrt(HEAD_DIM)
    query_pos = posq_ref[...]
    chunk = 2 * tokens
    wide = GROUP * tokens
    for g in range(KV_HEADS):
        lanes = pl.ds(g * 2 * HEAD_DIM, 2 * HEAD_DIM)
        query = group_rows(q_ref, g) * jnp.asarray(scale, bf16)
        query = jnp.concatenate([query, jnp.zeros_like(query)], axis=0)

        def score(i, total, lanes=lanes, query=query):
            keys = kv_ref[pl.ds(2 * i, 2), :, lanes].reshape(chunk, 2 * HEAD_DIM)
            rows = pl.ds(pl.multiple_of(i * chunk, chunk), chunk)
            scores = jnp.where(posk_ref[rows, :] <= query_pos, dot_nn(keys, query), MASKED)
            score_ref[rows, :] = scores
            return total + jnp.sum(jnp.exp(scores), axis=0, keepdims=True)

        log_total = jnp.log(lax.fori_loop(0, chips, score, jnp.zeros((1, wide), f32)))
        lse_ref[g] = log_total

        def gather_values(i, total, lanes=lanes, log_total=log_total):
            keys = kv_ref[pl.ds(2 * i, 2), :, lanes].reshape(chunk, 2 * HEAD_DIM)
            rows = pl.ds(pl.multiple_of(i * chunk, chunk), chunk)
            prob = jnp.exp(score_ref[rows, :] - log_total).astype(bf16)
            return total + dot_tn(keys, prob)

        total = lax.fori_loop(0, chips, gather_values, jnp.zeros((2 * HEAD_DIM, wide), f32))
        for j in range(GROUP):
            attn_ref[pl.ds((g * GROUP + j) * HEAD_DIM, HEAD_DIM), :] = total[
                HEAD_DIM:, j * tokens : (j + 1) * tokens
            ].astype(bf16)
        if g == 1:
            for step in range(chips):
                out.bend(step)
        if g == 3:
            for step in range(chips):
                out.settle(step)
    out.arrive()
    out_cols = wo_ref.shape[1]
    attn = attn_ref[...]
    for c in range(ctx):
        rows = pl.ds(c * out_cols, out_cols)
        mid_turned[rows, :] = dot_tn(wo_full[c].reshape(q_width, out_cols), attn)
    middle = (x_turned[...].astype(f32) + mid_turned[...]).T
    mid_ref[...] = middle
    n2_ref[...] = norm_forward(middle, gain2_ref[...])[2]
    cot.arrive()
    mlp.arrive()
    spread.arrive()
    down_cols = wd_ref.shape[1]
    for c in range(ctx):
        wd_wide[pl.ds(c * down_cols, down_cols), :] = wd_full[c].astype(f32).T
    wd_turned[...] = wd_wide[...].astype(bf16)
    for part in (qkv, kv, out, mlp, down, cot, spread):
        part.finish()


def mlp_kernel(sizes, *refs):
    refs = iter(refs)
    n_ref, cot_ref, wm_ref, wd_ref = take(refs, 4)
    ngrad_ref, osums_ref, dwm_ref, dwd_ref = take(refs, 4)
    n_all, gub_all, hid_all, part_ref, sib_ref, far_ref, wide_ref = take(refs, 7)
    n_sems = take(refs, 4)
    bs, br, zs, zr = take(refs, 4)

    place = Place(sizes)
    ctx, chips = place.ctx, place.chips
    tokens, width = n_ref.shape
    ff = wd_ref.shape[1]
    chunk = 2 * tokens
    gather = LineGather(place, n_ref, n_all, n_sems)

    place.greet(line=True, sibling=True)
    gather.start()

    def work(p):
        rows = pl.ds(pl.multiple_of(p * chunk, chunk), chunk)
        normed = n_all[pl.ds(2 * p, 2)].reshape(chunk, width)
        cot = cot_ref[pl.ds(2 * p, 2)].reshape(chunk, width)
        gate_up = dot_nn(normed, wm_ref[...])
        gate, up = gate_up[:, :ff], gate_up[:, ff:]
        sigmoid_gate = jax.nn.sigmoid(gate)
        silu_gate = gate * sigmoid_gate
        hidden = (silu_gate * up).astype(bf16)
        hidden_grad = dot_nn(cot, wd_ref[...])
        gate_back = hidden_grad * up * sigmoid_gate * (1.0 + gate * (1.0 - sigmoid_gate))
        up_back = hidden_grad * silu_gate
        both = jnp.concatenate([gate_back, up_back], axis=1).astype(bf16)
        gub_all[rows, :] = both
        hid_all[rows, :] = hidden
        part_ref[p, :, 0] = dot_nt(both, wm_ref[...]).astype(bf16).reshape(2, tokens, width)
        part_ref[p, :, 1] = dot_nt(hidden, wd_ref[...]).astype(bf16).reshape(2, tokens, width)
        to_sibling(p).start()

    def to_sibling(p):
        return remote(part_ref.at[p, 1 - place.core], sib_ref.at[p], bs.at[p], br.at[p], place.sibling())

    def settle(p):
        to_sibling(p).wait_recv()
        both = (part_ref[p, place.core].astype(f32) + sib_ref[p].astype(f32)).astype(bf16)
        part_ref[p, place.core, 0] = both[0]
        osums_ref[p] = both[1]

    def target(way, d):
        return place.chip + d if way == 0 else place.chip - d

    def exists(way, d):
        return place.chip + d < chips if way == 0 else place.chip >= d

    def upstream(way):
        return place.chip >= 1 if way == 0 else place.chip + 1 < chips

    def landing(way, d):
        return target(way, d) if (way == 0 or d) else chips

    def onward(way, d):
        p = target(way, d)
        slot = p if (way == 0 or d > 1) else chips
        return remote(
            part_ref.at[p, place.core, 0],
            far_ref.at[slot],
            zs.at[way, d],
            zr.at[way, d],
            place.along(1 - 2 * way),
        )

    def inward(way, d):
        mine = far_ref.at[landing(way, d)]
        return remote(mine, mine, zs.at[way, d + 1], zr.at[way, d + 1], place.along(1 - 2 * way))

    gather.from_sibling(0, 0).wait_recv()
    work(place.chip)
    for d in range(1, chips):
        gather.forward(d)
        for way in range(2):
            @pl.when(exists(way, d))
            def _(way=way, d=d):
                gather.from_sibling(1 - way, d).wait_recv()
                work(target(way, d))

        if d == 1:
            settle(place.chip)
        for way in range(2):

            @pl.when(exists(way, d))
            def _(way=way, d=d):
                settle(target(way, d))

                @pl.when(jnp.logical_not(upstream(way)))
                def _():
                    onward(way, d).start()

    seq = ctx * tokens
    dwm_ref[...] = dot_tn(n_all[...].reshape(seq, width), gub_all[...]).astype(bf16).reshape(dwm_ref.shape)
    for d in range(chips - 1, 0, -1):
        for way in range(2):

            @pl.when(jnp.logical_and(exists(way, d), upstream(way)))
            def _(way=way, d=d):
                p = target(way, d)
                inward(way, d).wait_recv()
                both = part_ref[p, place.core, 0].astype(f32) + far_ref[p].astype(f32)
                part_ref[p, place.core, 0] = both.astype(bf16)
                onward(way, d).start()

    down_cols = dwd_ref.shape[2]
    wide_ref[...] = dot_tn(cot_ref[...].reshape(seq, width), hid_all[...])
    for c in range(ctx):
        dwd_ref[c] = wide_ref[pl.ds(c * down_cols, down_cols), :].T.astype(bf16)
    ngrad_ref[...] = part_ref[place.chip, place.core, 0].astype(f32)
    for way in range(2):

        @pl.when(upstream(way))
        def _(way=way):
            inward(way, 0).wait_recv()
            ngrad_ref[...] += far_ref[landing(way, 0)].astype(f32)

    gather.finish()
    for p in range(chips):
        to_sibling(p).wait_send()
    for d in range(1, chips):
        for way in range(2):

            @pl.when(exists(way, d))
            def _(way=way, d=d):
                onward(way, d).wait_send()


def back_kernel(sizes, *refs):
    refs = iter(refs)
    (q_ref, attn_ref, kv_ref, lse_ref, cos_ref, sin_ref, posk_ref, posq_ref, dwm_ref, dwd_ref) = take(refs, 10)
    ngrad_ref, mid_ref, gain_ref, cot_ref, wo_ref = take(refs, 5)
    qkvb_ref, fin_mlp, fin_down, mgrad_ref, midb_ref, gain_part = take(refs, 6)
    g_ref, mid_turned, q_back, kv_back = take(refs, 4)
    delta_ref, qz_ref, gz_ref, acc_ref, part_ref, sib_ref, far_ref = take(refs, 7)
    dwm_recv, down_rows, down_recv = take(refs, 3)
    bs, br, zs, zr = take(refs, 4)
    wm_sems, a2a_sems, wd_sems = take(refs, 2), take(refs, 2), take(refs, 2)

    place = Place(sizes)
    ctx, chips, row_parts = place.ctx, place.chips, place.row_parts
    tokens = q_ref.shape[1]
    chunk, wide = 2 * tokens, GROUP * tokens
    ff_part = dwd_ref.shape[1]
    per_row = ctx // row_parts
    scale = 1.0 / math.sqrt(HEAD_DIM)

    mlp = RowExchange(place, lambda k: dwm_ref.at[place.row_at(k)], lambda k, back: dwm_recv.at[k], wm_sems)

    def down_slot(c):
        return down_rows.at[c // per_row, pl.ds(pl.multiple_of((c % per_row) * ff_part, 16), ff_part), :]

    spread = CtxExchange(place, lambda c: dwd_ref.at[c], down_slot, a2a_sems)
    down = RowExchange(place, lambda k: down_rows.at[place.row_at(k)], lambda k, back: down_recv.at[k], wd_sems)

    place.greet(ctx=True, rows=True)
    mlp.start()
    spread.start()
    down_slot(place.c)[...] = dwd_ref[place.c]

    inverse_rms, unit, _ = norm_forward(mid_ref[...], gain_ref[...])
    mlp_back, gain_part[0] = norm_backward(ngrad_ref[...], inverse_rms, unit, gain_ref[...])
    mid_grad = cot_ref[...].astype(f32).T + mlp_back
    mgrad_ref[...] = mid_grad
    mid_turned[...] = mid_grad.T
    out_cols = wo_ref.shape[3]
    total = jnp.zeros(g_ref.shape, f32)
    for c in range(ctx):
        piece = mid_turned[pl.ds(c * out_cols, out_cols), :].astype(bf16)
        midb_ref[c] = piece
        total = total + dot_nn(wo_ref[c].reshape(g_ref.shape[0], out_cols), piece)
    g_ref[...] = total.astype(bf16)

    zeros = jnp.zeros((HEAD_DIM, wide), bf16)
    for g in range(KV_HEADS):
        query = group_rows(q_ref, g) * jnp.asarray(scale, bf16)
        grad = group_rows(g_ref, g)
        qz_ref[g] = jnp.concatenate([query, zeros], axis=0)
        gz_ref[g] = jnp.concatenate([zeros, grad], axis=0)
        delta_ref[g] = jnp.sum(grad.astype(f32) * group_rows(attn_ref, g).astype(f32), axis=0, keepdims=True)
        acc_ref[g] = jnp.zeros_like(acc_ref[g])
    query_pos = posq_ref[...]

    def to_sibling(j):
        return remote(part_ref.at[j, 1 - place.core], sib_ref.at[j], bs.at[j], br.at[j], place.sibling())

    def to_owner(j):
        return remote(part_ref.at[j, place.core], far_ref.at[j], zs.at[j], zr.at[j], place.along(j))

    def settle(j):
        to_sibling(j).wait_recv()
        both = part_ref[j, place.core].astype(f32) + sib_ref[j].astype(f32)
        part_ref[j, place.core] = both.astype(bf16)

    def work(j):
        p = place.chip_at(j)
        rows = pl.ds(pl.multiple_of(p * chunk, chunk), chunk)
        allowed = posk_ref[rows, :] <= query_pos
        for g in range(KV_HEADS):
            lanes = pl.ds(g * 2 * HEAD_DIM, 2 * HEAD_DIM)
            keys = kv_ref[pl.ds(2 * p, 2), :, lanes].reshape(chunk, 2 * HEAD_DIM)
            query, grad = qz_ref[g], gz_ref[g]
            scores = jnp.where(allowed, dot_nn(keys, query), MASKED)
            prob = jnp.exp(scores - lse_ref[g])
            score_grad = (prob * (dot_nn(keys, grad) - delta_ref[g])).astype(bf16)
            both = dot_nt(score_grad, query) + dot_nt(prob.astype(bf16), grad)
            part_ref[j, :, :, lanes] = both.astype(bf16).reshape(2, tokens, 2 * HEAD_DIM)
            acc_ref[g] += dot_tn(keys, score_grad)
        to_sibling(j).start()

    work(1)

    def turn(j, carry):
        work(j)
        settle(j - 1)
        to_owner(j - 1).start()
        return carry

    lax.fori_loop(2, chips, turn, 0)
    spread.arrive()
    down.start()
    work(0)
    settle(chips - 1)
    to_owner(chips - 1).start()
    cosine, sine = cos_ref[...], sin_ref[...]
    for h in range(HEADS):
        g, j = h // GROUP, h % GROUP
        head = acc_ref[g, pl.ds(0, HEAD_DIM), pl.ds(j * tokens, tokens)] * scale
        q_back[pl.ds(h * HEAD_DIM, HEAD_DIM), :] = rotate_rows_back(head, cosine, sine)
    settle(0)
    mlp.arrive()
    total = dwm_ref[place.row].astype(f32)
    for k in range(1, row_parts):
        total = total + dwm_recv[k].astype(f32)
    fin_mlp[...] = total
    total = part_ref[0, place.core].astype(f32)
    for j in range(1, chips):
        to_owner(j).wait_recv()
        total = total + far_ref[j].astype(f32)
    total = total.T
    kv_width = KV_HEADS * HEAD_DIM
    for g in range(KV_HEADS):
        pair = total[g * 2 * HEAD_DIM : (g + 1) * 2 * HEAD_DIM]
        rows = pl.ds(g * HEAD_DIM, HEAD_DIM)
        kv_back[rows, :] = rotate_rows_back(pair[:HEAD_DIM], cosine, sine)
        kv_back[pl.ds(kv_width + g * HEAD_DIM, HEAD_DIM), :] = pair[HEAD_DIM:]
    q_cols, kv_cols = q_back.shape[0] // ctx, kv_width // ctx
    for c in range(ctx):
        qkvb_ref[c] = jnp.concatenate(
            [
                q_back[pl.ds(c * q_cols, q_cols), :],
                kv_back[pl.ds(c * kv_cols, kv_cols), :],
                kv_back[pl.ds(kv_width + c * kv_cols, kv_cols), :],
            ],
            axis=0,
        ).astype(bf16)
    down.arrive()
    total = down_rows[place.row].astype(f32)
    for k in range(1, row_parts):
        total = total + down_recv[k].astype(f32)
    fin_down[...] = total
    for part in (mlp, spread, down):
        part.finish()
    for j in range(chips):
        to_sibling(j).wait_send()
        if j:
            to_owner(j).wait_send()


def last_kernel(sizes, *refs):
    refs = iter(refs)
    n1_ref, qkvb_ref, attn_ref, midb_ref, osums_ref, mid_ref = take(refs, 6)
    x_ref, gain_ref, gain_part, mgrad_ref, wqkv_ref = take(refs, 5)
    fin_ref, gain_out, result_ref, input_ref = take(refs, 4)
    part_ref, sib_ref, bent_ref, row_ref, far_send, far_ref = take(refs, 6)
    gain_sib, gain_row, gain_far, gain_a, gain_b, gain_c = take(refs, 6)
    bs, br, vs, vr, xs, xr, zs, zr = take(refs, 8)
    gb, gx, gz = take(refs, 2), take(refs, 2), take(refs, 2)
    osum_far, os, orr = take(refs, 3)

    place = Place(sizes)
    chips, row_parts, outer, inner = place.chips, place.row_parts, place.rows_outer, place.rows_inner
    core, row, chip = place.core, place.row, place.chip
    in_rows = fin_ref.shape[0]
    half = (in_rows // 2 + 15) // 16 * 16
    parts = (pl.ds(0, half), pl.ds(half, in_rows - half))
    sized = (pl.ds(0, half), pl.ds(0, in_rows - half))
    sides = [(a, 0) for a in range(1, outer)] + [(0, b) for b in range(1, inner)]
    diagonal = [(a, b) for a in range(1, outer) for b in range(1, inner)]
    place.greet(line=True, sibling=True, rows=True)

    def row_of(a, b):
        return wrap(place.seq + a, outer) * inner + wrap(place.fsdp + b, inner)

    def device(a, b):
        return (wrap(place.seq + a, outer), wrap(place.fsdp + b, inner), place.c)

    def to_sibling(j):
        return remote(
            part_ref.at[place.chip_at(j) * 2 + 1 - core], sib_ref.at[j], bs.at[j], br.at[j], place.sibling()
        )

    def bent(j, part, n):
        a, b = diagonal[n]
        return remote(
            sib_ref.at[j, row_of(a, b), parts[part]],
            bent_ref.at[j, part, n, sized[part]],
            vs.at[j, part, n],
            vr.at[j, part, n],
            device(0, b) if part == 0 else device(a, 0),
        )

    def direct(j, n):
        a, b = sides[n]
        return remote(sib_ref.at[j, row_of(a, b)], row_ref.at[j, n], xs.at[j, n], xr.at[j, n], device(a, b))

    def to_owner(j):
        return remote(far_send.at[j], far_ref.at[j], zs.at[j], zr.at[j], place.along(j))

    def g_sib():
        return remote(gain_a, gain_sib.at[core], gb[0].at[0], gb[1].at[0], place.sibling())

    def g_row(k):
        return remote(gain_b, gain_row.at[row], gx[0].at[k], gx[1].at[k], place.across(k))

    def g_far(j):
        return remote(gain_c, gain_far.at[chip], gz[0].at[j], gz[1].at[j], place.along(j))

    def input_gradient():
        width = x_ref.shape[0]
        total = jnp.zeros(x_ref.shape, f32)
        for c in range(place.ctx):
            total = total + dot_nn(wqkv_ref[c].reshape(width, wqkv_ref.shape[3]), qkvb_ref[c])
        inverse_rms, unit, _ = norm_forward(x_ref[...].astype(f32).T, gain_ref[...])
        back, gain_a[0] = norm_backward(total.T, inverse_rms, unit, gain_ref[...])
        input_ref[...] = (mgrad_ref[...] + back).T.astype(bf16)
        gain_a[1] = gain_part[0]
        gain_sib[core] = gain_a[...]
        g_sib().start()

    def multiply(j):
        for k in range(2):
            c = place.chip_at(j) * 2 + k
            both = jnp.concatenate(
                [dot_nt(n1_ref[...], qkvb_ref[c]), dot_nt(attn_ref[...], midb_ref[c])], axis=1
            )
            part_ref[c] = both.astype(bf16).reshape(part_ref.shape[1:])
        to_sibling(j).start()

    def add_sibling(j):
        to_sibling(j).wait_recv()
        both = part_ref[place.chip_at(j) * 2 + core].astype(f32) + sib_ref[j].astype(f32)
        sib_ref[j] = both.astype(bf16)
        for n in range(len(diagonal)):
            for part in range(2):
                bent(j, part, n).start()

    def add_bent(j):
        for n, (a, b) in enumerate(diagonal):
            for part in range(2):
                bent(j, part, n).wait_recv()
                at = (j, row_of(a, 0) if part == 0 else row_of(0, b), parts[part])
                both = sib_ref[at].astype(f32) + bent_ref[j, part, n, sized[part]].astype(f32)
                sib_ref[at] = both.astype(bf16)
        for n in range(len(sides)):
            direct(j, n).start()

    def add_rows(j):
        total = sib_ref[j, row].astype(f32)
        for n in range(len(sides)):
            direct(j, n).wait_recv()
            total = total + row_ref[j, n].astype(f32)
        if j:
            far_send[j] = total.astype(bf16)
            to_owner(j).start()
        else:
            fin_ref[...] = total

    def output_to(j):
        return remote(osums_ref.at[place.chip_at(j)], osum_far.at[j], os.at[j], orr.at[j], place.along(j))

    for j in range(1, chips):
        output_to(j).start()
    order = list(range(1, chips)) + [0]
    stages = (multiply, add_sibling, add_bent, add_rows)
    for t in range(chips + len(stages) - 1):
        for depth, stage in enumerate(stages):
            if 0 <= t - depth < chips:
                stage(order[t - depth])
        if t == 1:
            input_gradient()
        if t == 3:
            remote(gain_a, gain_sib.at[1 - core], gb[0].at[0], gb[1].at[0], place.sibling()).wait_recv()
            gain_b[...] = gain_sib[0] + gain_sib[1]
            gain_row[row] = gain_b[...]
            for k in range(1, row_parts):
                g_row(k).start()

    for k in range(1, row_parts):
        remote(gain_b, gain_row.at[place.row_at(-k)], gx[0].at[k], gx[1].at[k], place.across(k)).wait_recv()
    total = gain_row[0]
    for k in range(1, row_parts):
        total = total + gain_row[k]
    gain_c[...] = total
    gain_far[chip] = gain_c[...]
    for j in range(1, chips):
        g_far(j).start()
    total = mid_ref[...] + osums_ref[chip].astype(f32)
    for j in range(1, chips):
        output_to(j).wait_recv()
        total = total + osum_far[j].astype(f32)
    result_ref[...] = total.T.astype(bf16)
    total = fin_ref[...]
    for j in range(1, chips):
        to_owner(j).wait_recv()
        total = total + far_ref[j].astype(f32)
    fin_ref[...] = total
    for j in range(1, chips):
        remote(gain_c, gain_far.at[place.chip_at(-j)], gz[0].at[j], gz[1].at[j], place.along(j)).wait_recv()
    total = gain_far[0]
    for j in range(1, chips):
        total = total + gain_far[j]
    gain_out[...] = total

    g_sib().wait_send()
    for k in range(1, row_parts):
        g_row(k).wait_send()
    for j in range(1, chips):
        g_far(j).wait_send()
    for j in order:
        to_sibling(j).wait_send()
        for n in range(len(diagonal)):
            for part in range(2):
                bent(j, part, n).wait_send()
        for n in range(len(sides)):
            direct(j, n).wait_send()
        if j:
            to_owner(j).wait_send()
            output_to(j).wait_send()


def call(kernel, sizes, inputs, outs, scratch, collective_id, raw=()):
    vmem = pl.BlockSpec(memory_space=pltpu.VMEM)
    anywhere = pl.BlockSpec(memory_space=pl.ANY)
    return pl.pallas_call(
        functools.partial(kernel, sizes),
        out_shape=[jax.ShapeDtypeStruct(shape, kind) for shape, kind in outs],
        in_specs=[anywhere if i in raw else vmem for i in range(len(inputs))],
        out_specs=[vmem] * len(outs),
        scratch_shapes=scratch,
        compiler_params=pltpu.CompilerParams(
            collective_id=collective_id, has_side_effects=True, vmem_limit_bytes=60 * 1024 * 1024
        ),
    )(*inputs)


def on_device(
    tokens,
    cotangent,
    block_order,
    gain_attn,
    gain_mlp,
    w_query,
    w_key,
    w_value,
    w_out,
    w_gate,
    w_up,
    w_down,
):
    sizes = tuple(lax.axis_size(n) for n in ("seq", "fsdp", "ctx"))
    rows, ctx = sizes[0] * sizes[1], sizes[2]
    chips = ctx // 2
    row_count, width = tokens.shape[1], tokens.shape[2]
    seq_len = row_count * ctx
    block_total = block_order.shape[0]
    block_len = seq_len // block_total
    kv_width = KV_HEADS * HEAD_DIM
    q_width = HEADS * HEAD_DIM
    q_cols, kv_cols, ff_cols = w_query.shape[1], w_key.shape[1], w_gate.shape[1]
    out_cols, down_cols, down_rows = w_out.shape[1], w_down.shape[1], w_down.shape[0]
    in_rows = w_query.shape[0]
    qkv_cols = q_cols + 2 * kv_cols
    wide = GROUP * row_count

    slot_index = jnp.arange(seq_len, dtype=jnp.int32)
    owner_hit = (slot_index // block_len)[:, None] == jnp.arange(block_total, dtype=jnp.int32)[None, :]
    all_pos = (
        jnp.sum(jnp.where(owner_hit, block_order[None, :], 0), axis=1) * block_len + slot_index % block_len
    )
    own_pos = lax.dynamic_slice_in_dim(all_pos, lax.axis_index("ctx") * row_count, row_count)
    inverse = rope_base ** (-jnp.arange(HALF, dtype=f32) / HALF)
    angles = inverse[:, None] * own_pos.astype(f32)[None, :]
    cosine, sine = jnp.cos(angles), jnp.sin(angles)
    pos_keys = all_pos[:, None]
    pos_query = jnp.tile(own_pos, GROUP)[None, :]

    x = tokens[0]
    cot_rows = cotangent[0]
    turned = [jnp.transpose(w) for w in (w_key, w_value, w_gate, w_up, w_down)]
    wk_t, wv_t, wg_t, wu_t, wd_t = turned

    (
        attn_t,
        query_t,
        kv_all,
        lse,
        qkv_full,
        out_full,
        mlp_full,
        down_t,
        cot_all,
        normed_attn_t,
        middle,
        normed_mlp,
    ) = call(
        first_kernel,
        sizes,
        (
            jnp.transpose(x),
            gain_attn[None],
            gain_mlp[None],
            w_query,
            wk_t,
            wv_t,
            w_out,
            wg_t,
            wu_t,
            wd_t,
            jnp.transpose(cot_rows),
            cosine,
            sine,
            pos_keys,
            pos_query,
        ),
        [
            ((q_width, row_count), bf16),
            ((q_width, row_count), bf16),
            ((ctx, row_count, 2 * kv_width), bf16),
            ((KV_HEADS, 1, wide), f32),
            ((ctx, rows, in_rows, qkv_cols), bf16),
            ((ctx, rows, in_rows, out_cols), bf16),
            ((rows, in_rows, 2 * ff_cols), bf16),
            ((width, ff_cols), bf16),
            ((ctx, row_count, width), bf16),
            ((width, row_count), bf16),
            ((row_count, width), f32),
            ((row_count, width), bf16),
        ],
        [
            pltpu.VMEM((q_width + 2 * kv_width, row_count), f32),
            pltpu.VMEM((row_count, 2 * kv_width), bf16),
            pltpu.VMEM((rows, down_rows, down_cols), bf16),
            pltpu.VMEM((seq_len, wide), f32),
            pltpu.VMEM((ctx, ff_cols, down_cols), bf16),
            pltpu.VMEM((width, row_count), f32),
            pltpu.VMEM((width, ff_cols), f32),
            pltpu.VMEM((width, row_count), bf16),
        ]
        + [pltpu.VMEM(w.shape, bf16) for w in (w_query, wk_t, wv_t, w_out, wg_t, wu_t, wd_t)]
        + [
            pltpu.VMEM((width, row_count), bf16),
            pltpu.VMEM((in_rows, qkv_cols), bf16),
            pltpu.VMEM((in_rows, 2 * ff_cols), bf16),
            pltpu.VMEM(w_down.shape, bf16),
            pltpu.VMEM((row_count, width), bf16),
            dma(9),
        ]
        + FullGather.scratch(sizes)
        + FullGather.scratch(sizes)
        + LineGather.scratch(sizes)
        + LineGather.scratch(sizes)
        + RowExchange.scratch(sizes)
        + RowExchange.scratch(sizes)
        + CtxExchange.scratch(sizes),
        1,
        raw=(0, 3, 4, 5, 6, 7, 8, 9, 10),
    )

    w_mlp_cat = mlp_full.reshape(width, 2 * ff_cols)

    normed_mlp_grad, output_sums, d_mlp, d_down = call(
        mlp_kernel,
        sizes,
        (normed_mlp, cot_all, w_mlp_cat, down_t),
        [
            ((row_count, width), f32),
            ((chips, row_count, width), bf16),
            ((rows, in_rows, 2 * ff_cols), bf16),
            ((ctx, ff_cols, down_cols), bf16),
        ],
        [
            pltpu.VMEM((ctx, row_count, width), bf16),
            pltpu.VMEM((seq_len, 2 * ff_cols), bf16),
            pltpu.VMEM((seq_len, ff_cols), bf16),
            pltpu.VMEM((chips, 2, 2, row_count, width), bf16),
            pltpu.VMEM((chips, 2, row_count, width), bf16),
            pltpu.VMEM((chips + 1, row_count, width), bf16),
            pltpu.VMEM((width, ff_cols), f32),
        ]
        + LineGather.scratch(sizes)
        + [dma(chips)] * 2
        + [dma(2, chips)] * 2,
        2,
    )
    qkv_back_t, fin_mlp, fin_down, mid_grad, mid_back_t, gain_mlp_part = call(
        back_kernel,
        sizes,
        (
            query_t,
            attn_t,
            kv_all,
            lse,
            cosine,
            sine,
            pos_keys,
            pos_query,
            d_mlp,
            d_down,
            normed_mlp_grad,
            middle,
            gain_mlp[None],
            jnp.transpose(cot_rows),
            out_full,
        ),
        [
            ((ctx, qkv_cols, row_count), bf16),
            ((in_rows, 2 * ff_cols), f32),
            ((down_rows, down_cols), f32),
            ((row_count, width), f32),
            ((ctx, out_cols, row_count), bf16),
            ((1, width), f32),
        ],
        [
            pltpu.VMEM((q_width, row_count), bf16),
            pltpu.VMEM((width, row_count), f32),
            pltpu.VMEM((q_width, row_count), f32),
            pltpu.VMEM((2 * kv_width, row_count), f32),
            pltpu.VMEM((KV_HEADS, 1, wide), f32),
            pltpu.VMEM((KV_HEADS, 2 * HEAD_DIM, wide), bf16),
            pltpu.VMEM((KV_HEADS, 2 * HEAD_DIM, wide), bf16),
            pltpu.VMEM((KV_HEADS, 2 * HEAD_DIM, wide), f32),
            pltpu.VMEM((chips, 2, row_count, 2 * kv_width), bf16),
            pltpu.VMEM((chips, row_count, 2 * kv_width), bf16),
            pltpu.VMEM((chips, row_count, 2 * kv_width), bf16),
            pltpu.VMEM((rows, in_rows, 2 * ff_cols), bf16),
            pltpu.VMEM((rows, down_rows, down_cols), bf16),
            pltpu.VMEM((rows, down_rows, down_cols), bf16),
        ]
        + [dma(chips)] * 4
        + RowExchange.scratch(sizes)
        + CtxExchange.scratch(sizes)
        + RowExchange.scratch(sizes),
        3,
    )

    attn_cols = qkv_cols + out_cols
    gains = pltpu.VMEM((2, width), f32)
    half = (in_rows // 2 + 15) // 16 * 16
    corners, sides = (sizes[0] - 1) * (sizes[1] - 1), sizes[0] + sizes[1] - 2
    fin_attn, gain_sums, result_t, input_t = call(
        last_kernel,
        sizes,
        (
            normed_attn_t,
            qkv_back_t,
            attn_t,
            mid_back_t,
            output_sums,
            middle,
            jnp.transpose(x),
            gain_attn[None],
            gain_mlp_part,
            mid_grad,
            qkv_full,
        ),
        [
            ((in_rows, attn_cols), f32),
            ((2, width), f32),
            ((width, row_count), bf16),
            ((width, row_count), bf16),
        ],
        [
            pltpu.VMEM((ctx, rows, in_rows, attn_cols), bf16),
            pltpu.VMEM((chips, rows, in_rows, attn_cols), bf16),
            pltpu.VMEM((chips, 2, corners, half, attn_cols), bf16),
            pltpu.VMEM((chips, sides, in_rows, attn_cols), bf16),
            pltpu.VMEM((chips, in_rows, attn_cols), bf16),
            pltpu.VMEM((chips, in_rows, attn_cols), bf16),
            pltpu.VMEM((2, 2, width), f32),
            pltpu.VMEM((rows, 2, width), f32),
            pltpu.VMEM((chips, 2, width), f32),
            gains,
            gains,
            gains,
            dma(chips),
            dma(chips),
            dma(chips, 2, corners),
            dma(chips, 2, corners),
            dma(chips, sides),
            dma(chips, sides),
            dma(chips),
            dma(chips),
            dma(1),
            dma(1),
            dma(rows),
            dma(rows),
            dma(chips),
            dma(chips),
            pltpu.VMEM((chips, row_count, width), bf16),
            dma(chips),
            dma(chips),
        ],
        4,
    )
    return (
        jnp.transpose(result_t).reshape(1, row_count, width),
        jnp.transpose(input_t).reshape(1, row_count, width),
        gain_sums[0],
        gain_sums[1],
        fin_attn[:, :q_cols],
        fin_attn[:, q_cols : q_cols + kv_cols],
        fin_attn[:, q_cols + kv_cols : qkv_cols],
        fin_attn[:, qkv_cols:attn_cols],
        fin_mlp[:, :ff_cols],
        fin_mlp[:, ff_cols:],
        fin_down,
    )


def solution(mesh):
    return jax.shard_map(
        on_device,
        mesh=mesh,
        in_specs=(
            P(("seq", "fsdp"), "ctx", None),
            P(("seq", "fsdp"), "ctx", None),
            P(),
            P(),
            P(),
            P(("seq", "fsdp"), "ctx"),
            P(("seq", "fsdp"), "ctx"),
            P(("seq", "fsdp"), "ctx"),
            P(("seq", "fsdp"), "ctx"),
            P(("seq", "fsdp"), "ctx"),
            P(("seq", "fsdp"), "ctx"),
            P(("seq", "fsdp"), "ctx"),
        ),
        out_specs=(
            P(("seq", "fsdp"), "ctx", None),
            P(("seq", "fsdp"), "ctx", None),
            P(),
            P(),
            P(("seq", "fsdp"), "ctx"),
            P(("seq", "fsdp"), "ctx"),
            P(("seq", "fsdp"), "ctx"),
            P(("seq", "fsdp"), "ctx"),
            P(("seq", "fsdp"), "ctx"),
            P(("seq", "fsdp"), "ctx"),
            P(("seq", "fsdp"), "ctx"),
        ),
        check_vma=False,
    )
```

```python
import functools
import math

import jax
import jax.numpy as jnp
from jax import lax
from jax.experimental import pallas as pl
from jax.experimental.pallas import tpu as pltpu
from jax.sharding import PartitionSpec as P

HEADS = 15
KV_HEADS = 5
HEAD_DIM = 64
GROUP = HEADS // KV_HEADS
HALF = HEAD_DIM // 2
MESH = pl.DeviceIdType.MESH
MASKED = -1e30
UNROLL = 4

rope_base = 100000.0
norm_eps = 1e-05
bf16 = jnp.bfloat16
f32 = jnp.float32


def norm_forward(values, gain):
    inverse_rms = lax.rsqrt(jnp.mean(values * values, axis=1, keepdims=True) + norm_eps)
    scaled = values * inverse_rms
    return (inverse_rms, scaled, (scaled * gain).astype(bf16))


def norm_backward(grad_in, inverse_rms, scaled, gain):
    weighted = grad_in * gain
    back = inverse_rms * (weighted - scaled * jnp.mean(weighted * scaled, axis=1, keepdims=True))
    return (back, jnp.sum(grad_in * scaled, axis=0))


def dot_nn(left, right):
    return jnp.dot(left, right, preferred_element_type=f32)


def dot_nt(left, right):
    return lax.dot_general(left, right, (((1,), (1,)), ((), ())), preferred_element_type=f32)


def dot_tn(left, right):
    return lax.dot_general(left, right, (((0,), (0,)), ((), ())), preferred_element_type=f32)


def wrap(index, count):
    return lax.rem(index + count, count)


class Place:
    def __init__(self, sizes):
        self.rows_outer, self.rows_inner, self.ctx = sizes
        self.row_parts = self.rows_outer * self.rows_inner
        self.chips = self.ctx // 2
        self.seq, self.fsdp, self.c = (lax.axis_index(n) for n in ("seq", "fsdp", "ctx"))
        self.row = self.seq * self.rows_inner + self.fsdp
        self.chip = self.c // 2
        self.core = self.c % 2

    def sibling(self):
        return (self.seq, self.fsdp, self.chip * 2 + 1 - self.core)

    def along(self, step):
        return (self.seq, self.fsdp, wrap(self.chip + step, self.chips) * 2 + self.core)

    def any_ctx(self, step):
        return (self.seq, self.fsdp, wrap(self.c + step, self.ctx))

    def across(self, step):
        row = wrap(self.row + step, self.row_parts)
        return (row // self.rows_inner, row % self.rows_inner, self.c)

    def chip_at(self, step):
        return wrap(self.chip + step, self.chips)

    def row_at(self, step):
        return wrap(self.row + step, self.row_parts)

    def greet(self, ctx=False, line=False, sibling=False, rows=False):
        devices = []
        if ctx:
            devices += [self.any_ctx(t) for t in range(1, self.ctx)]
        if line:
            devices += [self.along(t) for t in range(1, self.chips)]
        if sibling:
            devices += [self.sibling()]
        if rows:
            devices += [self.across(t) for t in range(1, self.row_parts)]
        barrier = pltpu.get_barrier_semaphore()
        for device in devices:
            pl.semaphore_signal(barrier, inc=1, device_id=device, device_id_type=MESH)
        pl.semaphore_wait(barrier, len(devices))


def remote(src, dst, send, recv, device):
    return pltpu.make_async_remote_copy(
        src_ref=src, dst_ref=dst, send_sem=send, recv_sem=recv, device_id=device, device_id_type=MESH
    )


def dma(*shape):
    return pltpu.SemaphoreType.DMA(shape)


class LineGather:
    def __init__(self, place, ref, out, sems):
        self.p, self.ref, self.out = place, ref, out
        self.zs, self.zr, self.bs, self.br = sems

    @staticmethod
    def scratch(sizes):
        chips = sizes[2] // 2
        return [dma(2, chips), dma(2, chips), dma(2, chips), dma(2, chips)]

    def source(self, way, d):
        return self.p.chip - d if way == 0 else self.p.chip + d

    def has(self, way, d):
        return self.p.chip >= d if way == 0 else self.p.chip + d < self.p.chips

    def onward(self, way):
        return self.p.chip + 1 < self.p.chips if way == 0 else self.p.chip >= 1

    def slot(self, way, d, core):
        return self.out.at[self.source(way, d) * 2 + core]

    def hop(self, way, d, own=False):
        mine = self.slot(way, d, self.p.core)
        src = self.ref if own else mine
        return remote(src, mine, self.zs.at[way, d], self.zr.at[way, d], self.p.along(1 - 2 * way))

    def landed(self, way, d):
        mine = self.slot(way, d, self.p.core)
        return remote(mine, mine, self.zs.at[way, d - 1], self.zr.at[way, d - 1], self.p.along(1 - 2 * way))

    def to_sibling(self, way, d, own=False):
        mine = self.slot(way, d, self.p.core)
        src = self.ref if own else mine
        return remote(src, mine, self.bs.at[way, d], self.br.at[way, d], self.p.sibling())

    def from_sibling(self, way, d):
        mine = self.slot(way, d, 1 - self.p.core)
        return remote(mine, mine, self.bs.at[way, d], self.br.at[way, d], self.p.sibling())

    def start(self):
        for way in range(2):
            pl.when(self.onward(way))(lambda way=way: self.hop(way, 0, True).start())
        self.to_sibling(0, 0, True).start()
        self.out[self.p.c] = self.ref[...]

    def forward_way(self, way, d):
        self.landed(way, d).wait_recv()
        pl.when(self.onward(way))(lambda: self.hop(way, d).start())
        self.to_sibling(way, d).start()

    def forward(self, d):
        for way in range(2):
            pl.when(self.has(way, d))(lambda way=way: self.forward_way(way, d))

    def arrive(self):
        self.from_sibling(0, 0).wait_recv()
        for d in range(1, self.p.chips):
            for way in range(2):
                pl.when(self.has(way, d))(lambda way=way, d=d: self.from_sibling(way, d).wait_recv())

    def finish(self):
        self.to_sibling(0, 0, True).wait_send()
        for d in range(self.p.chips):
            for way in range(2):

                @pl.when(self.has(way, d))
                def _(way=way, d=d):
                    pl.when(self.onward(way))(lambda: self.hop(way, d, d == 0).wait_send())
                    if d:
                        self.to_sibling(way, d).wait_send()


class FullGather:
    def __init__(self, place, ref, out, sems):
        self.p, self.ref, self.out = place, ref, out
        self.zs, self.zr = sems[:2]
        self.row_sems = sems[2:8]
        self.bs, self.br = sems[8:10]
        rows = ref.shape[0]
        self.half = (rows // 2 + 15) // 16 * 16
        self.parts = (pl.ds(0, self.half), pl.ds(self.half, rows - self.half))
        self.tags = [(0, 0)] + [(way, d) for d in range(1, place.chips) for way in range(2)]

    @staticmethod
    def scratch(sizes):
        chips = sizes[2] // 2
        count, outer, inner = 2 * chips - 1, sizes[0], sizes[1]
        line = [dma(2, chips)] * 2
        direct = [dma(count, 2, max(outer, inner))] * 2
        bent = [dma(count, 2, outer, inner)] * 2
        spare = [dma(1)] * 2
        return line + direct + bent + spare + [dma(count, outer, inner)] * 2

    def source(self, way, d):
        return self.p.chip - d if way == 0 else self.p.chip + d

    def has(self, way, d):
        return self.p.chip >= d if way == 0 else self.p.chip + d < self.p.chips

    def onward(self, way):
        return self.p.chip + 1 < self.p.chips if way == 0 else self.p.chip >= 1

    def when_has(self, tag, action):
        if tag[1] == 0:
            action()
        else:
            pl.when(self.has(*tag))(action)

    def row(self, a, b):
        seq = wrap(self.p.seq - a, self.p.rows_outer)
        return seq * self.p.rows_inner + wrap(self.p.fsdp - b, self.p.rows_inner)

    def slot(self, tag, core, a=0, b=0):
        return self.out.at[self.source(*tag) * 2 + core, self.row(a, b)]

    def device(self, a, b):
        return (wrap(self.p.seq + a, self.p.rows_outer), wrap(self.p.fsdp + b, self.p.rows_inner), self.p.c)

    def hop(self, way, d):
        mine = self.slot((way, d), self.p.core)
        src = self.ref if d == 0 else mine
        return remote(src, mine, self.zs.at[way, d], self.zr.at[way, d], self.p.along(1 - 2 * way))

    def landed(self, way, d):
        mine = self.slot((way, d), self.p.core)
        return remote(mine, mine, self.zs.at[way, d - 1], self.zr.at[way, d - 1], self.p.along(1 - 2 * way))

    def direct(self, tag, a, b):
        q, axis = self.tags.index(tag), 0 if a else 1
        mine = self.slot(tag, self.p.core)
        src = self.ref if tag[1] == 0 else mine
        sems = [sem.at[q, axis, a + b] for sem in self.row_sems[:2]]
        return remote(src, mine, *sems, self.device(a, b))

    def direct_in(self, tag, a, b):
        q, axis = self.tags.index(tag), 0 if a else 1
        mine = self.slot(tag, self.p.core, a, b)
        sems = [sem.at[q, axis, a + b] for sem in self.row_sems[:2]]
        return remote(mine, mine, *sems, self.device(a, b))

    def bent(self, tag, part, a, b):
        q = self.tags.index(tag)
        mine = (self.slot(tag, self.p.core, a, 0) if part == 0 else self.slot(tag, self.p.core, 0, b)).at[self.parts[part]]
        sems = [sem.at[q, part, a, b] for sem in self.row_sems[2:4]]
        return remote(mine, mine, *sems, self.device(0, b) if part == 0 else self.device(a, 0))

    def bent_in(self, tag, part, a, b):
        q = self.tags.index(tag)
        mine = self.slot(tag, self.p.core, a, b).at[self.parts[part]]
        sems = [sem.at[q, part, a, b] for sem in self.row_sems[2:4]]
        return remote(mine, mine, *sems, self.device(0, b))

    def to_sibling(self, tag, a, b):
        q = self.tags.index(tag)
        mine = self.slot(tag, self.p.core, a, b)
        src = self.ref if (tag[1] == 0 and a == 0 and b == 0) else mine
        return remote(src, mine, self.bs.at[q, a, b], self.br.at[q, a, b], self.p.sibling())

    def from_sibling(self, tag, a, b):
        q = self.tags.index(tag)
        mine = self.slot(tag, 1 - self.p.core, a, b)
        return remote(mine, mine, self.bs.at[q, a, b], self.br.at[q, a, b], self.p.sibling())

    def steps(self):
        outer = [(a, 0) for a in range(1, self.p.rows_outer)]
        inner = [(0, b) for b in range(1, self.p.rows_inner)]
        diagonal = [(a, b) for a in range(1, self.p.rows_outer) for b in range(1, self.p.rows_inner)]
        return outer, inner, diagonal

    def send_rows(self, tag):
        outer, inner, _ = self.steps()
        for a, b in outer + inner:
            self.direct(tag, a, b).start()
        self.to_sibling(tag, 0, 0).start()

    def start(self, rows=True):
        for way in range(2):
            pl.when(self.onward(way))(lambda way=way: self.hop(way, 0).start())
        if rows:
            self.send_rows((0, 0))
        self.out[self.p.c, self.p.row] = self.ref[...]

    def forward(self, d, rows=True):
        for way in range(2):

            @pl.when(self.has(way, d))
            def _(way=way):
                self.landed(way, d).wait_recv()
                pl.when(self.onward(way))(lambda: self.hop(way, d).start())
                if rows:
                    self.send_rows((way, d))

    def cross(self):
        for tag in self.tags:
            self.when_has(tag, lambda tag=tag: self.send_rows(tag))

    def bend(self, d):
        outer, inner, _ = self.steps()
        for tag in [(0, 0)] if d == 0 else [(0, d), (1, d)]:

            def action(tag=tag):
                for a, b in outer:
                    self.direct_in(tag, a, b).wait_recv()
                    for _, other in inner:
                        self.bent(tag, 0, a, other).start()
                    self.to_sibling(tag, a, b).start()
                for a, b in inner:
                    self.direct_in(tag, a, b).wait_recv()
                    for other, _ in outer:
                        self.bent(tag, 1, other, b).start()
                    self.to_sibling(tag, a, b).start()

            self.when_has(tag, action)

    def settle(self, d):
        for tag in [(0, 0)] if d == 0 else [(0, d), (1, d)]:

            def action(tag=tag):
                for a, b in self.steps()[2]:
                    for part in range(2):
                        self.bent_in(tag, part, a, b).wait_recv()
                    self.to_sibling(tag, a, b).start()

            self.when_has(tag, action)

    def every(self):
        return [(a, b) for a in range(self.p.rows_outer) for b in range(self.p.rows_inner)]

    def arrive(self):
        for tag in self.tags:

            def action(tag=tag):
                for a, b in self.every():
                    self.from_sibling(tag, a, b).wait_recv()

            self.when_has(tag, action)

    def finish(self):
        outer, inner, diagonal = self.steps()
        for tag in self.tags:

            def action(tag=tag):
                for way in range(2) if tag[1] == 0 else (tag[0],):
                    pl.when(self.onward(way))(lambda way=way: self.hop(way, tag[1]).wait_send())
                for a, b in outer + inner:
                    self.direct(tag, a, b).wait_send()
                for a, b in diagonal:
                    for part in range(2):
                        self.bent(tag, part, a, b).wait_send()
                for a, b in self.every():
                    self.to_sibling(tag, a, b).wait_send()

            self.when_has(tag, action)


class RowExchange:
    def __init__(self, place, src_of, dst_of, sems):
        self.p, self.src_of, self.dst_of = place, src_of, dst_of
        self.xs, self.xr = sems

    @staticmethod
    def scratch(sizes):
        rows = sizes[0] * sizes[1]
        return [dma(rows), dma(rows)]

    def send(self, k):
        return remote(self.src_of(k), self.dst_of(k, 0), self.xs.at[k], self.xr.at[k], self.p.across(k))

    def recv(self, k):
        mine = self.dst_of(k, k)
        return remote(mine, mine, self.xs.at[k], self.xr.at[k], self.p.across(k))

    def start(self):
        for k in range(1, self.p.row_parts):
            self.send(k).start()

    def arrive(self):
        for k in range(1, self.p.row_parts):
            self.recv(k).wait_recv()

    def finish(self):
        for k in range(1, self.p.row_parts):
            self.send(k).wait_send()


class CtxExchange:
    def __init__(self, place, src_of, dst_of, sems):
        self.p, self.src_of, self.dst_of = place, src_of, dst_of
        self.ss, self.sr = sems

    @staticmethod
    def scratch(sizes):
        return [dma(sizes[2]), dma(sizes[2])]

    def send(self, t):
        return remote(
            self.src_of(wrap(self.p.c + t, self.p.ctx)),
            self.dst_of(self.p.c),
            self.ss.at[t],
            self.sr.at[t],
            self.p.any_ctx(t),
        )

    def recv(self, t):
        mine = self.dst_of(wrap(self.p.c - t, self.p.ctx))
        return remote(mine, mine, self.ss.at[t], self.sr.at[t], self.p.any_ctx(t))

    def start(self):
        for t in range(1, self.p.ctx):
            self.send(t).start()

    def arrive(self):
        for t in range(1, self.p.ctx):
            self.recv(t).wait_recv()

    def finish(self):
        for t in range(1, self.p.ctx):
            self.send(t).wait_send()


def take(refs, count):
    return [next(refs) for _ in range(count)]


def rotate_rows(rows, cosine, sine):
    first, second = rows[:HALF], rows[HALF:]
    return jnp.concatenate([first * cosine - second * sine, second * cosine + first * sine], axis=0)


def rotate_rows_back(rows, cosine, sine):
    first, second = rows[:HALF], rows[HALF:]
    return jnp.concatenate([first * cosine + second * sine, second * cosine - first * sine], axis=0)


def group_rows(ref, g):
    return jnp.concatenate(
        [ref[pl.ds((g * GROUP + j) * HEAD_DIM, HEAD_DIM), :] for j in range(GROUP)], axis=1
    )


def turn(values):
    return values.astype(f32).T.astype(values.dtype)


def first_kernel(sizes, *refs):
    refs = iter(refs)
    (x_in, gain_ref, gain2_ref, wq_in, wk_in, wv_in, wo_in, wg_in, wu_in, wd_in, cot_in) = take(refs, 11)
    (cos_ref, sin_ref, posk_ref, posq_ref) = take(refs, 4)
    (attn_ref, q_ref, kv_ref, lse_ref, wqkv_full, wo_full, wm_full, wd_turned, cot_full) = take(refs, 9)
    (n1_turned, mid_ref, n2_ref) = take(refs, 3)
    (qkv_raw, kv_own, wd_rows, score_ref, wd_full, mid_turned, wd_wide) = take(refs, 7)
    (x_turned, wq_ref, wk_turned, wv_turned, wo_ref, wg_turned, wu_turned, wd_in_ref, cot_turned) = take(refs, 9)
    (wqkv_ref, wm_ref, wd_ref, cot_ref, load_sems) = take(refs, 5)
    qkv_sems, wo_sems = take(refs, 10), take(refs, 10)
    kv_sems, cot_sems = take(refs, 4), take(refs, 4)
    wm_sems, wd_sems, a2a_sems = take(refs, 2), take(refs, 2), take(refs, 2)

    place = Place(sizes)
    ctx, chips, row_parts = place.ctx, place.chips, place.row_parts
    width, tokens = x_turned.shape
    q_cols = HEADS * HEAD_DIM // ctx
    kv_cols = KV_HEADS * HEAD_DIM // ctx
    q_width, kv_width = HEADS * HEAD_DIM, KV_HEADS * HEAD_DIM
    qkv_cols = q_cols + 2 * kv_cols
    ff_part = wd_full.shape[1]
    per_row = ctx // row_parts

    qkv = FullGather(place, wqkv_ref, wqkv_full, qkv_sems)
    out = FullGather(place, wo_ref, wo_full, wo_sems)
    kv = LineGather(place, kv_own, kv_ref, kv_sems)
    cot = LineGather(place, cot_ref, cot_full, cot_sems)
    mlp = RowExchange(place, lambda k: wm_ref, lambda k, back: wm_full.at[place.row_at(-back)], wm_sems)
    down = RowExchange(place, lambda k: wd_ref, lambda k, back: wd_rows.at[place.row_at(-back)], wd_sems)

    def down_slice(c):
        return wd_rows.at[c // per_row, pl.ds(pl.multiple_of((c % per_row) * ff_part, 16), ff_part), :]

    spread = CtxExchange(place, down_slice, lambda c: wd_full.at[c], a2a_sems)

    loads = [
        pltpu.make_async_copy(src, dst, load_sems.at[i])
        for i, (src, dst) in enumerate(
            [
                (wq_in, wq_ref),
                (wk_in, wk_turned),
                (wv_in, wv_turned),
                (x_in, x_turned),
                (cot_in, cot_turned),
                (wo_in, wo_ref),
                (wg_in, wg_turned),
                (wu_in, wu_turned),
                (wd_in, wd_in_ref),
            ]
        )
    ]
    for load in loads:
        load.start()
    for load in loads[:3]:
        load.wait()
    wqkv_ref[...] = jnp.concatenate([wq_ref[...], turn(wk_turned[...]), turn(wv_turned[...])], axis=1)
    place.greet(ctx=True, rows=True)
    qkv.start()
    for load in loads[3:]:
        load.wait()
    out.start(rows=False)
    normed = norm_forward(x_turned[...].astype(f32).T, gain_ref[...])[2]
    n1_turned[...] = turn(normed)
    cot_ref[...] = turn(cot_turned[...])
    for step in range(1, chips):
        qkv.forward(step)
        if step == 1:
            qkv.bend(0)
    for step in range(1, chips):
        out.forward(step, rows=False)
    cot.start()
    wd_ref[...] = turn(wd_in_ref[...])
    wd_rows[place.row] = wd_ref[...]
    wm_ref[...] = jnp.concatenate([turn(wg_turned[...]), turn(wu_turned[...])], axis=1)
    for step in range(1, chips):
        qkv.bend(step)
        qkv.settle(step - 1)
        if step == chips // 2:
            cot.forward(1)
    wm_full[place.row] = wm_ref[...]
    qkv.settle(chips - 1)
    down.start()
    for step in range(2, chips):
        cot.forward(step)
    qkv.arrive()

    for c in range(ctx):
        part = dot_nn(normed, wqkv_full[c].reshape(width, qkv_cols)).T
        qkv_raw[pl.ds(c * q_cols, q_cols), :] = part[:q_cols]
        qkv_raw[pl.ds(q_width + c * kv_cols, kv_cols), :] = part[q_cols : q_cols + kv_cols]
        qkv_raw[pl.ds(q_width + kv_width + c * kv_cols, kv_cols), :] = part[q_cols + kv_cols :]
    cosine, sine = cos_ref[...], sin_ref[...]
    for g in range(KV_HEADS):
        key = rotate_rows(qkv_raw[pl.ds(q_width + g * HEAD_DIM, HEAD_DIM), :], cosine, sine)
        value = qkv_raw[pl.ds(q_width + kv_width + g * HEAD_DIM, HEAD_DIM), :]
        pair = jnp.concatenate([key, value], axis=0).T
        kv_own[:, pl.ds(g * 2 * HEAD_DIM, 2 * HEAD_DIM)] = pair.astype(bf16)
    kv.start()
    out.cross()
    mlp.start()
    for h in range(HEADS):
        q_ref[pl.ds(h * HEAD_DIM, HEAD_DIM), :] = rotate_rows(
            qkv_raw[pl.ds(h * HEAD_DIM, HEAD_DIM), :], cosine, sine
        ).astype(bf16)
    for step in range(1, chips):
        kv.forward(step)
    down.arrive()
    spread.start()
    wd_full[place.c] = down_slice(place.c)[...]
    kv.arrive()

    scale = 1.0 / math.sqrt(HEAD_DIM)
    query_pos = posq_ref[...]
    chunk = 2 * tokens
    wide = GROUP * tokens
    for g in range(KV_HEADS):
        lanes = pl.ds(g * 2 * HEAD_DIM, 2 * HEAD_DIM)
        query = group_rows(q_ref, g) * jnp.asarray(scale, bf16)
        query = jnp.concatenate([query, jnp.zeros_like(query)], axis=0)

        def score(i, total, lanes=lanes, query=query):
            keys = kv_ref[pl.ds(2 * i, 2), :, lanes].reshape(chunk, 2 * HEAD_DIM)
            rows = pl.ds(pl.multiple_of(i * chunk, chunk), chunk)
            scores = jnp.where(posk_ref[rows, :] <= query_pos, dot_nn(keys, query), MASKED)
            score_ref[rows, :] = scores
            return total + jnp.sum(jnp.exp(scores), axis=0, keepdims=True)

        log_total = jnp.log(lax.fori_loop(0, chips, score, jnp.zeros((1, wide), f32), unroll=UNROLL))
        lse_ref[g] = log_total

        def gather_values(i, total, lanes=lanes, log_total=log_total):
            keys = kv_ref[pl.ds(2 * i, 2), :, lanes].reshape(chunk, 2 * HEAD_DIM)
            rows = pl.ds(pl.multiple_of(i * chunk, chunk), chunk)
            prob = jnp.exp(score_ref[rows, :] - log_total).astype(bf16)
            return total + dot_tn(keys, prob)

        total = lax.fori_loop(
            0, chips, gather_values, jnp.zeros((2 * HEAD_DIM, wide), f32), unroll=UNROLL
        )
        for j in range(GROUP):
            attn_ref[pl.ds((g * GROUP + j) * HEAD_DIM, HEAD_DIM), :] = total[
                HEAD_DIM:, j * tokens : (j + 1) * tokens
            ].astype(bf16)
        if g == 1:
            for step in range(chips):
                out.bend(step)
        if g == 3:
            for step in range(chips):
                out.settle(step)
    out.arrive()
    out_cols = wo_ref.shape[1]
    attn = attn_ref[...]
    for c in range(ctx):
        rows = pl.ds(c * out_cols, out_cols)
        mid_turned[rows, :] = dot_tn(wo_full[c].reshape(q_width, out_cols), attn)
    middle = (x_turned[...].astype(f32) + mid_turned[...]).T
    mid_ref[...] = middle
    n2_ref[...] = norm_forward(middle, gain2_ref[...])[2]
    cot.arrive()
    mlp.arrive()
    spread.arrive()
    down_cols = wd_ref.shape[1]
    for c in range(ctx):
        wd_wide[pl.ds(c * down_cols, down_cols), :] = wd_full[c].astype(f32).T
    wd_turned[...] = wd_wide[...].astype(bf16)
    for part in (qkv, kv, out, mlp, down, cot, spread):
        part.finish()


def mlp_kernel(sizes, *refs):
    refs = iter(refs)
    n_ref, cot_ref, wm_ref, wd_ref = take(refs, 4)
    ngrad_ref, osums_ref, dwm_ref, dwd_ref = take(refs, 4)
    n_all, gub_all, hid_all, part_ref, sib_ref, far_ref, wide_ref = take(refs, 7)
    n_sems = take(refs, 4)
    bs, br, zs, zr = take(refs, 4)

    place = Place(sizes)
    ctx, chips = place.ctx, place.chips
    tokens, width = n_ref.shape
    ff = wd_ref.shape[1]
    chunk = 2 * tokens
    gather = LineGather(place, n_ref, n_all, n_sems)

    place.greet(line=True, sibling=True)
    gather.start()

    def work(p):
        rows = pl.ds(pl.multiple_of(p * chunk, chunk), chunk)
        normed = n_all[pl.ds(2 * p, 2)].reshape(chunk, width)
        cot = cot_ref[pl.ds(2 * p, 2)].reshape(chunk, width)
        gate_up = dot_nn(normed, wm_ref[...])
        gate, up = gate_up[:, :ff], gate_up[:, ff:]
        sigmoid_gate = jax.nn.sigmoid(gate)
        silu_gate = gate * sigmoid_gate
        hidden = (silu_gate * up).astype(bf16)
        hidden_grad = dot_nn(cot, wd_ref[...])
        gate_back = hidden_grad * up * sigmoid_gate * (1.0 + gate * (1.0 - sigmoid_gate))
        up_back = hidden_grad * silu_gate
        both = jnp.concatenate([gate_back, up_back], axis=1).astype(bf16)
        gub_all[rows, :] = both
        hid_all[rows, :] = hidden
        part_ref[p, :, 0] = dot_nt(both, wm_ref[...]).astype(bf16).reshape(2, tokens, width)
        part_ref[p, :, 1] = dot_nt(hidden, wd_ref[...]).astype(bf16).reshape(2, tokens, width)
        to_sibling(p).start()

    def to_sibling(p):
        return remote(part_ref.at[p, 1 - place.core], sib_ref.at[p], bs.at[p], br.at[p], place.sibling())

    def settle(p):
        to_sibling(p).wait_recv()
        both = (part_ref[p, place.core].astype(f32) + sib_ref[p].astype(f32)).astype(bf16)
        part_ref[p, place.core, 0] = both[0]
        osums_ref[p] = both[1]

    def target(way, d):
        return place.chip + d if way == 0 else place.chip - d

    def exists(way, d):
        return place.chip + d < chips if way == 0 else place.chip >= d

    def upstream(way):
        return place.chip >= 1 if way == 0 else place.chip + 1 < chips

    def landing(way, d):
        return target(way, d) if (way == 0 or d) else chips

    piece_rows = tokens // 2 // 16 * 16
    pieces = (pl.ds(0, piece_rows), pl.ds(piece_rows, tokens - piece_rows))

    def onward(way, d, n):
        p = target(way, d)
        slot = p if (way == 0 or d > 1) else chips
        return remote(
            part_ref.at[p, place.core, 0, pieces[n]],
            far_ref.at[slot, pieces[n]],
            zs.at[way, d, n],
            zr.at[way, d, n],
            place.along(1 - 2 * way),
        )

    def inward(way, d, n):
        mine = far_ref.at[landing(way, d), pieces[n]]
        return remote(mine, mine, zs.at[way, d + 1, n], zr.at[way, d + 1, n], place.along(1 - 2 * way))

    gather.from_sibling(0, 0).wait_recv()
    work(place.chip)
    for d in range(1, chips):
        gather.forward(d)
        for way in range(2):
            @pl.when(exists(way, d))
            def _(way=way, d=d):
                gather.from_sibling(1 - way, d).wait_recv()
                work(target(way, d))

        if d == 1:
            settle(place.chip)
        for way in range(2):

            @pl.when(exists(way, d))
            def _(way=way, d=d):
                settle(target(way, d))

                @pl.when(jnp.logical_not(upstream(way)))
                def _():
                    for n in range(2):
                        onward(way, d, n).start()

    seq = ctx * tokens
    dwm_ref[...] = dot_tn(n_all[...].reshape(seq, width), gub_all[...]).astype(bf16).reshape(dwm_ref.shape)
    down_cols = dwd_ref.shape[2]
    wide_ref[...] = dot_tn(cot_ref[...].reshape(seq, width), hid_all[...])
    for c in range(ctx):
        dwd_ref[c] = wide_ref[pl.ds(c * down_cols, down_cols), :].T.astype(bf16)

    for d in range(chips - 1, 0, -1):
        for way in range(2):

            @pl.when(jnp.logical_and(exists(way, d), upstream(way)))
            def _(way=way, d=d):
                p = target(way, d)
                for n, rows in enumerate(pieces):
                    inward(way, d, n).wait_recv()
                    both = part_ref[p, place.core, 0, rows].astype(f32) + far_ref[p, rows].astype(f32)
                    part_ref[p, place.core, 0, rows] = both.astype(bf16)
                    onward(way, d, n).start()

    ngrad_ref[...] = part_ref[place.chip, place.core, 0].astype(f32)
    for way in range(2):

        @pl.when(upstream(way))
        def _(way=way):
            for n in range(2):
                inward(way, 0, n).wait_recv()
            ngrad_ref[...] += far_ref[landing(way, 0)].astype(f32)

    gather.finish()
    for p in range(chips):
        to_sibling(p).wait_send()
    for d in range(1, chips):
        for way in range(2):

            @pl.when(exists(way, d))
            def _(way=way, d=d):
                for n in range(2):
                    onward(way, d, n).wait_send()


def back_kernel(sizes, *refs):
    refs = iter(refs)
    (q_ref, attn_ref, kv_ref, lse_ref, cos_ref, sin_ref, posk_ref, posq_ref, dwm_ref, dwd_ref) = take(refs, 10)
    ngrad_ref, mid_ref, gain_ref, cot_ref, wo_ref = take(refs, 5)
    qkvb_ref, fin_mlp, fin_down, mgrad_ref, midb_ref, gain_part = take(refs, 6)
    g_ref, mid_turned, q_back, kv_back = take(refs, 4)
    delta_ref, qz_ref, gz_ref, acc_ref, part_ref, sib_ref, far_ref = take(refs, 7)
    dwm_recv, down_rows, down_recv = take(refs, 3)
    bs, br, zs, zr = take(refs, 4)
    wm_sems, a2a_sems, wd_sems = take(refs, 2), take(refs, 2), take(refs, 2)

    place = Place(sizes)
    ctx, chips, row_parts = place.ctx, place.chips, place.row_parts
    tokens = q_ref.shape[1]
    chunk, wide = 2 * tokens, GROUP * tokens
    ff_part = dwd_ref.shape[1]
    per_row = ctx // row_parts
    scale = 1.0 / math.sqrt(HEAD_DIM)

    mlp = RowExchange(place, lambda k: dwm_ref.at[place.row_at(k)], lambda k, back: dwm_recv.at[k], wm_sems)

    def down_slot(c):
        return down_rows.at[c // per_row, pl.ds(pl.multiple_of((c % per_row) * ff_part, 16), ff_part), :]

    spread = CtxExchange(place, lambda c: dwd_ref.at[c], down_slot, a2a_sems)
    down = RowExchange(place, lambda k: down_rows.at[place.row_at(k)], lambda k, back: down_recv.at[k], wd_sems)

    place.greet(ctx=True, rows=True)
    mlp.start()
    spread.start()
    down_slot(place.c)[...] = dwd_ref[place.c]

    inverse_rms, unit, _ = norm_forward(mid_ref[...], gain_ref[...])
    mlp_back, gain_part[0] = norm_backward(ngrad_ref[...], inverse_rms, unit, gain_ref[...])
    mid_grad = cot_ref[...].astype(f32).T + mlp_back
    mgrad_ref[...] = mid_grad
    mid_turned[...] = mid_grad.T
    out_cols = wo_ref.shape[3]
    total = jnp.zeros(g_ref.shape, f32)
    for c in range(ctx):
        piece = mid_turned[pl.ds(c * out_cols, out_cols), :].astype(bf16)
        midb_ref[c] = piece
        total = total + dot_nn(wo_ref[c].reshape(g_ref.shape[0], out_cols), piece)
    g_ref[...] = total.astype(bf16)

    zeros = jnp.zeros((HEAD_DIM, wide), bf16)
    for g in range(KV_HEADS):
        query = group_rows(q_ref, g) * jnp.asarray(scale, bf16)
        grad = group_rows(g_ref, g)
        qz_ref[g] = jnp.concatenate([query, zeros], axis=0)
        gz_ref[g] = jnp.concatenate([zeros, grad], axis=0)
        delta_ref[g] = jnp.sum(grad.astype(f32) * group_rows(attn_ref, g).astype(f32), axis=0, keepdims=True)
        acc_ref[g] = jnp.zeros_like(acc_ref[g])
    query_pos = posq_ref[...]

    def to_sibling(j):
        return remote(part_ref.at[j, 1 - place.core], sib_ref.at[j], bs.at[j], br.at[j], place.sibling())

    def to_owner(j):
        return remote(part_ref.at[j, place.core], far_ref.at[j], zs.at[j], zr.at[j], place.along(j))

    def settle(j):
        to_sibling(j).wait_recv()
        both = part_ref[j, place.core].astype(f32) + sib_ref[j].astype(f32)
        part_ref[j, place.core] = both.astype(bf16)

    def work(j):
        p = place.chip_at(j)
        rows = pl.ds(pl.multiple_of(p * chunk, chunk), chunk)
        allowed = posk_ref[rows, :] <= query_pos
        for g in range(KV_HEADS):
            lanes = pl.ds(g * 2 * HEAD_DIM, 2 * HEAD_DIM)
            keys = kv_ref[pl.ds(2 * p, 2), :, lanes].reshape(chunk, 2 * HEAD_DIM)
            query, grad = qz_ref[g], gz_ref[g]
            scores = jnp.where(allowed, dot_nn(keys, query), MASKED)
            prob = jnp.exp(scores - lse_ref[g])
            score_grad = (prob * (dot_nn(keys, grad) - delta_ref[g])).astype(bf16)
            both = dot_nt(score_grad, query) + dot_nt(prob.astype(bf16), grad)
            part_ref[j, :, :, lanes] = both.astype(bf16).reshape(2, tokens, 2 * HEAD_DIM)
            acc_ref[g] += dot_tn(keys, score_grad)
        to_sibling(j).start()

    work(1)

    def turn(j, carry):
        work(j)
        settle(j - 1)
        to_owner(j - 1).start()
        return carry

    lax.fori_loop(2, chips, turn, 0)
    spread.arrive()
    down.start()
    work(0)
    settle(chips - 1)
    to_owner(chips - 1).start()
    cosine, sine = cos_ref[...], sin_ref[...]
    for h in range(HEADS):
        g, j = h // GROUP, h % GROUP
        head = acc_ref[g, pl.ds(0, HEAD_DIM), pl.ds(j * tokens, tokens)] * scale
        q_back[pl.ds(h * HEAD_DIM, HEAD_DIM), :] = rotate_rows_back(head, cosine, sine)
    settle(0)
    mlp.arrive()
    total = dwm_ref[place.row].astype(f32)
    for k in range(1, row_parts):
        total = total + dwm_recv[k].astype(f32)
    fin_mlp[...] = total
    total = part_ref[0, place.core].astype(f32)
    for j in range(1, chips):
        to_owner(j).wait_recv()
        total = total + far_ref[j].astype(f32)
    total = total.T
    kv_width = KV_HEADS * HEAD_DIM
    for g in range(KV_HEADS):
        pair = total[g * 2 * HEAD_DIM : (g + 1) * 2 * HEAD_DIM]
        rows = pl.ds(g * HEAD_DIM, HEAD_DIM)
        kv_back[rows, :] = rotate_rows_back(pair[:HEAD_DIM], cosine, sine)
        kv_back[pl.ds(kv_width + g * HEAD_DIM, HEAD_DIM), :] = pair[HEAD_DIM:]
    q_cols, kv_cols = q_back.shape[0] // ctx, kv_width // ctx
    for c in range(ctx):
        qkvb_ref[c] = jnp.concatenate(
            [
                q_back[pl.ds(c * q_cols, q_cols), :],
                kv_back[pl.ds(c * kv_cols, kv_cols), :],
                kv_back[pl.ds(kv_width + c * kv_cols, kv_cols), :],
            ],
            axis=0,
        ).astype(bf16)
    down.arrive()
    total = down_rows[place.row].astype(f32)
    for k in range(1, row_parts):
        total = total + down_recv[k].astype(f32)
    fin_down[...] = total
    for part in (mlp, spread, down):
        part.finish()
    for j in range(chips):
        to_sibling(j).wait_send()
        if j:
            to_owner(j).wait_send()


def last_kernel(sizes, *refs):
    refs = iter(refs)
    n1_ref, qkvb_ref, attn_ref, midb_ref, osums_ref, mid_ref = take(refs, 6)
    x_ref, gain_ref, gain_part, mgrad_ref, wqkv_ref = take(refs, 5)
    fin_ref, gain_out, result_ref, input_ref = take(refs, 4)
    part_ref, sib_ref, bent_ref, row_ref, far_send, far_ref = take(refs, 6)
    gain_sib, gain_row, gain_far, gain_a, gain_b, gain_c = take(refs, 6)
    bs, br, vs, vr, xs, xr, zs, zr = take(refs, 8)
    gb, gx, gz = take(refs, 2), take(refs, 2), take(refs, 2)
    osum_far, os, orr = take(refs, 3)

    place = Place(sizes)
    chips, row_parts, outer, inner = place.chips, place.row_parts, place.rows_outer, place.rows_inner
    core, row, chip = place.core, place.row, place.chip
    in_rows = fin_ref.shape[0]
    half = (in_rows // 2 + 15) // 16 * 16
    parts = (pl.ds(0, half), pl.ds(half, in_rows - half))
    sized = (pl.ds(0, half), pl.ds(0, in_rows - half))
    sides = [(a, 0) for a in range(1, outer)] + [(0, b) for b in range(1, inner)]
    diagonal = [(a, b) for a in range(1, outer) for b in range(1, inner)]
    place.greet(line=True, sibling=True, rows=True)

    def row_of(a, b):
        return wrap(place.seq + a, outer) * inner + wrap(place.fsdp + b, inner)

    def device(a, b):
        return (wrap(place.seq + a, outer), wrap(place.fsdp + b, inner), place.c)

    def to_sibling(j):
        return remote(
            part_ref.at[place.chip_at(j) * 2 + 1 - core], sib_ref.at[j], bs.at[j], br.at[j], place.sibling()
        )

    def bent(j, part, n):
        a, b = diagonal[n]
        return remote(
            sib_ref.at[j, row_of(a, b), parts[part]],
            bent_ref.at[j, part, n, sized[part]],
            vs.at[j, part, n],
            vr.at[j, part, n],
            device(0, b) if part == 0 else device(a, 0),
        )

    def direct(j, n):
        a, b = sides[n]
        return remote(sib_ref.at[j, row_of(a, b)], row_ref.at[j, n], xs.at[j, n], xr.at[j, n], device(a, b))

    def to_owner(j):
        return remote(far_send.at[j], far_ref.at[j], zs.at[j], zr.at[j], place.along(j))

    def g_sib():
        return remote(gain_a, gain_sib.at[core], gb[0].at[0], gb[1].at[0], place.sibling())

    def g_row(k):
        return remote(gain_b, gain_row.at[row], gx[0].at[k], gx[1].at[k], place.across(k))

    def g_far(j):
        return remote(gain_c, gain_far.at[chip], gz[0].at[j], gz[1].at[j], place.along(j))

    def input_gradient():
        width = x_ref.shape[0]
        total = jnp.zeros(x_ref.shape, f32)
        for c in range(place.ctx):
            total = total + dot_nn(wqkv_ref[c].reshape(width, wqkv_ref.shape[3]), qkvb_ref[c])
        inverse_rms, unit, _ = norm_forward(x_ref[...].astype(f32).T, gain_ref[...])
        back, gain_a[0] = norm_backward(total.T, inverse_rms, unit, gain_ref[...])
        input_ref[...] = (mgrad_ref[...] + back).T.astype(bf16)
        gain_a[1] = gain_part[0]
        gain_sib[core] = gain_a[...]
        g_sib().start()

    def multiply(j):
        for k in range(2):
            c = place.chip_at(j) * 2 + k
            both = jnp.concatenate(
                [dot_nt(n1_ref[...], qkvb_ref[c]), dot_nt(attn_ref[...], midb_ref[c])], axis=1
            )
            part_ref[c] = both.astype(bf16).reshape(part_ref.shape[1:])
        to_sibling(j).start()

    def add_sibling(j):
        to_sibling(j).wait_recv()
        both = part_ref[place.chip_at(j) * 2 + core].astype(f32) + sib_ref[j].astype(f32)
        sib_ref[j] = both.astype(bf16)
        for n in range(len(diagonal)):
            for part in range(2):
                bent(j, part, n).start()

    def add_bent(j):
        for n, (a, b) in enumerate(diagonal):
            for part in range(2):
                bent(j, part, n).wait_recv()
                at = (j, row_of(a, 0) if part == 0 else row_of(0, b), parts[part])
                both = sib_ref[at].astype(f32) + bent_ref[j, part, n, sized[part]].astype(f32)
                sib_ref[at] = both.astype(bf16)
        for n in range(len(sides)):
            direct(j, n).start()

    def add_rows(j):
        total = sib_ref[j, row].astype(f32)
        for n in range(len(sides)):
            direct(j, n).wait_recv()
            total = total + row_ref[j, n].astype(f32)
        if j:
            far_send[j] = total.astype(bf16)
            to_owner(j).start()
        else:
            fin_ref[...] = total

    def output_to(j):
        return remote(osums_ref.at[place.chip_at(j)], osum_far.at[j], os.at[j], orr.at[j], place.along(j))

    for j in range(1, chips):
        output_to(j).start()
    order = list(range(1, chips)) + [0]
    stages = (multiply, add_sibling, add_bent, add_rows)
    for t in range(chips + len(stages) - 1):
        for depth, stage in enumerate(stages):
            if 0 <= t - depth < chips:
                stage(order[t - depth])
        if t == 1:
            input_gradient()
        if t == 3:
            remote(gain_a, gain_sib.at[1 - core], gb[0].at[0], gb[1].at[0], place.sibling()).wait_recv()
            gain_b[...] = gain_sib[0] + gain_sib[1]
            gain_row[row] = gain_b[...]
            for k in range(1, row_parts):
                g_row(k).start()

    for k in range(1, row_parts):
        remote(gain_b, gain_row.at[place.row_at(-k)], gx[0].at[k], gx[1].at[k], place.across(k)).wait_recv()
    total = gain_row[0]
    for k in range(1, row_parts):
        total = total + gain_row[k]
    gain_c[...] = total
    gain_far[chip] = gain_c[...]
    for j in range(1, chips):
        g_far(j).start()
    total = mid_ref[...] + osums_ref[chip].astype(f32)
    for j in range(1, chips):
        output_to(j).wait_recv()
        total = total + osum_far[j].astype(f32)
    result_ref[...] = total.T.astype(bf16)
    total = fin_ref[...]
    for j in range(1, chips):
        to_owner(j).wait_recv()
        total = total + far_ref[j].astype(f32)
    fin_ref[...] = total
    for j in range(1, chips):
        remote(gain_c, gain_far.at[place.chip_at(-j)], gz[0].at[j], gz[1].at[j], place.along(j)).wait_recv()
    total = gain_far[0]
    for j in range(1, chips):
        total = total + gain_far[j]
    gain_out[...] = total

    g_sib().wait_send()
    for k in range(1, row_parts):
        g_row(k).wait_send()
    for j in range(1, chips):
        g_far(j).wait_send()
    for j in order:
        to_sibling(j).wait_send()
        for n in range(len(diagonal)):
            for part in range(2):
                bent(j, part, n).wait_send()
        for n in range(len(sides)):
            direct(j, n).wait_send()
        if j:
            to_owner(j).wait_send()
            output_to(j).wait_send()


def finish_kernel(cuts, *refs):
    refs = iter(refs)
    attn_ref, mlp_ref, down_ref, result_ref, input_ref, gain_ref = take(refs, 6)
    q_cols, kv_cols, ff_cols = cuts
    outs = take(refs, 11)
    attn, mlp = attn_ref[...], mlp_ref[...]
    outs[0][...] = result_ref[...]
    outs[1][...] = input_ref[...]
    outs[2][...] = gain_ref[0]
    outs[3][...] = gain_ref[1]
    outs[4][...] = attn[:, :q_cols]
    outs[5][...] = attn[:, q_cols : q_cols + kv_cols].T
    outs[6][...] = attn[:, q_cols + kv_cols : q_cols + 2 * kv_cols].T
    outs[7][...] = attn[:, q_cols + 2 * kv_cols :]
    outs[8][...] = mlp[:, :ff_cols].T
    outs[9][...] = mlp[:, ff_cols:].T
    outs[10][...] = down_ref[...].T


def finish(cuts, inputs, outs):
    vmem = pl.BlockSpec(memory_space=pltpu.VMEM)
    return pl.pallas_call(
        functools.partial(finish_kernel, cuts),
        out_shape=[jax.ShapeDtypeStruct(shape, kind) for shape, kind in outs],
        in_specs=[vmem] * len(inputs),
        out_specs=[vmem] * len(outs),
    )(*inputs)


def call(kernel, sizes, inputs, outs, scratch, collective_id, raw=()):
    vmem = pl.BlockSpec(memory_space=pltpu.VMEM)
    anywhere = pl.BlockSpec(memory_space=pl.ANY)
    return pl.pallas_call(
        functools.partial(kernel, sizes),
        out_shape=[jax.ShapeDtypeStruct(shape, kind) for shape, kind in outs],
        in_specs=[anywhere if i in raw else vmem for i in range(len(inputs))],
        out_specs=[vmem] * len(outs),
        scratch_shapes=scratch,
        compiler_params=pltpu.CompilerParams(
            collective_id=collective_id, has_side_effects=True, vmem_limit_bytes=60 * 1024 * 1024
        ),
    )(*inputs)


def on_device(
    tokens,
    cotangent,
    block_order,
    gain_attn,
    gain_mlp,
    w_query,
    w_key,
    w_value,
    w_out,
    w_gate,
    w_up,
    w_down,
):
    sizes = tuple(lax.axis_size(n) for n in ("seq", "fsdp", "ctx"))
    rows, ctx = sizes[0] * sizes[1], sizes[2]
    chips = ctx // 2
    row_count, width = tokens.shape[1], tokens.shape[2]
    seq_len = row_count * ctx
    block_total = block_order.shape[0]
    block_len = seq_len // block_total
    kv_width = KV_HEADS * HEAD_DIM
    q_width = HEADS * HEAD_DIM
    q_cols, kv_cols, ff_cols = w_query.shape[1], w_key.shape[1], w_gate.shape[1]
    out_cols, down_cols, down_rows = w_out.shape[1], w_down.shape[1], w_down.shape[0]
    in_rows = w_query.shape[0]
    qkv_cols = q_cols + 2 * kv_cols
    wide = GROUP * row_count

    slot_index = jnp.arange(seq_len, dtype=jnp.int32)
    owner_hit = (slot_index // block_len)[:, None] == jnp.arange(block_total, dtype=jnp.int32)[None, :]
    all_pos = (
        jnp.sum(jnp.where(owner_hit, block_order[None, :], 0), axis=1) * block_len + slot_index % block_len
    )
    own_pos = lax.dynamic_slice_in_dim(all_pos, lax.axis_index("ctx") * row_count, row_count)
    inverse = rope_base ** (-jnp.arange(HALF, dtype=f32) / HALF)
    angles = inverse[:, None] * own_pos.astype(f32)[None, :]
    cosine, sine = jnp.cos(angles), jnp.sin(angles)
    pos_keys = all_pos[:, None]
    pos_query = jnp.tile(own_pos, GROUP)[None, :]

    x = tokens[0]
    cot_rows = cotangent[0]
    turned = [jnp.transpose(w) for w in (w_key, w_value, w_gate, w_up, w_down)]
    wk_t, wv_t, wg_t, wu_t, wd_t = turned

    (
        attn_t,
        query_t,
        kv_all,
        lse,
        qkv_full,
        out_full,
        mlp_full,
        down_t,
        cot_all,
        normed_attn_t,
        middle,
        normed_mlp,
    ) = call(
        first_kernel,
        sizes,
        (
            jnp.transpose(x),
            gain_attn[None],
            gain_mlp[None],
            w_query,
            wk_t,
            wv_t,
            w_out,
            wg_t,
            wu_t,
            wd_t,
            jnp.transpose(cot_rows),
            cosine,
            sine,
            pos_keys,
            pos_query,
        ),
        [
            ((q_width, row_count), bf16),
            ((q_width, row_count), bf16),
            ((ctx, row_count, 2 * kv_width), bf16),
            ((KV_HEADS, 1, wide), f32),
            ((ctx, rows, in_rows, qkv_cols), bf16),
            ((ctx, rows, in_rows, out_cols), bf16),
            ((rows, in_rows, 2 * ff_cols), bf16),
            ((width, ff_cols), bf16),
            ((ctx, row_count, width), bf16),
            ((width, row_count), bf16),
            ((row_count, width), f32),
            ((row_count, width), bf16),
        ],
        [
            pltpu.VMEM((q_width + 2 * kv_width, row_count), f32),
            pltpu.VMEM((row_count, 2 * kv_width), bf16),
            pltpu.VMEM((rows, down_rows, down_cols), bf16),
            pltpu.VMEM((seq_len, wide), f32),
            pltpu.VMEM((ctx, ff_cols, down_cols), bf16),
            pltpu.VMEM((width, row_count), f32),
            pltpu.VMEM((width, ff_cols), f32),
            pltpu.VMEM((width, row_count), bf16),
        ]
        + [pltpu.VMEM(w.shape, bf16) for w in (w_query, wk_t, wv_t, w_out, wg_t, wu_t, wd_t)]
        + [
            pltpu.VMEM((width, row_count), bf16),
            pltpu.VMEM((in_rows, qkv_cols), bf16),
            pltpu.VMEM((in_rows, 2 * ff_cols), bf16),
            pltpu.VMEM(w_down.shape, bf16),
            pltpu.VMEM((row_count, width), bf16),
            dma(9),
        ]
        + FullGather.scratch(sizes)
        + FullGather.scratch(sizes)
        + LineGather.scratch(sizes)
        + LineGather.scratch(sizes)
        + RowExchange.scratch(sizes)
        + RowExchange.scratch(sizes)
        + CtxExchange.scratch(sizes),
        1,
        raw=(0, 3, 4, 5, 6, 7, 8, 9, 10),
    )

    w_mlp_cat = mlp_full.reshape(width, 2 * ff_cols)

    normed_mlp_grad, output_sums, d_mlp, d_down = call(
        mlp_kernel,
        sizes,
        (normed_mlp, cot_all, w_mlp_cat, down_t),
        [
            ((row_count, width), f32),
            ((chips, row_count, width), bf16),
            ((rows, in_rows, 2 * ff_cols), bf16),
            ((ctx, ff_cols, down_cols), bf16),
        ],
        [
            pltpu.VMEM((ctx, row_count, width), bf16),
            pltpu.VMEM((seq_len, 2 * ff_cols), bf16),
            pltpu.VMEM((seq_len, ff_cols), bf16),
            pltpu.VMEM((chips, 2, 2, row_count, width), bf16),
            pltpu.VMEM((chips, 2, row_count, width), bf16),
            pltpu.VMEM((chips + 1, row_count, width), bf16),
            pltpu.VMEM((width, ff_cols), f32),
        ]
        + LineGather.scratch(sizes)
        + [dma(chips)] * 2
        + [dma(2, chips, 2)] * 2,
        2,
    )
    qkv_back_t, fin_mlp, fin_down, mid_grad, mid_back_t, gain_mlp_part = call(
        back_kernel,
        sizes,
        (
            query_t,
            attn_t,
            kv_all,
            lse,
            cosine,
            sine,
            pos_keys,
            pos_query,
            d_mlp,
            d_down,
            normed_mlp_grad,
            middle,
            gain_mlp[None],
            jnp.transpose(cot_rows),
            out_full,
        ),
        [
            ((ctx, qkv_cols, row_count), bf16),
            ((in_rows, 2 * ff_cols), f32),
            ((down_rows, down_cols), f32),
            ((row_count, width), f32),
            ((ctx, out_cols, row_count), bf16),
            ((1, width), f32),
        ],
        [
            pltpu.VMEM((q_width, row_count), bf16),
            pltpu.VMEM((width, row_count), f32),
            pltpu.VMEM((q_width, row_count), f32),
            pltpu.VMEM((2 * kv_width, row_count), f32),
            pltpu.VMEM((KV_HEADS, 1, wide), f32),
            pltpu.VMEM((KV_HEADS, 2 * HEAD_DIM, wide), bf16),
            pltpu.VMEM((KV_HEADS, 2 * HEAD_DIM, wide), bf16),
            pltpu.VMEM((KV_HEADS, 2 * HEAD_DIM, wide), f32),
            pltpu.VMEM((chips, 2, row_count, 2 * kv_width), bf16),
            pltpu.VMEM((chips, row_count, 2 * kv_width), bf16),
            pltpu.VMEM((chips, row_count, 2 * kv_width), bf16),
            pltpu.VMEM((rows, in_rows, 2 * ff_cols), bf16),
            pltpu.VMEM((rows, down_rows, down_cols), bf16),
            pltpu.VMEM((rows, down_rows, down_cols), bf16),
        ]
        + [dma(chips)] * 4
        + RowExchange.scratch(sizes)
        + CtxExchange.scratch(sizes)
        + RowExchange.scratch(sizes),
        3,
    )

    attn_cols = qkv_cols + out_cols
    gains = pltpu.VMEM((2, width), f32)
    half = (in_rows // 2 + 15) // 16 * 16
    corners, sides = (sizes[0] - 1) * (sizes[1] - 1), sizes[0] + sizes[1] - 2
    fin_attn, gain_sums, result_t, input_t = call(
        last_kernel,
        sizes,
        (
            normed_attn_t,
            qkv_back_t,
            attn_t,
            mid_back_t,
            output_sums,
            middle,
            jnp.transpose(x),
            gain_attn[None],
            gain_mlp_part,
            mid_grad,
            qkv_full,
        ),
        [
            ((in_rows, attn_cols), f32),
            ((2, width), f32),
            ((width, row_count), bf16),
            ((width, row_count), bf16),
        ],
        [
            pltpu.VMEM((ctx, rows, in_rows, attn_cols), bf16),
            pltpu.VMEM((chips, rows, in_rows, attn_cols), bf16),
            pltpu.VMEM((chips, 2, corners, half, attn_cols), bf16),
            pltpu.VMEM((chips, sides, in_rows, attn_cols), bf16),
            pltpu.VMEM((chips, in_rows, attn_cols), bf16),
            pltpu.VMEM((chips, in_rows, attn_cols), bf16),
            pltpu.VMEM((2, 2, width), f32),
            pltpu.VMEM((rows, 2, width), f32),
            pltpu.VMEM((chips, 2, width), f32),
            gains,
            gains,
            gains,
            dma(chips),
            dma(chips),
            dma(chips, 2, corners),
            dma(chips, 2, corners),
            dma(chips, sides),
            dma(chips, sides),
            dma(chips),
            dma(chips),
            dma(1),
            dma(1),
            dma(rows),
            dma(rows),
            dma(chips),
            dma(chips),
            pltpu.VMEM((chips, row_count, width), bf16),
            dma(chips),
            dma(chips),
        ],
        4,
    )
    outs = finish(
        (q_cols, kv_cols, ff_cols),
        (fin_attn, fin_mlp, fin_down, result_t, input_t, gain_sums),
        [
            ((width, row_count), bf16),
            ((width, row_count), bf16),
            ((width,), f32),
            ((width,), f32),
            ((in_rows, q_cols), f32),
            ((kv_cols, in_rows), f32),
            ((kv_cols, in_rows), f32),
            ((in_rows, out_cols), f32),
            ((ff_cols, in_rows), f32),
            ((ff_cols, in_rows), f32),
            ((down_cols, down_rows), f32),
        ],
    )
    flip = jnp.transpose
    return (
        flip(outs[0]).reshape(1, row_count, width),
        flip(outs[1]).reshape(1, row_count, width),
        outs[2],
        outs[3],
        outs[4],
        flip(outs[5]),
        flip(outs[6]),
        outs[7],
        flip(outs[8]),
        flip(outs[9]),
        flip(outs[10]),
    )


def solution(mesh):
    return jax.shard_map(
        on_device,
        mesh=mesh,
        in_specs=(
            P(("seq", "fsdp"), "ctx", None),
            P(("seq", "fsdp"), "ctx", None),
            P(),
            P(),
            P(),
            P(("seq", "fsdp"), "ctx"),
            P(("seq", "fsdp"), "ctx"),
            P(("seq", "fsdp"), "ctx"),
            P(("seq", "fsdp"), "ctx"),
            P(("seq", "fsdp"), "ctx"),
            P(("seq", "fsdp"), "ctx"),
            P(("seq", "fsdp"), "ctx"),
        ),
        out_specs=(
            P(("seq", "fsdp"), "ctx", None),
            P(("seq", "fsdp"), "ctx", None),
            P(),
            P(),
            P(("seq", "fsdp"), "ctx"),
            P(("seq", "fsdp"), "ctx"),
            P(("seq", "fsdp"), "ctx"),
            P(("seq", "fsdp"), "ctx"),
            P(("seq", "fsdp"), "ctx"),
            P(("seq", "fsdp"), "ctx"),
            P(("seq", "fsdp"), "ctx"),
        ),
        check_vma=False,
    )
```

```python
import functools
import math

import jax
import jax.numpy as jnp
from jax import lax
from jax.experimental import pallas as pl
from jax.experimental.pallas import tpu as pltpu
from jax.sharding import PartitionSpec as P

HEADS = 15
KV_HEADS = 5
HEAD_DIM = 64
GROUP = HEADS // KV_HEADS
HALF = HEAD_DIM // 2
MESH = pl.DeviceIdType.MESH
MASKED = -1e30
UNROLL = 4

rope_base = 100000.0
norm_eps = 1e-05
bf16 = jnp.bfloat16
f32 = jnp.float32


def norm_forward(values, gain):
    inverse_rms = lax.rsqrt(jnp.mean(values * values, axis=1, keepdims=True) + norm_eps)
    scaled = values * inverse_rms
    return (inverse_rms, scaled, (scaled * gain).astype(bf16))


def norm_backward(grad_in, inverse_rms, scaled, gain):
    weighted = grad_in * gain
    back = inverse_rms * (weighted - scaled * jnp.mean(weighted * scaled, axis=1, keepdims=True))
    return (back, jnp.sum(grad_in * scaled, axis=0))


def dot_nn(left, right):
    return jnp.dot(left, right, preferred_element_type=f32)


def dot_nt(left, right):
    return lax.dot_general(left, right, (((1,), (1,)), ((), ())), preferred_element_type=f32)


def dot_tn(left, right):
    return lax.dot_general(left, right, (((0,), (0,)), ((), ())), preferred_element_type=f32)


def wrap(index, count):
    return lax.rem(index + count, count)


class Place:
    def __init__(self, sizes):
        self.rows_outer, self.rows_inner, self.ctx = sizes
        self.row_parts = self.rows_outer * self.rows_inner
        self.chips = self.ctx // 2
        self.seq, self.fsdp, self.c = (lax.axis_index(n) for n in ("seq", "fsdp", "ctx"))
        self.row = self.seq * self.rows_inner + self.fsdp
        self.chip = self.c // 2
        self.core = self.c % 2

    def sibling(self):
        return (self.seq, self.fsdp, self.chip * 2 + 1 - self.core)

    def along(self, step):
        return (self.seq, self.fsdp, wrap(self.chip + step, self.chips) * 2 + self.core)

    def any_ctx(self, step):
        return (self.seq, self.fsdp, wrap(self.c + step, self.ctx))

    def across(self, step):
        row = wrap(self.row + step, self.row_parts)
        return (row // self.rows_inner, row % self.rows_inner, self.c)

    def chip_at(self, step):
        return wrap(self.chip + step, self.chips)

    def row_at(self, step):
        return wrap(self.row + step, self.row_parts)

    def greet(self, ctx=False, line=False, sibling=False, rows=False):
        devices = []
        if ctx:
            devices += [self.any_ctx(t) for t in range(1, self.ctx)]
        if line:
            devices += [self.along(t) for t in range(1, self.chips)]
        if sibling:
            devices += [self.sibling()]
        if rows:
            devices += [self.across(t) for t in range(1, self.row_parts)]
        barrier = pltpu.get_barrier_semaphore()
        for device in devices:
            pl.semaphore_signal(barrier, inc=1, device_id=device, device_id_type=MESH)
        pl.semaphore_wait(barrier, len(devices))


def remote(src, dst, send, recv, device):
    return pltpu.make_async_remote_copy(
        src_ref=src, dst_ref=dst, send_sem=send, recv_sem=recv, device_id=device, device_id_type=MESH
    )


def dma(*shape):
    return pltpu.SemaphoreType.DMA(shape)


class LineGather:
    def __init__(self, place, ref, out, sems):
        self.p, self.ref, self.out = place, ref, out
        self.zs, self.zr, self.bs, self.br = sems

    @staticmethod
    def scratch(sizes):
        chips = sizes[2] // 2
        return [dma(2, chips), dma(2, chips), dma(2, chips), dma(2, chips)]

    def source(self, way, d):
        return self.p.chip - d if way == 0 else self.p.chip + d

    def has(self, way, d):
        return self.p.chip >= d if way == 0 else self.p.chip + d < self.p.chips

    def onward(self, way):
        return self.p.chip + 1 < self.p.chips if way == 0 else self.p.chip >= 1

    def slot(self, way, d, core):
        return self.out.at[self.source(way, d) * 2 + core]

    def hop(self, way, d, own=False):
        mine = self.slot(way, d, self.p.core)
        src = self.ref if own else mine
        return remote(src, mine, self.zs.at[way, d], self.zr.at[way, d], self.p.along(1 - 2 * way))

    def landed(self, way, d):
        mine = self.slot(way, d, self.p.core)
        return remote(mine, mine, self.zs.at[way, d - 1], self.zr.at[way, d - 1], self.p.along(1 - 2 * way))

    def to_sibling(self, way, d, own=False):
        mine = self.slot(way, d, self.p.core)
        src = self.ref if own else mine
        return remote(src, mine, self.bs.at[way, d], self.br.at[way, d], self.p.sibling())

    def from_sibling(self, way, d):
        mine = self.slot(way, d, 1 - self.p.core)
        return remote(mine, mine, self.bs.at[way, d], self.br.at[way, d], self.p.sibling())

    def start(self):
        for way in range(2):
            pl.when(self.onward(way))(lambda way=way: self.hop(way, 0, True).start())
        self.to_sibling(0, 0, True).start()
        self.out[self.p.c] = self.ref[...]

    def forward_way(self, way, d):
        self.landed(way, d).wait_recv()
        pl.when(self.onward(way))(lambda: self.hop(way, d).start())
        self.to_sibling(way, d).start()

    def forward(self, d):
        for way in range(2):
            pl.when(self.has(way, d))(lambda way=way: self.forward_way(way, d))

    def arrive(self):
        self.from_sibling(0, 0).wait_recv()
        for d in range(1, self.p.chips):
            for way in range(2):
                pl.when(self.has(way, d))(lambda way=way, d=d: self.from_sibling(way, d).wait_recv())

    def finish(self):
        self.to_sibling(0, 0, True).wait_send()
        for d in range(self.p.chips):
            for way in range(2):

                @pl.when(self.has(way, d))
                def _(way=way, d=d):
                    pl.when(self.onward(way))(lambda: self.hop(way, d, d == 0).wait_send())
                    if d:
                        self.to_sibling(way, d).wait_send()


class FullGather:
    def __init__(self, place, ref, out, sems):
        self.p, self.ref, self.out = place, ref, out
        self.zs, self.zr = sems[:2]
        self.row_sems = sems[2:8]
        self.bs, self.br = sems[8:10]
        rows = ref.shape[0]
        self.half = (rows // 2 + 15) // 16 * 16
        self.parts = (pl.ds(0, self.half), pl.ds(self.half, rows - self.half))
        self.tags = [(0, 0)] + [(way, d) for d in range(1, place.chips) for way in range(2)]

    @staticmethod
    def scratch(sizes):
        chips = sizes[2] // 2
        count, outer, inner = 2 * chips - 1, sizes[0], sizes[1]
        line = [dma(2, chips)] * 2
        direct = [dma(count, 2, max(outer, inner))] * 2
        bent = [dma(count, 2, outer, inner)] * 2
        spare = [dma(1)] * 2
        return line + direct + bent + spare + [dma(count, outer, inner)] * 2

    def source(self, way, d):
        return self.p.chip - d if way == 0 else self.p.chip + d

    def has(self, way, d):
        return self.p.chip >= d if way == 0 else self.p.chip + d < self.p.chips

    def onward(self, way):
        return self.p.chip + 1 < self.p.chips if way == 0 else self.p.chip >= 1

    def when_has(self, tag, action):
        if tag[1] == 0:
            action()
        else:
            pl.when(self.has(*tag))(action)

    def row(self, a, b):
        seq = wrap(self.p.seq - a, self.p.rows_outer)
        return seq * self.p.rows_inner + wrap(self.p.fsdp - b, self.p.rows_inner)

    def slot(self, tag, core, a=0, b=0):
        return self.out.at[self.source(*tag) * 2 + core, self.row(a, b)]

    def device(self, a, b):
        return (wrap(self.p.seq + a, self.p.rows_outer), wrap(self.p.fsdp + b, self.p.rows_inner), self.p.c)

    def hop(self, way, d):
        mine = self.slot((way, d), self.p.core)
        src = self.ref if d == 0 else mine
        return remote(src, mine, self.zs.at[way, d], self.zr.at[way, d], self.p.along(1 - 2 * way))

    def landed(self, way, d):
        mine = self.slot((way, d), self.p.core)
        return remote(mine, mine, self.zs.at[way, d - 1], self.zr.at[way, d - 1], self.p.along(1 - 2 * way))

    def direct(self, tag, a, b):
        q, axis = self.tags.index(tag), 0 if a else 1
        mine = self.slot(tag, self.p.core)
        src = self.ref if tag[1] == 0 else mine
        sems = [sem.at[q, axis, a + b] for sem in self.row_sems[:2]]
        return remote(src, mine, *sems, self.device(a, b))

    def direct_in(self, tag, a, b):
        q, axis = self.tags.index(tag), 0 if a else 1
        mine = self.slot(tag, self.p.core, a, b)
        sems = [sem.at[q, axis, a + b] for sem in self.row_sems[:2]]
        return remote(mine, mine, *sems, self.device(a, b))

    def bent(self, tag, part, a, b):
        q = self.tags.index(tag)
        mine = (self.slot(tag, self.p.core, a, 0) if part == 0 else self.slot(tag, self.p.core, 0, b)).at[self.parts[part]]
        sems = [sem.at[q, part, a, b] for sem in self.row_sems[2:4]]
        return remote(mine, mine, *sems, self.device(0, b) if part == 0 else self.device(a, 0))

    def bent_in(self, tag, part, a, b):
        q = self.tags.index(tag)
        mine = self.slot(tag, self.p.core, a, b).at[self.parts[part]]
        sems = [sem.at[q, part, a, b] for sem in self.row_sems[2:4]]
        return remote(mine, mine, *sems, self.device(0, b))

    def to_sibling(self, tag, a, b):
        q = self.tags.index(tag)
        mine = self.slot(tag, self.p.core, a, b)
        src = self.ref if (tag[1] == 0 and a == 0 and b == 0) else mine
        return remote(src, mine, self.bs.at[q, a, b], self.br.at[q, a, b], self.p.sibling())

    def from_sibling(self, tag, a, b):
        q = self.tags.index(tag)
        mine = self.slot(tag, 1 - self.p.core, a, b)
        return remote(mine, mine, self.bs.at[q, a, b], self.br.at[q, a, b], self.p.sibling())

    def steps(self):
        outer = [(a, 0) for a in range(1, self.p.rows_outer)]
        inner = [(0, b) for b in range(1, self.p.rows_inner)]
        diagonal = [(a, b) for a in range(1, self.p.rows_outer) for b in range(1, self.p.rows_inner)]
        return outer, inner, diagonal

    def send_rows(self, tag):
        outer, inner, _ = self.steps()
        for a, b in outer + inner:
            self.direct(tag, a, b).start()
        self.to_sibling(tag, 0, 0).start()

    def start(self, rows=True):
        for way in range(2):
            pl.when(self.onward(way))(lambda way=way: self.hop(way, 0).start())
        if rows:
            self.send_rows((0, 0))
        self.out[self.p.c, self.p.row] = self.ref[...]

    def forward(self, d, rows=True):
        for way in range(2):

            @pl.when(self.has(way, d))
            def _(way=way):
                self.landed(way, d).wait_recv()
                pl.when(self.onward(way))(lambda: self.hop(way, d).start())
                if rows:
                    self.send_rows((way, d))

    def cross(self):
        for tag in self.tags:
            self.when_has(tag, lambda tag=tag: self.send_rows(tag))

    def bend(self, d):
        outer, inner, _ = self.steps()
        for tag in [(0, 0)] if d == 0 else [(0, d), (1, d)]:

            def action(tag=tag):
                for a, b in outer:
                    self.direct_in(tag, a, b).wait_recv()
                    for _, other in inner:
                        self.bent(tag, 0, a, other).start()
                    self.to_sibling(tag, a, b).start()
                for a, b in inner:
                    self.direct_in(tag, a, b).wait_recv()
                    for other, _ in outer:
                        self.bent(tag, 1, other, b).start()
                    self.to_sibling(tag, a, b).start()

            self.when_has(tag, action)

    def settle(self, d):
        for tag in [(0, 0)] if d == 0 else [(0, d), (1, d)]:

            def action(tag=tag):
                for a, b in self.steps()[2]:
                    for part in range(2):
                        self.bent_in(tag, part, a, b).wait_recv()
                    self.to_sibling(tag, a, b).start()

            self.when_has(tag, action)

    def every(self):
        return [(a, b) for a in range(self.p.rows_outer) for b in range(self.p.rows_inner)]

    def arrive(self):
        for tag in self.tags:

            def action(tag=tag):
                for a, b in self.every():
                    self.from_sibling(tag, a, b).wait_recv()

            self.when_has(tag, action)

    def finish(self):
        outer, inner, diagonal = self.steps()
        for tag in self.tags:

            def action(tag=tag):
                for way in range(2) if tag[1] == 0 else (tag[0],):
                    pl.when(self.onward(way))(lambda way=way: self.hop(way, tag[1]).wait_send())
                for a, b in outer + inner:
                    self.direct(tag, a, b).wait_send()
                for a, b in diagonal:
                    for part in range(2):
                        self.bent(tag, part, a, b).wait_send()
                for a, b in self.every():
                    self.to_sibling(tag, a, b).wait_send()

            self.when_has(tag, action)


class RowExchange:
    def __init__(self, place, src_of, dst_of, sems):
        self.p, self.src_of, self.dst_of = place, src_of, dst_of
        self.xs, self.xr = sems

    @staticmethod
    def scratch(sizes):
        rows = sizes[0] * sizes[1]
        return [dma(rows), dma(rows)]

    def send(self, k):
        return remote(self.src_of(k), self.dst_of(k, 0), self.xs.at[k], self.xr.at[k], self.p.across(k))

    def recv(self, k):
        mine = self.dst_of(k, k)
        return remote(mine, mine, self.xs.at[k], self.xr.at[k], self.p.across(k))

    def start(self):
        for k in range(1, self.p.row_parts):
            self.send(k).start()

    def arrive(self):
        for k in range(1, self.p.row_parts):
            self.recv(k).wait_recv()

    def finish(self):
        for k in range(1, self.p.row_parts):
            self.send(k).wait_send()


class CtxExchange:
    def __init__(self, place, src_of, dst_of, sems):
        self.p, self.src_of, self.dst_of = place, src_of, dst_of
        self.ss, self.sr = sems

    @staticmethod
    def scratch(sizes):
        return [dma(sizes[2]), dma(sizes[2])]

    def send(self, t):
        return remote(
            self.src_of(wrap(self.p.c + t, self.p.ctx)),
            self.dst_of(self.p.c),
            self.ss.at[t],
            self.sr.at[t],
            self.p.any_ctx(t),
        )

    def recv(self, t):
        mine = self.dst_of(wrap(self.p.c - t, self.p.ctx))
        return remote(mine, mine, self.ss.at[t], self.sr.at[t], self.p.any_ctx(t))

    def start(self):
        for t in range(1, self.p.ctx):
            self.send(t).start()

    def arrive(self):
        for t in range(1, self.p.ctx):
            self.recv(t).wait_recv()

    def finish(self):
        for t in range(1, self.p.ctx):
            self.send(t).wait_send()


def take(refs, count):
    return [next(refs) for _ in range(count)]


def rotate_rows(rows, cosine, sine):
    first, second = rows[:HALF], rows[HALF:]
    return jnp.concatenate([first * cosine - second * sine, second * cosine + first * sine], axis=0)


def rotate_rows_back(rows, cosine, sine):
    first, second = rows[:HALF], rows[HALF:]
    return jnp.concatenate([first * cosine + second * sine, second * cosine - first * sine], axis=0)


def group_rows(ref, g):
    return jnp.concatenate(
        [ref[pl.ds((g * GROUP + j) * HEAD_DIM, HEAD_DIM), :] for j in range(GROUP)], axis=1
    )


def turn(values):
    return values.astype(f32).T.astype(values.dtype)


def first_kernel(sizes, *refs):
    refs = iter(refs)
    (x_in, gain_ref, gain2_ref, wq_in, wk_in, wv_in, wo_in, wg_in, wu_in, wd_in, cot_in) = take(refs, 11)
    (cos_ref, sin_ref, posk_ref, posq_ref) = take(refs, 4)
    (attn_ref, q_ref, kv_ref, lse_ref, wqkv_full, wo_full, wm_full, wd_turned, cot_full) = take(refs, 9)
    (n1_turned, mid_ref, n2_ref) = take(refs, 3)
    (qkv_raw, kv_own, wd_rows, score_ref, wd_full, mid_turned, wd_wide) = take(refs, 7)
    (x_turned, wq_ref, wk_turned, wv_turned, wo_ref, wg_turned, wu_turned, wd_in_ref, cot_turned) = take(refs, 9)
    (wqkv_ref, wm_ref, wd_ref, cot_ref, load_sems) = take(refs, 5)
    qkv_sems, wo_sems = take(refs, 10), take(refs, 10)
    kv_sems, cot_sems = take(refs, 4), take(refs, 4)
    wm_sems, wd_sems, a2a_sems = take(refs, 2), take(refs, 2), take(refs, 2)

    place = Place(sizes)
    ctx, chips, row_parts = place.ctx, place.chips, place.row_parts
    width, tokens = x_turned.shape
    q_cols = HEADS * HEAD_DIM // ctx
    kv_cols = KV_HEADS * HEAD_DIM // ctx
    q_width, kv_width = HEADS * HEAD_DIM, KV_HEADS * HEAD_DIM
    qkv_cols = q_cols + 2 * kv_cols
    ff_part = wd_full.shape[1]
    per_row = ctx // row_parts

    qkv = FullGather(place, wqkv_ref, wqkv_full, qkv_sems)
    out = FullGather(place, wo_ref, wo_full, wo_sems)
    kv = LineGather(place, kv_own, kv_ref, kv_sems)
    cot = LineGather(place, cot_ref, cot_full, cot_sems)
    mlp = RowExchange(place, lambda k: wm_ref, lambda k, back: wm_full.at[place.row_at(-back)], wm_sems)
    down = RowExchange(place, lambda k: wd_ref, lambda k, back: wd_rows.at[place.row_at(-back)], wd_sems)

    def down_slice(c):
        return wd_rows.at[c // per_row, pl.ds(pl.multiple_of((c % per_row) * ff_part, 16), ff_part), :]

    spread = CtxExchange(place, down_slice, lambda c: wd_full.at[c], a2a_sems)

    loads = [
        pltpu.make_async_copy(src, dst, load_sems.at[i])
        for i, (src, dst) in enumerate(
            [
                (wq_in, wq_ref),
                (wk_in, wk_turned),
                (wv_in, wv_turned),
                (x_in, x_turned),
                (cot_in, cot_turned),
                (wo_in, wo_ref),
                (wg_in, wg_turned),
                (wu_in, wu_turned),
                (wd_in, wd_in_ref),
            ]
        )
    ]
    for load in loads:
        load.start()
    for load in loads[:3]:
        load.wait()
    wqkv_ref[...] = jnp.concatenate([wq_ref[...], turn(wk_turned[...]), turn(wv_turned[...])], axis=1)
    place.greet(ctx=True, rows=True)
    qkv.start()
    for load in loads[3:]:
        load.wait()
    out.start(rows=False)
    normed = norm_forward(x_turned[...].astype(f32).T, gain_ref[...])[2]
    n1_turned[...] = turn(normed)
    cot_ref[...] = turn(cot_turned[...])
    for step in range(1, chips):
        qkv.forward(step)
        if step == 1:
            qkv.bend(0)
    for step in range(1, chips):
        out.forward(step, rows=False)
    cot.start()
    wd_ref[...] = turn(wd_in_ref[...])
    wd_rows[place.row] = wd_ref[...]
    wm_ref[...] = jnp.concatenate([turn(wg_turned[...]), turn(wu_turned[...])], axis=1)
    for step in range(1, chips):
        qkv.bend(step)
        qkv.settle(step - 1)
        if step == chips // 2:
            cot.forward(1)
    wm_full[place.row] = wm_ref[...]
    qkv.settle(chips - 1)
    down.start()
    for step in range(2, chips):
        cot.forward(step)
    qkv.arrive()

    for c in range(ctx):
        part = dot_nn(normed, wqkv_full[c].reshape(width, qkv_cols)).T
        qkv_raw[pl.ds(c * q_cols, q_cols), :] = part[:q_cols]
        qkv_raw[pl.ds(q_width + c * kv_cols, kv_cols), :] = part[q_cols : q_cols + kv_cols]
        qkv_raw[pl.ds(q_width + kv_width + c * kv_cols, kv_cols), :] = part[q_cols + kv_cols :]
    cosine, sine = cos_ref[...], sin_ref[...]
    for g in range(KV_HEADS):
        key = rotate_rows(qkv_raw[pl.ds(q_width + g * HEAD_DIM, HEAD_DIM), :], cosine, sine)
        value = qkv_raw[pl.ds(q_width + kv_width + g * HEAD_DIM, HEAD_DIM), :]
        pair = jnp.concatenate([key, value], axis=0).T
        kv_own[:, pl.ds(g * 2 * HEAD_DIM, 2 * HEAD_DIM)] = pair.astype(bf16)
    kv.start()
    out.cross()
    mlp.start()
    for h in range(HEADS):
        q_ref[pl.ds(h * HEAD_DIM, HEAD_DIM), :] = rotate_rows(
            qkv_raw[pl.ds(h * HEAD_DIM, HEAD_DIM), :], cosine, sine
        ).astype(bf16)
    for step in range(1, chips):
        kv.forward(step)
    down.arrive()
    spread.start()
    wd_full[place.c] = down_slice(place.c)[...]
    kv.arrive()

    scale = 1.0 / math.sqrt(HEAD_DIM)
    query_pos = posq_ref[...]
    chunk = 2 * tokens
    wide = GROUP * tokens
    for g in range(KV_HEADS):
        lanes = pl.ds(g * 2 * HEAD_DIM, 2 * HEAD_DIM)
        query = group_rows(q_ref, g) * jnp.asarray(scale, bf16)
        query = jnp.concatenate([query, jnp.zeros_like(query)], axis=0)

        def score(i, total, lanes=lanes, query=query):
            keys = kv_ref[pl.ds(2 * i, 2), :, lanes].reshape(chunk, 2 * HEAD_DIM)
            rows = pl.ds(pl.multiple_of(i * chunk, chunk), chunk)
            scores = jnp.where(posk_ref[rows, :] <= query_pos, dot_nn(keys, query), MASKED)
            score_ref[rows, :] = scores
            return total + jnp.sum(jnp.exp(scores), axis=0, keepdims=True)

        log_total = jnp.log(lax.fori_loop(0, chips, score, jnp.zeros((1, wide), f32), unroll=UNROLL))
        lse_ref[g] = log_total

        def gather_values(i, total, lanes=lanes, log_total=log_total):
            keys = kv_ref[pl.ds(2 * i, 2), :, lanes].reshape(chunk, 2 * HEAD_DIM)
            rows = pl.ds(pl.multiple_of(i * chunk, chunk), chunk)
            prob = jnp.exp(score_ref[rows, :] - log_total).astype(bf16)
            return total + dot_tn(keys, prob)

        total = lax.fori_loop(
            0, chips, gather_values, jnp.zeros((2 * HEAD_DIM, wide), f32), unroll=UNROLL
        )
        for j in range(GROUP):
            attn_ref[pl.ds((g * GROUP + j) * HEAD_DIM, HEAD_DIM), :] = total[
                HEAD_DIM:, j * tokens : (j + 1) * tokens
            ].astype(bf16)
        if g == 1:
            for step in range(chips):
                out.bend(step)
        if g == 3:
            for step in range(chips):
                out.settle(step)
    out.arrive()
    out_cols = wo_ref.shape[1]
    attn = attn_ref[...]
    for c in range(ctx):
        rows = pl.ds(c * out_cols, out_cols)
        mid_turned[rows, :] = dot_tn(wo_full[c].reshape(q_width, out_cols), attn)
    middle = (x_turned[...].astype(f32) + mid_turned[...]).T
    mid_ref[...] = middle
    n2_ref[...] = norm_forward(middle, gain2_ref[...])[2]
    cot.arrive()
    mlp.arrive()
    spread.arrive()
    down_cols = wd_ref.shape[1]
    for c in range(ctx):
        wd_wide[pl.ds(c * down_cols, down_cols), :] = wd_full[c].astype(f32).T
    wd_turned[...] = wd_wide[...].astype(bf16)
    for part in (qkv, kv, out, mlp, down, cot, spread):
        part.finish()


def mlp_kernel(sizes, *refs):
    refs = iter(refs)
    n_ref, cot_ref, wm_ref, wd_ref = take(refs, 4)
    ngrad_ref, osums_ref, dwm_ref, dwd_ref = take(refs, 4)
    n_all, gub_all, hid_all, part_ref, sib_ref, far_ref, wide_ref = take(refs, 7)
    n_sems = take(refs, 4)
    bs, br, zs, zr = take(refs, 4)

    place = Place(sizes)
    ctx, chips = place.ctx, place.chips
    tokens, width = n_ref.shape
    ff = wd_ref.shape[1]
    chunk = 2 * tokens
    gather = LineGather(place, n_ref, n_all, n_sems)

    place.greet(line=True, sibling=True)
    gather.start()

    def work(p):
        rows = pl.ds(pl.multiple_of(p * chunk, chunk), chunk)
        normed = n_all[pl.ds(2 * p, 2)].reshape(chunk, width)
        cot = cot_ref[pl.ds(2 * p, 2)].reshape(chunk, width)
        gate_up = dot_nn(normed, wm_ref[...])
        gate, up = gate_up[:, :ff], gate_up[:, ff:]
        sigmoid_gate = jax.nn.sigmoid(gate)
        silu_gate = gate * sigmoid_gate
        hidden = (silu_gate * up).astype(bf16)
        hidden_grad = dot_nn(cot, wd_ref[...])
        gate_back = hidden_grad * up * sigmoid_gate * (1.0 + gate * (1.0 - sigmoid_gate))
        up_back = hidden_grad * silu_gate
        both = jnp.concatenate([gate_back, up_back], axis=1).astype(bf16)
        gub_all[rows, :] = both
        hid_all[rows, :] = hidden
        part_ref[p, :, 0] = dot_nt(both, wm_ref[...]).astype(bf16).reshape(2, tokens, width)
        part_ref[p, :, 1] = dot_nt(hidden, wd_ref[...]).astype(bf16).reshape(2, tokens, width)
        to_sibling(p).start()

    def to_sibling(p):
        return remote(part_ref.at[p, 1 - place.core], sib_ref.at[p], bs.at[p], br.at[p], place.sibling())

    def settle(p):
        to_sibling(p).wait_recv()
        both = (part_ref[p, place.core].astype(f32) + sib_ref[p].astype(f32)).astype(bf16)
        part_ref[p, place.core, 0] = both[0]
        osums_ref[p] = both[1]

    def target(way, d):
        return place.chip + d if way == 0 else place.chip - d

    def exists(way, d):
        return place.chip + d < chips if way == 0 else place.chip >= d

    def upstream(way):
        return place.chip >= 1 if way == 0 else place.chip + 1 < chips

    def landing(way, d):
        return target(way, d) if (way == 0 or d) else chips

    piece_rows = tokens // 2 // 16 * 16
    pieces = (pl.ds(0, piece_rows), pl.ds(piece_rows, tokens - piece_rows))

    def onward(way, d, n):
        p = target(way, d)
        slot = p if (way == 0 or d > 1) else chips
        return remote(
            part_ref.at[p, place.core, 0, pieces[n]],
            far_ref.at[slot, pieces[n]],
            zs.at[way, d, n],
            zr.at[way, d, n],
            place.along(1 - 2 * way),
        )

    def inward(way, d, n):
        mine = far_ref.at[landing(way, d), pieces[n]]
        return remote(mine, mine, zs.at[way, d + 1, n], zr.at[way, d + 1, n], place.along(1 - 2 * way))

    gather.from_sibling(0, 0).wait_recv()
    work(place.chip)
    for d in range(1, chips):
        gather.forward(d)
        for way in range(2):
            @pl.when(exists(way, d))
            def _(way=way, d=d):
                gather.from_sibling(1 - way, d).wait_recv()
                work(target(way, d))

        if d == 1:
            settle(place.chip)
        for way in range(2):

            @pl.when(exists(way, d))
            def _(way=way, d=d):
                settle(target(way, d))

                @pl.when(jnp.logical_not(upstream(way)))
                def _():
                    for n in range(2):
                        onward(way, d, n).start()

    seq = ctx * tokens
    dwm_ref[...] = dot_tn(n_all[...].reshape(seq, width), gub_all[...]).astype(bf16).reshape(dwm_ref.shape)
    down_cols = dwd_ref.shape[2]
    wide_ref[...] = dot_tn(cot_ref[...].reshape(seq, width), hid_all[...])
    for c in range(ctx):
        dwd_ref[c] = wide_ref[pl.ds(c * down_cols, down_cols), :].T.astype(bf16)

    for d in range(chips - 1, 0, -1):
        for way in range(2):

            @pl.when(jnp.logical_and(exists(way, d), upstream(way)))
            def _(way=way, d=d):
                p = target(way, d)
                for n, rows in enumerate(pieces):
                    inward(way, d, n).wait_recv()
                    both = part_ref[p, place.core, 0, rows].astype(f32) + far_ref[p, rows].astype(f32)
                    part_ref[p, place.core, 0, rows] = both.astype(bf16)
                    onward(way, d, n).start()

    ngrad_ref[...] = part_ref[place.chip, place.core, 0].astype(f32)
    for way in range(2):

        @pl.when(upstream(way))
        def _(way=way):
            for n in range(2):
                inward(way, 0, n).wait_recv()
            ngrad_ref[...] += far_ref[landing(way, 0)].astype(f32)

    gather.finish()
    for p in range(chips):
        to_sibling(p).wait_send()
    for d in range(1, chips):
        for way in range(2):

            @pl.when(exists(way, d))
            def _(way=way, d=d):
                for n in range(2):
                    onward(way, d, n).wait_send()


def back_kernel(sizes, *refs):
    refs = iter(refs)
    (q_ref, attn_ref, kv_ref, lse_ref, cos_ref, sin_ref, posk_ref, posq_ref, dwm_ref, dwd_ref) = take(refs, 10)
    ngrad_ref, mid_ref, gain_ref, cot_ref, wo_ref = take(refs, 5)
    qkvb_ref, fin_mlp, fin_down, mgrad_ref, midb_ref, gain_part = take(refs, 6)
    g_ref, mid_turned, q_back, kv_back = take(refs, 4)
    delta_ref, qz_ref, gz_ref, acc_ref, part_ref, sib_ref, far_ref = take(refs, 7)
    dwm_recv, down_rows, down_recv = take(refs, 3)
    bs, br, zs, zr = take(refs, 4)
    wm_sems, a2a_sems, wd_sems = take(refs, 2), take(refs, 2), take(refs, 2)

    place = Place(sizes)
    ctx, chips, row_parts = place.ctx, place.chips, place.row_parts
    tokens = q_ref.shape[1]
    chunk, wide = 2 * tokens, GROUP * tokens
    ff_part = dwd_ref.shape[1]
    per_row = ctx // row_parts
    scale = 1.0 / math.sqrt(HEAD_DIM)

    mlp = RowExchange(place, lambda k: dwm_ref.at[place.row_at(k)], lambda k, back: dwm_recv.at[k], wm_sems)

    def down_slot(c):
        return down_rows.at[c // per_row, pl.ds(pl.multiple_of((c % per_row) * ff_part, 16), ff_part), :]

    spread = CtxExchange(place, lambda c: dwd_ref.at[c], down_slot, a2a_sems)
    down = RowExchange(place, lambda k: down_rows.at[place.row_at(k)], lambda k, back: down_recv.at[k], wd_sems)

    place.greet(ctx=True, rows=True)
    mlp.start()
    spread.start()
    down_slot(place.c)[...] = dwd_ref[place.c]

    inverse_rms, unit, _ = norm_forward(mid_ref[...], gain_ref[...])
    mlp_back, gain_part[0] = norm_backward(ngrad_ref[...], inverse_rms, unit, gain_ref[...])
    mid_grad = cot_ref[...].astype(f32).T + mlp_back
    mgrad_ref[...] = mid_grad
    mid_turned[...] = mid_grad.T
    out_cols = wo_ref.shape[3]
    total = jnp.zeros(g_ref.shape, f32)
    for c in range(ctx):
        piece = mid_turned[pl.ds(c * out_cols, out_cols), :].astype(bf16)
        midb_ref[c] = piece
        total = total + dot_nn(wo_ref[c].reshape(g_ref.shape[0], out_cols), piece)
    g_ref[...] = total.astype(bf16)

    zeros = jnp.zeros((HEAD_DIM, wide), bf16)
    for g in range(KV_HEADS):
        query = group_rows(q_ref, g) * jnp.asarray(scale, bf16)
        grad = group_rows(g_ref, g)
        qz_ref[g] = jnp.concatenate([query, zeros], axis=0)
        gz_ref[g] = jnp.concatenate([zeros, grad], axis=0)
        delta_ref[g] = jnp.sum(grad.astype(f32) * group_rows(attn_ref, g).astype(f32), axis=0, keepdims=True)
        acc_ref[g] = jnp.zeros_like(acc_ref[g])
    query_pos = posq_ref[...]

    def to_sibling(j):
        return remote(part_ref.at[j, 1 - place.core], sib_ref.at[j], bs.at[j], br.at[j], place.sibling())

    def to_owner(j):
        return remote(part_ref.at[j, place.core], far_ref.at[j], zs.at[j], zr.at[j], place.along(j))

    def settle(j):
        to_sibling(j).wait_recv()
        both = part_ref[j, place.core].astype(f32) + sib_ref[j].astype(f32)
        part_ref[j, place.core] = both.astype(bf16)

    def work(j):
        p = place.chip_at(j)
        rows = pl.ds(pl.multiple_of(p * chunk, chunk), chunk)
        allowed = posk_ref[rows, :] <= query_pos
        for g in range(KV_HEADS):
            lanes = pl.ds(g * 2 * HEAD_DIM, 2 * HEAD_DIM)
            keys = kv_ref[pl.ds(2 * p, 2), :, lanes].reshape(chunk, 2 * HEAD_DIM)
            query, grad = qz_ref[g], gz_ref[g]
            scores = jnp.where(allowed, dot_nn(keys, query), MASKED)
            prob = jnp.exp(scores - lse_ref[g])
            score_grad = (prob * (dot_nn(keys, grad) - delta_ref[g])).astype(bf16)
            both = dot_nt(score_grad, query) + dot_nt(prob.astype(bf16), grad)
            part_ref[j, :, :, lanes] = both.astype(bf16).reshape(2, tokens, 2 * HEAD_DIM)
            acc_ref[g] += dot_tn(keys, score_grad)
        to_sibling(j).start()

    work(1)

    def turn(j, carry):
        work(j)
        settle(j - 1)
        to_owner(j - 1).start()
        return carry

    lax.fori_loop(2, chips, turn, 0)
    spread.arrive()
    down.start()
    work(0)
    settle(chips - 1)
    to_owner(chips - 1).start()
    cosine, sine = cos_ref[...], sin_ref[...]
    for h in range(HEADS):
        g, j = h // GROUP, h % GROUP
        head = acc_ref[g, pl.ds(0, HEAD_DIM), pl.ds(j * tokens, tokens)] * scale
        q_back[pl.ds(h * HEAD_DIM, HEAD_DIM), :] = rotate_rows_back(head, cosine, sine)
    settle(0)
    mlp.arrive()
    total = dwm_ref[place.row].astype(f32)
    for k in range(1, row_parts):
        total = total + dwm_recv[k].astype(f32)
    fin_mlp[...] = total
    down.arrive()
    total = down_rows[place.row].astype(f32)
    for k in range(1, row_parts):
        total = total + down_recv[k].astype(f32)
    fin_down[...] = total
    total = part_ref[0, place.core].astype(f32)
    for j in range(1, chips):
        to_owner(j).wait_recv()
        total = total + far_ref[j].astype(f32)
    total = total.T
    kv_width = KV_HEADS * HEAD_DIM
    for g in range(KV_HEADS):
        pair = total[g * 2 * HEAD_DIM : (g + 1) * 2 * HEAD_DIM]
        rows = pl.ds(g * HEAD_DIM, HEAD_DIM)
        kv_back[rows, :] = rotate_rows_back(pair[:HEAD_DIM], cosine, sine)
        kv_back[pl.ds(kv_width + g * HEAD_DIM, HEAD_DIM), :] = pair[HEAD_DIM:]
    q_cols, kv_cols = q_back.shape[0] // ctx, kv_width // ctx
    for c in range(ctx):
        qkvb_ref[c] = jnp.concatenate(
            [
                q_back[pl.ds(c * q_cols, q_cols), :],
                kv_back[pl.ds(c * kv_cols, kv_cols), :],
                kv_back[pl.ds(kv_width + c * kv_cols, kv_cols), :],
            ],
            axis=0,
        ).astype(bf16)
    for part in (mlp, spread, down):
        part.finish()
    for j in range(chips):
        to_sibling(j).wait_send()
        if j:
            to_owner(j).wait_send()


def last_kernel(sizes, *refs):
    refs = iter(refs)
    n1_ref, qkvb_ref, attn_ref, midb_ref, osums_ref, mid_ref = take(refs, 6)
    x_ref, gain_ref, gain_part, mgrad_ref, wqkv_ref = take(refs, 5)
    fin_ref, gain_out, result_ref, input_ref = take(refs, 4)
    part_ref, sib_ref, bent_ref, row_ref, far_send, far_ref = take(refs, 6)
    gain_sib, gain_row, gain_far, gain_a, gain_b, gain_c = take(refs, 6)
    bs, br, vs, vr, xs, xr, zs, zr = take(refs, 8)
    gb, gx, gz = take(refs, 2), take(refs, 2), take(refs, 2)
    osum_own, osum_far, mid_sum, os, orr = take(refs, 5)

    place = Place(sizes)
    chips, row_parts, outer, inner = place.chips, place.row_parts, place.rows_outer, place.rows_inner
    core, row, chip = place.core, place.row, place.chip
    in_rows = fin_ref.shape[0]
    half = (in_rows // 2 + 15) // 16 * 16
    parts = (pl.ds(0, half), pl.ds(half, in_rows - half))
    sized = (pl.ds(0, half), pl.ds(0, in_rows - half))
    sides = [(a, 0) for a in range(1, outer)] + [(0, b) for b in range(1, inner)]
    diagonal = [(a, b) for a in range(1, outer) for b in range(1, inner)]
    place.greet(line=True, sibling=True, rows=True)

    def row_of(a, b):
        return wrap(place.seq + a, outer) * inner + wrap(place.fsdp + b, inner)

    def device(a, b):
        return (wrap(place.seq + a, outer), wrap(place.fsdp + b, inner), place.c)

    def to_sibling(j):
        return remote(
            part_ref.at[place.chip_at(j) * 2 + 1 - core], sib_ref.at[j], bs.at[j], br.at[j], place.sibling()
        )

    def bent(j, part, n):
        a, b = diagonal[n]
        return remote(
            sib_ref.at[j, row_of(a, b), parts[part]],
            bent_ref.at[j, part, n, sized[part]],
            vs.at[j, part, n],
            vr.at[j, part, n],
            device(0, b) if part == 0 else device(a, 0),
        )

    def direct(j, n):
        a, b = sides[n]
        return remote(sib_ref.at[j, row_of(a, b)], row_ref.at[j, n], xs.at[j, n], xr.at[j, n], device(a, b))

    def to_owner(j):
        return remote(far_send.at[j], far_ref.at[j], zs.at[j], zr.at[j], place.along(j))

    def g_sib():
        return remote(gain_a, gain_sib.at[core], gb[0].at[0], gb[1].at[0], place.sibling())

    def g_row(k):
        return remote(gain_b, gain_row.at[row], gx[0].at[k], gx[1].at[k], place.across(k))

    def g_far(j):
        return remote(gain_c, gain_far.at[chip], gz[0].at[j], gz[1].at[j], place.along(j))

    def input_gradient():
        width = x_ref.shape[0]
        total = jnp.zeros(x_ref.shape, f32)
        for c in range(place.ctx):
            total = total + dot_nn(wqkv_ref[c].reshape(width, wqkv_ref.shape[3]), qkvb_ref[c])
        inverse_rms, unit, _ = norm_forward(x_ref[...].astype(f32).T, gain_ref[...])
        back, gain_a[0] = norm_backward(total.T, inverse_rms, unit, gain_ref[...])
        input_ref[...] = (mgrad_ref[...] + back).T.astype(bf16)
        gain_a[1] = gain_part[0]
        gain_sib[core] = gain_a[...]
        g_sib().start()

    def multiply(j):
        for k in range(2):
            c = place.chip_at(j) * 2 + k
            both = jnp.concatenate(
                [dot_nt(n1_ref[...], qkvb_ref[c]), dot_nt(attn_ref[...], midb_ref[c])], axis=1
            )
            part_ref[c] = both.astype(bf16).reshape(part_ref.shape[1:])
        to_sibling(j).start()

    def add_sibling(j):
        to_sibling(j).wait_recv()
        both = part_ref[place.chip_at(j) * 2 + core].astype(f32) + sib_ref[j].astype(f32)
        sib_ref[j] = both.astype(bf16)
        for n in range(len(diagonal)):
            for part in range(2):
                bent(j, part, n).start()

    def add_bent(j):
        for n, (a, b) in enumerate(diagonal):
            for part in range(2):
                bent(j, part, n).wait_recv()
                at = (j, row_of(a, 0) if part == 0 else row_of(0, b), parts[part])
                both = sib_ref[at].astype(f32) + bent_ref[j, part, n, sized[part]].astype(f32)
                sib_ref[at] = both.astype(bf16)
        for n in range(len(sides)):
            direct(j, n).start()

    def add_rows(j):
        total = sib_ref[j, row].astype(f32)
        for n in range(len(sides)):
            direct(j, n).wait_recv()
            total = total + row_ref[j, n].astype(f32)
        if j:
            far_send[j] = total.astype(bf16)
            to_owner(j).start()
        else:
            fin_ref[...] = total

    def target(way, d):
        return chip + d if way == 0 else chip - d

    def exists(way, d):
        return chip + d < chips if way == 0 else chip >= d

    def upstream(way):
        return chip >= 1 if way == 0 else chip + 1 < chips

    def output_on(way, d):
        p = target(way, d)
        slot = p if (way == 0 or d > 1) else chips
        return remote(osum_own.at[p], osum_far.at[slot], os.at[way, d], orr.at[way, d], place.along(1 - 2 * way))

    def output_in(way, d):
        mine = osum_far.at[target(way, d) if (way == 0 or d) else chips]
        return remote(mine, mine, os.at[way, d + 1], orr.at[way, d + 1], place.along(1 - 2 * way))

    osum_own[...] = osums_ref[...]
    for d in range(chips - 1, 0, -1):
        for way in range(2):

            @pl.when(jnp.logical_and(exists(way, d), jnp.logical_not(upstream(way))))
            def _(way=way, d=d):
                output_on(way, d).start()

    def output_turn(d):
        for way in range(2):

            @pl.when(jnp.logical_and(exists(way, d), upstream(way)))
            def _(way=way):
                p = target(way, d)
                output_in(way, d).wait_recv()
                osum_own[p] = (osum_own[p].astype(f32) + osum_far[p].astype(f32)).astype(bf16)
                output_on(way, d).start()

    order = list(range(1, chips)) + [0]
    stages = (multiply, add_sibling, add_bent, add_rows)
    for t in range(chips + len(stages) - 1):
        for depth, stage in enumerate(stages):
            if 0 <= t - depth < chips:
                stage(order[t - depth])
        if t == 1:
            input_gradient()
        if 1 <= chips - 1 - t < chips - 1:
            output_turn(chips - 1 - t)
        if t == 3:
            remote(gain_a, gain_sib.at[1 - core], gb[0].at[0], gb[1].at[0], place.sibling()).wait_recv()
            gain_b[...] = gain_sib[0] + gain_sib[1]
            gain_row[row] = gain_b[...]
            for k in range(1, row_parts):
                g_row(k).start()

    for k in range(1, row_parts):
        remote(gain_b, gain_row.at[place.row_at(-k)], gx[0].at[k], gx[1].at[k], place.across(k)).wait_recv()
    total = gain_row[0]
    for k in range(1, row_parts):
        total = total + gain_row[k]
    gain_c[...] = total
    gain_far[chip] = gain_c[...]
    for j in range(1, chips):
        g_far(j).start()
    mid_sum[...] = mid_ref[...] + osum_own[chip].astype(f32)
    for way in range(2):

        @pl.when(upstream(way))
        def _(way=way):
            output_in(way, 0).wait_recv()
            mid_sum[...] += osum_far[chip if way == 0 else chips].astype(f32)

    result_ref[...] = mid_sum[...].T.astype(bf16)
    total = fin_ref[...]
    for j in range(1, chips):
        to_owner(j).wait_recv()
        total = total + far_ref[j].astype(f32)
    fin_ref[...] = total
    for j in range(1, chips):
        remote(gain_c, gain_far.at[place.chip_at(-j)], gz[0].at[j], gz[1].at[j], place.along(j)).wait_recv()
    total = gain_far[0]
    for j in range(1, chips):
        total = total + gain_far[j]
    gain_out[...] = total

    g_sib().wait_send()
    for k in range(1, row_parts):
        g_row(k).wait_send()
    for j in range(1, chips):
        g_far(j).wait_send()
    for j in order:
        to_sibling(j).wait_send()
        for n in range(len(diagonal)):
            for part in range(2):
                bent(j, part, n).wait_send()
        for n in range(len(sides)):
            direct(j, n).wait_send()
        if j:
            to_owner(j).wait_send()
    for d in range(1, chips):
        for way in range(2):

            @pl.when(exists(way, d))
            def _(way=way, d=d):
                output_on(way, d).wait_send()


def finish_kernel(cuts, *refs):
    refs = iter(refs)
    attn_ref, mlp_ref, down_ref, result_ref, input_ref, gain_ref = take(refs, 6)
    q_cols, kv_cols, ff_cols = cuts
    outs = take(refs, 11)
    attn, mlp = attn_ref[...], mlp_ref[...]
    outs[0][...] = result_ref[...]
    outs[1][...] = input_ref[...]
    outs[2][...] = gain_ref[0]
    outs[3][...] = gain_ref[1]
    outs[4][...] = attn[:, :q_cols]
    outs[5][...] = attn[:, q_cols : q_cols + kv_cols].T
    outs[6][...] = attn[:, q_cols + kv_cols : q_cols + 2 * kv_cols].T
    outs[7][...] = attn[:, q_cols + 2 * kv_cols :]
    outs[8][...] = mlp[:, :ff_cols].T
    outs[9][...] = mlp[:, ff_cols:].T
    outs[10][...] = down_ref[...].T


def finish(cuts, inputs, outs):
    vmem = pl.BlockSpec(memory_space=pltpu.VMEM)
    return pl.pallas_call(
        functools.partial(finish_kernel, cuts),
        out_shape=[jax.ShapeDtypeStruct(shape, kind) for shape, kind in outs],
        in_specs=[vmem] * len(inputs),
        out_specs=[vmem] * len(outs),
    )(*inputs)


def call(kernel, sizes, inputs, outs, scratch, collective_id, raw=()):
    vmem = pl.BlockSpec(memory_space=pltpu.VMEM)
    anywhere = pl.BlockSpec(memory_space=pl.ANY)
    return pl.pallas_call(
        functools.partial(kernel, sizes),
        out_shape=[jax.ShapeDtypeStruct(shape, kind) for shape, kind in outs],
        in_specs=[anywhere if i in raw else vmem for i in range(len(inputs))],
        out_specs=[vmem] * len(outs),
        scratch_shapes=scratch,
        compiler_params=pltpu.CompilerParams(
            collective_id=collective_id, has_side_effects=True, vmem_limit_bytes=60 * 1024 * 1024
        ),
    )(*inputs)


def on_device(
    tokens,
    cotangent,
    block_order,
    gain_attn,
    gain_mlp,
    w_query,
    w_key,
    w_value,
    w_out,
    w_gate,
    w_up,
    w_down,
):
    sizes = tuple(lax.axis_size(n) for n in ("seq", "fsdp", "ctx"))
    rows, ctx = sizes[0] * sizes[1], sizes[2]
    chips = ctx // 2
    row_count, width = tokens.shape[1], tokens.shape[2]
    seq_len = row_count * ctx
    block_total = block_order.shape[0]
    block_len = seq_len // block_total
    kv_width = KV_HEADS * HEAD_DIM
    q_width = HEADS * HEAD_DIM
    q_cols, kv_cols, ff_cols = w_query.shape[1], w_key.shape[1], w_gate.shape[1]
    out_cols, down_cols, down_rows = w_out.shape[1], w_down.shape[1], w_down.shape[0]
    in_rows = w_query.shape[0]
    qkv_cols = q_cols + 2 * kv_cols
    wide = GROUP * row_count

    slot_index = jnp.arange(seq_len, dtype=jnp.int32)
    owner_hit = (slot_index // block_len)[:, None] == jnp.arange(block_total, dtype=jnp.int32)[None, :]
    all_pos = (
        jnp.sum(jnp.where(owner_hit, block_order[None, :], 0), axis=1) * block_len + slot_index % block_len
    )
    own_pos = lax.dynamic_slice_in_dim(all_pos, lax.axis_index("ctx") * row_count, row_count)
    inverse = rope_base ** (-jnp.arange(HALF, dtype=f32) / HALF)
    angles = inverse[:, None] * own_pos.astype(f32)[None, :]
    cosine, sine = jnp.cos(angles), jnp.sin(angles)
    pos_keys = all_pos[:, None]
    pos_query = jnp.tile(own_pos, GROUP)[None, :]

    x = tokens[0]
    cot_rows = cotangent[0]
    turned = [jnp.transpose(w) for w in (w_key, w_value, w_gate, w_up, w_down)]
    wk_t, wv_t, wg_t, wu_t, wd_t = turned

    (
        attn_t,
        query_t,
        kv_all,
        lse,
        qkv_full,
        out_full,
        mlp_full,
        down_t,
        cot_all,
        normed_attn_t,
        middle,
        normed_mlp,
    ) = call(
        first_kernel,
        sizes,
        (
            jnp.transpose(x),
            gain_attn[None],
            gain_mlp[None],
            w_query,
            wk_t,
            wv_t,
            w_out,
            wg_t,
            wu_t,
            wd_t,
            jnp.transpose(cot_rows),
            cosine,
            sine,
            pos_keys,
            pos_query,
        ),
        [
            ((q_width, row_count), bf16),
            ((q_width, row_count), bf16),
            ((ctx, row_count, 2 * kv_width), bf16),
            ((KV_HEADS, 1, wide), f32),
            ((ctx, rows, in_rows, qkv_cols), bf16),
            ((ctx, rows, in_rows, out_cols), bf16),
            ((rows, in_rows, 2 * ff_cols), bf16),
            ((width, ff_cols), bf16),
            ((ctx, row_count, width), bf16),
            ((width, row_count), bf16),
            ((row_count, width), f32),
            ((row_count, width), bf16),
        ],
        [
            pltpu.VMEM((q_width + 2 * kv_width, row_count), f32),
            pltpu.VMEM((row_count, 2 * kv_width), bf16),
            pltpu.VMEM((rows, down_rows, down_cols), bf16),
            pltpu.VMEM((seq_len, wide), f32),
            pltpu.VMEM((ctx, ff_cols, down_cols), bf16),
            pltpu.VMEM((width, row_count), f32),
            pltpu.VMEM((width, ff_cols), f32),
            pltpu.VMEM((width, row_count), bf16),
        ]
        + [pltpu.VMEM(w.shape, bf16) for w in (w_query, wk_t, wv_t, w_out, wg_t, wu_t, wd_t)]
        + [
            pltpu.VMEM((width, row_count), bf16),
            pltpu.VMEM((in_rows, qkv_cols), bf16),
            pltpu.VMEM((in_rows, 2 * ff_cols), bf16),
            pltpu.VMEM(w_down.shape, bf16),
            pltpu.VMEM((row_count, width), bf16),
            dma(9),
        ]
        + FullGather.scratch(sizes)
        + FullGather.scratch(sizes)
        + LineGather.scratch(sizes)
        + LineGather.scratch(sizes)
        + RowExchange.scratch(sizes)
        + RowExchange.scratch(sizes)
        + CtxExchange.scratch(sizes),
        1,
        raw=(0, 3, 4, 5, 6, 7, 8, 9, 10),
    )

    w_mlp_cat = mlp_full.reshape(width, 2 * ff_cols)

    normed_mlp_grad, output_sums, d_mlp, d_down = call(
        mlp_kernel,
        sizes,
        (normed_mlp, cot_all, w_mlp_cat, down_t),
        [
            ((row_count, width), f32),
            ((chips, row_count, width), bf16),
            ((rows, in_rows, 2 * ff_cols), bf16),
            ((ctx, ff_cols, down_cols), bf16),
        ],
        [
            pltpu.VMEM((ctx, row_count, width), bf16),
            pltpu.VMEM((seq_len, 2 * ff_cols), bf16),
            pltpu.VMEM((seq_len, ff_cols), bf16),
            pltpu.VMEM((chips, 2, 2, row_count, width), bf16),
            pltpu.VMEM((chips, 2, row_count, width), bf16),
            pltpu.VMEM((chips + 1, row_count, width), bf16),
            pltpu.VMEM((width, ff_cols), f32),
        ]
        + LineGather.scratch(sizes)
        + [dma(chips)] * 2
        + [dma(2, chips, 2)] * 2,
        2,
    )
    qkv_back_t, fin_mlp, fin_down, mid_grad, mid_back_t, gain_mlp_part = call(
        back_kernel,
        sizes,
        (
            query_t,
            attn_t,
            kv_all,
            lse,
            cosine,
            sine,
            pos_keys,
            pos_query,
            d_mlp,
            d_down,
            normed_mlp_grad,
            middle,
            gain_mlp[None],
            jnp.transpose(cot_rows),
            out_full,
        ),
        [
            ((ctx, qkv_cols, row_count), bf16),
            ((in_rows, 2 * ff_cols), f32),
            ((down_rows, down_cols), f32),
            ((row_count, width), f32),
            ((ctx, out_cols, row_count), bf16),
            ((1, width), f32),
        ],
        [
            pltpu.VMEM((q_width, row_count), bf16),
            pltpu.VMEM((width, row_count), f32),
            pltpu.VMEM((q_width, row_count), f32),
            pltpu.VMEM((2 * kv_width, row_count), f32),
            pltpu.VMEM((KV_HEADS, 1, wide), f32),
            pltpu.VMEM((KV_HEADS, 2 * HEAD_DIM, wide), bf16),
            pltpu.VMEM((KV_HEADS, 2 * HEAD_DIM, wide), bf16),
            pltpu.VMEM((KV_HEADS, 2 * HEAD_DIM, wide), f32),
            pltpu.VMEM((chips, 2, row_count, 2 * kv_width), bf16),
            pltpu.VMEM((chips, row_count, 2 * kv_width), bf16),
            pltpu.VMEM((chips, row_count, 2 * kv_width), bf16),
            pltpu.VMEM((rows, in_rows, 2 * ff_cols), bf16),
            pltpu.VMEM((rows, down_rows, down_cols), bf16),
            pltpu.VMEM((rows, down_rows, down_cols), bf16),
        ]
        + [dma(chips)] * 4
        + RowExchange.scratch(sizes)
        + CtxExchange.scratch(sizes)
        + RowExchange.scratch(sizes),
        3,
    )

    attn_cols = qkv_cols + out_cols
    gains = pltpu.VMEM((2, width), f32)
    half = (in_rows // 2 + 15) // 16 * 16
    corners, sides = (sizes[0] - 1) * (sizes[1] - 1), sizes[0] + sizes[1] - 2
    fin_attn, gain_sums, result_t, input_t = call(
        last_kernel,
        sizes,
        (
            normed_attn_t,
            qkv_back_t,
            attn_t,
            mid_back_t,
            output_sums,
            middle,
            jnp.transpose(x),
            gain_attn[None],
            gain_mlp_part,
            mid_grad,
            qkv_full,
        ),
        [
            ((in_rows, attn_cols), f32),
            ((2, width), f32),
            ((width, row_count), bf16),
            ((width, row_count), bf16),
        ],
        [
            pltpu.VMEM((ctx, rows, in_rows, attn_cols), bf16),
            pltpu.VMEM((chips, rows, in_rows, attn_cols), bf16),
            pltpu.VMEM((chips, 2, corners, half, attn_cols), bf16),
            pltpu.VMEM((chips, sides, in_rows, attn_cols), bf16),
            pltpu.VMEM((chips, in_rows, attn_cols), bf16),
            pltpu.VMEM((chips, in_rows, attn_cols), bf16),
            pltpu.VMEM((2, 2, width), f32),
            pltpu.VMEM((rows, 2, width), f32),
            pltpu.VMEM((chips, 2, width), f32),
            gains,
            gains,
            gains,
            dma(chips),
            dma(chips),
            dma(chips, 2, corners),
            dma(chips, 2, corners),
            dma(chips, sides),
            dma(chips, sides),
            dma(chips),
            dma(chips),
            dma(1),
            dma(1),
            dma(rows),
            dma(rows),
            dma(chips),
            dma(chips),
            pltpu.VMEM((chips, row_count, width), bf16),
            pltpu.VMEM((chips + 1, row_count, width), bf16),
            pltpu.VMEM((row_count, width), f32),
            dma(2, chips),
            dma(2, chips),
        ],
        4,
    )
    outs = finish(
        (q_cols, kv_cols, ff_cols),
        (fin_attn, fin_mlp, fin_down, result_t, input_t, gain_sums),
        [
            ((width, row_count), bf16),
            ((width, row_count), bf16),
            ((width,), f32),
            ((width,), f32),
            ((in_rows, q_cols), f32),
            ((kv_cols, in_rows), f32),
            ((kv_cols, in_rows), f32),
            ((in_rows, out_cols), f32),
            ((ff_cols, in_rows), f32),
            ((ff_cols, in_rows), f32),
            ((down_cols, down_rows), f32),
        ],
    )
    flip = jnp.transpose
    return (
        flip(outs[0]).reshape(1, row_count, width),
        flip(outs[1]).reshape(1, row_count, width),
        outs[2],
        outs[3],
        outs[4],
        flip(outs[5]),
        flip(outs[6]),
        outs[7],
        flip(outs[8]),
        flip(outs[9]),
        flip(outs[10]),
    )


def solution(mesh):
    return jax.shard_map(
        on_device,
        mesh=mesh,
        in_specs=(
            P(("seq", "fsdp"), "ctx", None),
            P(("seq", "fsdp"), "ctx", None),
            P(),
            P(),
            P(),
            P(("seq", "fsdp"), "ctx"),
            P(("seq", "fsdp"), "ctx"),
            P(("seq", "fsdp"), "ctx"),
            P(("seq", "fsdp"), "ctx"),
            P(("seq", "fsdp"), "ctx"),
            P(("seq", "fsdp"), "ctx"),
            P(("seq", "fsdp"), "ctx"),
        ),
        out_specs=(
            P(("seq", "fsdp"), "ctx", None),
            P(("seq", "fsdp"), "ctx", None),
            P(),
            P(),
            P(("seq", "fsdp"), "ctx"),
            P(("seq", "fsdp"), "ctx"),
            P(("seq", "fsdp"), "ctx"),
            P(("seq", "fsdp"), "ctx"),
            P(("seq", "fsdp"), "ctx"),
            P(("seq", "fsdp"), "ctx"),
            P(("seq", "fsdp"), "ctx"),
        ),
        check_vma=False,
    )
```

```python
import functools
import math

import jax
import jax.numpy as jnp
from jax import lax
from jax.experimental import pallas as pl
from jax.experimental.pallas import tpu as pltpu
from jax.sharding import PartitionSpec as P

HEADS = 15
KV_HEADS = 5
HEAD_DIM = 64
GROUP = HEADS // KV_HEADS
HALF = HEAD_DIM // 2
MESH = pl.DeviceIdType.MESH
MASKED = -1e30
UNROLL = 4

rope_base = 100000.0
norm_eps = 1e-05
bf16 = jnp.bfloat16
f32 = jnp.float32


def norm_forward(values, gain):
    inverse_rms = lax.rsqrt(jnp.mean(values * values, axis=1, keepdims=True) + norm_eps)
    scaled = values * inverse_rms
    return (inverse_rms, scaled, (scaled * gain).astype(bf16))


def norm_backward(grad_in, inverse_rms, scaled, gain):
    weighted = grad_in * gain
    back = inverse_rms * (weighted - scaled * jnp.mean(weighted * scaled, axis=1, keepdims=True))
    return (back, jnp.sum(grad_in * scaled, axis=0))


def dot_nn(left, right):
    return jnp.dot(left, right, preferred_element_type=f32)


def dot_nt(left, right):
    return lax.dot_general(left, right, (((1,), (1,)), ((), ())), preferred_element_type=f32)


def dot_tn(left, right):
    return lax.dot_general(left, right, (((0,), (0,)), ((), ())), preferred_element_type=f32)


def wrap(index, count):
    return lax.rem(index + count, count)


class Place:
    def __init__(self, sizes):
        self.rows_outer, self.rows_inner, self.ctx = sizes
        self.row_parts = self.rows_outer * self.rows_inner
        self.chips = self.ctx // 2
        self.seq, self.fsdp, self.c = (lax.axis_index(n) for n in ("seq", "fsdp", "ctx"))
        self.row = self.seq * self.rows_inner + self.fsdp
        self.chip = self.c // 2
        self.core = self.c % 2

    def sibling(self):
        return (self.seq, self.fsdp, self.chip * 2 + 1 - self.core)

    def along(self, step):
        return (self.seq, self.fsdp, wrap(self.chip + step, self.chips) * 2 + self.core)

    def any_ctx(self, step):
        return (self.seq, self.fsdp, wrap(self.c + step, self.ctx))

    def across(self, step):
        row = wrap(self.row + step, self.row_parts)
        return (row // self.rows_inner, row % self.rows_inner, self.c)

    def chip_at(self, step):
        return wrap(self.chip + step, self.chips)

    def row_at(self, step):
        return wrap(self.row + step, self.row_parts)

    def greet(self, ctx=False, line=False, sibling=False, rows=False):
        devices = []
        if ctx:
            devices += [self.any_ctx(t) for t in range(1, self.ctx)]
        if line:
            devices += [self.along(t) for t in range(1, self.chips)]
        if sibling:
            devices += [self.sibling()]
        if rows:
            devices += [self.across(t) for t in range(1, self.row_parts)]
        barrier = pltpu.get_barrier_semaphore()
        for device in devices:
            pl.semaphore_signal(barrier, inc=1, device_id=device, device_id_type=MESH)
        pl.semaphore_wait(barrier, len(devices))


def remote(src, dst, send, recv, device):
    return pltpu.make_async_remote_copy(
        src_ref=src, dst_ref=dst, send_sem=send, recv_sem=recv, device_id=device, device_id_type=MESH
    )


def dma(*shape):
    return pltpu.SemaphoreType.DMA(shape)


class LineGather:
    def __init__(self, place, ref, out, sems):
        self.p, self.ref, self.out = place, ref, out
        self.zs, self.zr, self.bs, self.br = sems

    @staticmethod
    def scratch(sizes):
        chips = sizes[2] // 2
        return [dma(2, chips), dma(2, chips), dma(2, chips), dma(2, chips)]

    def source(self, way, d):
        return self.p.chip - d if way == 0 else self.p.chip + d

    def has(self, way, d):
        return self.p.chip >= d if way == 0 else self.p.chip + d < self.p.chips

    def onward(self, way):
        return self.p.chip + 1 < self.p.chips if way == 0 else self.p.chip >= 1

    def slot(self, way, d, core):
        return self.out.at[self.source(way, d) * 2 + core]

    def hop(self, way, d, own=False):
        mine = self.slot(way, d, self.p.core)
        src = self.ref if own else mine
        return remote(src, mine, self.zs.at[way, d], self.zr.at[way, d], self.p.along(1 - 2 * way))

    def landed(self, way, d):
        mine = self.slot(way, d, self.p.core)
        return remote(mine, mine, self.zs.at[way, d - 1], self.zr.at[way, d - 1], self.p.along(1 - 2 * way))

    def to_sibling(self, way, d, own=False):
        mine = self.slot(way, d, self.p.core)
        src = self.ref if own else mine
        return remote(src, mine, self.bs.at[way, d], self.br.at[way, d], self.p.sibling())

    def from_sibling(self, way, d):
        mine = self.slot(way, d, 1 - self.p.core)
        return remote(mine, mine, self.bs.at[way, d], self.br.at[way, d], self.p.sibling())

    def start(self):
        for way in range(2):
            pl.when(self.onward(way))(lambda way=way: self.hop(way, 0, True).start())
        self.to_sibling(0, 0, True).start()
        self.out[self.p.c] = self.ref[...]

    def forward_way(self, way, d):
        self.landed(way, d).wait_recv()
        pl.when(self.onward(way))(lambda: self.hop(way, d).start())
        self.to_sibling(way, d).start()

    def forward(self, d):
        for way in range(2):
            pl.when(self.has(way, d))(lambda way=way: self.forward_way(way, d))

    def arrive(self):
        self.from_sibling(0, 0).wait_recv()
        for d in range(1, self.p.chips):
            for way in range(2):
                pl.when(self.has(way, d))(lambda way=way, d=d: self.from_sibling(way, d).wait_recv())

    def finish(self):
        self.to_sibling(0, 0, True).wait_send()
        for d in range(self.p.chips):
            for way in range(2):

                @pl.when(self.has(way, d))
                def _(way=way, d=d):
                    pl.when(self.onward(way))(lambda: self.hop(way, d, d == 0).wait_send())
                    if d:
                        self.to_sibling(way, d).wait_send()


class FullGather:
    def __init__(self, place, ref, out, sems):
        self.p, self.ref, self.out = place, ref, out
        self.zs, self.zr = sems[:2]
        self.row_sems = sems[2:8]
        self.bs, self.br = sems[8:10]
        rows = ref.shape[0]
        self.half = (rows // 2 + 15) // 16 * 16
        self.parts = (pl.ds(0, self.half), pl.ds(self.half, rows - self.half))
        self.tags = [(0, 0)] + [(way, d) for d in range(1, place.chips) for way in range(2)]

    @staticmethod
    def scratch(sizes):
        chips = sizes[2] // 2
        count, outer, inner = 2 * chips - 1, sizes[0], sizes[1]
        line = [dma(2, chips)] * 2
        direct = [dma(count, 2, max(outer, inner))] * 2
        bent = [dma(count, 2, outer, inner)] * 2
        spare = [dma(1)] * 2
        return line + direct + bent + spare + [dma(count, outer, inner)] * 2

    def source(self, way, d):
        return self.p.chip - d if way == 0 else self.p.chip + d

    def has(self, way, d):
        return self.p.chip >= d if way == 0 else self.p.chip + d < self.p.chips

    def onward(self, way):
        return self.p.chip + 1 < self.p.chips if way == 0 else self.p.chip >= 1

    def when_has(self, tag, action):
        if tag[1] == 0:
            action()
        else:
            pl.when(self.has(*tag))(action)

    def row(self, a, b):
        seq = wrap(self.p.seq - a, self.p.rows_outer)
        return seq * self.p.rows_inner + wrap(self.p.fsdp - b, self.p.rows_inner)

    def slot(self, tag, core, a=0, b=0):
        return self.out.at[self.source(*tag) * 2 + core, self.row(a, b)]

    def device(self, a, b):
        return (wrap(self.p.seq + a, self.p.rows_outer), wrap(self.p.fsdp + b, self.p.rows_inner), self.p.c)

    def hop(self, way, d):
        mine = self.slot((way, d), self.p.core)
        src = self.ref if d == 0 else mine
        return remote(src, mine, self.zs.at[way, d], self.zr.at[way, d], self.p.along(1 - 2 * way))

    def landed(self, way, d):
        mine = self.slot((way, d), self.p.core)
        return remote(mine, mine, self.zs.at[way, d - 1], self.zr.at[way, d - 1], self.p.along(1 - 2 * way))

    def direct(self, tag, a, b):
        q, axis = self.tags.index(tag), 0 if a else 1
        mine = self.slot(tag, self.p.core)
        src = self.ref if tag[1] == 0 else mine
        sems = [sem.at[q, axis, a + b] for sem in self.row_sems[:2]]
        return remote(src, mine, *sems, self.device(a, b))

    def direct_in(self, tag, a, b):
        q, axis = self.tags.index(tag), 0 if a else 1
        mine = self.slot(tag, self.p.core, a, b)
        sems = [sem.at[q, axis, a + b] for sem in self.row_sems[:2]]
        return remote(mine, mine, *sems, self.device(a, b))

    def bent(self, tag, part, a, b):
        q = self.tags.index(tag)
        mine = (self.slot(tag, self.p.core, a, 0) if part == 0 else self.slot(tag, self.p.core, 0, b)).at[self.parts[part]]
        sems = [sem.at[q, part, a, b] for sem in self.row_sems[2:4]]
        return remote(mine, mine, *sems, self.device(0, b) if part == 0 else self.device(a, 0))

    def bent_in(self, tag, part, a, b):
        q = self.tags.index(tag)
        mine = self.slot(tag, self.p.core, a, b).at[self.parts[part]]
        sems = [sem.at[q, part, a, b] for sem in self.row_sems[2:4]]
        return remote(mine, mine, *sems, self.device(0, b))

    def to_sibling(self, tag, a, b):
        q = self.tags.index(tag)
        mine = self.slot(tag, self.p.core, a, b)
        src = self.ref if (tag[1] == 0 and a == 0 and b == 0) else mine
        return remote(src, mine, self.bs.at[q, a, b], self.br.at[q, a, b], self.p.sibling())

    def from_sibling(self, tag, a, b):
        q = self.tags.index(tag)
        mine = self.slot(tag, 1 - self.p.core, a, b)
        return remote(mine, mine, self.bs.at[q, a, b], self.br.at[q, a, b], self.p.sibling())

    def steps(self):
        outer = [(a, 0) for a in range(1, self.p.rows_outer)]
        inner = [(0, b) for b in range(1, self.p.rows_inner)]
        diagonal = [(a, b) for a in range(1, self.p.rows_outer) for b in range(1, self.p.rows_inner)]
        return outer, inner, diagonal

    def send_rows(self, tag):
        outer, inner, _ = self.steps()
        for a, b in outer + inner:
            self.direct(tag, a, b).start()
        self.to_sibling(tag, 0, 0).start()

    def start(self, rows=True):
        for way in range(2):
            pl.when(self.onward(way))(lambda way=way: self.hop(way, 0).start())
        if rows:
            self.send_rows((0, 0))
        self.out[self.p.c, self.p.row] = self.ref[...]

    def forward(self, d, rows=True):
        for way in range(2):

            @pl.when(self.has(way, d))
            def _(way=way):
                self.landed(way, d).wait_recv()
                pl.when(self.onward(way))(lambda: self.hop(way, d).start())
                if rows:
                    self.send_rows((way, d))

    def cross(self):
        for tag in self.tags:
            self.when_has(tag, lambda tag=tag: self.send_rows(tag))

    def bend(self, d):
        outer, inner, _ = self.steps()
        for tag in [(0, 0)] if d == 0 else [(0, d), (1, d)]:

            def action(tag=tag):
                for a, b in outer:
                    self.direct_in(tag, a, b).wait_recv()
                    for _, other in inner:
                        self.bent(tag, 0, a, other).start()
                    self.to_sibling(tag, a, b).start()
                for a, b in inner:
                    self.direct_in(tag, a, b).wait_recv()
                    for other, _ in outer:
                        self.bent(tag, 1, other, b).start()
                    self.to_sibling(tag, a, b).start()

            self.when_has(tag, action)

    def settle(self, d):
        for tag in [(0, 0)] if d == 0 else [(0, d), (1, d)]:

            def action(tag=tag):
                for a, b in self.steps()[2]:
                    for part in range(2):
                        self.bent_in(tag, part, a, b).wait_recv()
                    self.to_sibling(tag, a, b).start()

            self.when_has(tag, action)

    def every(self):
        return [(a, b) for a in range(self.p.rows_outer) for b in range(self.p.rows_inner)]

    def arrive(self):
        for tag in self.tags:

            def action(tag=tag):
                for a, b in self.every():
                    self.from_sibling(tag, a, b).wait_recv()

            self.when_has(tag, action)

    def finish(self):
        outer, inner, diagonal = self.steps()
        for tag in self.tags:

            def action(tag=tag):
                for way in range(2) if tag[1] == 0 else (tag[0],):
                    pl.when(self.onward(way))(lambda way=way: self.hop(way, tag[1]).wait_send())
                for a, b in outer + inner:
                    self.direct(tag, a, b).wait_send()
                for a, b in diagonal:
                    for part in range(2):
                        self.bent(tag, part, a, b).wait_send()
                for a, b in self.every():
                    self.to_sibling(tag, a, b).wait_send()

            self.when_has(tag, action)


class RowExchange:
    def __init__(self, place, src_of, dst_of, sems):
        self.p, self.src_of, self.dst_of = place, src_of, dst_of
        self.xs, self.xr = sems

    @staticmethod
    def scratch(sizes):
        rows = sizes[0] * sizes[1]
        return [dma(rows), dma(rows)]

    def send(self, k):
        return remote(self.src_of(k), self.dst_of(k, 0), self.xs.at[k], self.xr.at[k], self.p.across(k))

    def recv(self, k):
        mine = self.dst_of(k, k)
        return remote(mine, mine, self.xs.at[k], self.xr.at[k], self.p.across(k))

    def start(self):
        for k in range(1, self.p.row_parts):
            self.send(k).start()

    def arrive(self):
        for k in range(1, self.p.row_parts):
            self.recv(k).wait_recv()

    def finish(self):
        for k in range(1, self.p.row_parts):
            self.send(k).wait_send()


class CtxExchange:
    def __init__(self, place, src_of, dst_of, sems):
        self.p, self.src_of, self.dst_of = place, src_of, dst_of
        self.ss, self.sr = sems

    @staticmethod
    def scratch(sizes):
        return [dma(sizes[2]), dma(sizes[2])]

    def send(self, t):
        return remote(
            self.src_of(wrap(self.p.c + t, self.p.ctx)),
            self.dst_of(self.p.c),
            self.ss.at[t],
            self.sr.at[t],
            self.p.any_ctx(t),
        )

    def recv(self, t):
        mine = self.dst_of(wrap(self.p.c - t, self.p.ctx))
        return remote(mine, mine, self.ss.at[t], self.sr.at[t], self.p.any_ctx(t))

    def start(self):
        for t in range(1, self.p.ctx):
            self.send(t).start()

    def arrive(self):
        for t in range(1, self.p.ctx):
            self.recv(t).wait_recv()

    def finish(self):
        for t in range(1, self.p.ctx):
            self.send(t).wait_send()


def take(refs, count):
    return [next(refs) for _ in range(count)]


def rotate_rows(rows, cosine, sine):
    first, second = rows[:HALF], rows[HALF:]
    return jnp.concatenate([first * cosine - second * sine, second * cosine + first * sine], axis=0)


def rotate_rows_back(rows, cosine, sine):
    first, second = rows[:HALF], rows[HALF:]
    return jnp.concatenate([first * cosine + second * sine, second * cosine - first * sine], axis=0)


def group_rows(ref, g):
    return jnp.concatenate(
        [ref[pl.ds((g * GROUP + j) * HEAD_DIM, HEAD_DIM), :] for j in range(GROUP)], axis=1
    )


def turn(values):
    return values.astype(f32).T.astype(values.dtype)


def first_kernel(sizes, *refs):
    refs = iter(refs)
    (x_in, gain_ref, gain2_ref, wq_in, wk_in, wv_in, wo_in, wg_in, wu_in, wd_in, cot_in) = take(refs, 11)
    (cos_ref, sin_ref, posk_ref, posq_ref) = take(refs, 4)
    (attn_ref, q_ref, kv_out, lse_ref, wqkv_out, wo_out, wm_full, wd_turned, cot_full) = take(refs, 9)
    (n1_turned, mid_ref, n2_ref) = take(refs, 3)
    (qkv_raw, kv_own, wd_rows, score_ref, wd_full, mid_turned, wd_wide) = take(refs, 7)
    (x_turned, wq_ref, wk_turned, wv_turned, wo_ref, wg_turned, wu_turned, wd_in_ref, cot_turned) = take(refs, 9)
    (wqkv_ref, wm_ref, wd_ref, cot_ref, load_sems) = take(refs, 5)
    qkv_sems, wo_sems = take(refs, 10), take(refs, 10)
    kv_sems, cot_sems = take(refs, 4), take(refs, 4)
    wm_sems, wd_sems, a2a_sems = take(refs, 2), take(refs, 2), take(refs, 2)
    kv_ref, wqkv_full, wo_full, store_sems = take(refs, 4)

    place = Place(sizes)
    ctx, chips, row_parts = place.ctx, place.chips, place.row_parts
    width, tokens = x_turned.shape
    q_cols = HEADS * HEAD_DIM // ctx
    kv_cols = KV_HEADS * HEAD_DIM // ctx
    q_width, kv_width = HEADS * HEAD_DIM, KV_HEADS * HEAD_DIM
    qkv_cols = q_cols + 2 * kv_cols
    ff_part = wd_full.shape[1]
    per_row = ctx // row_parts

    qkv = FullGather(place, wqkv_ref, wqkv_full, qkv_sems)
    out = FullGather(place, wo_ref, wo_full, wo_sems)
    kv = LineGather(place, kv_own, kv_ref, kv_sems)
    cot = LineGather(place, cot_ref, cot_full, cot_sems)
    mlp = RowExchange(place, lambda k: wm_ref, lambda k, back: wm_full.at[place.row_at(-back)], wm_sems)
    down = RowExchange(place, lambda k: wd_ref, lambda k, back: wd_rows.at[place.row_at(-back)], wd_sems)

    def down_slice(c):
        return wd_rows.at[c // per_row, pl.ds(pl.multiple_of((c % per_row) * ff_part, 16), ff_part), :]

    spread = CtxExchange(place, down_slice, lambda c: wd_full.at[c], a2a_sems)

    loads = [
        pltpu.make_async_copy(src, dst, load_sems.at[i])
        for i, (src, dst) in enumerate(
            [
                (wq_in, wq_ref),
                (wk_in, wk_turned),
                (wv_in, wv_turned),
                (x_in, x_turned),
                (cot_in, cot_turned),
                (wo_in, wo_ref),
                (wg_in, wg_turned),
                (wu_in, wu_turned),
                (wd_in, wd_in_ref),
            ]
        )
    ]
    stores = [
        pltpu.make_async_copy(src, dst, store_sems.at[i])
        for i, (src, dst) in enumerate([(wqkv_full, wqkv_out), (kv_ref, kv_out), (wo_full, wo_out)])
    ]
    for load in loads:
        load.start()
    for load in loads[:3]:
        load.wait()
    wqkv_ref[...] = jnp.concatenate([wq_ref[...], turn(wk_turned[...]), turn(wv_turned[...])], axis=1)
    place.greet(ctx=True, rows=True)
    qkv.start()
    for load in loads[3:]:
        load.wait()
    out.start(rows=False)
    normed = norm_forward(x_turned[...].astype(f32).T, gain_ref[...])[2]
    n1_turned[...] = turn(normed)
    cot_ref[...] = turn(cot_turned[...])
    for step in range(1, chips):
        qkv.forward(step)
        if step == 1:
            qkv.bend(0)
    for step in range(1, chips):
        out.forward(step, rows=False)
    cot.start()
    wd_ref[...] = turn(wd_in_ref[...])
    wd_rows[place.row] = wd_ref[...]
    wm_ref[...] = jnp.concatenate([turn(wg_turned[...]), turn(wu_turned[...])], axis=1)
    for step in range(1, chips):
        qkv.bend(step)
        qkv.settle(step - 1)
        if step == chips // 2:
            cot.forward(1)
    wm_full[place.row] = wm_ref[...]
    qkv.settle(chips - 1)
    down.start()
    for step in range(2, chips):
        cot.forward(step)
    qkv.arrive()
    stores[0].start()

    for c in range(ctx):
        part = dot_nn(normed, wqkv_full[c].reshape(width, qkv_cols)).T
        qkv_raw[pl.ds(c * q_cols, q_cols), :] = part[:q_cols]
        qkv_raw[pl.ds(q_width + c * kv_cols, kv_cols), :] = part[q_cols : q_cols + kv_cols]
        qkv_raw[pl.ds(q_width + kv_width + c * kv_cols, kv_cols), :] = part[q_cols + kv_cols :]
    cosine, sine = cos_ref[...], sin_ref[...]
    for g in range(KV_HEADS):
        key = rotate_rows(qkv_raw[pl.ds(q_width + g * HEAD_DIM, HEAD_DIM), :], cosine, sine)
        value = qkv_raw[pl.ds(q_width + kv_width + g * HEAD_DIM, HEAD_DIM), :]
        pair = jnp.concatenate([key, value], axis=0).T
        kv_own[:, pl.ds(g * 2 * HEAD_DIM, 2 * HEAD_DIM)] = pair.astype(bf16)
    kv.start()
    out.cross()
    mlp.start()
    for h in range(HEADS):
        q_ref[pl.ds(h * HEAD_DIM, HEAD_DIM), :] = rotate_rows(
            qkv_raw[pl.ds(h * HEAD_DIM, HEAD_DIM), :], cosine, sine
        ).astype(bf16)
    for step in range(1, chips):
        kv.forward(step)
    down.arrive()
    spread.start()
    wd_full[place.c] = down_slice(place.c)[...]
    kv.arrive()
    stores[1].start()

    scale = 1.0 / math.sqrt(HEAD_DIM)
    query_pos = posq_ref[...]
    chunk = 2 * tokens
    wide = GROUP * tokens
    for g in range(KV_HEADS):
        lanes = pl.ds(g * 2 * HEAD_DIM, 2 * HEAD_DIM)
        query = group_rows(q_ref, g) * jnp.asarray(scale, bf16)
        query = jnp.concatenate([query, jnp.zeros_like(query)], axis=0)

        def score(i, total, lanes=lanes, query=query):
            keys = kv_ref[pl.ds(2 * i, 2), :, lanes].reshape(chunk, 2 * HEAD_DIM)
            rows = pl.ds(pl.multiple_of(i * chunk, chunk), chunk)
            scores = jnp.where(posk_ref[rows, :] <= query_pos, dot_nn(keys, query), MASKED)
            score_ref[rows, :] = scores
            return total + jnp.sum(jnp.exp(scores), axis=0, keepdims=True)

        log_total = jnp.log(lax.fori_loop(0, chips, score, jnp.zeros((1, wide), f32), unroll=UNROLL))
        lse_ref[g] = log_total

        def gather_values(i, total, lanes=lanes, log_total=log_total):
            keys = kv_ref[pl.ds(2 * i, 2), :, lanes].reshape(chunk, 2 * HEAD_DIM)
            rows = pl.ds(pl.multiple_of(i * chunk, chunk), chunk)
            prob = jnp.exp(score_ref[rows, :] - log_total).astype(bf16)
            return total + dot_tn(keys, prob)

        total = lax.fori_loop(
            0, chips, gather_values, jnp.zeros((2 * HEAD_DIM, wide), f32), unroll=UNROLL
        )
        for j in range(GROUP):
            attn_ref[pl.ds((g * GROUP + j) * HEAD_DIM, HEAD_DIM), :] = total[
                HEAD_DIM:, j * tokens : (j + 1) * tokens
            ].astype(bf16)
        if g == 1:
            for step in range(chips):
                out.bend(step)
        if g == 3:
            for step in range(chips):
                out.settle(step)
    out.arrive()
    stores[2].start()
    out_cols = wo_ref.shape[1]
    attn = attn_ref[...]
    for c in range(ctx):
        rows = pl.ds(c * out_cols, out_cols)
        mid_turned[rows, :] = dot_tn(wo_full[c].reshape(q_width, out_cols), attn)
    middle = (x_turned[...].astype(f32) + mid_turned[...]).T
    mid_ref[...] = middle
    n2_ref[...] = norm_forward(middle, gain2_ref[...])[2]
    cot.arrive()
    mlp.arrive()
    spread.arrive()
    down_cols = wd_ref.shape[1]
    for c in range(ctx):
        wd_wide[pl.ds(c * down_cols, down_cols), :] = wd_full[c].astype(f32).T
    wd_turned[...] = wd_wide[...].astype(bf16)
    for store in stores:
        store.wait()
    for part in (qkv, kv, out, mlp, down, cot, spread):
        part.finish()


def mlp_kernel(sizes, *refs):
    refs = iter(refs)
    n_ref, cot_ref, wm_ref, wd_ref = take(refs, 4)
    ngrad_ref, osums_ref, dwm_ref, dwd_ref = take(refs, 4)
    n_all, gub_all, hid_all, part_ref, sib_ref, far_ref, wide_ref = take(refs, 7)
    n_sems = take(refs, 4)
    bs, br, zs, zr = take(refs, 4)

    place = Place(sizes)
    ctx, chips = place.ctx, place.chips
    tokens, width = n_ref.shape
    ff = wd_ref.shape[1]
    chunk = 2 * tokens
    gather = LineGather(place, n_ref, n_all, n_sems)

    place.greet(line=True, sibling=True)
    gather.start()

    def work(p):
        rows = pl.ds(pl.multiple_of(p * chunk, chunk), chunk)
        normed = n_all[pl.ds(2 * p, 2)].reshape(chunk, width)
        cot = cot_ref[pl.ds(2 * p, 2)].reshape(chunk, width)
        gate_up = dot_nn(normed, wm_ref[...])
        gate, up = gate_up[:, :ff], gate_up[:, ff:]
        sigmoid_gate = jax.nn.sigmoid(gate)
        silu_gate = gate * sigmoid_gate
        hidden = (silu_gate * up).astype(bf16)
        hidden_grad = dot_nn(cot, wd_ref[...])
        gate_back = hidden_grad * up * sigmoid_gate * (1.0 + gate * (1.0 - sigmoid_gate))
        up_back = hidden_grad * silu_gate
        both = jnp.concatenate([gate_back, up_back], axis=1).astype(bf16)
        gub_all[rows, :] = both
        hid_all[rows, :] = hidden
        part_ref[p, :, 0] = dot_nt(both, wm_ref[...]).astype(bf16).reshape(2, tokens, width)
        part_ref[p, :, 1] = dot_nt(hidden, wd_ref[...]).astype(bf16).reshape(2, tokens, width)
        to_sibling(p).start()

    def to_sibling(p):
        return remote(part_ref.at[p, 1 - place.core], sib_ref.at[p], bs.at[p], br.at[p], place.sibling())

    def settle(p):
        to_sibling(p).wait_recv()
        both = (part_ref[p, place.core].astype(f32) + sib_ref[p].astype(f32)).astype(bf16)
        part_ref[p, place.core, 0] = both[0]
        osums_ref[p] = both[1]

    def target(way, d):
        return place.chip + d if way == 0 else place.chip - d

    def exists(way, d):
        return place.chip + d < chips if way == 0 else place.chip >= d

    def upstream(way):
        return place.chip >= 1 if way == 0 else place.chip + 1 < chips

    def landing(way, d):
        return target(way, d) if (way == 0 or d) else chips

    piece_rows = tokens // 2 // 16 * 16
    pieces = (pl.ds(0, piece_rows), pl.ds(piece_rows, tokens - piece_rows))

    def onward(way, d, n):
        p = target(way, d)
        slot = p if (way == 0 or d > 1) else chips
        return remote(
            part_ref.at[p, place.core, 0, pieces[n]],
            far_ref.at[slot, pieces[n]],
            zs.at[way, d, n],
            zr.at[way, d, n],
            place.along(1 - 2 * way),
        )

    def inward(way, d, n):
        mine = far_ref.at[landing(way, d), pieces[n]]
        return remote(mine, mine, zs.at[way, d + 1, n], zr.at[way, d + 1, n], place.along(1 - 2 * way))

    gather.from_sibling(0, 0).wait_recv()
    work(place.chip)
    for d in range(1, chips):
        gather.forward(d)
        for way in range(2):
            @pl.when(exists(way, d))
            def _(way=way, d=d):
                gather.from_sibling(1 - way, d).wait_recv()
                work(target(way, d))

        if d == 1:
            settle(place.chip)
        for way in range(2):

            @pl.when(exists(way, d))
            def _(way=way, d=d):
                settle(target(way, d))

                @pl.when(jnp.logical_not(upstream(way)))
                def _():
                    for n in range(2):
                        onward(way, d, n).start()

    seq = ctx * tokens
    dwm_ref[...] = dot_tn(n_all[...].reshape(seq, width), gub_all[...]).astype(bf16).reshape(dwm_ref.shape)
    down_cols = dwd_ref.shape[2]
    wide_ref[...] = dot_tn(cot_ref[...].reshape(seq, width), hid_all[...])
    for c in range(ctx):
        dwd_ref[c] = wide_ref[pl.ds(c * down_cols, down_cols), :].T.astype(bf16)

    for d in range(chips - 1, 0, -1):
        for way in range(2):

            @pl.when(jnp.logical_and(exists(way, d), upstream(way)))
            def _(way=way, d=d):
                p = target(way, d)
                for n, rows in enumerate(pieces):
                    inward(way, d, n).wait_recv()
                    both = part_ref[p, place.core, 0, rows].astype(f32) + far_ref[p, rows].astype(f32)
                    part_ref[p, place.core, 0, rows] = both.astype(bf16)
                    onward(way, d, n).start()

    ngrad_ref[...] = part_ref[place.chip, place.core, 0].astype(f32)
    for way in range(2):

        @pl.when(upstream(way))
        def _(way=way):
            for n in range(2):
                inward(way, 0, n).wait_recv()
            ngrad_ref[...] += far_ref[landing(way, 0)].astype(f32)

    gather.finish()
    for p in range(chips):
        to_sibling(p).wait_send()
    for d in range(1, chips):
        for way in range(2):

            @pl.when(exists(way, d))
            def _(way=way, d=d):
                for n in range(2):
                    onward(way, d, n).wait_send()


def back_kernel(sizes, *refs):
    refs = iter(refs)
    (q_ref, attn_ref, kv_in, lse_ref, cos_ref, sin_ref, posk_ref, posq_ref, dwm_ref, dwd_ref) = take(refs, 10)
    ngrad_ref, mid_ref, gain_ref, cot_ref, wo_in = take(refs, 5)
    qkvb_ref, fin_mlp, fin_down, mgrad_ref, midb_ref, gain_part = take(refs, 6)
    g_ref, mid_turned, q_back, kv_back = take(refs, 4)
    delta_ref, qz_ref, gz_ref, acc_ref, part_ref, sib_ref, far_ref = take(refs, 7)
    dwm_recv, down_rows, down_recv = take(refs, 3)
    bs, br, zs, zr = take(refs, 4)
    wm_sems, a2a_sems, wd_sems = take(refs, 2), take(refs, 2), take(refs, 2)
    kv_ref, wo_ref, load_sems = take(refs, 3)
    load_out = pltpu.make_async_copy(wo_in, wo_ref, load_sems.at[0])
    load_kv = pltpu.make_async_copy(kv_in, kv_ref, load_sems.at[1])
    load_out.start()
    load_kv.start()

    place = Place(sizes)
    ctx, chips, row_parts = place.ctx, place.chips, place.row_parts
    tokens = q_ref.shape[1]
    chunk, wide = 2 * tokens, GROUP * tokens
    ff_part = dwd_ref.shape[1]
    per_row = ctx // row_parts
    scale = 1.0 / math.sqrt(HEAD_DIM)

    mlp = RowExchange(place, lambda k: dwm_ref.at[place.row_at(k)], lambda k, back: dwm_recv.at[k], wm_sems)

    def down_slot(c):
        return down_rows.at[c // per_row, pl.ds(pl.multiple_of((c % per_row) * ff_part, 16), ff_part), :]

    spread = CtxExchange(place, lambda c: dwd_ref.at[c], down_slot, a2a_sems)
    down = RowExchange(place, lambda k: down_rows.at[place.row_at(k)], lambda k, back: down_recv.at[k], wd_sems)

    place.greet(ctx=True, rows=True)
    mlp.start()
    spread.start()
    down_slot(place.c)[...] = dwd_ref[place.c]

    inverse_rms, unit, _ = norm_forward(mid_ref[...], gain_ref[...])
    mlp_back, gain_part[0] = norm_backward(ngrad_ref[...], inverse_rms, unit, gain_ref[...])
    mid_grad = cot_ref[...].astype(f32).T + mlp_back
    mgrad_ref[...] = mid_grad
    mid_turned[...] = mid_grad.T
    out_cols = wo_ref.shape[3]
    load_out.wait()
    load_kv.wait()
    total = jnp.zeros(g_ref.shape, f32)
    for c in range(ctx):
        piece = mid_turned[pl.ds(c * out_cols, out_cols), :].astype(bf16)
        midb_ref[c] = piece
        total = total + dot_nn(wo_ref[c].reshape(g_ref.shape[0], out_cols), piece)
    g_ref[...] = total.astype(bf16)

    zeros = jnp.zeros((HEAD_DIM, wide), bf16)
    for g in range(KV_HEADS):
        query = group_rows(q_ref, g) * jnp.asarray(scale, bf16)
        grad = group_rows(g_ref, g)
        qz_ref[g] = jnp.concatenate([query, zeros], axis=0)
        gz_ref[g] = jnp.concatenate([zeros, grad], axis=0)
        delta_ref[g] = jnp.sum(grad.astype(f32) * group_rows(attn_ref, g).astype(f32), axis=0, keepdims=True)
        acc_ref[g] = jnp.zeros_like(acc_ref[g])
    query_pos = posq_ref[...]

    def to_sibling(j):
        return remote(part_ref.at[j, 1 - place.core], sib_ref.at[j], bs.at[j], br.at[j], place.sibling())

    def to_owner(j):
        return remote(part_ref.at[j, place.core], far_ref.at[j], zs.at[j], zr.at[j], place.along(j))

    def settle(j):
        to_sibling(j).wait_recv()
        both = part_ref[j, place.core].astype(f32) + sib_ref[j].astype(f32)
        part_ref[j, place.core] = both.astype(bf16)

    def work(j):
        p = place.chip_at(j)
        rows = pl.ds(pl.multiple_of(p * chunk, chunk), chunk)
        allowed = posk_ref[rows, :] <= query_pos
        for g in range(KV_HEADS):
            lanes = pl.ds(g * 2 * HEAD_DIM, 2 * HEAD_DIM)
            keys = kv_ref[pl.ds(2 * p, 2), :, lanes].reshape(chunk, 2 * HEAD_DIM)
            query, grad = qz_ref[g], gz_ref[g]
            scores = jnp.where(allowed, dot_nn(keys, query), MASKED)
            prob = jnp.exp(scores - lse_ref[g])
            score_grad = (prob * (dot_nn(keys, grad) - delta_ref[g])).astype(bf16)
            both = dot_nt(score_grad, query) + dot_nt(prob.astype(bf16), grad)
            part_ref[j, :, :, lanes] = both.astype(bf16).reshape(2, tokens, 2 * HEAD_DIM)
            acc_ref[g] += dot_tn(keys, score_grad)
        to_sibling(j).start()

    work(1)

    def turn(j, carry):
        work(j)
        settle(j - 1)
        to_owner(j - 1).start()
        return carry

    lax.fori_loop(2, chips, turn, 0)
    spread.arrive()
    down.start()
    work(0)
    settle(chips - 1)
    to_owner(chips - 1).start()
    cosine, sine = cos_ref[...], sin_ref[...]
    for h in range(HEADS):
        g, j = h // GROUP, h % GROUP
        head = acc_ref[g, pl.ds(0, HEAD_DIM), pl.ds(j * tokens, tokens)] * scale
        q_back[pl.ds(h * HEAD_DIM, HEAD_DIM), :] = rotate_rows_back(head, cosine, sine)
    settle(0)
    mlp.arrive()
    total = dwm_ref[place.row].astype(f32)
    for k in range(1, row_parts):
        total = total + dwm_recv[k].astype(f32)
    fin_mlp[...] = total
    down.arrive()
    total = down_rows[place.row].astype(f32)
    for k in range(1, row_parts):
        total = total + down_recv[k].astype(f32)
    fin_down[...] = total
    total = part_ref[0, place.core].astype(f32)
    for j in range(1, chips):
        to_owner(j).wait_recv()
        total = total + far_ref[j].astype(f32)
    total = total.T
    kv_width = KV_HEADS * HEAD_DIM
    for g in range(KV_HEADS):
        pair = total[g * 2 * HEAD_DIM : (g + 1) * 2 * HEAD_DIM]
        rows = pl.ds(g * HEAD_DIM, HEAD_DIM)
        kv_back[rows, :] = rotate_rows_back(pair[:HEAD_DIM], cosine, sine)
        kv_back[pl.ds(kv_width + g * HEAD_DIM, HEAD_DIM), :] = pair[HEAD_DIM:]
    q_cols, kv_cols = q_back.shape[0] // ctx, kv_width // ctx
    for c in range(ctx):
        qkvb_ref[c] = jnp.concatenate(
            [
                q_back[pl.ds(c * q_cols, q_cols), :],
                kv_back[pl.ds(c * kv_cols, kv_cols), :],
                kv_back[pl.ds(kv_width + c * kv_cols, kv_cols), :],
            ],
            axis=0,
        ).astype(bf16)
    for part in (mlp, spread, down):
        part.finish()
    for j in range(chips):
        to_sibling(j).wait_send()
        if j:
            to_owner(j).wait_send()


def last_kernel(sizes, *refs):
    refs = iter(refs)
    n1_ref, qkvb_ref, attn_ref, midb_ref, osums_ref, mid_ref = take(refs, 6)
    x_ref, gain_ref, gain_part, mgrad_ref, wqkv_in = take(refs, 5)
    fin_ref, gain_out, result_ref, input_ref = take(refs, 4)
    part_ref, sib_ref, bent_ref, row_ref, far_send, far_ref = take(refs, 6)
    gain_sib, gain_row, gain_far, gain_a, gain_b, gain_c = take(refs, 6)
    bs, br, vs, vr, xs, xr, zs, zr = take(refs, 8)
    gb, gx, gz = take(refs, 2), take(refs, 2), take(refs, 2)
    osum_own, osum_far, mid_sum, os, orr = take(refs, 5)
    wqkv_ref, load_sems = take(refs, 2)
    load = pltpu.make_async_copy(wqkv_in, wqkv_ref, load_sems.at[0])
    load.start()

    place = Place(sizes)
    chips, row_parts, outer, inner = place.chips, place.row_parts, place.rows_outer, place.rows_inner
    core, row, chip = place.core, place.row, place.chip
    in_rows = fin_ref.shape[0]
    half = (in_rows // 2 + 15) // 16 * 16
    parts = (pl.ds(0, half), pl.ds(half, in_rows - half))
    sized = (pl.ds(0, half), pl.ds(0, in_rows - half))
    sides = [(a, 0) for a in range(1, outer)] + [(0, b) for b in range(1, inner)]
    diagonal = [(a, b) for a in range(1, outer) for b in range(1, inner)]
    place.greet(line=True, sibling=True, rows=True)

    def row_of(a, b):
        return wrap(place.seq + a, outer) * inner + wrap(place.fsdp + b, inner)

    def device(a, b):
        return (wrap(place.seq + a, outer), wrap(place.fsdp + b, inner), place.c)

    def to_sibling(j):
        return remote(
            part_ref.at[place.chip_at(j) * 2 + 1 - core], sib_ref.at[j], bs.at[j], br.at[j], place.sibling()
        )

    def bent(j, part, n):
        a, b = diagonal[n]
        return remote(
            sib_ref.at[j, row_of(a, b), parts[part]],
            bent_ref.at[j, part, n, sized[part]],
            vs.at[j, part, n],
            vr.at[j, part, n],
            device(0, b) if part == 0 else device(a, 0),
        )

    def direct(j, n):
        a, b = sides[n]
        return remote(sib_ref.at[j, row_of(a, b)], row_ref.at[j, n], xs.at[j, n], xr.at[j, n], device(a, b))

    def to_owner(j):
        return remote(far_send.at[j], far_ref.at[j], zs.at[j], zr.at[j], place.along(j))

    def g_sib():
        return remote(gain_a, gain_sib.at[core], gb[0].at[0], gb[1].at[0], place.sibling())

    def g_row(k):
        return remote(gain_b, gain_row.at[row], gx[0].at[k], gx[1].at[k], place.across(k))

    def g_far(j):
        return remote(gain_c, gain_far.at[chip], gz[0].at[j], gz[1].at[j], place.along(j))

    def input_gradient():
        width = x_ref.shape[0]
        load.wait()
        total = jnp.zeros(x_ref.shape, f32)
        for c in range(place.ctx):
            total = total + dot_nn(wqkv_ref[c].reshape(width, wqkv_ref.shape[3]), qkvb_ref[c])
        inverse_rms, unit, _ = norm_forward(x_ref[...].astype(f32).T, gain_ref[...])
        back, gain_a[0] = norm_backward(total.T, inverse_rms, unit, gain_ref[...])
        input_ref[...] = (mgrad_ref[...] + back).T.astype(bf16)
        gain_a[1] = gain_part[0]
        gain_sib[core] = gain_a[...]
        g_sib().start()

    def multiply(j):
        for k in range(2):
            c = place.chip_at(j) * 2 + k
            both = jnp.concatenate(
                [dot_nt(n1_ref[...], qkvb_ref[c]), dot_nt(attn_ref[...], midb_ref[c])], axis=1
            )
            part_ref[c] = both.astype(bf16).reshape(part_ref.shape[1:])
        to_sibling(j).start()

    def add_sibling(j):
        to_sibling(j).wait_recv()
        both = part_ref[place.chip_at(j) * 2 + core].astype(f32) + sib_ref[j].astype(f32)
        sib_ref[j] = both.astype(bf16)
        for n in range(len(diagonal)):
            for part in range(2):
                bent(j, part, n).start()

    def add_bent(j):
        for n, (a, b) in enumerate(diagonal):
            for part in range(2):
                bent(j, part, n).wait_recv()
                at = (j, row_of(a, 0) if part == 0 else row_of(0, b), parts[part])
                both = sib_ref[at].astype(f32) + bent_ref[j, part, n, sized[part]].astype(f32)
                sib_ref[at] = both.astype(bf16)
        for n in range(len(sides)):
            direct(j, n).start()

    def add_rows(j):
        total = sib_ref[j, row].astype(f32)
        for n in range(len(sides)):
            direct(j, n).wait_recv()
            total = total + row_ref[j, n].astype(f32)
        if j:
            far_send[j] = total.astype(bf16)
            to_owner(j).start()
        else:
            fin_ref[...] = total

    def target(way, d):
        return chip + d if way == 0 else chip - d

    def exists(way, d):
        return chip + d < chips if way == 0 else chip >= d

    def upstream(way):
        return chip >= 1 if way == 0 else chip + 1 < chips

    def output_on(way, d):
        p = target(way, d)
        slot = p if (way == 0 or d > 1) else chips
        return remote(osum_own.at[p], osum_far.at[slot], os.at[way, d], orr.at[way, d], place.along(1 - 2 * way))

    def output_in(way, d):
        mine = osum_far.at[target(way, d) if (way == 0 or d) else chips]
        return remote(mine, mine, os.at[way, d + 1], orr.at[way, d + 1], place.along(1 - 2 * way))

    osum_own[...] = osums_ref[...]
    for d in range(chips - 1, 0, -1):
        for way in range(2):

            @pl.when(jnp.logical_and(exists(way, d), jnp.logical_not(upstream(way))))
            def _(way=way, d=d):
                output_on(way, d).start()

    def output_turn(d):
        for way in range(2):

            @pl.when(jnp.logical_and(exists(way, d), upstream(way)))
            def _(way=way):
                p = target(way, d)
                output_in(way, d).wait_recv()
                osum_own[p] = (osum_own[p].astype(f32) + osum_far[p].astype(f32)).astype(bf16)
                output_on(way, d).start()

    order = list(range(1, chips)) + [0]
    stages = (multiply, add_sibling, add_bent, add_rows)
    for t in range(chips + len(stages) - 1):
        for depth, stage in enumerate(stages):
            if 0 <= t - depth < chips:
                stage(order[t - depth])
        if t == 1:
            input_gradient()
        if 1 <= chips - 1 - t < chips - 1:
            output_turn(chips - 1 - t)
        if t == 3:
            remote(gain_a, gain_sib.at[1 - core], gb[0].at[0], gb[1].at[0], place.sibling()).wait_recv()
            gain_b[...] = gain_sib[0] + gain_sib[1]
            gain_row[row] = gain_b[...]
            for k in range(1, row_parts):
                g_row(k).start()

    for k in range(1, row_parts):
        remote(gain_b, gain_row.at[place.row_at(-k)], gx[0].at[k], gx[1].at[k], place.across(k)).wait_recv()
    total = gain_row[0]
    for k in range(1, row_parts):
        total = total + gain_row[k]
    gain_c[...] = total
    gain_far[chip] = gain_c[...]
    for j in range(1, chips):
        g_far(j).start()
    mid_sum[...] = mid_ref[...] + osum_own[chip].astype(f32)
    for way in range(2):

        @pl.when(upstream(way))
        def _(way=way):
            output_in(way, 0).wait_recv()
            mid_sum[...] += osum_far[chip if way == 0 else chips].astype(f32)

    result_ref[...] = mid_sum[...].T.astype(bf16)
    total = fin_ref[...]
    for j in range(1, chips):
        to_owner(j).wait_recv()
        total = total + far_ref[j].astype(f32)
    fin_ref[...] = total
    for j in range(1, chips):
        remote(gain_c, gain_far.at[place.chip_at(-j)], gz[0].at[j], gz[1].at[j], place.along(j)).wait_recv()
    total = gain_far[0]
    for j in range(1, chips):
        total = total + gain_far[j]
    gain_out[...] = total

    g_sib().wait_send()
    for k in range(1, row_parts):
        g_row(k).wait_send()
    for j in range(1, chips):
        g_far(j).wait_send()
    for j in order:
        to_sibling(j).wait_send()
        for n in range(len(diagonal)):
            for part in range(2):
                bent(j, part, n).wait_send()
        for n in range(len(sides)):
            direct(j, n).wait_send()
        if j:
            to_owner(j).wait_send()
    for d in range(1, chips):
        for way in range(2):

            @pl.when(exists(way, d))
            def _(way=way, d=d):
                output_on(way, d).wait_send()


def finish_kernel(cuts, *refs):
    refs = iter(refs)
    attn_ref, mlp_ref, down_ref, result_ref, input_ref, gain_ref = take(refs, 6)
    q_cols, kv_cols, ff_cols = cuts
    outs = take(refs, 11)
    attn, mlp = attn_ref[...], mlp_ref[...]
    outs[0][...] = result_ref[...]
    outs[1][...] = input_ref[...]
    outs[2][...] = gain_ref[0]
    outs[3][...] = gain_ref[1]
    outs[4][...] = attn[:, :q_cols]
    outs[5][...] = attn[:, q_cols : q_cols + kv_cols].T
    outs[6][...] = attn[:, q_cols + kv_cols : q_cols + 2 * kv_cols].T
    outs[7][...] = attn[:, q_cols + 2 * kv_cols :]
    outs[8][...] = mlp[:, :ff_cols].T
    outs[9][...] = mlp[:, ff_cols:].T
    outs[10][...] = down_ref[...].T


def finish(cuts, inputs, outs):
    vmem = pl.BlockSpec(memory_space=pltpu.VMEM)
    return pl.pallas_call(
        functools.partial(finish_kernel, cuts),
        out_shape=[jax.ShapeDtypeStruct(shape, kind) for shape, kind in outs],
        in_specs=[vmem] * len(inputs),
        out_specs=[vmem] * len(outs),
    )(*inputs)


def call(kernel, sizes, inputs, outs, scratch, collective_id, raw=(), raw_outs=()):
    vmem = pl.BlockSpec(memory_space=pltpu.VMEM)
    anywhere = pl.BlockSpec(memory_space=pl.ANY)
    return pl.pallas_call(
        functools.partial(kernel, sizes),
        out_shape=[jax.ShapeDtypeStruct(shape, kind) for shape, kind in outs],
        in_specs=[anywhere if i in raw else vmem for i in range(len(inputs))],
        out_specs=[anywhere if i in raw_outs else vmem for i in range(len(outs))],
        scratch_shapes=scratch,
        compiler_params=pltpu.CompilerParams(
            collective_id=collective_id, has_side_effects=True, vmem_limit_bytes=60 * 1024 * 1024
        ),
    )(*inputs)


def on_device(
    tokens,
    cotangent,
    block_order,
    gain_attn,
    gain_mlp,
    w_query,
    w_key,
    w_value,
    w_out,
    w_gate,
    w_up,
    w_down,
):
    sizes = tuple(lax.axis_size(n) for n in ("seq", "fsdp", "ctx"))
    rows, ctx = sizes[0] * sizes[1], sizes[2]
    chips = ctx // 2
    row_count, width = tokens.shape[1], tokens.shape[2]
    seq_len = row_count * ctx
    block_total = block_order.shape[0]
    block_len = seq_len // block_total
    kv_width = KV_HEADS * HEAD_DIM
    q_width = HEADS * HEAD_DIM
    q_cols, kv_cols, ff_cols = w_query.shape[1], w_key.shape[1], w_gate.shape[1]
    out_cols, down_cols, down_rows = w_out.shape[1], w_down.shape[1], w_down.shape[0]
    in_rows = w_query.shape[0]
    qkv_cols = q_cols + 2 * kv_cols
    wide = GROUP * row_count

    slot_index = jnp.arange(seq_len, dtype=jnp.int32)
    owner_hit = (slot_index // block_len)[:, None] == jnp.arange(block_total, dtype=jnp.int32)[None, :]
    all_pos = (
        jnp.sum(jnp.where(owner_hit, block_order[None, :], 0), axis=1) * block_len + slot_index % block_len
    )
    own_pos = lax.dynamic_slice_in_dim(all_pos, lax.axis_index("ctx") * row_count, row_count)
    inverse = rope_base ** (-jnp.arange(HALF, dtype=f32) / HALF)
    angles = inverse[:, None] * own_pos.astype(f32)[None, :]
    cosine, sine = jnp.cos(angles), jnp.sin(angles)
    pos_keys = all_pos[:, None]
    pos_query = jnp.tile(own_pos, GROUP)[None, :]

    x = tokens[0]
    cot_rows = cotangent[0]
    turned = [jnp.transpose(w) for w in (w_key, w_value, w_gate, w_up, w_down)]
    wk_t, wv_t, wg_t, wu_t, wd_t = turned

    (
        attn_t,
        query_t,
        kv_all,
        lse,
        qkv_full,
        out_full,
        mlp_full,
        down_t,
        cot_all,
        normed_attn_t,
        middle,
        normed_mlp,
    ) = call(
        first_kernel,
        sizes,
        (
            jnp.transpose(x),
            gain_attn[None],
            gain_mlp[None],
            w_query,
            wk_t,
            wv_t,
            w_out,
            wg_t,
            wu_t,
            wd_t,
            jnp.transpose(cot_rows),
            cosine,
            sine,
            pos_keys,
            pos_query,
        ),
        [
            ((q_width, row_count), bf16),
            ((q_width, row_count), bf16),
            ((ctx, row_count, 2 * kv_width), bf16),
            ((KV_HEADS, 1, wide), f32),
            ((ctx, rows, in_rows, qkv_cols), bf16),
            ((ctx, rows, in_rows, out_cols), bf16),
            ((rows, in_rows, 2 * ff_cols), bf16),
            ((width, ff_cols), bf16),
            ((ctx, row_count, width), bf16),
            ((width, row_count), bf16),
            ((row_count, width), f32),
            ((row_count, width), bf16),
        ],
        [
            pltpu.VMEM((q_width + 2 * kv_width, row_count), f32),
            pltpu.VMEM((row_count, 2 * kv_width), bf16),
            pltpu.VMEM((rows, down_rows, down_cols), bf16),
            pltpu.VMEM((seq_len, wide), f32),
            pltpu.VMEM((ctx, ff_cols, down_cols), bf16),
            pltpu.VMEM((width, row_count), f32),
            pltpu.VMEM((width, ff_cols), f32),
            pltpu.VMEM((width, row_count), bf16),
        ]
        + [pltpu.VMEM(w.shape, bf16) for w in (w_query, wk_t, wv_t, w_out, wg_t, wu_t, wd_t)]
        + [
            pltpu.VMEM((width, row_count), bf16),
            pltpu.VMEM((in_rows, qkv_cols), bf16),
            pltpu.VMEM((in_rows, 2 * ff_cols), bf16),
            pltpu.VMEM(w_down.shape, bf16),
            pltpu.VMEM((row_count, width), bf16),
            dma(9),
        ]
        + FullGather.scratch(sizes)
        + FullGather.scratch(sizes)
        + LineGather.scratch(sizes)
        + LineGather.scratch(sizes)
        + RowExchange.scratch(sizes)
        + RowExchange.scratch(sizes)
        + CtxExchange.scratch(sizes)
        + [
            pltpu.VMEM((ctx, row_count, 2 * kv_width), bf16),
            pltpu.VMEM((ctx, rows, in_rows, qkv_cols), bf16),
            pltpu.VMEM((ctx, rows, in_rows, out_cols), bf16),
            dma(3),
        ],
        1,
        raw=(0, 3, 4, 5, 6, 7, 8, 9, 10),
        raw_outs=(2, 4, 5),
    )

    w_mlp_cat = mlp_full.reshape(width, 2 * ff_cols)

    normed_mlp_grad, output_sums, d_mlp, d_down = call(
        mlp_kernel,
        sizes,
        (normed_mlp, cot_all, w_mlp_cat, down_t),
        [
            ((row_count, width), f32),
            ((chips, row_count, width), bf16),
            ((rows, in_rows, 2 * ff_cols), bf16),
            ((ctx, ff_cols, down_cols), bf16),
        ],
        [
            pltpu.VMEM((ctx, row_count, width), bf16),
            pltpu.VMEM((seq_len, 2 * ff_cols), bf16),
            pltpu.VMEM((seq_len, ff_cols), bf16),
            pltpu.VMEM((chips, 2, 2, row_count, width), bf16),
            pltpu.VMEM((chips, 2, row_count, width), bf16),
            pltpu.VMEM((chips + 1, row_count, width), bf16),
            pltpu.VMEM((width, ff_cols), f32),
        ]
        + LineGather.scratch(sizes)
        + [dma(chips)] * 2
        + [dma(2, chips, 2)] * 2,
        2,
    )
    qkv_back_t, fin_mlp, fin_down, mid_grad, mid_back_t, gain_mlp_part = call(
        back_kernel,
        sizes,
        (
            query_t,
            attn_t,
            kv_all,
            lse,
            cosine,
            sine,
            pos_keys,
            pos_query,
            d_mlp,
            d_down,
            normed_mlp_grad,
            middle,
            gain_mlp[None],
            jnp.transpose(cot_rows),
            out_full,
        ),
        [
            ((ctx, qkv_cols, row_count), bf16),
            ((in_rows, 2 * ff_cols), f32),
            ((down_rows, down_cols), f32),
            ((row_count, width), f32),
            ((ctx, out_cols, row_count), bf16),
            ((1, width), f32),
        ],
        [
            pltpu.VMEM((q_width, row_count), bf16),
            pltpu.VMEM((width, row_count), f32),
            pltpu.VMEM((q_width, row_count), f32),
            pltpu.VMEM((2 * kv_width, row_count), f32),
            pltpu.VMEM((KV_HEADS, 1, wide), f32),
            pltpu.VMEM((KV_HEADS, 2 * HEAD_DIM, wide), bf16),
            pltpu.VMEM((KV_HEADS, 2 * HEAD_DIM, wide), bf16),
            pltpu.VMEM((KV_HEADS, 2 * HEAD_DIM, wide), f32),
            pltpu.VMEM((chips, 2, row_count, 2 * kv_width), bf16),
            pltpu.VMEM((chips, row_count, 2 * kv_width), bf16),
            pltpu.VMEM((chips, row_count, 2 * kv_width), bf16),
            pltpu.VMEM((rows, in_rows, 2 * ff_cols), bf16),
            pltpu.VMEM((rows, down_rows, down_cols), bf16),
            pltpu.VMEM((rows, down_rows, down_cols), bf16),
        ]
        + [dma(chips)] * 4
        + RowExchange.scratch(sizes)
        + CtxExchange.scratch(sizes)
        + RowExchange.scratch(sizes)
        + [
            pltpu.VMEM((ctx, row_count, 2 * kv_width), bf16),
            pltpu.VMEM((ctx, rows, in_rows, out_cols), bf16),
            dma(2),
        ],
        3,
        raw=(2, 14),
    )

    attn_cols = qkv_cols + out_cols
    gains = pltpu.VMEM((2, width), f32)
    half = (in_rows // 2 + 15) // 16 * 16
    corners, sides = (sizes[0] - 1) * (sizes[1] - 1), sizes[0] + sizes[1] - 2
    fin_attn, gain_sums, result_t, input_t = call(
        last_kernel,
        sizes,
        (
            normed_attn_t,
            qkv_back_t,
            attn_t,
            mid_back_t,
            output_sums,
            middle,
            jnp.transpose(x),
            gain_attn[None],
            gain_mlp_part,
            mid_grad,
            qkv_full,
        ),
        [
            ((in_rows, attn_cols), f32),
            ((2, width), f32),
            ((width, row_count), bf16),
            ((width, row_count), bf16),
        ],
        [
            pltpu.VMEM((ctx, rows, in_rows, attn_cols), bf16),
            pltpu.VMEM((chips, rows, in_rows, attn_cols), bf16),
            pltpu.VMEM((chips, 2, corners, half, attn_cols), bf16),
            pltpu.VMEM((chips, sides, in_rows, attn_cols), bf16),
            pltpu.VMEM((chips, in_rows, attn_cols), bf16),
            pltpu.VMEM((chips, in_rows, attn_cols), bf16),
            pltpu.VMEM((2, 2, width), f32),
            pltpu.VMEM((rows, 2, width), f32),
            pltpu.VMEM((chips, 2, width), f32),
            gains,
            gains,
            gains,
            dma(chips),
            dma(chips),
            dma(chips, 2, corners),
            dma(chips, 2, corners),
            dma(chips, sides),
            dma(chips, sides),
            dma(chips),
            dma(chips),
            dma(1),
            dma(1),
            dma(rows),
            dma(rows),
            dma(chips),
            dma(chips),
            pltpu.VMEM((chips, row_count, width), bf16),
            pltpu.VMEM((chips + 1, row_count, width), bf16),
            pltpu.VMEM((row_count, width), f32),
            dma(2, chips),
            dma(2, chips),
            pltpu.VMEM((ctx, rows, in_rows, qkv_cols), bf16),
            dma(1),
        ],
        4,
        raw=(10,),
    )
    outs = finish(
        (q_cols, kv_cols, ff_cols),
        (fin_attn, fin_mlp, fin_down, result_t, input_t, gain_sums),
        [
            ((width, row_count), bf16),
            ((width, row_count), bf16),
            ((width,), f32),
            ((width,), f32),
            ((in_rows, q_cols), f32),
            ((kv_cols, in_rows), f32),
            ((kv_cols, in_rows), f32),
            ((in_rows, out_cols), f32),
            ((ff_cols, in_rows), f32),
            ((ff_cols, in_rows), f32),
            ((down_cols, down_rows), f32),
        ],
    )
    flip = jnp.transpose
    return (
        flip(outs[0]).reshape(1, row_count, width),
        flip(outs[1]).reshape(1, row_count, width),
        outs[2],
        outs[3],
        outs[4],
        flip(outs[5]),
        flip(outs[6]),
        outs[7],
        flip(outs[8]),
        flip(outs[9]),
        flip(outs[10]),
    )


def solution(mesh):
    return jax.shard_map(
        on_device,
        mesh=mesh,
        in_specs=(
            P(("seq", "fsdp"), "ctx", None),
            P(("seq", "fsdp"), "ctx", None),
            P(),
            P(),
            P(),
            P(("seq", "fsdp"), "ctx"),
            P(("seq", "fsdp"), "ctx"),
            P(("seq", "fsdp"), "ctx"),
            P(("seq", "fsdp"), "ctx"),
            P(("seq", "fsdp"), "ctx"),
            P(("seq", "fsdp"), "ctx"),
            P(("seq", "fsdp"), "ctx"),
        ),
        out_specs=(
            P(("seq", "fsdp"), "ctx", None),
            P(("seq", "fsdp"), "ctx", None),
            P(),
            P(),
            P(("seq", "fsdp"), "ctx"),
            P(("seq", "fsdp"), "ctx"),
            P(("seq", "fsdp"), "ctx"),
            P(("seq", "fsdp"), "ctx"),
            P(("seq", "fsdp"), "ctx"),
            P(("seq", "fsdp"), "ctx"),
            P(("seq", "fsdp"), "ctx"),
        ),
        check_vma=False,
    )
```

```python
import functools
import math

import jax
import jax.numpy as jnp
from jax import lax
from jax.experimental import pallas as pl
from jax.experimental.pallas import tpu as pltpu
from jax.sharding import PartitionSpec as P

HEADS = 15
KV_HEADS = 5
HEAD_DIM = 64
GROUP = HEADS // KV_HEADS
HALF = HEAD_DIM // 2
MESH = pl.DeviceIdType.MESH
MASKED = -1e30
UNROLL = 4

rope_base = 100000.0
norm_eps = 1e-05
bf16 = jnp.bfloat16
f32 = jnp.float32


def norm_forward(values, gain):
    inverse_rms = lax.rsqrt(jnp.mean(values * values, axis=1, keepdims=True) + norm_eps)
    scaled = values * inverse_rms
    return (inverse_rms, scaled, (scaled * gain).astype(bf16))


def norm_backward(grad_in, inverse_rms, scaled, gain):
    weighted = grad_in * gain
    back = inverse_rms * (weighted - scaled * jnp.mean(weighted * scaled, axis=1, keepdims=True))
    return (back, jnp.sum(grad_in * scaled, axis=0))


def dot_nn(left, right):
    return jnp.dot(left, right, preferred_element_type=f32)


def dot_nt(left, right):
    return lax.dot_general(left, right, (((1,), (1,)), ((), ())), preferred_element_type=f32)


def dot_tn(left, right):
    return lax.dot_general(left, right, (((0,), (0,)), ((), ())), preferred_element_type=f32)


def wrap(index, count):
    return lax.rem(index + count, count)


class Place:
    def __init__(self, sizes):
        self.rows_outer, self.rows_inner, self.ctx = sizes
        self.row_parts = self.rows_outer * self.rows_inner
        self.chips = self.ctx // 2
        self.seq, self.fsdp, self.c = (lax.axis_index(n) for n in ("seq", "fsdp", "ctx"))
        self.row = self.seq * self.rows_inner + self.fsdp
        self.chip = self.c // 2
        self.core = self.c % 2

    def sibling(self):
        return (self.seq, self.fsdp, self.chip * 2 + 1 - self.core)

    def along(self, step):
        return (self.seq, self.fsdp, wrap(self.chip + step, self.chips) * 2 + self.core)

    def any_ctx(self, step):
        return (self.seq, self.fsdp, wrap(self.c + step, self.ctx))

    def across(self, step):
        row = wrap(self.row + step, self.row_parts)
        return (row // self.rows_inner, row % self.rows_inner, self.c)

    def chip_at(self, step):
        return wrap(self.chip + step, self.chips)

    def row_at(self, step):
        return wrap(self.row + step, self.row_parts)

    def greet(self, ctx=False, line=False, sibling=False, rows=False):
        devices = []
        if ctx:
            devices += [self.any_ctx(t) for t in range(1, self.ctx)]
        if line:
            devices += [self.along(t) for t in range(1, self.chips)]
        if sibling:
            devices += [self.sibling()]
        if rows:
            devices += [self.across(t) for t in range(1, self.row_parts)]
        barrier = pltpu.get_barrier_semaphore()
        for device in devices:
            pl.semaphore_signal(barrier, inc=1, device_id=device, device_id_type=MESH)
        pl.semaphore_wait(barrier, len(devices))


def remote(src, dst, send, recv, device):
    return pltpu.make_async_remote_copy(
        src_ref=src, dst_ref=dst, send_sem=send, recv_sem=recv, device_id=device, device_id_type=MESH
    )


def dma(*shape):
    return pltpu.SemaphoreType.DMA(shape)


class LineGather:
    def __init__(self, place, ref, out, sems):
        self.p, self.ref, self.out = place, ref, out
        self.zs, self.zr, self.bs, self.br = sems

    @staticmethod
    def scratch(sizes):
        chips = sizes[2] // 2
        return [dma(2, chips), dma(2, chips), dma(2, chips), dma(2, chips)]

    def source(self, way, d):
        return self.p.chip - d if way == 0 else self.p.chip + d

    def has(self, way, d):
        return self.p.chip >= d if way == 0 else self.p.chip + d < self.p.chips

    def onward(self, way):
        return self.p.chip + 1 < self.p.chips if way == 0 else self.p.chip >= 1

    def slot(self, way, d, core):
        return self.out.at[self.source(way, d) * 2 + core]

    def hop(self, way, d, own=False):
        mine = self.slot(way, d, self.p.core)
        src = self.ref if own else mine
        return remote(src, mine, self.zs.at[way, d], self.zr.at[way, d], self.p.along(1 - 2 * way))

    def landed(self, way, d):
        mine = self.slot(way, d, self.p.core)
        return remote(mine, mine, self.zs.at[way, d - 1], self.zr.at[way, d - 1], self.p.along(1 - 2 * way))

    def to_sibling(self, way, d, own=False):
        mine = self.slot(way, d, self.p.core)
        src = self.ref if own else mine
        return remote(src, mine, self.bs.at[way, d], self.br.at[way, d], self.p.sibling())

    def from_sibling(self, way, d):
        mine = self.slot(way, d, 1 - self.p.core)
        return remote(mine, mine, self.bs.at[way, d], self.br.at[way, d], self.p.sibling())

    def start(self):
        for way in range(2):
            pl.when(self.onward(way))(lambda way=way: self.hop(way, 0, True).start())
        self.to_sibling(0, 0, True).start()
        self.out[self.p.c] = self.ref[...]

    def forward_way(self, way, d):
        self.landed(way, d).wait_recv()
        pl.when(self.onward(way))(lambda: self.hop(way, d).start())
        self.to_sibling(way, d).start()

    def forward(self, d):
        for way in range(2):
            pl.when(self.has(way, d))(lambda way=way: self.forward_way(way, d))

    def arrive(self):
        self.from_sibling(0, 0).wait_recv()
        for d in range(1, self.p.chips):
            for way in range(2):
                pl.when(self.has(way, d))(lambda way=way, d=d: self.from_sibling(way, d).wait_recv())

    def finish(self):
        self.to_sibling(0, 0, True).wait_send()
        for d in range(self.p.chips):
            for way in range(2):

                @pl.when(self.has(way, d))
                def _(way=way, d=d):
                    pl.when(self.onward(way))(lambda: self.hop(way, d, d == 0).wait_send())
                    if d:
                        self.to_sibling(way, d).wait_send()


class FullGather:
    def __init__(self, place, ref, out, sems):
        self.p, self.ref, self.out = place, ref, out
        self.zs, self.zr = sems[:2]
        self.row_sems = sems[2:8]
        self.bs, self.br = sems[8:10]
        rows = ref.shape[0]
        self.half = (rows // 2 + 15) // 16 * 16
        self.parts = (pl.ds(0, self.half), pl.ds(self.half, rows - self.half))
        self.tags = [(0, 0)] + [(way, d) for d in range(1, place.chips) for way in range(2)]

    @staticmethod
    def scratch(sizes):
        chips = sizes[2] // 2
        count, outer, inner = 2 * chips - 1, sizes[0], sizes[1]
        line = [dma(2, chips)] * 2
        direct = [dma(count, 2, max(outer, inner))] * 2
        bent = [dma(count, 2, outer, inner)] * 2
        spare = [dma(1)] * 2
        return line + direct + bent + spare + [dma(count, outer, inner)] * 2

    def source(self, way, d):
        return self.p.chip - d if way == 0 else self.p.chip + d

    def has(self, way, d):
        return self.p.chip >= d if way == 0 else self.p.chip + d < self.p.chips

    def onward(self, way):
        return self.p.chip + 1 < self.p.chips if way == 0 else self.p.chip >= 1

    def when_has(self, tag, action):
        if tag[1] == 0:
            action()
        else:
            pl.when(self.has(*tag))(action)

    def row(self, a, b):
        seq = wrap(self.p.seq - a, self.p.rows_outer)
        return seq * self.p.rows_inner + wrap(self.p.fsdp - b, self.p.rows_inner)

    def slot(self, tag, core, a=0, b=0):
        return self.out.at[self.source(*tag) * 2 + core, self.row(a, b)]

    def device(self, a, b):
        return (wrap(self.p.seq + a, self.p.rows_outer), wrap(self.p.fsdp + b, self.p.rows_inner), self.p.c)

    def hop(self, way, d):
        mine = self.slot((way, d), self.p.core)
        src = self.ref if d == 0 else mine
        return remote(src, mine, self.zs.at[way, d], self.zr.at[way, d], self.p.along(1 - 2 * way))

    def landed(self, way, d):
        mine = self.slot((way, d), self.p.core)
        return remote(mine, mine, self.zs.at[way, d - 1], self.zr.at[way, d - 1], self.p.along(1 - 2 * way))

    def direct(self, tag, a, b):
        q, axis = self.tags.index(tag), 0 if a else 1
        mine = self.slot(tag, self.p.core)
        src = self.ref if tag[1] == 0 else mine
        sems = [sem.at[q, axis, a + b] for sem in self.row_sems[:2]]
        return remote(src, mine, *sems, self.device(a, b))

    def direct_in(self, tag, a, b):
        q, axis = self.tags.index(tag), 0 if a else 1
        mine = self.slot(tag, self.p.core, a, b)
        sems = [sem.at[q, axis, a + b] for sem in self.row_sems[:2]]
        return remote(mine, mine, *sems, self.device(a, b))

    def bent(self, tag, part, a, b):
        q = self.tags.index(tag)
        mine = (self.slot(tag, self.p.core, a, 0) if part == 0 else self.slot(tag, self.p.core, 0, b)).at[self.parts[part]]
        sems = [sem.at[q, part, a, b] for sem in self.row_sems[2:4]]
        return remote(mine, mine, *sems, self.device(0, b) if part == 0 else self.device(a, 0))

    def bent_in(self, tag, part, a, b):
        q = self.tags.index(tag)
        mine = self.slot(tag, self.p.core, a, b).at[self.parts[part]]
        sems = [sem.at[q, part, a, b] for sem in self.row_sems[2:4]]
        return remote(mine, mine, *sems, self.device(0, b))

    def to_sibling(self, tag, a, b):
        q = self.tags.index(tag)
        mine = self.slot(tag, self.p.core, a, b)
        src = self.ref if (tag[1] == 0 and a == 0 and b == 0) else mine
        return remote(src, mine, self.bs.at[q, a, b], self.br.at[q, a, b], self.p.sibling())

    def from_sibling(self, tag, a, b):
        q = self.tags.index(tag)
        mine = self.slot(tag, 1 - self.p.core, a, b)
        return remote(mine, mine, self.bs.at[q, a, b], self.br.at[q, a, b], self.p.sibling())

    def steps(self):
        outer = [(a, 0) for a in range(1, self.p.rows_outer)]
        inner = [(0, b) for b in range(1, self.p.rows_inner)]
        diagonal = [(a, b) for a in range(1, self.p.rows_outer) for b in range(1, self.p.rows_inner)]
        return outer, inner, diagonal

    def send_rows(self, tag):
        outer, inner, _ = self.steps()
        for a, b in outer + inner:
            self.direct(tag, a, b).start()
        self.to_sibling(tag, 0, 0).start()

    def start(self, rows=True):
        for way in range(2):
            pl.when(self.onward(way))(lambda way=way: self.hop(way, 0).start())
        if rows:
            self.send_rows((0, 0))
        self.out[self.p.c, self.p.row] = self.ref[...]

    def forward(self, d, rows=True):
        for way in range(2):

            @pl.when(self.has(way, d))
            def _(way=way):
                self.landed(way, d).wait_recv()
                pl.when(self.onward(way))(lambda: self.hop(way, d).start())
                if rows:
                    self.send_rows((way, d))

    def cross(self):
        for tag in self.tags:
            self.when_has(tag, lambda tag=tag: self.send_rows(tag))

    def bend(self, d):
        outer, inner, _ = self.steps()
        for tag in [(0, 0)] if d == 0 else [(0, d), (1, d)]:

            def action(tag=tag):
                for a, b in outer:
                    self.direct_in(tag, a, b).wait_recv()
                    for _, other in inner:
                        self.bent(tag, 0, a, other).start()
                    self.to_sibling(tag, a, b).start()
                for a, b in inner:
                    self.direct_in(tag, a, b).wait_recv()
                    for other, _ in outer:
                        self.bent(tag, 1, other, b).start()
                    self.to_sibling(tag, a, b).start()

            self.when_has(tag, action)

    def settle(self, d):
        for tag in [(0, 0)] if d == 0 else [(0, d), (1, d)]:

            def action(tag=tag):
                for a, b in self.steps()[2]:
                    for part in range(2):
                        self.bent_in(tag, part, a, b).wait_recv()
                    self.to_sibling(tag, a, b).start()

            self.when_has(tag, action)

    def every(self):
        return [(a, b) for a in range(self.p.rows_outer) for b in range(self.p.rows_inner)]

    def arrive(self):
        for tag in self.tags:

            def action(tag=tag):
                for a, b in self.every():
                    self.from_sibling(tag, a, b).wait_recv()

            self.when_has(tag, action)

    def finish(self):
        outer, inner, diagonal = self.steps()
        for tag in self.tags:

            def action(tag=tag):
                for way in range(2) if tag[1] == 0 else (tag[0],):
                    pl.when(self.onward(way))(lambda way=way: self.hop(way, tag[1]).wait_send())
                for a, b in outer + inner:
                    self.direct(tag, a, b).wait_send()
                for a, b in diagonal:
                    for part in range(2):
                        self.bent(tag, part, a, b).wait_send()
                for a, b in self.every():
                    self.to_sibling(tag, a, b).wait_send()

            self.when_has(tag, action)


class RowExchange:
    def __init__(self, place, src_of, dst_of, sems):
        self.p, self.src_of, self.dst_of = place, src_of, dst_of
        self.xs, self.xr = sems

    @staticmethod
    def scratch(sizes):
        rows = sizes[0] * sizes[1]
        return [dma(rows), dma(rows)]

    def send(self, k):
        return remote(self.src_of(k), self.dst_of(k, 0), self.xs.at[k], self.xr.at[k], self.p.across(k))

    def recv(self, k):
        mine = self.dst_of(k, k)
        return remote(mine, mine, self.xs.at[k], self.xr.at[k], self.p.across(k))

    def start(self):
        for k in range(1, self.p.row_parts):
            self.send(k).start()

    def arrive(self):
        for k in range(1, self.p.row_parts):
            self.recv(k).wait_recv()

    def finish(self):
        for k in range(1, self.p.row_parts):
            self.send(k).wait_send()


class CtxExchange:
    def __init__(self, place, src_of, dst_of, sems):
        self.p, self.src_of, self.dst_of = place, src_of, dst_of
        self.ss, self.sr = sems

    @staticmethod
    def scratch(sizes):
        return [dma(sizes[2]), dma(sizes[2])]

    def send(self, t):
        return remote(
            self.src_of(wrap(self.p.c + t, self.p.ctx)),
            self.dst_of(self.p.c),
            self.ss.at[t],
            self.sr.at[t],
            self.p.any_ctx(t),
        )

    def recv(self, t):
        mine = self.dst_of(wrap(self.p.c - t, self.p.ctx))
        return remote(mine, mine, self.ss.at[t], self.sr.at[t], self.p.any_ctx(t))

    def start(self):
        for t in range(1, self.p.ctx):
            self.send(t).start()

    def arrive(self):
        for t in range(1, self.p.ctx):
            self.recv(t).wait_recv()

    def finish(self):
        for t in range(1, self.p.ctx):
            self.send(t).wait_send()


def take(refs, count):
    return [next(refs) for _ in range(count)]


def rotate_rows(rows, cosine, sine):
    first, second = rows[:HALF], rows[HALF:]
    return jnp.concatenate([first * cosine - second * sine, second * cosine + first * sine], axis=0)


def rotate_rows_back(rows, cosine, sine):
    first, second = rows[:HALF], rows[HALF:]
    return jnp.concatenate([first * cosine + second * sine, second * cosine - first * sine], axis=0)


def group_rows(ref, g):
    return jnp.concatenate(
        [ref[pl.ds((g * GROUP + j) * HEAD_DIM, HEAD_DIM), :] for j in range(GROUP)], axis=1
    )


def turn(values):
    return values.astype(f32).T.astype(values.dtype)


def first_kernel(sizes, *refs):
    refs = iter(refs)
    (x_in, gain_ref, gain2_ref, wq_in, wk_in, wv_in, wo_in, wg_in, wu_in, wd_in, cot_in) = take(refs, 11)
    (cos_ref, sin_ref, posk_ref, posq_ref) = take(refs, 4)
    (attn_ref, q_ref, kv_out, lse_ref, wqkv_out, wo_out, wm_full, wd_turned, cot_out) = take(refs, 9)
    (n1_turned, mid_ref, n2_ref) = take(refs, 3)
    (qkv_raw, kv_own, wd_rows, score_ref, wd_full, mid_turned, wd_wide) = take(refs, 7)
    (x_turned, wq_ref, wk_turned, wv_turned, wo_ref, wg_turned, wu_turned, wd_in_ref, cot_turned) = take(refs, 9)
    (wqkv_ref, wm_ref, wd_ref, cot_ref, load_sems) = take(refs, 5)
    qkv_sems, wo_sems = take(refs, 10), take(refs, 10)
    kv_sems, cot_sems = take(refs, 4), take(refs, 4)
    wm_sems, wd_sems, a2a_sems = take(refs, 2), take(refs, 2), take(refs, 2)
    kv_ref, wqkv_full, wo_full, cot_full, store_sems = take(refs, 5)

    place = Place(sizes)
    ctx, chips, row_parts = place.ctx, place.chips, place.row_parts
    width, tokens = x_turned.shape
    q_cols = HEADS * HEAD_DIM // ctx
    kv_cols = KV_HEADS * HEAD_DIM // ctx
    q_width, kv_width = HEADS * HEAD_DIM, KV_HEADS * HEAD_DIM
    qkv_cols = q_cols + 2 * kv_cols
    ff_part = wd_full.shape[1]
    per_row = ctx // row_parts

    qkv = FullGather(place, wqkv_ref, wqkv_full, qkv_sems)
    out = FullGather(place, wo_ref, wo_full, wo_sems)
    kv = LineGather(place, kv_own, kv_ref, kv_sems)
    cot = LineGather(place, cot_ref, cot_full, cot_sems)
    mlp = RowExchange(place, lambda k: wm_ref, lambda k, back: wm_full.at[place.row_at(-back)], wm_sems)
    down = RowExchange(place, lambda k: wd_ref, lambda k, back: wd_rows.at[place.row_at(-back)], wd_sems)

    def down_slice(c):
        return wd_rows.at[c // per_row, pl.ds(pl.multiple_of((c % per_row) * ff_part, 16), ff_part), :]

    spread = CtxExchange(place, down_slice, lambda c: wd_full.at[c], a2a_sems)

    loads = [
        pltpu.make_async_copy(src, dst, load_sems.at[i])
        for i, (src, dst) in enumerate(
            [
                (wq_in, wq_ref),
                (wk_in, wk_turned),
                (wv_in, wv_turned),
                (x_in, x_turned),
                (cot_in, cot_turned),
                (wo_in, wo_ref),
                (wg_in, wg_turned),
                (wu_in, wu_turned),
                (wd_in, wd_in_ref),
            ]
        )
    ]
    stores = [
        pltpu.make_async_copy(src, dst, store_sems.at[i])
        for i, (src, dst) in enumerate([(wqkv_full, wqkv_out), (kv_ref, kv_out), (wo_full, wo_out), (cot_full, cot_out)])
    ]
    for load in loads:
        load.start()
    for load in loads[:3]:
        load.wait()
    wqkv_ref[...] = jnp.concatenate([wq_ref[...], turn(wk_turned[...]), turn(wv_turned[...])], axis=1)
    place.greet(ctx=True, rows=True)
    qkv.start()
    for load in loads[3:]:
        load.wait()
    out.start(rows=False)
    normed = norm_forward(x_turned[...].astype(f32).T, gain_ref[...])[2]
    n1_turned[...] = turn(normed)
    cot_ref[...] = turn(cot_turned[...])
    for step in range(1, chips):
        qkv.forward(step)
        if step == 1:
            qkv.bend(0)
    for step in range(1, chips):
        out.forward(step, rows=False)
    cot.start()
    wd_ref[...] = turn(wd_in_ref[...])
    wd_rows[place.row] = wd_ref[...]
    wm_ref[...] = jnp.concatenate([turn(wg_turned[...]), turn(wu_turned[...])], axis=1)
    for step in range(1, chips):
        qkv.bend(step)
        qkv.settle(step - 1)
        if step == chips // 2:
            cot.forward(1)
    wm_full[place.row] = wm_ref[...]
    qkv.settle(chips - 1)
    down.start()
    for step in range(2, chips):
        cot.forward(step)
    qkv.arrive()
    stores[0].start()

    for c in range(ctx):
        part = dot_nn(normed, wqkv_full[c].reshape(width, qkv_cols)).T
        qkv_raw[pl.ds(c * q_cols, q_cols), :] = part[:q_cols]
        qkv_raw[pl.ds(q_width + c * kv_cols, kv_cols), :] = part[q_cols : q_cols + kv_cols]
        qkv_raw[pl.ds(q_width + kv_width + c * kv_cols, kv_cols), :] = part[q_cols + kv_cols :]
    cosine, sine = cos_ref[...], sin_ref[...]
    for g in range(KV_HEADS):
        key = rotate_rows(qkv_raw[pl.ds(q_width + g * HEAD_DIM, HEAD_DIM), :], cosine, sine)
        value = qkv_raw[pl.ds(q_width + kv_width + g * HEAD_DIM, HEAD_DIM), :]
        pair = jnp.concatenate([key, value], axis=0).T
        kv_own[:, pl.ds(g * 2 * HEAD_DIM, 2 * HEAD_DIM)] = pair.astype(bf16)
    kv.start()
    out.cross()
    mlp.start()
    for h in range(HEADS):
        q_ref[pl.ds(h * HEAD_DIM, HEAD_DIM), :] = rotate_rows(
            qkv_raw[pl.ds(h * HEAD_DIM, HEAD_DIM), :], cosine, sine
        ).astype(bf16)
    for step in range(1, chips):
        kv.forward(step)
    down.arrive()
    spread.start()
    wd_full[place.c] = down_slice(place.c)[...]
    kv.arrive()
    stores[1].start()

    scale = 1.0 / math.sqrt(HEAD_DIM)
    query_pos = posq_ref[...]
    chunk = 2 * tokens
    wide = GROUP * tokens
    for g in range(KV_HEADS):
        lanes = pl.ds(g * 2 * HEAD_DIM, 2 * HEAD_DIM)
        query = group_rows(q_ref, g) * jnp.asarray(scale, bf16)
        query = jnp.concatenate([query, jnp.zeros_like(query)], axis=0)

        def score(i, total, lanes=lanes, query=query):
            keys = kv_ref[pl.ds(2 * i, 2), :, lanes].reshape(chunk, 2 * HEAD_DIM)
            rows = pl.ds(pl.multiple_of(i * chunk, chunk), chunk)
            scores = jnp.where(posk_ref[rows, :] <= query_pos, dot_nn(keys, query), MASKED)
            score_ref[rows, :] = scores
            return total + jnp.sum(jnp.exp(scores), axis=0, keepdims=True)

        log_total = jnp.log(lax.fori_loop(0, chips, score, jnp.zeros((1, wide), f32), unroll=UNROLL))
        lse_ref[g] = log_total

        def gather_values(i, total, lanes=lanes, log_total=log_total):
            keys = kv_ref[pl.ds(2 * i, 2), :, lanes].reshape(chunk, 2 * HEAD_DIM)
            rows = pl.ds(pl.multiple_of(i * chunk, chunk), chunk)
            prob = jnp.exp(score_ref[rows, :] - log_total).astype(bf16)
            return total + dot_tn(keys, prob)

        total = lax.fori_loop(
            0, chips, gather_values, jnp.zeros((2 * HEAD_DIM, wide), f32), unroll=UNROLL
        )
        for j in range(GROUP):
            attn_ref[pl.ds((g * GROUP + j) * HEAD_DIM, HEAD_DIM), :] = total[
                HEAD_DIM:, j * tokens : (j + 1) * tokens
            ].astype(bf16)
        if g == 1:
            for step in range(chips):
                out.bend(step)
        if g == 3:
            for step in range(chips):
                out.settle(step)
    out.arrive()
    stores[2].start()
    out_cols = wo_ref.shape[1]
    attn = attn_ref[...]
    for c in range(ctx):
        rows = pl.ds(c * out_cols, out_cols)
        mid_turned[rows, :] = dot_tn(wo_full[c].reshape(q_width, out_cols), attn)
    middle = (x_turned[...].astype(f32) + mid_turned[...]).T
    mid_ref[...] = middle
    n2_ref[...] = norm_forward(middle, gain2_ref[...])[2]
    cot.arrive()
    stores[3].start()
    mlp.arrive()
    spread.arrive()
    down_cols = wd_ref.shape[1]
    for c in range(ctx):
        wd_wide[pl.ds(c * down_cols, down_cols), :] = wd_full[c].astype(f32).T
    wd_turned[...] = wd_wide[...].astype(bf16)
    for store in stores:
        store.wait()
    for part in (qkv, kv, out, mlp, down, cot, spread):
        part.finish()


def mlp_kernel(sizes, *refs):
    refs = iter(refs)
    n_ref, cot_in, wm_in, wd_in = take(refs, 4)
    ngrad_ref, osums_ref, dwm_ref, dwd_ref = take(refs, 4)
    n_all, gub_all, hid_all, part_ref, sib_ref, far_ref, wide_ref = take(refs, 7)
    n_sems = take(refs, 4)
    bs, br, zs, zr = take(refs, 4)
    cot_ref, wm_ref, wd_ref, load_sems = take(refs, 4)
    loads = [
        pltpu.make_async_copy(src, dst, load_sems.at[i])
        for i, (src, dst) in enumerate([(wm_in, wm_ref), (wd_in, wd_ref), (cot_in, cot_ref)])
    ]
    for load in loads:
        load.start()

    place = Place(sizes)
    ctx, chips = place.ctx, place.chips
    tokens, width = n_ref.shape
    ff = wd_ref.shape[1]
    chunk = 2 * tokens
    gather = LineGather(place, n_ref, n_all, n_sems)

    place.greet(line=True, sibling=True)
    gather.start()

    def work(p):
        rows = pl.ds(pl.multiple_of(p * chunk, chunk), chunk)
        normed = n_all[pl.ds(2 * p, 2)].reshape(chunk, width)
        cot = cot_ref[pl.ds(2 * p, 2)].reshape(chunk, width)
        gate_up = dot_nn(normed, wm_ref[...])
        gate, up = gate_up[:, :ff], gate_up[:, ff:]
        sigmoid_gate = jax.nn.sigmoid(gate)
        silu_gate = gate * sigmoid_gate
        hidden = (silu_gate * up).astype(bf16)
        hidden_grad = dot_nn(cot, wd_ref[...])
        gate_back = hidden_grad * up * sigmoid_gate * (1.0 + gate * (1.0 - sigmoid_gate))
        up_back = hidden_grad * silu_gate
        both = jnp.concatenate([gate_back, up_back], axis=1).astype(bf16)
        gub_all[rows, :] = both
        hid_all[rows, :] = hidden
        part_ref[p, :, 0] = dot_nt(both, wm_ref[...]).astype(bf16).reshape(2, tokens, width)
        part_ref[p, :, 1] = dot_nt(hidden, wd_ref[...]).astype(bf16).reshape(2, tokens, width)
        to_sibling(p).start()

    def to_sibling(p):
        return remote(part_ref.at[p, 1 - place.core], sib_ref.at[p], bs.at[p], br.at[p], place.sibling())

    def settle(p):
        to_sibling(p).wait_recv()
        both = (part_ref[p, place.core].astype(f32) + sib_ref[p].astype(f32)).astype(bf16)
        part_ref[p, place.core, 0] = both[0]
        osums_ref[p] = both[1]

    def target(way, d):
        return place.chip + d if way == 0 else place.chip - d

    def exists(way, d):
        return place.chip + d < chips if way == 0 else place.chip >= d

    def upstream(way):
        return place.chip >= 1 if way == 0 else place.chip + 1 < chips

    def landing(way, d):
        return target(way, d) if (way == 0 or d) else chips

    piece_rows = tokens // 2 // 16 * 16
    pieces = (pl.ds(0, piece_rows), pl.ds(piece_rows, tokens - piece_rows))

    def onward(way, d, n):
        p = target(way, d)
        slot = p if (way == 0 or d > 1) else chips
        return remote(
            part_ref.at[p, place.core, 0, pieces[n]],
            far_ref.at[slot, pieces[n]],
            zs.at[way, d, n],
            zr.at[way, d, n],
            place.along(1 - 2 * way),
        )

    def inward(way, d, n):
        mine = far_ref.at[landing(way, d), pieces[n]]
        return remote(mine, mine, zs.at[way, d + 1, n], zr.at[way, d + 1, n], place.along(1 - 2 * way))

    for load in loads:
        load.wait()
    gather.from_sibling(0, 0).wait_recv()
    work(place.chip)
    for d in range(1, chips):
        gather.forward(d)
        for way in range(2):
            @pl.when(exists(way, d))
            def _(way=way, d=d):
                gather.from_sibling(1 - way, d).wait_recv()
                work(target(way, d))

        if d == 1:
            settle(place.chip)
        for way in range(2):

            @pl.when(exists(way, d))
            def _(way=way, d=d):
                settle(target(way, d))

                @pl.when(jnp.logical_not(upstream(way)))
                def _():
                    for n in range(2):
                        onward(way, d, n).start()

    seq = ctx * tokens
    dwm_ref[...] = dot_tn(n_all[...].reshape(seq, width), gub_all[...]).astype(bf16).reshape(dwm_ref.shape)
    down_cols = dwd_ref.shape[2]
    wide_ref[...] = dot_tn(cot_ref[...].reshape(seq, width), hid_all[...])
    for c in range(ctx):
        dwd_ref[c] = wide_ref[pl.ds(c * down_cols, down_cols), :].T.astype(bf16)

    for d in range(chips - 1, 0, -1):
        for way in range(2):

            @pl.when(jnp.logical_and(exists(way, d), upstream(way)))
            def _(way=way, d=d):
                p = target(way, d)
                for n, rows in enumerate(pieces):
                    inward(way, d, n).wait_recv()
                    both = part_ref[p, place.core, 0, rows].astype(f32) + far_ref[p, rows].astype(f32)
                    part_ref[p, place.core, 0, rows] = both.astype(bf16)
                    onward(way, d, n).start()

    ngrad_ref[...] = part_ref[place.chip, place.core, 0].astype(f32)
    for way in range(2):

        @pl.when(upstream(way))
        def _(way=way):
            for n in range(2):
                inward(way, 0, n).wait_recv()
            ngrad_ref[...] += far_ref[landing(way, 0)].astype(f32)

    gather.finish()
    for p in range(chips):
        to_sibling(p).wait_send()
    for d in range(1, chips):
        for way in range(2):

            @pl.when(exists(way, d))
            def _(way=way, d=d):
                for n in range(2):
                    onward(way, d, n).wait_send()


def back_kernel(sizes, *refs):
    refs = iter(refs)
    (q_ref, attn_ref, kv_in, lse_ref, cos_ref, sin_ref, posk_ref, posq_ref, dwm_ref, dwd_ref) = take(refs, 10)
    ngrad_ref, mid_ref, gain_ref, cot_ref, wo_in = take(refs, 5)
    qkvb_ref, fin_mlp, fin_down, mgrad_ref, midb_ref, gain_part = take(refs, 6)
    g_ref, mid_turned, q_back, kv_back = take(refs, 4)
    delta_ref, qz_ref, gz_ref, acc_ref, part_ref, sib_ref, far_ref = take(refs, 7)
    dwm_recv, down_rows, down_recv = take(refs, 3)
    bs, br, zs, zr = take(refs, 4)
    wm_sems, a2a_sems, wd_sems = take(refs, 2), take(refs, 2), take(refs, 2)
    kv_ref, wo_ref, load_sems = take(refs, 3)
    load_out = pltpu.make_async_copy(wo_in, wo_ref, load_sems.at[0])
    load_kv = pltpu.make_async_copy(kv_in, kv_ref, load_sems.at[1])
    load_out.start()
    load_kv.start()

    place = Place(sizes)
    ctx, chips, row_parts = place.ctx, place.chips, place.row_parts
    tokens = q_ref.shape[1]
    chunk, wide = 2 * tokens, GROUP * tokens
    ff_part = dwd_ref.shape[1]
    per_row = ctx // row_parts
    scale = 1.0 / math.sqrt(HEAD_DIM)

    mlp = RowExchange(place, lambda k: dwm_ref.at[place.row_at(k)], lambda k, back: dwm_recv.at[k], wm_sems)

    def down_slot(c):
        return down_rows.at[c // per_row, pl.ds(pl.multiple_of((c % per_row) * ff_part, 16), ff_part), :]

    spread = CtxExchange(place, lambda c: dwd_ref.at[c], down_slot, a2a_sems)
    down = RowExchange(place, lambda k: down_rows.at[place.row_at(k)], lambda k, back: down_recv.at[k], wd_sems)

    place.greet(ctx=True, rows=True)
    mlp.start()
    spread.start()
    down_slot(place.c)[...] = dwd_ref[place.c]

    inverse_rms, unit, _ = norm_forward(mid_ref[...], gain_ref[...])
    mlp_back, gain_part[0] = norm_backward(ngrad_ref[...], inverse_rms, unit, gain_ref[...])
    mid_grad = cot_ref[...].astype(f32).T + mlp_back
    mgrad_ref[...] = mid_grad
    mid_turned[...] = mid_grad.T
    out_cols = wo_ref.shape[3]
    load_out.wait()
    load_kv.wait()
    total = jnp.zeros(g_ref.shape, f32)
    for c in range(ctx):
        piece = mid_turned[pl.ds(c * out_cols, out_cols), :].astype(bf16)
        midb_ref[c] = piece
        total = total + dot_nn(wo_ref[c].reshape(g_ref.shape[0], out_cols), piece)
    g_ref[...] = total.astype(bf16)

    zeros = jnp.zeros((HEAD_DIM, wide), bf16)
    for g in range(KV_HEADS):
        query = group_rows(q_ref, g) * jnp.asarray(scale, bf16)
        grad = group_rows(g_ref, g)
        qz_ref[g] = jnp.concatenate([query, zeros], axis=0)
        gz_ref[g] = jnp.concatenate([zeros, grad], axis=0)
        delta_ref[g] = jnp.sum(grad.astype(f32) * group_rows(attn_ref, g).astype(f32), axis=0, keepdims=True)
        acc_ref[g] = jnp.zeros_like(acc_ref[g])
    query_pos = posq_ref[...]

    def to_sibling(j):
        return remote(part_ref.at[j, 1 - place.core], sib_ref.at[j], bs.at[j], br.at[j], place.sibling())

    def to_owner(j):
        return remote(part_ref.at[j, place.core], far_ref.at[j], zs.at[j], zr.at[j], place.along(j))

    def settle(j):
        to_sibling(j).wait_recv()
        both = part_ref[j, place.core].astype(f32) + sib_ref[j].astype(f32)
        part_ref[j, place.core] = both.astype(bf16)

    def work(j):
        p = place.chip_at(j)
        rows = pl.ds(pl.multiple_of(p * chunk, chunk), chunk)
        allowed = posk_ref[rows, :] <= query_pos
        for g in range(KV_HEADS):
            lanes = pl.ds(g * 2 * HEAD_DIM, 2 * HEAD_DIM)
            keys = kv_ref[pl.ds(2 * p, 2), :, lanes].reshape(chunk, 2 * HEAD_DIM)
            query, grad = qz_ref[g], gz_ref[g]
            scores = jnp.where(allowed, dot_nn(keys, query), MASKED)
            prob = jnp.exp(scores - lse_ref[g])
            score_grad = (prob * (dot_nn(keys, grad) - delta_ref[g])).astype(bf16)
            both = dot_nt(score_grad, query) + dot_nt(prob.astype(bf16), grad)
            part_ref[j, :, :, lanes] = both.astype(bf16).reshape(2, tokens, 2 * HEAD_DIM)
            acc_ref[g] += dot_tn(keys, score_grad)
        to_sibling(j).start()

    work(1)

    def turn(j, carry):
        work(j)
        settle(j - 1)
        to_owner(j - 1).start()
        return carry

    lax.fori_loop(2, chips, turn, 0)
    spread.arrive()
    down.start()
    work(0)
    settle(chips - 1)
    to_owner(chips - 1).start()
    cosine, sine = cos_ref[...], sin_ref[...]
    for h in range(HEADS):
        g, j = h // GROUP, h % GROUP
        head = acc_ref[g, pl.ds(0, HEAD_DIM), pl.ds(j * tokens, tokens)] * scale
        q_back[pl.ds(h * HEAD_DIM, HEAD_DIM), :] = rotate_rows_back(head, cosine, sine)
    settle(0)
    mlp.arrive()
    total = dwm_ref[place.row].astype(f32)
    for k in range(1, row_parts):
        total = total + dwm_recv[k].astype(f32)
    fin_mlp[...] = total
    down.arrive()
    total = down_rows[place.row].astype(f32)
    for k in range(1, row_parts):
        total = total + down_recv[k].astype(f32)
    fin_down[...] = total
    total = part_ref[0, place.core].astype(f32)
    for j in range(1, chips):
        to_owner(j).wait_recv()
        total = total + far_ref[j].astype(f32)
    total = total.T
    kv_width = KV_HEADS * HEAD_DIM
    for g in range(KV_HEADS):
        pair = total[g * 2 * HEAD_DIM : (g + 1) * 2 * HEAD_DIM]
        rows = pl.ds(g * HEAD_DIM, HEAD_DIM)
        kv_back[rows, :] = rotate_rows_back(pair[:HEAD_DIM], cosine, sine)
        kv_back[pl.ds(kv_width + g * HEAD_DIM, HEAD_DIM), :] = pair[HEAD_DIM:]
    q_cols, kv_cols = q_back.shape[0] // ctx, kv_width // ctx
    for c in range(ctx):
        qkvb_ref[c] = jnp.concatenate(
            [
                q_back[pl.ds(c * q_cols, q_cols), :],
                kv_back[pl.ds(c * kv_cols, kv_cols), :],
                kv_back[pl.ds(kv_width + c * kv_cols, kv_cols), :],
            ],
            axis=0,
        ).astype(bf16)
    for part in (mlp, spread, down):
        part.finish()
    for j in range(chips):
        to_sibling(j).wait_send()
        if j:
            to_owner(j).wait_send()


def last_kernel(sizes, *refs):
    refs = iter(refs)
    n1_ref, qkvb_ref, attn_ref, midb_ref, osums_ref, mid_ref = take(refs, 6)
    x_ref, gain_ref, gain_part, mgrad_ref, wqkv_in = take(refs, 5)
    fin_ref, gain_out, result_ref, input_ref = take(refs, 4)
    part_ref, sib_ref, bent_ref, row_ref, far_send, far_ref = take(refs, 6)
    gain_sib, gain_row, gain_far, gain_a, gain_b, gain_c = take(refs, 6)
    bs, br, vs, vr, xs, xr, zs, zr = take(refs, 8)
    gb, gx, gz = take(refs, 2), take(refs, 2), take(refs, 2)
    osum_own, osum_far, mid_sum, os, orr = take(refs, 5)
    wqkv_ref, load_sems = take(refs, 2)
    load = pltpu.make_async_copy(wqkv_in, wqkv_ref, load_sems.at[0])
    load.start()

    place = Place(sizes)
    chips, row_parts, outer, inner = place.chips, place.row_parts, place.rows_outer, place.rows_inner
    core, row, chip = place.core, place.row, place.chip
    in_rows = fin_ref.shape[0]
    half = (in_rows // 2 + 15) // 16 * 16
    parts = (pl.ds(0, half), pl.ds(half, in_rows - half))
    sized = (pl.ds(0, half), pl.ds(0, in_rows - half))
    sides = [(a, 0) for a in range(1, outer)] + [(0, b) for b in range(1, inner)]
    diagonal = [(a, b) for a in range(1, outer) for b in range(1, inner)]
    place.greet(line=True, sibling=True, rows=True)

    def row_of(a, b):
        return wrap(place.seq + a, outer) * inner + wrap(place.fsdp + b, inner)

    def device(a, b):
        return (wrap(place.seq + a, outer), wrap(place.fsdp + b, inner), place.c)

    def to_sibling(j):
        return remote(
            part_ref.at[place.chip_at(j) * 2 + 1 - core], sib_ref.at[j], bs.at[j], br.at[j], place.sibling()
        )

    def bent(j, part, n):
        a, b = diagonal[n]
        return remote(
            sib_ref.at[j, row_of(a, b), parts[part]],
            bent_ref.at[j, part, n, sized[part]],
            vs.at[j, part, n],
            vr.at[j, part, n],
            device(0, b) if part == 0 else device(a, 0),
        )

    def direct(j, n):
        a, b = sides[n]
        return remote(sib_ref.at[j, row_of(a, b)], row_ref.at[j, n], xs.at[j, n], xr.at[j, n], device(a, b))

    def to_owner(j):
        return remote(far_send.at[j], far_ref.at[j], zs.at[j], zr.at[j], place.along(j))

    def g_sib():
        return remote(gain_a, gain_sib.at[core], gb[0].at[0], gb[1].at[0], place.sibling())

    def g_row(k):
        return remote(gain_b, gain_row.at[row], gx[0].at[k], gx[1].at[k], place.across(k))

    def g_far(j):
        return remote(gain_c, gain_far.at[chip], gz[0].at[j], gz[1].at[j], place.along(j))

    def input_gradient():
        width = x_ref.shape[0]
        load.wait()
        total = jnp.zeros(x_ref.shape, f32)
        for c in range(place.ctx):
            total = total + dot_nn(wqkv_ref[c].reshape(width, wqkv_ref.shape[3]), qkvb_ref[c])
        inverse_rms, unit, _ = norm_forward(x_ref[...].astype(f32).T, gain_ref[...])
        back, gain_a[0] = norm_backward(total.T, inverse_rms, unit, gain_ref[...])
        input_ref[...] = (mgrad_ref[...] + back).T.astype(bf16)
        gain_a[1] = gain_part[0]
        gain_sib[core] = gain_a[...]
        g_sib().start()

    def multiply(j):
        for k in range(2):
            c = place.chip_at(j) * 2 + k
            both = jnp.concatenate(
                [dot_nt(n1_ref[...], qkvb_ref[c]), dot_nt(attn_ref[...], midb_ref[c])], axis=1
            )
            part_ref[c] = both.astype(bf16).reshape(part_ref.shape[1:])
        to_sibling(j).start()

    def add_sibling(j):
        to_sibling(j).wait_recv()
        both = part_ref[place.chip_at(j) * 2 + core].astype(f32) + sib_ref[j].astype(f32)
        sib_ref[j] = both.astype(bf16)
        for n in range(len(diagonal)):
            for part in range(2):
                bent(j, part, n).start()

    def add_bent(j):
        for n, (a, b) in enumerate(diagonal):
            for part in range(2):
                bent(j, part, n).wait_recv()
                at = (j, row_of(a, 0) if part == 0 else row_of(0, b), parts[part])
                both = sib_ref[at].astype(f32) + bent_ref[j, part, n, sized[part]].astype(f32)
                sib_ref[at] = both.astype(bf16)
        for n in range(len(sides)):
            direct(j, n).start()

    def add_rows(j):
        total = sib_ref[j, row].astype(f32)
        for n in range(len(sides)):
            direct(j, n).wait_recv()
            total = total + row_ref[j, n].astype(f32)
        if j:
            far_send[j] = total.astype(bf16)
            to_owner(j).start()
        else:
            fin_ref[...] = total

    def target(way, d):
        return chip + d if way == 0 else chip - d

    def exists(way, d):
        return chip + d < chips if way == 0 else chip >= d

    def upstream(way):
        return chip >= 1 if way == 0 else chip + 1 < chips

    def output_on(way, d):
        p = target(way, d)
        slot = p if (way == 0 or d > 1) else chips
        return remote(osum_own.at[p], osum_far.at[slot], os.at[way, d], orr.at[way, d], place.along(1 - 2 * way))

    def output_in(way, d):
        mine = osum_far.at[target(way, d) if (way == 0 or d) else chips]
        return remote(mine, mine, os.at[way, d + 1], orr.at[way, d + 1], place.along(1 - 2 * way))

    osum_own[...] = osums_ref[...]
    for d in range(chips - 1, 0, -1):
        for way in range(2):

            @pl.when(jnp.logical_and(exists(way, d), jnp.logical_not(upstream(way))))
            def _(way=way, d=d):
                output_on(way, d).start()

    def output_turn(d):
        for way in range(2):

            @pl.when(jnp.logical_and(exists(way, d), upstream(way)))
            def _(way=way):
                p = target(way, d)
                output_in(way, d).wait_recv()
                osum_own[p] = (osum_own[p].astype(f32) + osum_far[p].astype(f32)).astype(bf16)
                output_on(way, d).start()

    order = list(range(1, chips)) + [0]
    stages = (multiply, add_sibling, add_bent, add_rows)
    for t in range(chips + len(stages) - 1):
        for depth, stage in enumerate(stages):
            if 0 <= t - depth < chips:
                stage(order[t - depth])
        if t == 1:
            input_gradient()
        if 1 <= chips - 1 - t < chips - 1:
            output_turn(chips - 1 - t)
        if t == 3:
            remote(gain_a, gain_sib.at[1 - core], gb[0].at[0], gb[1].at[0], place.sibling()).wait_recv()
            gain_b[...] = gain_sib[0] + gain_sib[1]
            gain_row[row] = gain_b[...]
            for k in range(1, row_parts):
                g_row(k).start()

    for k in range(1, row_parts):
        remote(gain_b, gain_row.at[place.row_at(-k)], gx[0].at[k], gx[1].at[k], place.across(k)).wait_recv()
    total = gain_row[0]
    for k in range(1, row_parts):
        total = total + gain_row[k]
    gain_c[...] = total
    gain_far[chip] = gain_c[...]
    for j in range(1, chips):
        g_far(j).start()
    mid_sum[...] = mid_ref[...] + osum_own[chip].astype(f32)
    for way in range(2):

        @pl.when(upstream(way))
        def _(way=way):
            output_in(way, 0).wait_recv()
            mid_sum[...] += osum_far[chip if way == 0 else chips].astype(f32)

    result_ref[...] = mid_sum[...].T.astype(bf16)
    total = fin_ref[...]
    for j in range(1, chips):
        to_owner(j).wait_recv()
        total = total + far_ref[j].astype(f32)
    fin_ref[...] = total
    for j in range(1, chips):
        remote(gain_c, gain_far.at[place.chip_at(-j)], gz[0].at[j], gz[1].at[j], place.along(j)).wait_recv()
    total = gain_far[0]
    for j in range(1, chips):
        total = total + gain_far[j]
    gain_out[...] = total

    g_sib().wait_send()
    for k in range(1, row_parts):
        g_row(k).wait_send()
    for j in range(1, chips):
        g_far(j).wait_send()
    for j in order:
        to_sibling(j).wait_send()
        for n in range(len(diagonal)):
            for part in range(2):
                bent(j, part, n).wait_send()
        for n in range(len(sides)):
            direct(j, n).wait_send()
        if j:
            to_owner(j).wait_send()
    for d in range(1, chips):
        for way in range(2):

            @pl.when(exists(way, d))
            def _(way=way, d=d):
                output_on(way, d).wait_send()


def finish_kernel(cuts, *refs):
    refs = iter(refs)
    attn_ref, mlp_ref, down_ref, result_ref, input_ref, gain_ref = take(refs, 6)
    q_cols, kv_cols, ff_cols = cuts
    outs = take(refs, 11)
    attn, mlp = attn_ref[...], mlp_ref[...]
    outs[0][...] = result_ref[...]
    outs[1][...] = input_ref[...]
    outs[2][...] = gain_ref[0]
    outs[3][...] = gain_ref[1]
    outs[4][...] = attn[:, :q_cols]
    outs[5][...] = attn[:, q_cols : q_cols + kv_cols].T
    outs[6][...] = attn[:, q_cols + kv_cols : q_cols + 2 * kv_cols].T
    outs[7][...] = attn[:, q_cols + 2 * kv_cols :]
    outs[8][...] = mlp[:, :ff_cols].T
    outs[9][...] = mlp[:, ff_cols:].T
    outs[10][...] = down_ref[...].T


def finish(cuts, inputs, outs):
    vmem = pl.BlockSpec(memory_space=pltpu.VMEM)
    return pl.pallas_call(
        functools.partial(finish_kernel, cuts),
        out_shape=[jax.ShapeDtypeStruct(shape, kind) for shape, kind in outs],
        in_specs=[vmem] * len(inputs),
        out_specs=[vmem] * len(outs),
    )(*inputs)


def call(kernel, sizes, inputs, outs, scratch, collective_id, raw=(), raw_outs=()):
    vmem = pl.BlockSpec(memory_space=pltpu.VMEM)
    anywhere = pl.BlockSpec(memory_space=pl.ANY)
    return pl.pallas_call(
        functools.partial(kernel, sizes),
        out_shape=[jax.ShapeDtypeStruct(shape, kind) for shape, kind in outs],
        in_specs=[anywhere if i in raw else vmem for i in range(len(inputs))],
        out_specs=[anywhere if i in raw_outs else vmem for i in range(len(outs))],
        scratch_shapes=scratch,
        compiler_params=pltpu.CompilerParams(
            collective_id=collective_id, has_side_effects=True, vmem_limit_bytes=60 * 1024 * 1024
        ),
    )(*inputs)


def on_device(
    tokens,
    cotangent,
    block_order,
    gain_attn,
    gain_mlp,
    w_query,
    w_key,
    w_value,
    w_out,
    w_gate,
    w_up,
    w_down,
):
    sizes = tuple(lax.axis_size(n) for n in ("seq", "fsdp", "ctx"))
    rows, ctx = sizes[0] * sizes[1], sizes[2]
    chips = ctx // 2
    row_count, width = tokens.shape[1], tokens.shape[2]
    seq_len = row_count * ctx
    block_total = block_order.shape[0]
    block_len = seq_len // block_total
    kv_width = KV_HEADS * HEAD_DIM
    q_width = HEADS * HEAD_DIM
    q_cols, kv_cols, ff_cols = w_query.shape[1], w_key.shape[1], w_gate.shape[1]
    out_cols, down_cols, down_rows = w_out.shape[1], w_down.shape[1], w_down.shape[0]
    in_rows = w_query.shape[0]
    qkv_cols = q_cols + 2 * kv_cols
    wide = GROUP * row_count

    slot_index = jnp.arange(seq_len, dtype=jnp.int32)
    owner_hit = (slot_index // block_len)[:, None] == jnp.arange(block_total, dtype=jnp.int32)[None, :]
    all_pos = (
        jnp.sum(jnp.where(owner_hit, block_order[None, :], 0), axis=1) * block_len + slot_index % block_len
    )
    own_pos = lax.dynamic_slice_in_dim(all_pos, lax.axis_index("ctx") * row_count, row_count)
    inverse = rope_base ** (-jnp.arange(HALF, dtype=f32) / HALF)
    angles = inverse[:, None] * own_pos.astype(f32)[None, :]
    cosine, sine = jnp.cos(angles), jnp.sin(angles)
    pos_keys = all_pos[:, None]
    pos_query = jnp.tile(own_pos, GROUP)[None, :]

    x = tokens[0]
    cot_rows = cotangent[0]
    turned = [jnp.transpose(w) for w in (w_key, w_value, w_gate, w_up, w_down)]
    wk_t, wv_t, wg_t, wu_t, wd_t = turned

    (
        attn_t,
        query_t,
        kv_all,
        lse,
        qkv_full,
        out_full,
        mlp_full,
        down_t,
        cot_all,
        normed_attn_t,
        middle,
        normed_mlp,
    ) = call(
        first_kernel,
        sizes,
        (
            jnp.transpose(x),
            gain_attn[None],
            gain_mlp[None],
            w_query,
            wk_t,
            wv_t,
            w_out,
            wg_t,
            wu_t,
            wd_t,
            jnp.transpose(cot_rows),
            cosine,
            sine,
            pos_keys,
            pos_query,
        ),
        [
            ((q_width, row_count), bf16),
            ((q_width, row_count), bf16),
            ((ctx, row_count, 2 * kv_width), bf16),
            ((KV_HEADS, 1, wide), f32),
            ((ctx, rows, in_rows, qkv_cols), bf16),
            ((ctx, rows, in_rows, out_cols), bf16),
            ((rows, in_rows, 2 * ff_cols), bf16),
            ((width, ff_cols), bf16),
            ((ctx, row_count, width), bf16),
            ((width, row_count), bf16),
            ((row_count, width), f32),
            ((row_count, width), bf16),
        ],
        [
            pltpu.VMEM((q_width + 2 * kv_width, row_count), f32),
            pltpu.VMEM((row_count, 2 * kv_width), bf16),
            pltpu.VMEM((rows, down_rows, down_cols), bf16),
            pltpu.VMEM((seq_len, wide), f32),
            pltpu.VMEM((ctx, ff_cols, down_cols), bf16),
            pltpu.VMEM((width, row_count), f32),
            pltpu.VMEM((width, ff_cols), f32),
            pltpu.VMEM((width, row_count), bf16),
        ]
        + [pltpu.VMEM(w.shape, bf16) for w in (w_query, wk_t, wv_t, w_out, wg_t, wu_t, wd_t)]
        + [
            pltpu.VMEM((width, row_count), bf16),
            pltpu.VMEM((in_rows, qkv_cols), bf16),
            pltpu.VMEM((in_rows, 2 * ff_cols), bf16),
            pltpu.VMEM(w_down.shape, bf16),
            pltpu.VMEM((row_count, width), bf16),
            dma(9),
        ]
        + FullGather.scratch(sizes)
        + FullGather.scratch(sizes)
        + LineGather.scratch(sizes)
        + LineGather.scratch(sizes)
        + RowExchange.scratch(sizes)
        + RowExchange.scratch(sizes)
        + CtxExchange.scratch(sizes)
        + [
            pltpu.VMEM((ctx, row_count, 2 * kv_width), bf16),
            pltpu.VMEM((ctx, rows, in_rows, qkv_cols), bf16),
            pltpu.VMEM((ctx, rows, in_rows, out_cols), bf16),
            pltpu.VMEM((ctx, row_count, width), bf16),
            dma(4),
        ],
        1,
        raw=(0, 3, 4, 5, 6, 7, 8, 9, 10),
        raw_outs=(2, 4, 5, 8),
    )

    w_mlp_cat = mlp_full.reshape(width, 2 * ff_cols)

    normed_mlp_grad, output_sums, d_mlp, d_down = call(
        mlp_kernel,
        sizes,
        (normed_mlp, cot_all, w_mlp_cat, down_t),
        [
            ((row_count, width), f32),
            ((chips, row_count, width), bf16),
            ((rows, in_rows, 2 * ff_cols), bf16),
            ((ctx, ff_cols, down_cols), bf16),
        ],
        [
            pltpu.VMEM((ctx, row_count, width), bf16),
            pltpu.VMEM((seq_len, 2 * ff_cols), bf16),
            pltpu.VMEM((seq_len, ff_cols), bf16),
            pltpu.VMEM((chips, 2, 2, row_count, width), bf16),
            pltpu.VMEM((chips, 2, row_count, width), bf16),
            pltpu.VMEM((chips + 1, row_count, width), bf16),
            pltpu.VMEM((width, ff_cols), f32),
        ]
        + LineGather.scratch(sizes)
        + [dma(chips)] * 2
        + [dma(2, chips, 2)] * 2
        + [
            pltpu.VMEM((ctx, row_count, width), bf16),
            pltpu.VMEM((width, 2 * ff_cols), bf16),
            pltpu.VMEM((width, ff_cols), bf16),
            dma(3),
        ],
        2,
        raw=(1, 2, 3),
    )
    qkv_back_t, fin_mlp, fin_down, mid_grad, mid_back_t, gain_mlp_part = call(
        back_kernel,
        sizes,
        (
            query_t,
            attn_t,
            kv_all,
            lse,
            cosine,
            sine,
            pos_keys,
            pos_query,
            d_mlp,
            d_down,
            normed_mlp_grad,
            middle,
            gain_mlp[None],
            jnp.transpose(cot_rows),
            out_full,
        ),
        [
            ((ctx, qkv_cols, row_count), bf16),
            ((in_rows, 2 * ff_cols), f32),
            ((down_rows, down_cols), f32),
            ((row_count, width), f32),
            ((ctx, out_cols, row_count), bf16),
            ((1, width), f32),
        ],
        [
            pltpu.VMEM((q_width, row_count), bf16),
            pltpu.VMEM((width, row_count), f32),
            pltpu.VMEM((q_width, row_count), f32),
            pltpu.VMEM((2 * kv_width, row_count), f32),
            pltpu.VMEM((KV_HEADS, 1, wide), f32),
            pltpu.VMEM((KV_HEADS, 2 * HEAD_DIM, wide), bf16),
            pltpu.VMEM((KV_HEADS, 2 * HEAD_DIM, wide), bf16),
            pltpu.VMEM((KV_HEADS, 2 * HEAD_DIM, wide), f32),
            pltpu.VMEM((chips, 2, row_count, 2 * kv_width), bf16),
            pltpu.VMEM((chips, row_count, 2 * kv_width), bf16),
            pltpu.VMEM((chips, row_count, 2 * kv_width), bf16),
            pltpu.VMEM((rows, in_rows, 2 * ff_cols), bf16),
            pltpu.VMEM((rows, down_rows, down_cols), bf16),
            pltpu.VMEM((rows, down_rows, down_cols), bf16),
        ]
        + [dma(chips)] * 4
        + RowExchange.scratch(sizes)
        + CtxExchange.scratch(sizes)
        + RowExchange.scratch(sizes)
        + [
            pltpu.VMEM((ctx, row_count, 2 * kv_width), bf16),
            pltpu.VMEM((ctx, rows, in_rows, out_cols), bf16),
            dma(2),
        ],
        3,
        raw=(2, 14),
    )

    attn_cols = qkv_cols + out_cols
    gains = pltpu.VMEM((2, width), f32)
    half = (in_rows // 2 + 15) // 16 * 16
    corners, sides = (sizes[0] - 1) * (sizes[1] - 1), sizes[0] + sizes[1] - 2
    fin_attn, gain_sums, result_t, input_t = call(
        last_kernel,
        sizes,
        (
            normed_attn_t,
            qkv_back_t,
            attn_t,
            mid_back_t,
            output_sums,
            middle,
            jnp.transpose(x),
            gain_attn[None],
            gain_mlp_part,
            mid_grad,
            qkv_full,
        ),
        [
            ((in_rows, attn_cols), f32),
            ((2, width), f32),
            ((width, row_count), bf16),
            ((width, row_count), bf16),
        ],
        [
            pltpu.VMEM((ctx, rows, in_rows, attn_cols), bf16),
            pltpu.VMEM((chips, rows, in_rows, attn_cols), bf16),
            pltpu.VMEM((chips, 2, corners, half, attn_cols), bf16),
            pltpu.VMEM((chips, sides, in_rows, attn_cols), bf16),
            pltpu.VMEM((chips, in_rows, attn_cols), bf16),
            pltpu.VMEM((chips, in_rows, attn_cols), bf16),
            pltpu.VMEM((2, 2, width), f32),
            pltpu.VMEM((rows, 2, width), f32),
            pltpu.VMEM((chips, 2, width), f32),
            gains,
            gains,
            gains,
            dma(chips),
            dma(chips),
            dma(chips, 2, corners),
            dma(chips, 2, corners),
            dma(chips, sides),
            dma(chips, sides),
            dma(chips),
            dma(chips),
            dma(1),
            dma(1),
            dma(rows),
            dma(rows),
            dma(chips),
            dma(chips),
            pltpu.VMEM((chips, row_count, width), bf16),
            pltpu.VMEM((chips + 1, row_count, width), bf16),
            pltpu.VMEM((row_count, width), f32),
            dma(2, chips),
            dma(2, chips),
            pltpu.VMEM((ctx, rows, in_rows, qkv_cols), bf16),
            dma(1),
        ],
        4,
        raw=(10,),
    )
    outs = finish(
        (q_cols, kv_cols, ff_cols),
        (fin_attn, fin_mlp, fin_down, result_t, input_t, gain_sums),
        [
            ((width, row_count), bf16),
            ((width, row_count), bf16),
            ((width,), f32),
            ((width,), f32),
            ((in_rows, q_cols), f32),
            ((kv_cols, in_rows), f32),
            ((kv_cols, in_rows), f32),
            ((in_rows, out_cols), f32),
            ((ff_cols, in_rows), f32),
            ((ff_cols, in_rows), f32),
            ((down_cols, down_rows), f32),
        ],
    )
    flip = jnp.transpose
    return (
        flip(outs[0]).reshape(1, row_count, width),
        flip(outs[1]).reshape(1, row_count, width),
        outs[2],
        outs[3],
        outs[4],
        flip(outs[5]),
        flip(outs[6]),
        outs[7],
        flip(outs[8]),
        flip(outs[9]),
        flip(outs[10]),
    )


def solution(mesh):
    return jax.shard_map(
        on_device,
        mesh=mesh,
        in_specs=(
            P(("seq", "fsdp"), "ctx", None),
            P(("seq", "fsdp"), "ctx", None),
            P(),
            P(),
            P(),
            P(("seq", "fsdp"), "ctx"),
            P(("seq", "fsdp"), "ctx"),
            P(("seq", "fsdp"), "ctx"),
            P(("seq", "fsdp"), "ctx"),
            P(("seq", "fsdp"), "ctx"),
            P(("seq", "fsdp"), "ctx"),
            P(("seq", "fsdp"), "ctx"),
        ),
        out_specs=(
            P(("seq", "fsdp"), "ctx", None),
            P(("seq", "fsdp"), "ctx", None),
            P(),
            P(),
            P(("seq", "fsdp"), "ctx"),
            P(("seq", "fsdp"), "ctx"),
            P(("seq", "fsdp"), "ctx"),
            P(("seq", "fsdp"), "ctx"),
            P(("seq", "fsdp"), "ctx"),
            P(("seq", "fsdp"), "ctx"),
            P(("seq", "fsdp"), "ctx"),
        ),
        check_vma=False,
    )
```
